32 devices in a mesh: ctx: 8 (over z, y), wt: 4 (over x, core).
Axes of the slice: x: 2, y: 2, z: 4, core: 2. Of those that a mesh axis runs over, the one named last changes fastest.
Arguments:
- layer_input: bfloat16 [4, 1024, 1024], P('wt', 'ctx'), may hold values from -6 to 6
- out_grad: bfloat16 [4, 1024, 1024], P('wt', 'ctx'), may hold values from -6 to 6
- deal: int32 [8, 2], replicated, may hold values from 0 to 15, as said below
- w_qkv: bfloat16 [1024, 3072], P('wt'), may hold values from -0.1875 to 0.1875
- w_out: bfloat16 [1024, 1024], P('wt'), may hold values from -0.1875 to 0.1875
- w_up: bfloat16 [1024, 4096], P('wt'), may hold values from -0.1875 to 0.1875
- w_down: bfloat16 [4096, 1024], P('wt'), may hold values from -0.09375 to 0.09375
- norm_gain: bfloat16 [4, 1024], P(None, 'wt'), may hold values from 0.099609375 to 1.8984375
- norm_shift: bfloat16 [4, 1024], P(None, 'wt'), may hold values from -1.5 to 1.5
- bias_width: bfloat16 [4, 1024], P(None, 'wt'), may hold values from -2.5 to 2.5
- up_bias: bfloat16 [4096], P('wt'), may hold values from -2.5 to 2.5
Outputs:
- layer_out: bfloat16 [4, 1024, 1024], P('wt', 'ctx')
- input_grad: float32 [4, 1024, 1024], P('wt', 'ctx')
- grad_qkv: float32 [1024, 3072], P('wt')
- grad_out: float32 [1024, 1024], P('wt')
- grad_up: float32 [1024, 4096], P('wt')
- grad_down: float32 [4096, 1024], P('wt')
- grad_gain: float32 [4, 1024], P(None, 'wt')
- grad_shift: float32 [4, 1024], P(None, 'wt')
- grad_bias: float32 [4, 1024], P(None, 'wt')
- grad_up_bias: float32 [4096], P('wt')
The draws below stay inside these ranges and needn't reach their ends.
Inputs may be any that keep to these rules, and one draw needn't show every extreme that they name: `deal`: pieces of 64 tokens are numbered along a sequence. Row j holds a number p below 8 and its mirror 1024 // 64 - 1 - p; every piece appears once.
All inputs are finite; a program needn't handle non-finite values.
Results may differ from the reference program's by a relative error of at most 0.015.
Values may be sent and summed in bfloat16 or wider, within the bound.
No kernel may reach another device: no remote copies, remote signals or barrier semaphores. Data moves between devices by JAX's collectives and lax.ppermute only.
A program may use at most 320 MiB of HBM per device.

```python
import math
import jax
import jax.numpy as jnp
from jax import lax

D = 1024
HEADS = 16
FF = 4096
BLK = 256
PIECE = 64
SEQ_LEN = 1024
SEQS = 4


def draw_deal(key, part):
    half = SEQ_LEN // PIECE // 2
    first = jax.random.permutation(key, half).astype(jnp.int32)
    return jnp.stack([first, 2 * half - 1 - first], axis=1)


def level_of(own_key, shape, pieces, least, high):
    level, own = 1.0, jax.random.fold_in(own_key, 6)
    for dim, blocks in pieces:
        draws = jnp.exp(jax.random.uniform(jax.random.fold_in(own, dim), (blocks,), jnp.float32, least / len(pieces), high / len(pieces)))
        level = level * jnp.repeat(draws, shape[dim] // blocks).reshape([-1 if axis == dim else 1 for axis in range(len(shape))])
    return level


def normal_values(own_key, dims, scale, most, cuts=(), dtype=jnp.bfloat16):
    entries = jax.random.normal(own_key, dims, jnp.float32) * scale
    if len(cuts) > 0:
        entries = level_of(own_key, dims, cuts, -0.22, 0.18) * entries
    return jnp.clip(entries, min=-most, max=most).astype(dtype)


def setup_inputs(seed: int = 0) -> dict:
    streams_of = jax.random.split(jax.random.key(seed), 12)
    layer_input = normal_values(streams_of[0], (SEQS, SEQ_LEN, D), 1.0, 6.0, ((0, 4), (1, 8)))
    out_grad = normal_values(streams_of[1], (SEQS, SEQ_LEN, D), 1.0, 6.0, ((0, 4), (1, 8)))
    deal = draw_deal(jax.random.fold_in(streams_of[11], 71), 0)
    w_qkv = normal_values(streams_of[3], (D, 3 * D), D ** -0.5, 0.1875, ((0, 4),))
    w_out = normal_values(streams_of[4], (D, D), D ** -0.5, 0.1875, ((0, 4),))
    w_up = normal_values(streams_of[5], (D, FF), D ** -0.5, 0.1875, ((0, 4),))
    w_down = normal_values(streams_of[6], (FF, D), FF ** -0.5, 0.09375, ((0, 4),))
    norm_gain = jnp.clip(1.0 + 0.18 * jax.random.normal(streams_of[7], (4, D), jnp.float32), 0.099609375, 1.8984375).astype(jnp.bfloat16)
    norm_shift = normal_values(streams_of[8], (4, D), 0.3, 1.5, ((1, 4),))
    bias_width = normal_values(streams_of[9], (4, D), 0.5, 2.5, ((1, 4),))
    up_bias = normal_values(streams_of[10], (FF,), 0.5, 2.5, ((0, 4),))
    return dict(layer_input=layer_input, out_grad=out_grad, deal=deal, w_qkv=w_qkv, w_out=w_out, w_up=w_up, w_down=w_down, norm_gain=norm_gain, norm_shift=norm_shift, bias_width=bias_width, up_bias=up_bias)


@jax.custom_vjp
def low(v):
    return lax.optimization_barrier(v.astype(jnp.bfloat16)).astype(jnp.float32)

@jax.custom_vjp
def low_back(v):
    return v

def low_keep(v):
    return (low(v), None)

def low_pass(kept, grad):
    return (grad,)

def back_keep(v):
    return (v, None)

def back_low(kept, grad):
    return (low(grad),)
low.defvjp(low_keep, low_pass)
low_back.defvjp(back_keep, back_low)
relax = 32.0

def layer_norm(value, gain, shift):
    mean = lax.optimization_barrier(jnp.mean(value, axis=-1, keepdims=True))
    centered = value - mean
    spread = lax.optimization_barrier(jnp.mean(centered * centered, axis=-1, keepdims=True))
    return centered * lax.rsqrt(spread + 1e-05) * gain + shift

def reference(layer_input, out_grad, deal, w_qkv, w_out, w_up, w_down, norm_gain, norm_shift, bias_width, up_bias):
    width = layer_input.shape[2]
    length = layer_input.shape[1]
    heads = HEADS
    head = width // heads
    prescale = 1.0 / (relax * math.sqrt(head))
    highest = lax.Precision.HIGHEST
    blocks = (jnp.repeat(deal.reshape(-1), PIECE) // (BLK // PIECE)).astype(jnp.int32)
    span = math.gcd(length, 512)
    count = length // span

    def attend(query, key_rows, value_rows):
        query4 = query.reshape(count, span, heads, head)
        key4 = key_rows.reshape(length, heads, head)
        value4 = value_rows.reshape(length, heads, head)

        def part(args):
            rows, row_blocks = args
            raw = low_back(jnp.einsum('qhd,khd->hqk', rows * prescale, key4, precision=highest))
            visible = (row_blocks[:, None] >= blocks[None, :])[None]
            top = lax.optimization_barrier(jnp.max(jnp.where(visible, raw, -1e+30), axis=-1, keepdims=True))
            relaxed = jnp.where(visible, (raw - top) * relax, -1e+30)
            total = jax.nn.logsumexp(relaxed, axis=-1, keepdims=True)
            probs = low(jnp.exp(relaxed - total))
            return jnp.einsum('hqk,khd->qhd', probs, value4, precision=highest)
        outs = lax.map(jax.checkpoint(part), (query4, blocks.reshape(count, span)))
        return outs.reshape(length, width)

    def layer(inputs, full_qkv, full_out, full_up, full_down, gains, shifts, biases, up_shift):

        def single(row_block):
            normed = low(layer_norm(row_block, gains[0], shifts[0]))
            mixed = jnp.dot(normed, full_qkv, precision=highest)
            query = low(low_back(mixed[:, :width] + biases[0]))
            keys = low(low_back(mixed[:, width:2 * width]))
            values = low(low_back(mixed[:, 2 * width:] + biases[1]))
            attended = low(low_back(attend(query, keys, values)))
            branch = low_back(jnp.dot(attended, full_out, precision=highest) + biases[2])
            resid = row_block + layer_norm(branch, gains[1], shifts[1])
            second = low(layer_norm(resid, gains[2], shifts[2]))
            upper = low_back(jnp.dot(second, full_up, precision=highest) + up_shift)
            hidden = low(jax.nn.gelu(upper, approximate=True))
            ffn = low_back(jnp.dot(hidden, full_down, precision=highest) + biases[3])
            return resid + layer_norm(ffn, gains[3], shifts[3])
        return lax.map(single, inputs)
    floats = [a.astype(jnp.float32) for a in (layer_input, w_qkv, w_out, w_up, w_down, norm_gain, norm_shift, bias_width, up_bias)]
    result, pull = jax.vjp(layer, *floats)
    grads = pull(out_grad.astype(jnp.float32))
    return (result.astype(jnp.bfloat16), grads[0], grads[1], grads[2], grads[3], grads[4], grads[5], grads[6], grads[7], grads[8])
```

```python
import math

import jax
import jax.numpy as jnp
from jax import lax
from jax.sharding import PartitionSpec as P

HEADS = 16
BLK = 256
PIECE = 64


epsilon = 1e-05
relax = 32.0


def layer_norm(value, gain, shift):
    mean = jnp.mean(value, axis=-1, keepdims=True)
    centered = value - mean
    spread = jnp.mean(centered * centered, axis=-1, keepdims=True)
    return centered * lax.rsqrt(spread + epsilon) * gain + shift


def gelu_tanh(value):
    return jax.nn.gelu(value, approximate=True)


def rows_dot(left, weight):
    return jnp.einsum("std,de->ste", left, weight, preferred_element_type=jnp.float32)


def weight_grad(left, right):
    return jnp.einsum("std,ste->de", left, right, preferred_element_type=jnp.float32)


def back_dot(grad, weight):
    return jnp.einsum("ste,de->std", grad, weight, preferred_element_type=jnp.float32)


def row_total(value):
    return jnp.sum(value.astype(jnp.float32), axis=(0, 1))


def general_device(
    layer_input,
    out_grad,
    deal,
    w_qkv,
    w_out,
    w_up,
    w_down,
    norm_gain,
    norm_shift,
    bias_width,
    up_bias,
):
    seqs, rows, width = layer_input.shape
    heads = HEADS
    head = width // heads
    prescale = 1.0 / (relax * math.sqrt(head))
    ranks = lax.axis_size("ctx")
    length = rows * ranks
    per_block = BLK // PIECE
    rank = lax.axis_index("ctx")
    chosen = jnp.arange(ranks, dtype=jnp.int32) == rank
    mine = jnp.sum(jnp.where(chosen[:, None], deal, 0), axis=0)
    query_blocks = jnp.repeat(mine, rows // 2) // per_block
    key_blocks = jnp.repeat(deal.reshape(-1), rows // 2) // per_block
    full_qkv, full_out, full_up, full_down, gains, shifts, biases, up_shift = (
        lax.all_gather(w_qkv, "wt", axis=0, tiled=True),
        lax.all_gather(w_out, "wt", axis=0, tiled=True),
        lax.all_gather(w_up, "wt", axis=0, tiled=True),
        lax.all_gather(w_down, "wt", axis=0, tiled=True),
        lax.all_gather(norm_gain, "wt", axis=1, tiled=True),
        lax.all_gather(norm_shift, "wt", axis=1, tiled=True),
        lax.all_gather(bias_width, "wt", axis=1, tiled=True),
        lax.all_gather(up_bias, "wt", axis=0, tiled=True),
    )
    gains = gains.astype(jnp.float32)
    shifts = shifts.astype(jnp.float32)
    biases = biases.astype(jnp.float32)
    up_shift = up_shift.astype(jnp.float32)
    input_float = layer_input.astype(jnp.float32)
    first = layer_norm(input_float, gains[0], shifts[0]).astype(jnp.bfloat16)
    mixed = rows_dot(first, full_qkv)
    query = (mixed[..., :width] + biases[0]).astype(jnp.bfloat16)
    kv_local = jnp.concatenate(
        [mixed[..., width : 2 * width], mixed[..., 2 * width :] + biases[1]], axis=-1
    ).astype(jnp.bfloat16)
    kv_all = lax.all_gather(kv_local, "ctx", axis=1, tiled=True)
    step = math.gcd(length, 1024)
    count = length // step
    query4 = query.reshape(seqs, rows, heads, head)

    def score_block(left, right):
        return (
            jnp.einsum("sqhd,skhd->shqk", left, right, preferred_element_type=jnp.float32)
            * prescale
        )

    def key_block(index):
        start = index * step
        piece = lax.dynamic_slice_in_dim(kv_all, start, step, 1)
        keys4 = piece[..., :width].reshape(seqs, step, heads, head)
        values4 = piece[..., width:].reshape(seqs, step, heads, head)
        visible = (
            query_blocks[:, None] >= lax.dynamic_slice_in_dim(key_blocks, start, step, 0)[None, :]
        )
        return (keys4, values4, visible)

    def probs(raw, visible, totals):
        return jnp.where(visible, jnp.exp(raw * relax - totals[..., None]), 0.0)

    def online(index, carry):
        top, total, acc = carry
        keys4, values4, visible = key_block(index)
        raw = jnp.where(visible, score_block(query4, keys4), -1e30)
        new_top = jnp.maximum(top, jnp.max(raw, axis=-1))
        terms = jnp.where(visible, jnp.exp((raw - new_top[..., None]) * relax), 0.0)
        factor = jnp.exp((top - new_top) * relax)
        total = total * factor + jnp.sum(terms, axis=-1)
        acc = acc * jnp.transpose(factor, (0, 2, 1))[..., None]
        acc = acc + jnp.einsum(
            "shqk,skhd->sqhd",
            terms.astype(jnp.bfloat16),
            values4,
            preferred_element_type=jnp.float32,
        )
        return (new_top, total, acc)

    start_top = jnp.full((seqs, heads, rows), -1e30, jnp.float32)
    start_total = jnp.zeros((seqs, heads, rows), jnp.float32)
    start_acc = jnp.zeros((seqs, rows, heads, head), jnp.float32)
    top, total, acc = lax.fori_loop(0, count, online, (start_top, start_total, start_acc))
    log_total = top * relax + jnp.log(total)
    attended_float = acc / jnp.transpose(total, (0, 2, 1))[..., None]
    attended = attended_float.reshape(seqs, rows, width).astype(jnp.bfloat16)
    branch = rows_dot(attended, full_out) + biases[2]
    resid = input_float + layer_norm(branch, gains[1], shifts[1])
    second = layer_norm(resid, gains[2], shifts[2]).astype(jnp.bfloat16)
    upper = rows_dot(second, full_up) + up_shift
    hidden = gelu_tanh(upper).astype(jnp.bfloat16)
    ffn = rows_dot(hidden, full_down) + biases[3]
    top_norm, pull_four = jax.vjp(layer_norm, ffn, gains[3], shifts[3])
    result = resid + top_norm
    d_out = out_grad.astype(jnp.float32)
    d_ffn, d_gain3, d_shift3 = pull_four(d_out)
    d_ffn = d_ffn.astype(jnp.bfloat16)
    d_bias3 = row_total(d_ffn)
    g_down = weight_grad(hidden, d_ffn)
    d_hidden = back_dot(d_ffn, full_down)
    _, pull_gelu = jax.vjp(gelu_tanh, upper)
    d_upper = pull_gelu(d_hidden)[0].astype(jnp.bfloat16)
    d_up_shift = row_total(d_upper)
    g_up = weight_grad(second, d_upper)
    d_second = back_dot(d_upper, full_up)
    _, pull_three = jax.vjp(layer_norm, resid, gains[2], shifts[2])
    d_resid_part, d_gain2, d_shift2 = pull_three(d_second)
    d_resid = d_out + d_resid_part
    _, pull_two = jax.vjp(layer_norm, branch, gains[1], shifts[1])
    d_branch, d_gain1, d_shift1 = pull_two(d_resid)
    d_branch = d_branch.astype(jnp.bfloat16)
    d_bias2 = row_total(d_branch)
    g_out = weight_grad(attended, d_branch)
    d_attended = back_dot(d_branch, full_out).astype(jnp.bfloat16)
    d_out4 = d_attended.reshape(seqs, rows, heads, head)
    delta = jnp.einsum("sqhd,sqhd->shq", d_out4.astype(jnp.float32), attended_float)

    def score_grads(q_rows, do_rows, k_rows, v_rows, visible, lse_rows, delta_rows):
        weights = probs(score_block(q_rows, k_rows), visible, lse_rows)
        d_probs = jnp.einsum("sqhd,skhd->shqk", do_rows, v_rows, preferred_element_type=jnp.float32)
        d_scores = (relax * weights * (d_probs - delta_rows[..., None])).astype(jnp.bfloat16)
        return (d_scores, weights.astype(jnp.bfloat16))

    zero_query = jnp.zeros((seqs, rows, heads, head), jnp.float32)

    def local_grads(d_query, index):
        keys4, values4, visible = key_block(index)
        d_scores, weights = score_grads(query4, d_out4, keys4, values4, visible, log_total, delta)
        d_query = (
            d_query
            + jnp.einsum("shqk,skhd->sqhd", d_scores, keys4, preferred_element_type=jnp.float32)
            * prescale
        )
        d_keys = (
            jnp.einsum("shqk,sqhd->kshd", d_scores, query4, preferred_element_type=jnp.float32)
            * prescale
        )
        d_values = jnp.einsum(
            "shqk,sqhd->kshd", weights, d_out4, preferred_element_type=jnp.float32
        )
        joined = jnp.concatenate(
            [d_keys.reshape(step, seqs, width), d_values.reshape(step, seqs, width)], axis=-1
        )
        return (d_query, joined)

    d_query, pieces = lax.scan(local_grads, zero_query, jnp.arange(count, dtype=jnp.int32))
    terms = pieces.reshape(length, seqs, 2 * width)
    d_kv = jnp.transpose(lax.psum_scatter(terms, "ctx", scatter_dimension=0, tiled=True), (1, 0, 2))
    d_query = d_query.reshape(seqs, rows, width).astype(jnp.bfloat16)
    d_kv = d_kv.astype(jnp.bfloat16)
    d_bias0 = row_total(d_query)
    d_bias1 = row_total(d_kv[..., width:])
    d_mixed = jnp.concatenate([d_query, d_kv], axis=-1)
    g_qkv = weight_grad(first, d_mixed)
    d_first = back_dot(d_mixed, full_qkv)
    _, pull_one = jax.vjp(layer_norm, input_float, gains[0], shifts[0])
    d_input_part, d_gain0, d_shift0 = pull_one(d_first)
    input_grad = d_resid + d_input_part
    grad_gain = jnp.stack([d_gain0, d_gain1, d_gain2, d_gain3])
    grad_shift = jnp.stack([d_shift0, d_shift1, d_shift2, d_shift3])
    grad_bias = jnp.stack([d_bias0, d_bias1, d_bias2, d_bias3])
    owned = (
        lax.psum_scatter(g_qkv.astype(jnp.bfloat16), "wt", scatter_dimension=0, tiled=True).astype(
            jnp.float32
        ),
        lax.psum_scatter(g_out.astype(jnp.bfloat16), "wt", scatter_dimension=0, tiled=True).astype(
            jnp.float32
        ),
        lax.psum_scatter(g_up.astype(jnp.bfloat16), "wt", scatter_dimension=0, tiled=True).astype(
            jnp.float32
        ),
        lax.psum_scatter(g_down.astype(jnp.bfloat16), "wt", scatter_dimension=0, tiled=True).astype(
            jnp.float32
        ),
        lax.psum_scatter(
            grad_gain.astype(jnp.bfloat16), "wt", scatter_dimension=1, tiled=True
        ).astype(jnp.float32),
        lax.psum_scatter(
            grad_shift.astype(jnp.bfloat16), "wt", scatter_dimension=1, tiled=True
        ).astype(jnp.float32),
        lax.psum_scatter(
            grad_bias.astype(jnp.bfloat16), "wt", scatter_dimension=1, tiled=True
        ).astype(jnp.float32),
        lax.psum_scatter(
            d_up_shift.astype(jnp.bfloat16), "wt", scatter_dimension=0, tiled=True
        ).astype(jnp.float32),
    )
    summed = lax.psum(
        (owned[0], owned[1], owned[2], owned[3], owned[4], owned[5], owned[6], owned[7]), "ctx"
    )
    return (
        result.astype(jnp.bfloat16),
        input_grad,
        summed[0],
        summed[1],
        summed[2],
        summed[3],
        summed[4],
        summed[5],
        summed[6],
        summed[7],
    )


F32 = jnp.float32
BF16 = jnp.bfloat16
Z_LINE = 4
WT = 4


def swap(value, axis, bit):
    size = lax.axis_size(axis)
    return lax.ppermute(value, axis, [(i, i ^ bit) for i in range(size)])


def swap_core(value):
    return swap(value, "wt", 1)


def swap_x(value):
    return swap(value, "wt", 2)


def swap_y(value):
    return swap(value, "ctx", 1)


def shift_z(value, step, senders):
    pairs = [(2 * z + y, 2 * (z + step) + y) for z in senders for y in range(2)]
    return lax.ppermute(value, "ctx", pairs)


def pick(stack, index, axis=0):
    return lax.dynamic_index_in_dim(stack, index, axis, keepdims=False)


def by_bit(bit, mine, other):
    return jnp.where(bit == 0, mine, other), jnp.where(bit == 0, other, mine)


def gather_wt(block):
    w = lax.axis_index("wt")
    core, x = w % 2, w // 2
    pair = jnp.stack([block, swap_x(block)])
    other = swap_core(pair)
    rows = []
    for xi in range(2):
        own = pick(pair, xi ^ x)
        far = pick(other, xi ^ x)
        rows.extend(by_bit(core, own, far))
    return jnp.stack(rows)


def exchange_wt(blocks):
    w = lax.axis_index("wt")
    core, x = w % 2, w // 2
    grid = blocks.reshape((2, 2) + blocks.shape[1:])
    keep = pick(grid, core, 1)
    got = swap_core(pick(grid, 1 - core, 1))
    both = jnp.stack([keep, got])
    here = pick(both, x, 1)
    far = swap_x(pick(both, 1 - x, 1))
    rows = []
    for xi in range(2):
        part = jnp.where(x == xi, here, far)
        rows.extend(by_bit(core, part[0], part[1]))
    return jnp.stack(rows)


def scatter_wt(blocks):
    w = lax.axis_index("wt")
    core, x = w % 2, w // 2
    grid = blocks.reshape((2, 2) + blocks.shape[1:])
    keep = pick(grid, core, 1)
    got = swap_core(pick(grid, 1 - core, 1))
    both = keep.astype(F32) + got.astype(F32)
    far = swap_x(pick(both, 1 - x).astype(BF16))
    return pick(both, x) + far.astype(F32)


def gather_ctx(block):
    c = lax.axis_index("ctx")
    y, z = c % 2, c // 2
    up, down = [block], [block]
    for step in range(1, Z_LINE):
        up.append(shift_z(up[-1], 1, range(step - 1, Z_LINE - 1)))
        down.append(shift_z(down[-1], -1, range(1, Z_LINE - step + 1)))
    mirrored = swap_y(block)
    far_up, far_down = [mirrored], [mirrored]
    for step in range(1, Z_LINE):
        pairs = [(i, i ^ 1) for i in range(2 * step, 2 * Z_LINE)]
        far_up.append(lax.ppermute(up[step], "ctx", pairs))
        pairs = [(i, i ^ 1) for i in range(0, 2 * (Z_LINE - step))]
        far_down.append(lax.ppermute(down[step], "ctx", pairs))

    def at(ups, downs, target):
        value = ups[0]
        for here in range(Z_LINE):
            if here > target:
                value = jnp.where(z == here, ups[here - target], value)
            elif here < target:
                value = jnp.where(z == here, downs[target - here], value)
        return value

    rows = []
    for target in range(Z_LINE):
        near, far = at(up, down, target), at(far_up, far_down, target)
        rows.extend(by_bit(y, near, far))
    return rows


def scatter_ctx(blocks):
    c = lax.axis_index("ctx")
    y, z = c % 2, c // 2
    grid = blocks.reshape((Z_LINE, 2) + blocks.shape[1:])
    got = swap_y(pick(grid, 1 - y, 1))
    sums = pick(grid, y, 1).astype(F32) + got.astype(F32)
    up = down = 0.0
    for step in range(1, Z_LINE):
        index = jnp.clip(Z_LINE - step + z, 0, Z_LINE - 1)
        send = (pick(sums, index) + up).astype(BF16)
        up = shift_z(send, 1, range(0, step)).astype(F32)
        index = jnp.clip(z - Z_LINE + step, 0, Z_LINE - 1)
        send = (pick(sums, index) + down).astype(BF16)
        down = shift_z(send, -1, range(Z_LINE - step, Z_LINE)).astype(F32)
    return pick(sums, z) + up + down


def total_ctx(value):
    for bit in (1, 2, 4):
        value = value + swap(value, "ctx", bit)
    return value


def total_wt(value):
    for bit in (1, 2):
        value = value + swap(value, "wt", bit)
    return value


def dot(left, right):
    return jnp.dot(left, right, preferred_element_type=F32)


def dot_t(left, right):
    return lax.dot_general(left, right, (((1,), (1,)), ((), ())), preferred_element_type=F32)


def t_dot(left, right):
    return lax.dot_general(left, right, (((0,), (0,)), ((), ())), preferred_element_type=F32)


def split_device(
    layer_input,
    out_grad,
    deal,
    w_qkv,
    w_out,
    w_up,
    w_down,
    norm_gain,
    norm_shift,
    bias_width,
    up_bias,
):
    _, rows, width = layer_input.shape
    ranks = lax.axis_size("ctx")
    groups = lax.axis_size("wt")
    c, w = lax.axis_index("ctx"), lax.axis_index("wt")
    head = width // HEADS
    per = HEADS // ranks
    span = per * head
    length = rows * ranks
    prescale = 1.0 / (relax * math.sqrt(head))
    own_rows = layer_input[0]

    small = gather_wt(jnp.concatenate([norm_gain, norm_shift, bias_width], axis=0))
    small = jnp.transpose(small, (1, 0, 2)).reshape(12, width).astype(F32)
    gains, shifts, biases = small[:4], small[4:8], small[8:]

    columns = [lax.dynamic_slice_in_dim(w_qkv, part * width + c * span, span, 1) for part in range(3)]
    own_qkv = gather_wt(jnp.concatenate(columns, axis=1)).reshape(width, 3 * span)
    full_out = gather_wt(w_out).reshape(width, width)
    hidden_width = w_up.shape[1] // groups
    own_up = exchange_wt(jnp.transpose(w_up.reshape(width // groups, groups, hidden_width), (1, 0, 2)))
    own_up = own_up.reshape(width, hidden_width)
    full_qkv = gather_wt(w_qkv).reshape(width, 3 * width)

    sequence = jnp.stack(gather_ctx(own_rows)).reshape(length, width)
    first = layer_norm(sequence.astype(F32), gains[0], shifts[0]).astype(BF16)
    mixed = dot(first, own_qkv)
    query = (mixed[:, :span] + lax.dynamic_slice_in_dim(biases[0], c * span, span, 0)).astype(BF16)
    keys = mixed[:, span : 2 * span].astype(BF16)
    values = (mixed[:, 2 * span :] + lax.dynamic_slice_in_dim(biases[1], c * span, span, 0)).astype(BF16)
    blocks = jnp.repeat(deal.reshape(-1), rows // 2) // (BLK // PIECE)
    visible = blocks[:, None] >= blocks[None, :]

    def heads_of(value):
        return jnp.transpose(value.reshape(length, per, head), (1, 0, 2))

    query_h, keys_h, values_h = heads_of(query), heads_of(keys), heads_of(values)
    raw = jnp.einsum("hqd,hkd->hqk", query_h, keys_h, preferred_element_type=F32) * prescale
    raw = jnp.where(visible, raw, -1e30)
    top = jnp.max(raw, axis=-1, keepdims=True)
    terms = jnp.where(visible, jnp.exp((raw - top) * relax), 0.0)
    total = jnp.sum(terms, axis=-1, keepdims=True)
    weights = terms / total
    weights_low = weights.astype(BF16)
    out_h = jnp.einsum("hqk,hkd->hqd", weights_low, values_h, preferred_element_type=F32)
    out_seq = jnp.transpose(out_h, (1, 0, 2)).reshape(ranks, rows, span).astype(BF16)
    attended = lax.all_to_all(out_seq, "ctx", 0, 0, tiled=True)
    attended = jnp.transpose(attended, (1, 0, 2)).reshape(rows, width)

    input_float = own_rows.astype(F32)
    branch = dot(attended, full_out) + biases[2]
    resid = input_float + layer_norm(branch, gains[1], shifts[1])
    second = layer_norm(resid, gains[2], shifts[2]).astype(BF16)

    def slots(value):
        pair = jnp.concatenate([value, swap_x(value)], axis=0)
        return jnp.concatenate([pair, swap_core(pair)], axis=0)

    def gather_back(value):
        half = 2 * rows
        both = value[:half] + swap_core(value[half:].astype(BF16)).astype(F32)
        return both[:rows] + swap_x(both[rows:].astype(BF16)).astype(F32)

    second_all = slots(second)
    upper = dot(second_all, own_up) + up_bias.astype(F32)
    hidden = gelu_tanh(upper).astype(BF16)
    ffn = gather_back(dot(hidden, w_down)) + biases[3]
    top_norm, pull_four = jax.vjp(layer_norm, ffn, gains[3], shifts[3])
    result = resid + top_norm
    d_out = out_grad[0].astype(F32)
    d_ffn, d_gain3, d_shift3 = pull_four(d_out)
    d_ffn = d_ffn.astype(BF16)
    d_ffn_all = slots(d_ffn)
    d_hidden = dot_t(d_ffn_all, w_down)
    _, pull_gelu = jax.vjp(gelu_tanh, upper)
    d_upper = pull_gelu(d_hidden)[0].astype(BF16)
    d_second = gather_back(dot_t(d_upper, own_up))
    g_down = t_dot(hidden, d_ffn_all)
    g_up = t_dot(second_all, d_upper)
    _, pull_three = jax.vjp(layer_norm, resid, gains[2], shifts[2])
    d_resid_part, d_gain2, d_shift2 = pull_three(d_second)
    d_resid = d_out + d_resid_part
    _, pull_two = jax.vjp(layer_norm, branch, gains[1], shifts[1])
    d_branch, d_gain1, d_shift1 = pull_two(d_resid)
    d_branch = d_branch.astype(BF16)
    g_out = t_dot(attended, d_branch)
    d_attended = dot_t(d_branch, full_out).astype(BF16)

    d_out_seq = jnp.transpose(d_attended.reshape(rows, ranks, span), (1, 0, 2))
    d_out_seq = lax.all_to_all(d_out_seq, "ctx", 0, 0, tiled=True).reshape(length, span)
    d_out_h = heads_of(d_out_seq)
    d_probs = jnp.einsum("hqd,hkd->hqk", d_out_h, values_h, preferred_element_type=F32)
    delta = jnp.sum(weights * d_probs, axis=-1, keepdims=True)
    d_scores = (relax * weights * (d_probs - delta)).astype(BF16)
    d_query = jnp.einsum("hqk,hkd->qhd", d_scores, keys_h, preferred_element_type=F32) * prescale
    d_keys = jnp.einsum("hqk,hqd->khd", d_scores, query_h, preferred_element_type=F32) * prescale
    d_values = jnp.einsum("hqk,hqd->khd", weights_low, d_out_h, preferred_element_type=F32)
    d_mixed = jnp.concatenate(
        [t.reshape(length, span).astype(BF16) for t in (d_query, d_keys, d_values)], axis=1
    )
    d_rows = lax.all_to_all(d_mixed.reshape(ranks, rows, 3 * span), "ctx", 0, 0, tiled=True)
    d_rows = jnp.transpose(d_rows.reshape(ranks, rows, 3, span), (1, 2, 0, 3)).reshape(rows, 3 * width)
    d_first = dot_t(d_rows, full_qkv)
    _, pull_one = jax.vjp(layer_norm, input_float, gains[0], shifts[0])
    d_input_part, d_gain0, d_shift0 = pull_one(d_first)
    input_grad = d_resid + d_input_part

    g_qkv = scatter_wt(t_dot(first, d_mixed).astype(BF16).reshape(groups, width // groups, 3 * span))
    g_out = scatter_wt(g_out.astype(BF16).reshape(groups, width // groups, width)).astype(BF16)
    part_out = scatter_ctx(g_out.reshape(ranks, width // groups // ranks, width))
    part_down = scatter_ctx(g_down.astype(BF16).reshape(ranks, hidden_width // ranks, width))
    cut = width // groups // ranks
    g_up = g_up.astype(BF16).reshape(groups, ranks, cut, hidden_width)
    part_up = scatter_ctx(jnp.transpose(g_up, (1, 0, 2, 3)))
    part_up = jnp.transpose(exchange_wt(part_up.astype(BF16)), (1, 0, 2)).reshape(cut, groups * hidden_width)
    full_g_down = jnp.concatenate(gather_ctx(part_down.astype(BF16)), axis=0).astype(F32)
    full_g_up = jnp.concatenate(gather_ctx(part_up), axis=0).astype(F32)
    full_g_out = jnp.concatenate(gather_ctx(part_out.astype(BF16)), axis=0).astype(F32)
    parts = jnp.stack(gather_ctx(g_qkv.astype(BF16)), axis=1)
    parts = parts.reshape(width // groups, ranks, 3, span)
    full_g_qkv = jnp.transpose(parts, (0, 2, 1, 3)).reshape(width // groups, 3 * width).astype(F32)

    def total_rows(value):
        return jnp.sum(value.astype(F32), axis=0)

    sums = jnp.stack(
        [
            d_gain0,
            d_gain1,
            d_gain2,
            d_gain3,
            d_shift0,
            d_shift1,
            d_shift2,
            d_shift3,
            total_rows(d_rows[:, :width]),
            total_rows(d_rows[:, 2 * width :]),
            total_rows(d_branch),
            total_rows(d_ffn),
        ]
    )
    sums = lax.dynamic_slice_in_dim(total_wt(sums), w * (width // groups), width // groups, 1)
    up_sum = total_rows(d_upper).reshape(groups, width // groups)
    sums = total_ctx(jnp.concatenate([sums, up_sum], axis=0))
    return (
        result.astype(BF16)[None],
        input_grad[None],
        full_g_qkv,
        full_g_out,
        full_g_up,
        full_g_down,
        sums[:4],
        sums[4:8],
        sums[8:12],
        sums[12:].reshape(hidden_width),
    )


def solution(mesh):
    small = mesh.shape["ctx"] == 2 * Z_LINE and mesh.shape["wt"] == WT
    per_device = split_device if small else general_device
    in_specs = (
        P("wt", "ctx", None),
        P("wt", "ctx", None),
        P(),
        P("wt", None),
        P("wt", None),
        P("wt", None),
        P("wt", None),
        P(None, "wt"),
        P(None, "wt"),
        P(None, "wt"),
        P("wt"),
    )
    out_specs = (
        P("wt", "ctx", None),
        P("wt", "ctx", None),
        P("wt", None),
        P("wt", None),
        P("wt", None),
        P("wt", None),
        P(None, "wt"),
        P(None, "wt"),
        P(None, "wt"),
        P("wt"),
    )
    return jax.shard_map(
        per_device, mesh=mesh, in_specs=in_specs, out_specs=out_specs, check_vma=False
    )
```

```python
import math

import jax
import jax.numpy as jnp
from jax import lax
from jax.experimental import pallas as pl
from jax.experimental.pallas import tpu as pltpu
from jax.sharding import PartitionSpec as P

HEADS = 16
BLK = 256
PIECE = 64


epsilon = 1e-05
relax = 32.0


def layer_norm(value, gain, shift):
    mean = jnp.mean(value, axis=-1, keepdims=True)
    centered = value - mean
    spread = jnp.mean(centered * centered, axis=-1, keepdims=True)
    return centered * lax.rsqrt(spread + epsilon) * gain + shift


def gelu_tanh(value):
    return jax.nn.gelu(value, approximate=True)


def rows_dot(left, weight):
    return jnp.einsum("std,de->ste", left, weight, preferred_element_type=jnp.float32)


def weight_grad(left, right):
    return jnp.einsum("std,ste->de", left, right, preferred_element_type=jnp.float32)


def back_dot(grad, weight):
    return jnp.einsum("ste,de->std", grad, weight, preferred_element_type=jnp.float32)


def row_total(value):
    return jnp.sum(value.astype(jnp.float32), axis=(0, 1))


def general_device(
    layer_input,
    out_grad,
    deal,
    w_qkv,
    w_out,
    w_up,
    w_down,
    norm_gain,
    norm_shift,
    bias_width,
    up_bias,
):
    seqs, rows, width = layer_input.shape
    heads = HEADS
    head = width // heads
    prescale = 1.0 / (relax * math.sqrt(head))
    ranks = lax.axis_size("ctx")
    length = rows * ranks
    per_block = BLK // PIECE
    rank = lax.axis_index("ctx")
    chosen = jnp.arange(ranks, dtype=jnp.int32) == rank
    mine = jnp.sum(jnp.where(chosen[:, None], deal, 0), axis=0)
    query_blocks = jnp.repeat(mine, rows // 2) // per_block
    key_blocks = jnp.repeat(deal.reshape(-1), rows // 2) // per_block
    full_qkv, full_out, full_up, full_down, gains, shifts, biases, up_shift = (
        lax.all_gather(w_qkv, "wt", axis=0, tiled=True),
        lax.all_gather(w_out, "wt", axis=0, tiled=True),
        lax.all_gather(w_up, "wt", axis=0, tiled=True),
        lax.all_gather(w_down, "wt", axis=0, tiled=True),
        lax.all_gather(norm_gain, "wt", axis=1, tiled=True),
        lax.all_gather(norm_shift, "wt", axis=1, tiled=True),
        lax.all_gather(bias_width, "wt", axis=1, tiled=True),
        lax.all_gather(up_bias, "wt", axis=0, tiled=True),
    )
    gains = gains.astype(jnp.float32)
    shifts = shifts.astype(jnp.float32)
    biases = biases.astype(jnp.float32)
    up_shift = up_shift.astype(jnp.float32)
    input_float = layer_input.astype(jnp.float32)
    first = layer_norm(input_float, gains[0], shifts[0]).astype(jnp.bfloat16)
    mixed = rows_dot(first, full_qkv)
    query = (mixed[..., :width] + biases[0]).astype(jnp.bfloat16)
    kv_local = jnp.concatenate(
        [mixed[..., width : 2 * width], mixed[..., 2 * width :] + biases[1]], axis=-1
    ).astype(jnp.bfloat16)
    kv_all = lax.all_gather(kv_local, "ctx", axis=1, tiled=True)
    step = math.gcd(length, 1024)
    count = length // step
    query4 = query.reshape(seqs, rows, heads, head)

    def score_block(left, right):
        return (
            jnp.einsum("sqhd,skhd->shqk", left, right, preferred_element_type=jnp.float32)
            * prescale
        )

    def key_block(index):
        start = index * step
        piece = lax.dynamic_slice_in_dim(kv_all, start, step, 1)
        keys4 = piece[..., :width].reshape(seqs, step, heads, head)
        values4 = piece[..., width:].reshape(seqs, step, heads, head)
        visible = (
            query_blocks[:, None] >= lax.dynamic_slice_in_dim(key_blocks, start, step, 0)[None, :]
        )
        return (keys4, values4, visible)

    def probs(raw, visible, totals):
        return jnp.where(visible, jnp.exp(raw * relax - totals[..., None]), 0.0)

    def online(index, carry):
        top, total, acc = carry
        keys4, values4, visible = key_block(index)
        raw = jnp.where(visible, score_block(query4, keys4), -1e30)
        new_top = jnp.maximum(top, jnp.max(raw, axis=-1))
        terms = jnp.where(visible, jnp.exp((raw - new_top[..., None]) * relax), 0.0)
        factor = jnp.exp((top - new_top) * relax)
        total = total * factor + jnp.sum(terms, axis=-1)
        acc = acc * jnp.transpose(factor, (0, 2, 1))[..., None]
        acc = acc + jnp.einsum(
            "shqk,skhd->sqhd",
            terms.astype(jnp.bfloat16),
            values4,
            preferred_element_type=jnp.float32,
        )
        return (new_top, total, acc)

    start_top = jnp.full((seqs, heads, rows), -1e30, jnp.float32)
    start_total = jnp.zeros((seqs, heads, rows), jnp.float32)
    start_acc = jnp.zeros((seqs, rows, heads, head), jnp.float32)
    top, total, acc = lax.fori_loop(0, count, online, (start_top, start_total, start_acc))
    log_total = top * relax + jnp.log(total)
    attended_float = acc / jnp.transpose(total, (0, 2, 1))[..., None]
    attended = attended_float.reshape(seqs, rows, width).astype(jnp.bfloat16)
    branch = rows_dot(attended, full_out) + biases[2]
    resid = input_float + layer_norm(branch, gains[1], shifts[1])
    second = layer_norm(resid, gains[2], shifts[2]).astype(jnp.bfloat16)
    upper = rows_dot(second, full_up) + up_shift
    hidden = gelu_tanh(upper).astype(jnp.bfloat16)
    ffn = rows_dot(hidden, full_down) + biases[3]
    top_norm, pull_four = jax.vjp(layer_norm, ffn, gains[3], shifts[3])
    result = resid + top_norm
    d_out = out_grad.astype(jnp.float32)
    d_ffn, d_gain3, d_shift3 = pull_four(d_out)
    d_ffn = d_ffn.astype(jnp.bfloat16)
    d_bias3 = row_total(d_ffn)
    g_down = weight_grad(hidden, d_ffn)
    d_hidden = back_dot(d_ffn, full_down)
    _, pull_gelu = jax.vjp(gelu_tanh, upper)
    d_upper = pull_gelu(d_hidden)[0].astype(jnp.bfloat16)
    d_up_shift = row_total(d_upper)
    g_up = weight_grad(second, d_upper)
    d_second = back_dot(d_upper, full_up)
    _, pull_three = jax.vjp(layer_norm, resid, gains[2], shifts[2])
    d_resid_part, d_gain2, d_shift2 = pull_three(d_second)
    d_resid = d_out + d_resid_part
    _, pull_two = jax.vjp(layer_norm, branch, gains[1], shifts[1])
    d_branch, d_gain1, d_shift1 = pull_two(d_resid)
    d_branch = d_branch.astype(jnp.bfloat16)
    d_bias2 = row_total(d_branch)
    g_out = weight_grad(attended, d_branch)
    d_attended = back_dot(d_branch, full_out).astype(jnp.bfloat16)
    d_out4 = d_attended.reshape(seqs, rows, heads, head)
    delta = jnp.einsum("sqhd,sqhd->shq", d_out4.astype(jnp.float32), attended_float)

    def score_grads(q_rows, do_rows, k_rows, v_rows, visible, lse_rows, delta_rows):
        weights = probs(score_block(q_rows, k_rows), visible, lse_rows)
        d_probs = jnp.einsum("sqhd,skhd->shqk", do_rows, v_rows, preferred_element_type=jnp.float32)
        d_scores = (relax * weights * (d_probs - delta_rows[..., None])).astype(jnp.bfloat16)
        return (d_scores, weights.astype(jnp.bfloat16))

    zero_query = jnp.zeros((seqs, rows, heads, head), jnp.float32)

    def local_grads(d_query, index):
        keys4, values4, visible = key_block(index)
        d_scores, weights = score_grads(query4, d_out4, keys4, values4, visible, log_total, delta)
        d_query = (
            d_query
            + jnp.einsum("shqk,skhd->sqhd", d_scores, keys4, preferred_element_type=jnp.float32)
            * prescale
        )
        d_keys = (
            jnp.einsum("shqk,sqhd->kshd", d_scores, query4, preferred_element_type=jnp.float32)
            * prescale
        )
        d_values = jnp.einsum(
            "shqk,sqhd->kshd", weights, d_out4, preferred_element_type=jnp.float32
        )
        joined = jnp.concatenate(
            [d_keys.reshape(step, seqs, width), d_values.reshape(step, seqs, width)], axis=-1
        )
        return (d_query, joined)

    d_query, pieces = lax.scan(local_grads, zero_query, jnp.arange(count, dtype=jnp.int32))
    terms = pieces.reshape(length, seqs, 2 * width)
    d_kv = jnp.transpose(lax.psum_scatter(terms, "ctx", scatter_dimension=0, tiled=True), (1, 0, 2))
    d_query = d_query.reshape(seqs, rows, width).astype(jnp.bfloat16)
    d_kv = d_kv.astype(jnp.bfloat16)
    d_bias0 = row_total(d_query)
    d_bias1 = row_total(d_kv[..., width:])
    d_mixed = jnp.concatenate([d_query, d_kv], axis=-1)
    g_qkv = weight_grad(first, d_mixed)
    d_first = back_dot(d_mixed, full_qkv)
    _, pull_one = jax.vjp(layer_norm, input_float, gains[0], shifts[0])
    d_input_part, d_gain0, d_shift0 = pull_one(d_first)
    input_grad = d_resid + d_input_part
    grad_gain = jnp.stack([d_gain0, d_gain1, d_gain2, d_gain3])
    grad_shift = jnp.stack([d_shift0, d_shift1, d_shift2, d_shift3])
    grad_bias = jnp.stack([d_bias0, d_bias1, d_bias2, d_bias3])
    owned = (
        lax.psum_scatter(g_qkv.astype(jnp.bfloat16), "wt", scatter_dimension=0, tiled=True).astype(
            jnp.float32
        ),
        lax.psum_scatter(g_out.astype(jnp.bfloat16), "wt", scatter_dimension=0, tiled=True).astype(
            jnp.float32
        ),
        lax.psum_scatter(g_up.astype(jnp.bfloat16), "wt", scatter_dimension=0, tiled=True).astype(
            jnp.float32
        ),
        lax.psum_scatter(g_down.astype(jnp.bfloat16), "wt", scatter_dimension=0, tiled=True).astype(
            jnp.float32
        ),
        lax.psum_scatter(
            grad_gain.astype(jnp.bfloat16), "wt", scatter_dimension=1, tiled=True
        ).astype(jnp.float32),
        lax.psum_scatter(
            grad_shift.astype(jnp.bfloat16), "wt", scatter_dimension=1, tiled=True
        ).astype(jnp.float32),
        lax.psum_scatter(
            grad_bias.astype(jnp.bfloat16), "wt", scatter_dimension=1, tiled=True
        ).astype(jnp.float32),
        lax.psum_scatter(
            d_up_shift.astype(jnp.bfloat16), "wt", scatter_dimension=0, tiled=True
        ).astype(jnp.float32),
    )
    summed = lax.psum(
        (owned[0], owned[1], owned[2], owned[3], owned[4], owned[5], owned[6], owned[7]), "ctx"
    )
    return (
        result.astype(jnp.bfloat16),
        input_grad,
        summed[0],
        summed[1],
        summed[2],
        summed[3],
        summed[4],
        summed[5],
        summed[6],
        summed[7],
    )


F32 = jnp.float32
BF16 = jnp.bfloat16
Z_LINE = 4
WT = 4
PART = 256
SMALL = 16
GELU_A = math.sqrt(2.0 / math.pi)
GELU_B = 0.044715


def swap(value, axis, bit):
    size = lax.axis_size(axis)
    return lax.ppermute(value, axis, [(i, i ^ bit) for i in range(size)])


def shift_z(value, step, senders):
    pairs = [(2 * z + y, 2 * (z + step) + y) for z in senders for y in range(2)]
    return lax.ppermute(value, "ctx", pairs)


def gather_wt(block):
    far = swap(block, "wt", 2)
    return block, swap(block, "wt", 1), far, swap(far, "wt", 1)


def gather_ctx(block):
    up, down = [], []
    for step in range(1, Z_LINE):
        up.append(shift_z(up[-1] if up else block, 1, range(step - 1, Z_LINE - 1)))
        down.append(shift_z(down[-1] if down else block, -1, range(1, Z_LINE - step + 1)))
    near = [block] + up + down
    far = [swap(block, "ctx", 1)]
    for step in range(1, Z_LINE):
        pairs = [(i, i ^ 1) for i in range(2 * step, 2 * Z_LINE)]
        far.append(lax.ppermute(up[step - 1], "ctx", pairs))
    for step in range(1, Z_LINE):
        pairs = [(i, i ^ 1) for i in range(0, 2 * (Z_LINE - step))]
        far.append(lax.ppermute(down[step - 1], "ctx", pairs))
    return near + far


def pick(stack, index, axis=0):
    return lax.dynamic_index_in_dim(stack, index, axis, keepdims=False)


def scatter_ctx(keep, send):
    z = lax.axis_index("ctx") // 2
    sums = keep.astype(F32) + swap(send, "ctx", 1).astype(F32)
    up = down = 0.0
    for step in range(1, Z_LINE):
        index = jnp.clip(Z_LINE - step + z, 0, Z_LINE - 1)
        up = shift_z((pick(sums, index) + up).astype(BF16), 1, range(0, step)).astype(F32)
        index = jnp.clip(z - Z_LINE + step, 0, Z_LINE - 1)
        down = shift_z((pick(sums, index) + down).astype(BF16), -1, range(Z_LINE - step, Z_LINE)).astype(F32)
    return (pick(sums, z) + up + down).astype(BF16)


def scatter_wt(keep, send):
    got = swap(send, "wt", 1)
    far = swap((keep[1].astype(F32) + got[1].astype(F32)).astype(BF16), "wt", 2)
    return (keep[0].astype(F32) + got[0].astype(F32) + far.astype(F32)).astype(BF16)


def dot(left, right):
    return jnp.dot(left, right, preferred_element_type=F32)


def dot_t(left, right):
    return lax.dot_general(left, right, (((1,), (1,)), ((), ())), preferred_element_type=F32)


def t_dot(left, right):
    return lax.dot_general(left, right, (((0,), (0,)), ((), ())), preferred_element_type=F32)


def at(start, size):
    return pl.ds(pl.multiple_of(start * size, size), size)


def call(body, name, ins, outs, places=None, out_places=None, scratch=(), flops=0, limit=32):
    places, out_places = places or {}, out_places or {}
    vmem = pltpu.VMEM
    nbytes = sum(math.prod(a.shape) * a.dtype.itemsize for a in (*ins, *outs))
    single = len(outs) == 1
    specs = [pl.BlockSpec(memory_space=out_places.get(i, vmem)) for i in range(len(outs))]
    return pl.pallas_call(
        body,
        name=name,
        out_shape=outs[0] if single else tuple(outs),
        in_specs=[pl.BlockSpec(memory_space=places.get(i, vmem)) for i in range(len(ins))],
        out_specs=specs[0] if single else tuple(specs),
        scratch_shapes=list(scratch),
        compiler_params=pltpu.CompilerParams(vmem_limit_bytes=limit << 20),
        cost_estimate=pl.CostEstimate(flops=flops, bytes_accessed=nbytes, transcendentals=0),
    )(*ins)


def shape(*dims, dtype=jnp.bfloat16):
    return jax.ShapeDtypeStruct(dims, dtype)


def unit(value):
    centered = value - jnp.mean(value, axis=-1, keepdims=True)
    spread = jnp.mean(centered * centered, axis=-1, keepdims=True)
    scale = lax.rsqrt(spread + epsilon)
    return centered * scale, scale


def unit_back(grad, normal, scale):
    mean = jnp.mean(grad, axis=-1, keepdims=True)
    along = jnp.mean(grad * normal, axis=-1, keepdims=True)
    return scale * (grad - mean - normal * along)


def column_sum(value):
    return jnp.sum(value, axis=0, keepdims=True)


def prepare(qkv, up, gain, shift, bias, pack, up0, up1, up2, up3, small, sems):
    c, w = lax.axis_index("ctx"), lax.axis_index("wt")
    width = qkv.shape[1] // 3
    span = pack.shape[1] // 3
    rows = qkv.shape[0]
    copies = []
    for part in range(3):
        source = qkv.at[:, at(part * (width // span) + c, span)]
        copies.append((source, pack.at[pl.ds(0, rows), pl.ds(part * span, span)]))
    size = up0.shape[1]
    for d, out in enumerate((up0, up1, up2, up3)):
        copies.append((up.at[:, at(w ^ d, size)], out))
    copies.append((small, pack.at[pl.ds(rows, SMALL), :]))
    small[...] = jnp.zeros_like(small)
    for i, ref in enumerate((gain, shift, bias)):
        small[pl.ds(4 * i, 4), pl.ds(0, ref.shape[1])] = ref[...]
    copies = [pltpu.make_async_copy(a, b, sems.at[i]) for i, (a, b) in enumerate(copies)]
    for copy in copies:
        copy.start()
    for copy in copies:
        copy.wait()


def slot_copies(slots, target, sems, each):
    c = lax.axis_index("ctx")
    y, z = c % 2, c // 2
    ways = [(z >= 0, z)]
    ways += [(z >= k, z - k) for k in range(1, Z_LINE)]
    ways += [(z + k < Z_LINE, z + k) for k in range(1, Z_LINE)]
    steps = []
    for i, ref in enumerate(slots):
        valid, zi = ways[i % len(ways)]
        ci = 2 * zi + (y if i < len(ways) else 1 - y)
        pairs = [
            pltpu.make_async_copy(a, b, sems.at[2 * i + j]) for j, (a, b) in enumerate(each(ref, ci))
        ]
        steps.append((valid, pairs))
    return steps


def attend(deal, *refs):
    slots, (p0, p1, p2, p3), rest = refs[:14], refs[14:18], refs[18:]
    first, mixed, out, stats, small, xs, norm, sems = rest
    c, w = lax.axis_index("ctx"), lax.axis_index("wt")
    length, width = xs.shape
    span = out.shape[2]
    heads = stats.shape[0] // 2
    head = span // heads
    packs = (p0, p1, p2, p3)

    def halves(ref, ci):
        ci = jnp.clip(ci, 0, deal.shape[0] - 1)
        return [(ref.at[pl.ds(PIECE * t, PIECE), :], xs.at[at(deal[ci, t], PIECE), :]) for t in range(2)]

    steps = slot_copies(slots, xs, sems, halves)
    for valid, pairs in steps:
        for copy in pairs:
            pl.when(valid)(copy.start)
    for d in range(WT):
        small[:, at(w ^ d, PART)] = packs[d][pl.ds(PART, SMALL), pl.ds(0, PART)].astype(F32)
    for valid, pairs in steps:
        for copy in pairs:
            pl.when(valid)(copy.wait)
    bias_q = small[pl.ds(8, 1), at(c, span)]
    bias_v = small[pl.ds(9, 1), at(c, span)]
    chunk = BLK

    @pl.loop(0, length // chunk)
    def _(i):
        rows = at(i, chunk)
        normal, _scale = unit(xs[rows, :].astype(F32))
        first[rows, :] = (normal * small[pl.ds(0, 1), :] + small[pl.ds(4, 1), :]).astype(BF16)
        total = dot(first[rows, at(w, PART)], packs[0][pl.ds(0, PART), :])
        for d in range(1, WT):
            total += dot(first[rows, at(w ^ d, PART)], packs[d][pl.ds(0, PART), :])
        mixed[rows, pl.ds(0, span)] = (total[:, :span] + bias_q).astype(BF16)
        mixed[rows, pl.ds(span, span)] = total[:, span : 2 * span].astype(BF16)
        mixed[rows, pl.ds(2 * span, span)] = (total[:, 2 * span :] + bias_v).astype(BF16)

    lane = lax.broadcasted_iota(jnp.int32, (BLK, span), 1) // head
    factor = 1.0 / math.sqrt(head)
    for b in range(length // BLK):
        rows, seen = pl.ds(b * BLK, BLK), pl.ds(0, (b + 1) * BLK)
        query = mixed[rows, pl.ds(0, span)]
        parts = []
        for h in range(heads):
            masked = jnp.where(lane == h, query, jnp.zeros_like(query))
            raw = dot_t(mixed[seen, pl.ds(span, span)], masked)
            top = jnp.max(raw, axis=0, keepdims=True)
            terms = jnp.exp((raw - top) * factor)
            inverse = 1.0 / jnp.sum(terms, axis=0, keepdims=True)
            stats[pl.ds(2 * h, 1), rows] = top
            stats[pl.ds(2 * h + 1, 1), rows] = inverse
            weights = (terms * inverse).astype(BF16)
            values = mixed[seen, pl.ds(2 * span, span)]
            parts.append(t_dot(values, weights)[h * head : (h + 1) * head, :])
        norm[rows, :] = jnp.concatenate(parts, axis=0).T.astype(BF16)
    for j in range(out.shape[0]):
        for t in range(2):
            out[j, pl.ds(PIECE * t, PIECE), :] = norm[at(deal[j, t], PIECE), :]


def project(attended, o0, o1, o2, o3, own, small, branch, resid, second):
    w = lax.axis_index("wt")
    span = attended.shape[2]
    total = small[pl.ds(10, 1), :]
    for d, ref in enumerate((o0, o1, o2, o3)):
        for j in range(PART // span):
            total = total + dot(attended[(w ^ d) * (PART // span) + j], ref[pl.ds(span * j, span), :])
    branch[...] = total
    normal, _ = unit(total)
    total = own[...].astype(F32) + (normal * small[pl.ds(1, 1), :] + small[pl.ds(5, 1), :])
    resid[...] = total
    normal, _ = unit(total)
    second[...] = (normal * small[pl.ds(2, 1), :] + small[pl.ds(6, 1), :]).astype(BF16)


def feed(s0, s1, s2, s3, u0, u1, u2, u3, bias, down, all_rows, hidden, slope, near, far):
    w = lax.axis_index("wt")
    rows = s0.shape[0]
    for i, ref in enumerate((s0, s2, s1, s3)):
        all_rows[pl.ds(rows * i, rows), :] = ref[...]

    @pl.loop(0, hidden.shape[1] // PART)
    def _(n):
        cols = at(n, PART)
        upper = bias[pl.ds(0, 1), cols].astype(F32)
        for d, ref in enumerate((u0, u1, u2, u3)):
            upper = upper + dot(all_rows[:, at(w ^ d, PART)], ref[:, cols])
        square = upper * upper
        curve = jnp.tanh(GELU_A * (upper + GELU_B * (square * upper)))
        half = 0.5 * (1.0 + curve)
        hidden[:, cols] = (upper * half).astype(BF16)
        slope[:, cols] = half + (0.5 * GELU_A) * upper * (1.0 - curve * curve) * (
            1.0 + (3.0 * GELU_B) * square
        )

    @pl.loop(0, near.shape[1] // PART)
    def _(n):
        cols = at(n, PART)
        total = dot(hidden[...], down[:, cols])
        near[:, cols] = total[: 2 * rows]
        far[:, cols] = total[2 * rows :].astype(BF16)


def top_norm(near, got, far, resid, grad, small, result, d_ffn, sums):
    rows = resid.shape[0]
    ffn = near[pl.ds(0, rows), :] + got[pl.ds(0, rows), :].astype(F32) + far[...].astype(F32)
    normal, scale = unit(ffn + small[pl.ds(11, 1), :])
    gain = small[pl.ds(3, 1), :]
    result[...] = (resid[...] + (normal * gain + small[pl.ds(7, 1), :])).astype(BF16)
    d_out = grad[...].astype(F32)
    low = unit_back(d_out * gain, normal, scale).astype(BF16)
    d_ffn[...] = low
    sums[pl.ds(0, 1), :] = column_sum(d_out * normal)
    sums[pl.ds(1, 1), :] = column_sum(d_out)
    sums[pl.ds(2, 1), :] = column_sum(low.astype(F32))


def feed_back(s0, s1, s2, s3, u0, u1, u2, u3, down, slope, all_rows, d_upper, near, far, sums):
    w = lax.axis_index("wt")
    rows = s0.shape[0]
    for i, ref in enumerate((s0, s2, s1, s3)):
        all_rows[pl.ds(rows * i, rows), :] = ref[...]

    @pl.loop(0, d_upper.shape[1] // PART)
    def _(n):
        cols = at(n, PART)
        low = (dot_t(all_rows[...], down[cols, :]) * slope[:, cols]).astype(BF16)
        d_upper[:, cols] = low
        sums[pl.ds(0, 1), cols] = column_sum(low.astype(F32))

    for d, ref in enumerate((u0, u1, u2, u3)):
        cols = at(w ^ d, PART)
        total = dot_t(d_upper[...], ref[...])
        near[:, cols] = total[: 2 * rows]
        far[:, cols] = total[2 * rows :].astype(BF16)


def grad_down(hidden, grads, keep, send):
    y = lax.axis_index("ctx") % 2
    size = keep.shape[1]

    @pl.loop(0, Z_LINE)
    def _(z):
        keep[z] = t_dot(hidden[:, at(2 * z + y, size)], grads[...]).astype(BF16)
        send[z] = t_dot(hidden[:, at(2 * z + 1 - y, size)], grads[...]).astype(BF16)


def grad_up(rows_in, grads, keep, send, part):
    y = lax.axis_index("ctx") % 2
    cut = PART // (2 * Z_LINE)

    @pl.loop(0, WT)
    def _(i):
        part[...] = t_dot(rows_in[:, at(i, PART)], grads[...]).astype(BF16)
        for z in range(Z_LINE):
            keep[z, at(i, cut), :] = part[at(2 * z + y, cut), :]
            send[z, at(i, cut), :] = part[at(2 * z + 1 - y, cut), :]


def middle_norms(near, got, far, resid, branch, grad, o0, o1, o2, o3, small, d_resid, d_att, d_out, sums):
    w = lax.axis_index("wt")
    rows, span = resid.shape[0], d_out.shape[2]
    d_second = near[pl.ds(0, rows), :] + got[pl.ds(0, rows), :].astype(F32) + far[...].astype(F32)
    normal, scale = unit(resid[...])
    sums[pl.ds(0, 1), :] = column_sum(d_second * normal)
    sums[pl.ds(1, 1), :] = column_sum(d_second)
    total = grad[...].astype(F32) + unit_back(d_second * small[pl.ds(2, 1), :], normal, scale)
    d_resid[...] = total
    normal, scale = unit(branch[...])
    sums[pl.ds(2, 1), :] = column_sum(total * normal)
    sums[pl.ds(3, 1), :] = column_sum(total)
    low = unit_back(total * small[pl.ds(1, 1), :], normal, scale).astype(BF16)
    d_att[...] = low
    sums[pl.ds(4, 1), :] = column_sum(low.astype(F32))
    for d, ref in enumerate((o0, o1, o2, o3)):
        part = dot_t(low, ref[...]).astype(BF16)
        for j in range(PART // span):
            d_out[(w ^ d) * (PART // span) + j] = part[:, span * j : span * (j + 1)]


def grad_out(attended, grads, keep, send):
    w = lax.axis_index("wt")
    span = attended.shape[2]
    for d in range(WT):
        target = send if d % 2 else keep
        for j in range(PART // span):
            part = t_dot(attended[(w ^ d) * (PART // span) + j], grads[...])
            target[d // 2, pl.ds(span * j, span), :] = part.astype(BF16)


def attend_back(deal, mixed, stats, got, natural, dealt, d_out, d_keys, d_values):
    length, span = d_out.shape
    heads = stats.shape[0] // 2
    head = span // heads
    factor = 1.0 / math.sqrt(head)
    prescale = factor / relax
    for j in range(got.shape[0]):
        for t in range(2):
            d_out[at(deal[j, t], PIECE), :] = got[j, pl.ds(PIECE * t, PIECE), :]
    d_keys[...] = jnp.zeros_like(d_keys)
    d_values[...] = jnp.zeros_like(d_values)
    lane = lax.broadcasted_iota(jnp.int32, (BLK, span), 1) // head
    for b in range(length // BLK):
        rows, seen = pl.ds(b * BLK, BLK), pl.ds(0, (b + 1) * BLK)
        query, grads = mixed[rows, pl.ds(0, span)], d_out[rows, :]
        parts = []
        for h in range(heads):
            query_h = jnp.where(lane == h, query, jnp.zeros_like(query))
            grads_h = jnp.where(lane == h, grads, jnp.zeros_like(grads))
            keys = mixed[seen, pl.ds(span, span)]
            raw = dot_t(keys, query_h)
            weights = jnp.exp((raw - stats[pl.ds(2 * h, 1), rows]) * factor) * stats[pl.ds(2 * h + 1, 1), rows]
            d_probs = dot_t(mixed[seen, pl.ds(2 * span, span)], grads_h)
            delta = jnp.sum(weights * d_probs, axis=0, keepdims=True)
            d_scores = (relax * weights * (d_probs - delta)).astype(BF16)
            d_values[seen, :] += dot(weights.astype(BF16), grads_h)
            d_keys[seen, :] += dot(d_scores, query_h)
            parts.append(t_dot(keys, d_scores)[h * head : (h + 1) * head, :])
        natural[rows, pl.ds(0, span)] = (jnp.concatenate(parts, axis=0).T * prescale).astype(BF16)
    natural[:, pl.ds(span, span)] = (d_keys[...] * prescale).astype(BF16)
    natural[:, pl.ds(2 * span, span)] = d_values[...].astype(BF16)
    for j in range(dealt.shape[0]):
        for t in range(2):
            dealt[j, pl.ds(PIECE * t, PIECE), :] = natural[at(deal[j, t], PIECE), :]


def grad_qkv(first, grads, keep, send):
    w = lax.axis_index("wt")
    for d in range(WT):
        target = send if d % 2 else keep
        target[d // 2] = t_dot(first[:, at(w ^ d, PART)], grads[...]).astype(BF16)


def bottom_norm(got, q0, q1, q2, q3, own, d_resid, small, input_grad, sums, joined, d_first):
    w = lax.axis_index("wt")
    ranks, rows, triple = got.shape
    span, width = triple // 3, own.shape[1]
    for j in range(ranks):
        for part in range(3):
            joined[:, pl.ds(part * width + span * j, span)] = got[j, :, pl.ds(span * part, span)]
    for d, ref in enumerate((q0, q1, q2, q3)):
        d_first[:, at(w ^ d, PART)] = dot_t(joined[...], ref[...])
    normal, scale = unit(own[...].astype(F32))
    grads = d_first[...]
    sums[pl.ds(0, 1), :] = column_sum(grads * normal)
    sums[pl.ds(1, 1), :] = column_sum(grads)
    sums[pl.ds(2, 1), :] = column_sum(joined[:, pl.ds(0, width)].astype(F32))
    sums[pl.ds(3, 1), :] = column_sum(joined[:, pl.ds(2 * width, width)].astype(F32))
    input_grad[...] = d_resid[...] + unit_back(grads * small[pl.ds(0, 1), :], normal, scale)


def arrived(slots, buffer, sems):
    def whole(ref, ci):
        return [(ref, buffer.at[jnp.clip(ci, 0, buffer.shape[0] - 1)])]

    steps = slot_copies(slots, buffer, sems, whole)
    for valid, (copy,) in steps:
        pl.when(valid)(copy.start)
    for valid, (copy,) in steps:
        pl.when(valid)(copy.wait)


def spread_qkv(*refs):
    slots, (full, buffer, sems) = refs[:14], refs[14:]
    arrived(slots, buffer, sems)
    ranks, _, triple = buffer.shape
    span = triple // 3
    for j in range(ranks):
        for part in range(3):
            cols = pl.ds((part * ranks + j) * span, span)
            full[:, cols] = buffer[j, :, pl.ds(span * part, span)].astype(F32)


def spread_rest(*refs):
    slots, (down, up, out, buffer, sems) = refs[:14], refs[14:]
    w = lax.axis_index("wt")
    arrived(slots, buffer, sems)
    ranks = buffer.shape[0]
    rows = down.shape[0] // ranks
    cut = up.shape[0] // ranks

    @pl.loop(0, ranks)
    def _(j):
        down[at(j, rows), :] = buffer[j, pl.ds(0, rows), :].astype(F32)
        for d in range(WT):
            cols = at(w ^ d, down.shape[1])
            up[at(j, cut), cols] = buffer[j, pl.ds(rows + cut * d, cut), :].astype(F32)
        out[at(j, cut), :] = buffer[j, pl.ds(rows + cut * WT, cut), :].astype(F32)


def split_device(
    layer_input,
    out_grad,
    deal,
    w_qkv,
    w_out,
    w_up,
    w_down,
    norm_gain,
    norm_shift,
    bias_width,
    up_bias,
):
    _, rows, width = layer_input.shape
    ranks = lax.axis_size("ctx")
    c, w = lax.axis_index("ctx"), lax.axis_index("wt")
    per = HEADS // ranks
    span = per * (width // HEADS)
    length = rows * ranks
    hidden_width = w_down.shape[0]
    own, grad = layer_input[0], out_grad[0]
    hbm, smem, dma = pl.ANY, pltpu.SMEM, pltpu.SemaphoreType.DMA

    sequence = gather_ctx(own)
    pack, *ups = call(
        prepare,
        "prepare",
        (w_qkv, w_up, norm_gain, norm_shift, bias_width),
        [shape(PART + SMALL, 3 * span)] + [shape(PART, hidden_width)] * WT,
        places={0: hbm, 1: hbm},
        out_places={i: hbm for i in range(5)},
        scratch=[pltpu.VMEM((SMALL, 3 * span), BF16), dma((8,))],
        limit=8,
    )
    packs = gather_wt(pack)
    ups = (ups[0], swap(ups[1], "wt", 1), swap(ups[2], "wt", 2), swap(ups[3], "wt", 3))
    outs = gather_wt(w_out)

    first, mixed, sent, stats, small = call(
        attend,
        "attend",
        (deal, *sequence, *packs),
        [
            shape(length, width),
            shape(length, 3 * span),
            shape(ranks, rows, span),
            shape(2 * per, length, dtype=F32),
            shape(SMALL, width, dtype=F32),
        ],
        places={0: smem} | {i: hbm for i in range(1, 15)},
        scratch=[pltpu.VMEM((length, width), BF16), pltpu.VMEM((length, span), BF16), dma((28,))],
        flops=2 * length * width * 3 * span + 4 * length * length * span,
        limit=40,
    )
    attended = lax.all_to_all(sent, "ctx", 0, 0, tiled=True)
    branch, resid, second = call(
        project,
        "project",
        (attended, *outs, own, small),
        [shape(rows, width, dtype=F32), shape(rows, width, dtype=F32), shape(rows, width)],
        flops=2 * rows * width * width,
    )

    everyone = WT * rows
    halves = [shape(2 * rows, width, dtype=F32), shape(2 * rows, width)]
    seconds, hidden, slope, near, far = call(
        feed,
        "feed",
        (*gather_wt(second), *ups, up_bias.reshape(1, hidden_width), w_down),
        [shape(everyone, width), shape(everyone, hidden_width), shape(everyone, hidden_width, dtype=F32)]
        + halves,
        flops=4 * everyone * width * hidden_width,
        limit=40,
    )

    def return_rows(near, far):
        got = swap(far, "wt", 1)
        back = (near[rows:] + got[rows:].astype(F32)).astype(BF16)
        return near, got, swap(back, "wt", 2)

    result, d_ffn, sums3 = call(
        top_norm,
        "top_norm",
        (*return_rows(near, far), resid, grad, small),
        [shape(rows, width), shape(rows, width), shape(3, width, dtype=F32)],
    )
    d_ffns, d_upper, near, far, up_sum = call(
        feed_back,
        "feed_back",
        (*gather_wt(d_ffn), *ups, w_down, slope),
        [shape(everyone, width), shape(everyone, hidden_width)] + halves + [shape(1, hidden_width, dtype=F32)],
        flops=4 * everyone * width * hidden_width,
        limit=40,
    )
    d_resid, d_att, sent, sums21 = call(
        middle_norms,
        "middle_norms",
        (*return_rows(near, far), resid, branch, grad, *outs, small),
        [
            shape(rows, width, dtype=F32),
            shape(rows, width),
            shape(ranks, rows, span),
            shape(5, width, dtype=F32),
        ],
        flops=2 * rows * width * width,
    )
    got = lax.all_to_all(sent, "ctx", 0, 0, tiled=True)

    eighth = hidden_width // ranks
    chunks = [shape(Z_LINE, eighth, width)] * 2
    down_part = scatter_ctx(
        *call(grad_down, "grad_down", (hidden, d_ffns), chunks, flops=2 * everyone * width * hidden_width)
    )
    keep_up, send_up = call(
        grad_up,
        "grad_up",
        (seconds, d_upper),
        chunks,
        scratch=[pltpu.VMEM((PART, hidden_width), BF16)],
        flops=2 * everyone * width * hidden_width,
    )
    pieces = [shape(2, PART, width)] * 2
    out_rows = scatter_wt(*call(grad_out, "grad_out", (attended, d_att), pieces, flops=2 * rows * width * width))
    cut = PART // ranks
    out_rows = out_rows.reshape(Z_LINE, 2, cut, width)
    y = c % 2
    rest_part = scatter_ctx(
        jnp.concatenate([keep_up, pick(out_rows, y, 1)], axis=1),
        jnp.concatenate([send_up, pick(out_rows, 1 - y, 1)], axis=1),
    )
    up_part = [lax.dynamic_slice_in_dim(rest_part, (w ^ d) * cut, cut, 0) for d in range(WT)]
    up_part = [up_part[0]] + [swap(up_part[d], "wt", d) for d in range(1, WT)]
    rest = jnp.concatenate([down_part, *up_part, rest_part[WT * cut :]], axis=0)

    natural, dealt = call(
        attend_back,
        "attend_back",
        (deal, mixed, stats, got),
        [shape(length, 3 * span), shape(ranks, rows, 3 * span)],
        places={0: smem},
        scratch=[
            pltpu.VMEM((length, span), BF16),
            pltpu.VMEM((length, span), F32),
            pltpu.VMEM((length, span), F32),
        ],
        flops=10 * length * length * span,
    )
    got = lax.all_to_all(dealt, "ctx", 0, 0, tiled=True)
    pieces = [shape(2, PART, 3 * span)] * 2
    qkv_part = scatter_wt(
        *call(grad_qkv, "grad_qkv", (first, natural), pieces, flops=2 * length * width * 3 * span)
    )
    late_qkv, _ = lax.optimization_barrier((w_qkv, d_att))
    input_grad, sums0 = call(
        bottom_norm,
        "bottom_norm",
        (got, *gather_wt(late_qkv), own, d_resid, small),
        [shape(rows, width, dtype=F32), shape(4, width, dtype=F32)],
        scratch=[pltpu.VMEM((rows, 3 * width), BF16), pltpu.VMEM((rows, width), F32)],
        flops=6 * rows * width * width,
    )

    qkv_slots, rest_slots = gather_ctx(qkv_part), gather_ctx(rest)
    full_qkv = call(
        spread_qkv,
        "spread_qkv",
        qkv_slots,
        [shape(PART, 3 * width, dtype=F32)],
        places={i: hbm for i in range(14)},
        scratch=[pltpu.VMEM((ranks, PART, 3 * span), BF16), dma((28,))],
    )
    full_down, full_up, full_out = call(
        spread_rest,
        "spread_rest",
        rest_slots,
        [
            shape(hidden_width, width, dtype=F32),
            shape(PART, WT * hidden_width, dtype=F32),
            shape(PART, width, dtype=F32),
        ],
        places={i: hbm for i in range(14)},
        scratch=[pltpu.VMEM((ranks,) + rest.shape, BF16), dma((28,))],
        limit=40,
    )

    sums = jnp.concatenate([sums0, sums21, sums3], axis=0)
    for bit in (1, 2):
        sums = sums + swap(sums, "wt", bit)
    sums = lax.dynamic_slice_in_dim(sums, w * PART, PART, 1)
    sums = jnp.concatenate([sums, up_sum.reshape(WT, PART)], axis=0)
    for bit in (1, 2, 4):
        sums = sums + swap(sums, "ctx", bit)
    g0, s0, b0, b1, g2, s2, g1, s1, b2, g3, s3, b3 = (sums[i] for i in range(12))
    return (
        result[None],
        input_grad[None],
        full_qkv,
        full_out,
        full_up,
        full_down,
        jnp.stack([g0, g1, g2, g3]),
        jnp.stack([s0, s1, s2, s3]),
        jnp.stack([b0, b1, b2, b3]),
        sums[12:].reshape(hidden_width),
    )


def solution(mesh):
    small = mesh.shape["ctx"] == 2 * Z_LINE and mesh.shape["wt"] == WT
    per_device = split_device if small else general_device
    in_specs = (
        P("wt", "ctx", None),
        P("wt", "ctx", None),
        P(),
        P("wt", None),
        P("wt", None),
        P("wt", None),
        P("wt", None),
        P(None, "wt"),
        P(None, "wt"),
        P(None, "wt"),
        P("wt"),
    )
    out_specs = (
        P("wt", "ctx", None),
        P("wt", "ctx", None),
        P("wt", None),
        P("wt", None),
        P("wt", None),
        P("wt", None),
        P(None, "wt"),
        P(None, "wt"),
        P(None, "wt"),
        P("wt"),
    )
    return jax.shard_map(
        per_device, mesh=mesh, in_specs=in_specs, out_specs=out_specs, check_vma=False
    )
```

```python
import math

import jax
import jax.numpy as jnp
from jax import lax
from jax.experimental import pallas as pl
from jax.experimental.pallas import tpu as pltpu
from jax.sharding import PartitionSpec as P

HEADS = 16
BLK = 256
PIECE = 64


epsilon = 1e-05
relax = 32.0


def layer_norm(value, gain, shift):
    mean = jnp.mean(value, axis=-1, keepdims=True)
    centered = value - mean
    spread = jnp.mean(centered * centered, axis=-1, keepdims=True)
    return centered * lax.rsqrt(spread + epsilon) * gain + shift


def gelu_tanh(value):
    return jax.nn.gelu(value, approximate=True)


def rows_dot(left, weight):
    return jnp.einsum("std,de->ste", left, weight, preferred_element_type=jnp.float32)


def weight_grad(left, right):
    return jnp.einsum("std,ste->de", left, right, preferred_element_type=jnp.float32)


def back_dot(grad, weight):
    return jnp.einsum("ste,de->std", grad, weight, preferred_element_type=jnp.float32)


def row_total(value):
    return jnp.sum(value.astype(jnp.float32), axis=(0, 1))


def general_device(
    layer_input,
    out_grad,
    deal,
    w_qkv,
    w_out,
    w_up,
    w_down,
    norm_gain,
    norm_shift,
    bias_width,
    up_bias,
):
    seqs, rows, width = layer_input.shape
    heads = HEADS
    head = width // heads
    prescale = 1.0 / (relax * math.sqrt(head))
    ranks = lax.axis_size("ctx")
    length = rows * ranks
    per_block = BLK // PIECE
    rank = lax.axis_index("ctx")
    chosen = jnp.arange(ranks, dtype=jnp.int32) == rank
    mine = jnp.sum(jnp.where(chosen[:, None], deal, 0), axis=0)
    query_blocks = jnp.repeat(mine, rows // 2) // per_block
    key_blocks = jnp.repeat(deal.reshape(-1), rows // 2) // per_block
    full_qkv, full_out, full_up, full_down, gains, shifts, biases, up_shift = (
        lax.all_gather(w_qkv, "wt", axis=0, tiled=True),
        lax.all_gather(w_out, "wt", axis=0, tiled=True),
        lax.all_gather(w_up, "wt", axis=0, tiled=True),
        lax.all_gather(w_down, "wt", axis=0, tiled=True),
        lax.all_gather(norm_gain, "wt", axis=1, tiled=True),
        lax.all_gather(norm_shift, "wt", axis=1, tiled=True),
        lax.all_gather(bias_width, "wt", axis=1, tiled=True),
        lax.all_gather(up_bias, "wt", axis=0, tiled=True),
    )
    gains = gains.astype(jnp.float32)
    shifts = shifts.astype(jnp.float32)
    biases = biases.astype(jnp.float32)
    up_shift = up_shift.astype(jnp.float32)
    input_float = layer_input.astype(jnp.float32)
    first = layer_norm(input_float, gains[0], shifts[0]).astype(jnp.bfloat16)
    mixed = rows_dot(first, full_qkv)
    query = (mixed[..., :width] + biases[0]).astype(jnp.bfloat16)
    kv_local = jnp.concatenate(
        [mixed[..., width : 2 * width], mixed[..., 2 * width :] + biases[1]], axis=-1
    ).astype(jnp.bfloat16)
    kv_all = lax.all_gather(kv_local, "ctx", axis=1, tiled=True)
    step = math.gcd(length, 1024)
    count = length // step
    query4 = query.reshape(seqs, rows, heads, head)

    def score_block(left, right):
        return (
            jnp.einsum("sqhd,skhd->shqk", left, right, preferred_element_type=jnp.float32)
            * prescale
        )

    def key_block(index):
        start = index * step
        piece = lax.dynamic_slice_in_dim(kv_all, start, step, 1)
        keys4 = piece[..., :width].reshape(seqs, step, heads, head)
        values4 = piece[..., width:].reshape(seqs, step, heads, head)
        visible = (
            query_blocks[:, None] >= lax.dynamic_slice_in_dim(key_blocks, start, step, 0)[None, :]
        )
        return (keys4, values4, visible)

    def probs(raw, visible, totals):
        return jnp.where(visible, jnp.exp(raw * relax - totals[..., None]), 0.0)

    def online(index, carry):
        top, total, acc = carry
        keys4, values4, visible = key_block(index)
        raw = jnp.where(visible, score_block(query4, keys4), -1e30)
        new_top = jnp.maximum(top, jnp.max(raw, axis=-1))
        terms = jnp.where(visible, jnp.exp((raw - new_top[..., None]) * relax), 0.0)
        factor = jnp.exp((top - new_top) * relax)
        total = total * factor + jnp.sum(terms, axis=-1)
        acc = acc * jnp.transpose(factor, (0, 2, 1))[..., None]
        acc = acc + jnp.einsum(
            "shqk,skhd->sqhd",
            terms.astype(jnp.bfloat16),
            values4,
            preferred_element_type=jnp.float32,
        )
        return (new_top, total, acc)

    start_top = jnp.full((seqs, heads, rows), -1e30, jnp.float32)
    start_total = jnp.zeros((seqs, heads, rows), jnp.float32)
    start_acc = jnp.zeros((seqs, rows, heads, head), jnp.float32)
    top, total, acc = lax.fori_loop(0, count, online, (start_top, start_total, start_acc))
    log_total = top * relax + jnp.log(total)
    attended_float = acc / jnp.transpose(total, (0, 2, 1))[..., None]
    attended = attended_float.reshape(seqs, rows, width).astype(jnp.bfloat16)
    branch = rows_dot(attended, full_out) + biases[2]
    resid = input_float + layer_norm(branch, gains[1], shifts[1])
    second = layer_norm(resid, gains[2], shifts[2]).astype(jnp.bfloat16)
    upper = rows_dot(second, full_up) + up_shift
    hidden = gelu_tanh(upper).astype(jnp.bfloat16)
    ffn = rows_dot(hidden, full_down) + biases[3]
    top_norm, pull_four = jax.vjp(layer_norm, ffn, gains[3], shifts[3])
    result = resid + top_norm
    d_out = out_grad.astype(jnp.float32)
    d_ffn, d_gain3, d_shift3 = pull_four(d_out)
    d_ffn = d_ffn.astype(jnp.bfloat16)
    d_bias3 = row_total(d_ffn)
    g_down = weight_grad(hidden, d_ffn)
    d_hidden = back_dot(d_ffn, full_down)
    _, pull_gelu = jax.vjp(gelu_tanh, upper)
    d_upper = pull_gelu(d_hidden)[0].astype(jnp.bfloat16)
    d_up_shift = row_total(d_upper)
    g_up = weight_grad(second, d_upper)
    d_second = back_dot(d_upper, full_up)
    _, pull_three = jax.vjp(layer_norm, resid, gains[2], shifts[2])
    d_resid_part, d_gain2, d_shift2 = pull_three(d_second)
    d_resid = d_out + d_resid_part
    _, pull_two = jax.vjp(layer_norm, branch, gains[1], shifts[1])
    d_branch, d_gain1, d_shift1 = pull_two(d_resid)
    d_branch = d_branch.astype(jnp.bfloat16)
    d_bias2 = row_total(d_branch)
    g_out = weight_grad(attended, d_branch)
    d_attended = back_dot(d_branch, full_out).astype(jnp.bfloat16)
    d_out4 = d_attended.reshape(seqs, rows, heads, head)
    delta = jnp.einsum("sqhd,sqhd->shq", d_out4.astype(jnp.float32), attended_float)

    def score_grads(q_rows, do_rows, k_rows, v_rows, visible, lse_rows, delta_rows):
        weights = probs(score_block(q_rows, k_rows), visible, lse_rows)
        d_probs = jnp.einsum("sqhd,skhd->shqk", do_rows, v_rows, preferred_element_type=jnp.float32)
        d_scores = (relax * weights * (d_probs - delta_rows[..., None])).astype(jnp.bfloat16)
        return (d_scores, weights.astype(jnp.bfloat16))

    zero_query = jnp.zeros((seqs, rows, heads, head), jnp.float32)

    def local_grads(d_query, index):
        keys4, values4, visible = key_block(index)
        d_scores, weights = score_grads(query4, d_out4, keys4, values4, visible, log_total, delta)
        d_query = (
            d_query
            + jnp.einsum("shqk,skhd->sqhd", d_scores, keys4, preferred_element_type=jnp.float32)
            * prescale
        )
        d_keys = (
            jnp.einsum("shqk,sqhd->kshd", d_scores, query4, preferred_element_type=jnp.float32)
            * prescale
        )
        d_values = jnp.einsum(
            "shqk,sqhd->kshd", weights, d_out4, preferred_element_type=jnp.float32
        )
        joined = jnp.concatenate(
            [d_keys.reshape(step, seqs, width), d_values.reshape(step, seqs, width)], axis=-1
        )
        return (d_query, joined)

    d_query, pieces = lax.scan(local_grads, zero_query, jnp.arange(count, dtype=jnp.int32))
    terms = pieces.reshape(length, seqs, 2 * width)
    d_kv = jnp.transpose(lax.psum_scatter(terms, "ctx", scatter_dimension=0, tiled=True), (1, 0, 2))
    d_query = d_query.reshape(seqs, rows, width).astype(jnp.bfloat16)
    d_kv = d_kv.astype(jnp.bfloat16)
    d_bias0 = row_total(d_query)
    d_bias1 = row_total(d_kv[..., width:])
    d_mixed = jnp.concatenate([d_query, d_kv], axis=-1)
    g_qkv = weight_grad(first, d_mixed)
    d_first = back_dot(d_mixed, full_qkv)
    _, pull_one = jax.vjp(layer_norm, input_float, gains[0], shifts[0])
    d_input_part, d_gain0, d_shift0 = pull_one(d_first)
    input_grad = d_resid + d_input_part
    grad_gain = jnp.stack([d_gain0, d_gain1, d_gain2, d_gain3])
    grad_shift = jnp.stack([d_shift0, d_shift1, d_shift2, d_shift3])
    grad_bias = jnp.stack([d_bias0, d_bias1, d_bias2, d_bias3])
    owned = (
        lax.psum_scatter(g_qkv.astype(jnp.bfloat16), "wt", scatter_dimension=0, tiled=True).astype(
            jnp.float32
        ),
        lax.psum_scatter(g_out.astype(jnp.bfloat16), "wt", scatter_dimension=0, tiled=True).astype(
            jnp.float32
        ),
        lax.psum_scatter(g_up.astype(jnp.bfloat16), "wt", scatter_dimension=0, tiled=True).astype(
            jnp.float32
        ),
        lax.psum_scatter(g_down.astype(jnp.bfloat16), "wt", scatter_dimension=0, tiled=True).astype(
            jnp.float32
        ),
        lax.psum_scatter(
            grad_gain.astype(jnp.bfloat16), "wt", scatter_dimension=1, tiled=True
        ).astype(jnp.float32),
        lax.psum_scatter(
            grad_shift.astype(jnp.bfloat16), "wt", scatter_dimension=1, tiled=True
        ).astype(jnp.float32),
        lax.psum_scatter(
            grad_bias.astype(jnp.bfloat16), "wt", scatter_dimension=1, tiled=True
        ).astype(jnp.float32),
        lax.psum_scatter(
            d_up_shift.astype(jnp.bfloat16), "wt", scatter_dimension=0, tiled=True
        ).astype(jnp.float32),
    )
    summed = lax.psum(
        (owned[0], owned[1], owned[2], owned[3], owned[4], owned[5], owned[6], owned[7]), "ctx"
    )
    return (
        result.astype(jnp.bfloat16),
        input_grad,
        summed[0],
        summed[1],
        summed[2],
        summed[3],
        summed[4],
        summed[5],
        summed[6],
        summed[7],
    )


F32 = jnp.float32
BF16 = jnp.bfloat16
WT = 4
CTX = 8
PART = 256
SMALL = 16
GELU_A = math.sqrt(2.0 / math.pi)
GELU_B = 0.044715


def swap(value, axis, bit):
    size = lax.axis_size(axis)
    return lax.ppermute(value, axis, [(i, i ^ bit) for i in range(size)])


def gather_wt(block):
    far = swap(block, "wt", 2)
    return block, swap(block, "wt", 1), far, swap(far, "wt", 1)


def gather_ctx(block, order=(4, 2, 1)):
    blocks = {0: block}
    for bit in order:
        blocks.update({d ^ bit: swap(value, "ctx", bit) for d, value in blocks.items()})
    return [blocks[d] for d in range(CTX)]


def after(value, *others):
    return lax.optimization_barrier((value, *others))[0]


def floats(value):
    return value.astype(F32)


def scatter_wt(keep, send, kind=BF16):
    got = swap(send, "wt", 1)
    far = swap((floats(keep[1]) + floats(got[1])).astype(kind), "wt", 2)
    return (floats(keep[0]) + floats(got[0]) + floats(far)).astype(kind)


def scatter_ctx(keep_low, keep_high, send_low, send_high, first, second, third):
    got_high, got_low = swap(send_high, "ctx", 1), swap(send_low, "ctx", 1)
    high = (floats(keep_high) + floats(after(got_high, *first))).astype(BF16)
    got = swap(high, "ctx", 2)
    low = floats(keep_low) + floats(got_low) + floats(after(got, *second))
    last = swap(low[1].astype(BF16), "ctx", 4)
    return (low[0] + floats(after(last, *third))).astype(BF16)


def dot(left, right):
    return jnp.dot(left, right, preferred_element_type=F32)


def dot_t(left, right):
    return lax.dot_general(left, right, (((1,), (1,)), ((), ())), preferred_element_type=F32)


def t_dot(left, right):
    return lax.dot_general(left, right, (((0,), (0,)), ((), ())), preferred_element_type=F32)


def at(start, size):
    return pl.ds(pl.multiple_of(start * size, size), size)


def shape(*dims, dtype=jnp.bfloat16):
    return jax.ShapeDtypeStruct(dims, dtype)


def call(body, name, ins, outs, smem=0, raw=(), hbm=(), views=None, hbm_out=(), scratch=(), parts=(), flops=0, slack=10):
    views = views or {}
    ends = [i for i in hbm_out if i not in parts]
    nbytes = sum(math.prod(a.shape) * a.dtype.itemsize for a in (*ins, *outs))
    vmem, dma = pltpu.VMEM, pltpu.SemaphoreType.DMA

    def kernel(*refs):
        sources, results = refs[: len(ins)], list(refs[len(ins) : len(ins) + len(outs)])
        rest = list(refs[len(ins) + len(outs) :])
        buffers = {i: rest.pop(0) for i in hbm}
        targets = {i: rest.pop(0) for i in hbm_out}
        in_sems, out_sems = rest.pop(0), rest.pop(0)
        loads, stores = {}, {}
        for i in hbm:
            source = views[i][1](sources[i]) if i in views else sources[i]
            loads[i] = pltpu.make_async_copy(source, buffers[i], in_sems.at[i])
            loads[i].start()

        def inn(i):
            if i not in buffers:
                return sources[i]
            if i in loads:
                loads.pop(i).wait()
            return buffers[i]

        def give(i):
            if i in targets:
                stores[i] = pltpu.make_async_copy(targets[i], results[i], out_sems.at[i])
                stores[i].start()

        body(inn, [targets.get(i, ref) for i, ref in enumerate(results)], give, *rest, *[results[i] for i in parts])
        for i in ends:
            if i not in stores:
                give(i)
        for store in stores.values():
            store.wait()

    buffers = [(views[i][0] if i in views else ins[i].shape, ins[i].dtype) for i in hbm]
    buffers += [(outs[i].shape, outs[i].dtype) for i in hbm_out]
    held = buffers + [(s.shape, s.dtype) for s in scratch if s.dtype in (BF16, F32)]
    limit = slack + -(-sum(math.prod(dims) * jnp.dtype(kind).itemsize for dims, kind in held) >> 20)
    spaces = [pltpu.SMEM if i < smem else pltpu.HBM if i in hbm or i in raw else vmem for i in range(len(ins))]
    out_spaces = [pltpu.HBM if i in hbm_out else vmem for i in range(len(outs))]
    results = [space(o.shape, o.dtype) for space, o in zip(out_spaces, outs)]
    out_specs = [pl.BlockSpec(memory_space=space) for space in out_spaces]
    single = len(outs) == 1
    return pl.pallas_call(
        kernel,
        name=name,
        out_shape=results[0] if single else tuple(results),
        in_specs=[pl.BlockSpec(memory_space=space) for space in spaces],
        out_specs=out_specs[0] if single else tuple(out_specs),
        scratch_shapes=[vmem(*b) for b in buffers] + [dma((len(ins),)), dma((len(outs),))] + list(scratch),
        compiler_params=pltpu.CompilerParams(vmem_limit_bytes=limit << 20),
        cost_estimate=pl.CostEstimate(flops=flops, bytes_accessed=nbytes, transcendentals=0),
    )(*ins[:smem], *[pltpu.with_memory_space_constraint(a, s) for a, s in list(zip(ins, spaces))[smem:]])


def unit(value):
    centered = value - jnp.mean(value, axis=-1, keepdims=True)
    spread = jnp.mean(centered * centered, axis=-1, keepdims=True)
    scale = lax.rsqrt(spread + epsilon)
    return centered * scale, scale


def unit_back(grad, normal, scale):
    mean = jnp.mean(grad, axis=-1, keepdims=True)
    along = jnp.mean(grad * normal, axis=-1, keepdims=True)
    return scale * (grad - mean - normal * along)


def column_sum(value):
    return jnp.sum(value, axis=0, keepdims=True)


def prepare(inn, out, give, sems):
    c, w = lax.axis_index("ctx"), lax.axis_index("wt")
    qkv, up, pack = inn(0), inn(1), out[0]
    rows, width = qkv.shape[0], qkv.shape[1] // 3
    span, size = pack.shape[1] // 3, out[1].shape[1]
    copies = []
    for part in range(3):
        source = qkv.at[:, at(part * (width // span) + c, span)]
        copies.append((source, pack.at[pl.ds(0, rows), pl.ds(part * span, span)]))
    copies += [(up.at[:, at(w ^ d, size)], out[d]) for d in (2, 3, 1)]
    copies = [pltpu.make_async_copy(a, b, sems.at[i]) for i, (a, b) in enumerate(copies)]
    for copy in copies:
        copy.start()
    low = pl.ds(rows, SMALL)
    pack[low, :] = jnp.zeros((SMALL, pack.shape[1]), BF16)
    for i in range(3):
        ref = inn(2 + i)
        pack[pl.ds(rows + 4 * i, 4), pl.ds(0, ref.shape[1])] = ref[...]
    for copy in copies:
        copy.wait()


def attend(inn, out, give, xs, norm):
    first, mixed, sent, stats, small = out
    c, w = lax.axis_index("ctx"), lax.axis_index("wt")
    deal = inn(0)
    length, width = xs.shape
    span = sent.shape[2]
    heads = stats.shape[0] // 2
    head = span // heads
    packs = [inn(1 + d) for d in range(WT)]
    for d in range(WT):
        small[:, at(w ^ d, PART)] = floats(packs[d][pl.ds(PART, SMALL), pl.ds(0, PART)])
    for d in range(CTX):
        block = inn(1 + WT + d)
        for t in range(2):
            xs[at(deal[c ^ d, t], PIECE), :] = block[pl.ds(PIECE * t, PIECE), :]
    bias_q = small[pl.ds(8, 1), at(c, span)]
    bias_v = small[pl.ds(9, 1), at(c, span)]

    @pl.loop(0, length // BLK)
    def _(i):
        rows = at(i, BLK)
        normal, _scale = unit(floats(xs[rows, :]))
        first[rows, :] = (normal * small[pl.ds(0, 1), :] + small[pl.ds(4, 1), :]).astype(BF16)
        total = dot(first[rows, at(w, PART)], packs[0][pl.ds(0, PART), :])
        for d in range(1, WT):
            total += dot(first[rows, at(w ^ d, PART)], packs[d][pl.ds(0, PART), :])
        mixed[rows, pl.ds(0, span)] = (total[:, :span] + bias_q).astype(BF16)
        mixed[rows, pl.ds(span, span)] = total[:, span : 2 * span].astype(BF16)
        mixed[rows, pl.ds(2 * span, span)] = (total[:, 2 * span :] + bias_v).astype(BF16)

    give(0)
    give(1)
    give(4)
    lane = lax.broadcasted_iota(jnp.int32, (BLK, span), 1) // head
    factor = 1.0 / math.sqrt(head)
    for b in range(length // BLK):
        rows, seen = pl.ds(b * BLK, BLK), pl.ds(0, (b + 1) * BLK)
        query = mixed[rows, pl.ds(0, span)]
        parts = []
        for h in range(heads):
            masked = jnp.where(lane == h, query, jnp.zeros_like(query))
            raw = dot_t(mixed[seen, pl.ds(span, span)], masked)
            top = jnp.max(raw, axis=0, keepdims=True)
            terms = jnp.exp((raw - top) * factor)
            inverse = 1.0 / jnp.sum(terms, axis=0, keepdims=True)
            stats[pl.ds(2 * h, 1), rows] = top
            stats[pl.ds(2 * h + 1, 1), rows] = inverse
            weights = (terms * inverse).astype(BF16)
            values = mixed[seen, pl.ds(2 * span, span)]
            parts.append(t_dot(values, weights)[h * head : (h + 1) * head, :])
        norm[rows, :] = jnp.concatenate(parts, axis=0).T.astype(BF16)
    for j in range(CTX):
        for t in range(2):
            sent[j, pl.ds(PIECE * t, PIECE), :] = norm[at(deal[j, t], PIECE), :]


def project(inn, out, give):
    branch, resid, second = out
    w = lax.axis_index("wt")
    small, attended, own = inn(0), inn(1), inn(2)
    span = attended.shape[2]
    total = small[pl.ds(10, 1), :]
    for d in range(WT):
        ref = inn(3 + d)
        for j in range(PART // span):
            total = total + dot(attended[(w ^ d) * (PART // span) + j], ref[pl.ds(span * j, span), :])
    branch[...] = total
    give(0)
    normal, _ = unit(total)
    total = floats(own[...]) + (normal * small[pl.ds(1, 1), :] + small[pl.ds(5, 1), :])
    resid[...] = total
    give(1)
    normal, _ = unit(total)
    second[...] = (normal * small[pl.ds(2, 1), :] + small[pl.ds(6, 1), :]).astype(BF16)


def join_slots(inn, start, target):
    for i, d in enumerate((0, 2, 1, 3)):
        ref = inn(start + d)
        rows = ref.shape[0]
        target[pl.ds(rows * i, rows), :] = ref[...]


def feed(inn, out, give):
    all_rows, hidden, slope, near, far = out
    w = lax.axis_index("wt")
    join_slots(inn, 0, all_rows)
    give(0)
    ups, bias = [inn(4 + d) for d in range(WT)], inn(8)
    half_rows = near.shape[0]

    @pl.loop(0, hidden.shape[1] // PART)
    def _(n):
        cols = at(n, PART)
        upper = floats(bias[pl.ds(0, 1), cols])
        for d in range(WT):
            upper = upper + dot(all_rows[:, at(w ^ d, PART)], ups[d][:, cols])
        square = upper * upper
        curve = jnp.tanh(GELU_A * (upper + GELU_B * (square * upper)))
        half = 0.5 * (1.0 + curve)
        hidden[:, cols] = (upper * half).astype(BF16)
        slope[:, cols] = half + (0.5 * GELU_A) * upper * (1.0 - curve * curve) * (
            1.0 + (3.0 * GELU_B) * square
        )

    give(1)
    give(2)
    down = inn(9)

    @pl.loop(0, near.shape[1] // PART)
    def _(n):
        cols = at(n, PART)
        total = dot(hidden[...], down[:, cols])
        near[:, cols] = total[:half_rows]
        far[:, cols] = total[half_rows:].astype(BF16)


def returned(inn, rows):
    own = pl.ds(0, rows)
    return inn(0)[own, :] + floats(inn(1)[own, :]) + floats(inn(2)[...])


def top_norm(inn, out, give):
    result, d_ffn, sums = out
    small, resid, grad = inn(3), inn(4), inn(5)
    normal, scale = unit(returned(inn, resid.shape[0]) + small[pl.ds(11, 1), :])
    gain = small[pl.ds(3, 1), :]
    d_out = floats(grad[...])
    low = unit_back(d_out * gain, normal, scale).astype(BF16)
    d_ffn[...] = low
    give(1)
    result[...] = (resid[...] + (normal * gain + small[pl.ds(7, 1), :])).astype(BF16)
    sums[pl.ds(0, 1), :] = column_sum(d_out * normal)
    sums[pl.ds(1, 1), :] = column_sum(d_out)
    sums[pl.ds(2, 1), :] = column_sum(floats(low))


def feed_back(inn, out, give):
    all_rows, d_upper, near, far, sums = out
    w = lax.axis_index("wt")
    join_slots(inn, 0, all_rows)
    give(0)
    down, slope = inn(4), inn(5)
    half_rows = near.shape[0]

    @pl.loop(0, d_upper.shape[1] // PART)
    def _(n):
        cols = at(n, PART)
        low = (dot_t(all_rows[...], down[cols, :]) * slope[:, cols]).astype(BF16)
        d_upper[:, cols] = low
        sums[pl.ds(0, 1), cols] = column_sum(floats(low))

    give(1)
    for d in range(WT):
        cols = at(w ^ d, PART)
        total = dot_t(d_upper[...], inn(6 + d)[...])
        near[:, cols] = total[:half_rows]
        far[:, cols] = total[half_rows:].astype(BF16)


PLACES = ((0, 0, 0), (0, 1, 4), (1, 0, 2), (1, 1, 6), (2, 0, 1), (2, 1, 5), (3, 0, 3), (3, 1, 7))


def grad_down(inn, out, give):
    c = lax.axis_index("ctx")
    hidden, grads = inn(0), inn(1)
    size = out[0].shape[1]
    for kind in (3, 2, 1, 0):
        for which, i, d in PLACES:
            if which == kind:
                out[kind][i] = t_dot(hidden[:, at(c ^ d, size)], grads[...]).astype(BF16)
        give(kind)


def grad_up(inn, out, give, part):
    c = lax.axis_index("ctx")
    cut = PART // CTX
    outs, rows_in, grads = inn(2), inn(0), inn(1)
    for which, i, d in PLACES:
        out[which][i, pl.ds(WT * cut, cut), :] = outs[at(c ^ d, cut), :]

    @pl.loop(0, WT)
    def _(k):
        part[...] = t_dot(rows_in[:, at(k, PART)], grads[...]).astype(BF16)
        for which, i, d in PLACES:
            out[which][i, at(k, cut), :] = part[at(c ^ d, cut), :]


def middle_norms(inn, out, give):
    sent, d_att, d_resid, sums = out
    w = lax.axis_index("wt")
    small, resid, branch, grad = inn(3), inn(4), inn(5), inn(6)
    rows, span = resid.shape[0], sent.shape[2]
    normal3, scale3 = unit(resid[...])
    normal2, scale2 = unit(branch[...])
    d_second = returned(inn, rows)
    total = floats(grad[...]) + unit_back(d_second * small[pl.ds(2, 1), :], normal3, scale3)
    low = unit_back(total * small[pl.ds(1, 1), :], normal2, scale2).astype(BF16)
    d_att[...] = low
    for d in range(WT):
        part = dot_t(low, inn(7 + d)[...]).astype(BF16)
        for j in range(PART // span):
            sent[(w ^ d) * (PART // span) + j] = part[:, span * j : span * (j + 1)]
    give(0)
    give(1)
    d_resid[...] = total
    sums[pl.ds(0, 1), :] = column_sum(d_second * normal3)
    sums[pl.ds(1, 1), :] = column_sum(d_second)
    sums[pl.ds(2, 1), :] = column_sum(total * normal2)
    sums[pl.ds(3, 1), :] = column_sum(total)
    sums[pl.ds(4, 1), :] = column_sum(floats(low))


def grad_out(inn, out, give):
    w = lax.axis_index("wt")
    attended, grads = inn(0), inn(1)
    span = attended.shape[2]
    for d in (1, 3, 0, 2):
        for j in range(PART // span):
            part = t_dot(attended[(w ^ d) * (PART // span) + j], grads[...])
            out[d % 2][d // 2, pl.ds(span * j, span), :] = part.astype(BF16)
        if d == 3:
            give(1)


def attend_back(inn, out, give, d_out, d_keys, d_values):
    natural, dealt = out
    deal, mixed, stats, got = (inn(i) for i in range(4))
    length, span = d_out.shape
    heads = stats.shape[0] // 2
    head = span // heads
    factor = 1.0 / math.sqrt(head)
    prescale = factor / relax
    for j in range(CTX):
        for t in range(2):
            d_out[at(deal[j, t], PIECE), :] = got[j, pl.ds(PIECE * t, PIECE), :]
    lane = lax.broadcasted_iota(jnp.int32, (BLK, span), 1) // head
    d_keys[...] = jnp.zeros_like(d_keys)
    d_values[...] = jnp.zeros_like(d_values)
    for b in range(length // BLK):
        rows, seen = pl.ds(b * BLK, BLK), pl.ds(0, (b + 1) * BLK)
        query, grads = mixed[rows, pl.ds(0, span)], d_out[rows, :]
        parts = []
        for h in range(heads):
            query_h = jnp.where(lane == h, query, jnp.zeros_like(query))
            grads_h = jnp.where(lane == h, grads, jnp.zeros_like(grads))
            keys = mixed[seen, pl.ds(span, span)]
            raw = dot_t(keys, query_h)
            weights = jnp.exp((raw - stats[pl.ds(2 * h, 1), rows]) * factor) * stats[pl.ds(2 * h + 1, 1), rows]
            d_probs = dot_t(mixed[seen, pl.ds(2 * span, span)], grads_h)
            delta = jnp.sum(weights * d_probs, axis=0, keepdims=True)
            d_scores = (relax * weights * (d_probs - delta)).astype(BF16)
            d_values[seen, :] += dot(weights.astype(BF16), grads_h)
            d_keys[seen, :] += dot(d_scores, query_h)
            parts.append(t_dot(keys, d_scores)[h * head : (h + 1) * head, :])
        natural[rows, pl.ds(0, span)] = (jnp.concatenate(parts, axis=0).T * prescale).astype(BF16)
    natural[:, pl.ds(span, span)] = (d_keys[...] * prescale).astype(BF16)
    natural[:, pl.ds(2 * span, span)] = d_values[...].astype(BF16)
    for j in range(CTX):
        for t in range(2):
            dealt[j, pl.ds(PIECE * t, PIECE), :] = natural[at(deal[j, t], PIECE), :]


def grad_qkv(inn, out, give):
    w = lax.axis_index("wt")
    first, grads = inn(0), inn(1)
    for d in (1, 3, 0, 2):
        out[d % 2][d // 2] = t_dot(first[:, at(w ^ d, PART)], grads[...]).astype(BF16)
        if d == 3:
            give(1)


def bottom_norm(inn, out, give, joined, d_first):
    input_grad, keep, send = out
    w = lax.axis_index("wt")
    got, own, d_resid, small = (inn(i) for i in range(4))
    _, rows, triple = got.shape
    span, width = triple // 3, own.shape[1]
    for j in range(CTX):
        for part in range(3):
            joined[:, pl.ds(part * width + span * j, span)] = got[j, :, pl.ds(span * part, span)]
    for d in range(WT):
        d_first[:, at(w ^ d, PART)] = dot_t(joined[...], inn(4 + d)[...])
    normal, scale = unit(floats(own[...]))
    grads = d_first[...]
    input_grad[...] = d_resid[...] + unit_back(grads * small[pl.ds(0, 1), :], normal, scale)
    give(0)
    middle, top, up = inn(8), inn(9), inn(10)
    lines = {
        0: column_sum(grads * normal),
        4: column_sum(grads),
        8: column_sum(floats(joined[:, pl.ds(0, width)])),
        9: column_sum(floats(joined[:, pl.ds(2 * width, width)])),
    }
    for i, line in enumerate((2, 6, 1, 5, 10)):
        lines[line] = middle[pl.ds(i, 1), :]
    for i, line in enumerate((3, 7, 11)):
        lines[line] = top[pl.ds(i, 1), :]
    for line, value in lines.items():
        d_first[pl.ds(line, 1), :] = value
    for d in range(WT):
        target = send if d % 2 else keep
        target[d // 2, pl.ds(0, 12), :] = d_first[pl.ds(0, 12), at(w ^ d, PART)]
        target[d // 2, pl.ds(12, 4), :] = jnp.zeros((4, PART), F32)
    for i in range(4):
        keep[0, pl.ds(12 + i, 1), :] = up[:, pl.ds(PART * i, PART)]


def spread_qkv(inn, out, give):
    c = lax.axis_index("ctx")
    (full,) = out
    span = full.shape[1] // (3 * CTX)
    for d in range(CTX):
        block = inn(d)
        for part in range(3):
            full[:, at(part * CTX + (c ^ d), span)] = floats(block[:, pl.ds(span * part, span)])


def spread_down(inn, out, give, sems, result):
    c = lax.axis_index("ctx")
    stores = []
    for d in range(CTX):
        block = inn(d)
        rows = at(c ^ d, block.shape[0])
        out[0][rows, :] = floats(block[...])
        stores.append(pltpu.make_async_copy(out[0].at[rows, :], result.at[rows, :], sems.at[d]))
        stores[-1].start()
    for store in stores:
        store.wait()


def spread_rest(inn, out, give, total):
    up, proj, gain, shift, bias, up_bias = out
    c, w = lax.axis_index("ctx"), lax.axis_index("wt")
    cut = PART // CTX
    width = proj.shape[1]
    total[...] = jnp.zeros_like(total)
    for d in range(CTX):
        block = inn(d)
        for k in range(WT):
            up[at(c ^ d, cut), at(w ^ k, width)] = floats(block[pl.ds(cut * k, cut), :])
        proj[at(c ^ d, cut), :] = floats(block[pl.ds(cut * WT, cut), :])
        total[...] += floats(block[pl.ds(cut * (WT + 1), SMALL), pl.ds(0, PART)])
    for i, ref in enumerate((gain, shift, bias, up_bias)):
        ref[...] = total[pl.ds(4 * i, 4), :]


def split_device(
    layer_input,
    out_grad,
    deal,
    w_qkv,
    w_out,
    w_up,
    w_down,
    norm_gain,
    norm_shift,
    bias_width,
    up_bias,
):
    _, rows, width = layer_input.shape
    w = lax.axis_index("wt")
    per = HEADS // CTX
    span = per * (width // HEADS)
    length = rows * CTX
    hidden_width = w_down.shape[0]
    everyone = WT * rows
    own, grad = layer_input[0], out_grad[0]
    vmem, dma = pltpu.VMEM, pltpu.SemaphoreType.DMA

    sequence = gather_ctx(own)
    begin = lax.optimization_barrier((w_qkv, w_up, norm_gain, norm_shift, bias_width, *sequence[1:3]))[:5]
    pack, *ups = call(
        prepare,
        "prepare",
        begin,
        [shape(PART + SMALL, 3 * span)] + [shape(PART, hidden_width)] * 3,
        raw=(0, 1),
        scratch=[dma((6,))],
    )
    packs = gather_wt(pack)
    ups = [w_up] + [swap(value, "wt", d) for d, value in zip((1, 2, 3), ups)]
    outs = gather_wt(w_out)

    packs = lax.optimization_barrier((*packs, *outs, *ups[1:]))
    packs, outs, ups = packs[:WT], packs[WT : 2 * WT], [w_up, *packs[2 * WT :]]
    first, mixed, sent, stats, small = call(
        attend,
        "attend",
        (deal, *packs, *sequence),
        [
            shape(length, width),
            shape(length, 3 * span),
            shape(CTX, rows, span),
            shape(2 * per, length, dtype=F32),
            shape(SMALL, width, dtype=F32),
        ],
        smem=1,
        hbm=range(1, 1 + WT + CTX),
        hbm_out=(0, 1),
        scratch=[vmem((length, width), BF16), vmem((length, span), BF16)],
        flops=2 * length * width * 3 * span + 4 * length * length * span,
    )
    attended = lax.all_to_all(sent, "ctx", 0, 0, tiled=True)

    branch, resid, second = call(
        project,
        "project",
        (small, attended, own, *outs),
        [shape(rows, width, dtype=F32), shape(rows, width, dtype=F32), shape(rows, width)],
        hbm=(2, 3),
        flops=2 * rows * width * width,
    )

    own_columns = ((PART, hidden_width), lambda ref: ref.at[:, at(lax.axis_index("wt"), hidden_width)])
    halves = [shape(2 * rows, width, dtype=F32), shape(2 * rows, width)]
    seconds, hidden, slope, near, far = call(
        feed,
        "feed",
        (*gather_wt(second), *ups, up_bias.reshape(1, hidden_width), w_down),
        [shape(everyone, width), shape(everyone, hidden_width), shape(everyone, hidden_width, dtype=F32)]
        + halves,
        hbm=(4, 8, 9),
        hbm_out=(0,),
        views={4: own_columns},
        flops=4 * everyone * width * hidden_width,
    )

    def return_rows(near, far, *others):
        got = swap(far, "wt", 1)
        back = (near[rows:] + floats(got[rows:])).astype(BF16)
        return near, got, after(swap(back, "wt", 2), *others)

    result, d_ffn, sums3 = call(
        top_norm,
        "top_norm",
        (*return_rows(near, far), small, resid, grad),
        [shape(rows, width), shape(rows, width), shape(3, width, dtype=F32)],
        hbm=(5,),
        hbm_out=(0,),
    )
    d_ffns, d_upper, near, far, up_sum = call(
        feed_back,
        "feed_back",
        (*gather_wt(d_ffn), w_down, slope, *ups),
        [shape(everyone, width), shape(everyone, hidden_width)] + halves + [shape(1, hidden_width, dtype=F32)],
        hbm=(4, 6),
        hbm_out=(1,),
        views={6: own_columns},
        flops=4 * everyone * width * hidden_width,
    )
    down_terms = call(
        grad_down,
        "grad_down",
        (hidden, d_ffns),
        [shape(2, hidden_width // CTX, width)] * 4,
        hbm_out=range(4),
        flops=2 * everyone * width * hidden_width,
    )
    near, got, far = return_rows(near, far, down_terms[0])
    sent, d_att, d_resid, sums21 = call(
        middle_norms,
        "middle_norms",
        (near, got, far, small, resid, branch, grad, *outs),
        [
            shape(CTX, rows, span),
            shape(rows, width),
            shape(rows, width, dtype=F32),
            shape(5, width, dtype=F32),
        ],
        hbm=(6, 7),
        hbm_out=(2,),
        flops=2 * rows * width * width,
    )
    got = lax.all_to_all(sent, "ctx", 0, 0, tiled=True)
    late_qkv = gather_wt(after(w_qkv, far))
    pieces = [shape(2, PART, width)] * 2
    out_terms = call(grad_out, "grad_out", (attended, d_att), pieces, hbm_out=(0, 1), flops=2 * rows * width * width)
    out_rows = scatter_wt(*out_terms)

    got = after(got, out_terms[0])
    natural, dealt = call(
        attend_back,
        "attend_back",
        (deal, mixed, stats, got),
        [shape(length, 3 * span), shape(CTX, rows, 3 * span)],
        smem=1,
        hbm=(1,),
        scratch=[vmem((length, span), BF16), vmem((length, span), F32), vmem((length, span), F32)],
        flops=10 * length * length * span,
    )
    got_rows = lax.all_to_all(dealt, "ctx", 0, 0, tiled=True)
    pieces = [shape(2, PART, 3 * span)] * 2
    qkv_terms = call(grad_qkv, "grad_qkv", (first, natural), pieces, hbm=(0,), hbm_out=(0, 1), flops=2 * length * width * 3 * span)
    cut = PART // CTX
    up_terms = call(
        grad_up,
        "grad_up",
        (seconds, d_upper, after(out_rows, qkv_terms[0])),
        [shape(2, (WT + 1) * cut, width)] * 4,
        hbm=(0, 1),
        hbm_out=range(4),
        scratch=[vmem((PART, hidden_width), BF16)],
        flops=2 * everyone * width * hidden_width,
    )
    input_grad, keep, send = call(
        bottom_norm,
        "bottom_norm",
        (after(got_rows, up_terms[0]), own, d_resid, small, *late_qkv, sums21, sums3, up_sum),
        [shape(rows, width, dtype=F32)] + [shape(2, SMALL, PART, dtype=F32)] * 2,
        hbm=(1, 2),
        hbm_out=(0,),
        scratch=[vmem((rows, 3 * width), BF16), vmem((rows, width), F32)],
        flops=6 * rows * width * width,
    )

    down_part = scatter_ctx(*down_terms, (got,), (natural,), (natural,))
    rest_part = scatter_ctx(*up_terms, (), (), ())
    qkv_slots = gather_ctx(scatter_wt(*qkv_terms), (1, 4, 2))
    down_slots = gather_ctx(down_part)
    sums = scatter_wt(keep, send, F32).astype(BF16)
    up_part = [lax.dynamic_slice_in_dim(rest_part, (w ^ d) * cut, cut, 0) for d in range(WT)]
    up_part = [up_part[0]] + [swap(up_part[d], "wt", d) for d in range(1, WT)]
    sums = jnp.pad(sums, ((0, 0), (0, width - PART)))
    rest_slots = gather_ctx(jnp.concatenate([*up_part, rest_part[WT * cut :], sums], axis=0))
    full_qkv = call(spread_qkv, "spread_qkv", qkv_slots, [shape(PART, 3 * width, dtype=F32)], hbm_out=(0,))
    full_down = call(
        spread_down,
        "spread_down",
        down_slots,
        [shape(hidden_width, width, dtype=F32)],
        hbm_out=(0,),
        scratch=[dma((CTX,))],
        parts=(0,),
    )
    four = [shape(4, PART, dtype=F32)] * 4
    full_up, full_out, gain, shift, bias, up_total = call(
        spread_rest,
        "spread_rest",
        rest_slots,
        [shape(PART, WT * hidden_width, dtype=F32), shape(PART, width, dtype=F32)] + four,
        hbm_out=range(6),
        scratch=[vmem((SMALL, PART), F32)],
    )
    return (
        result[None],
        input_grad[None],
        full_qkv,
        full_out,
        full_up,
        full_down,
        gain,
        shift,
        bias,
        up_total.reshape(hidden_width),
    )


def solution(mesh):
    small = mesh.shape["ctx"] == CTX and mesh.shape["wt"] == WT
    per_device = split_device if small else general_device
    in_specs = (
        P("wt", "ctx", None),
        P("wt", "ctx", None),
        P(),
        P("wt", None),
        P("wt", None),
        P("wt", None),
        P("wt", None),
        P(None, "wt"),
        P(None, "wt"),
        P(None, "wt"),
        P("wt"),
    )
    out_specs = (
        P("wt", "ctx", None),
        P("wt", "ctx", None),
        P("wt", None),
        P("wt", None),
        P("wt", None),
        P("wt", None),
        P(None, "wt"),
        P(None, "wt"),
        P(None, "wt"),
        P("wt"),
    )
    return jax.shard_map(
        per_device, mesh=mesh, in_specs=in_specs, out_specs=out_specs, check_vma=False
    )
```

```python
import functools
import math

import jax
import jax.numpy as jnp
from jax import lax
from jax.experimental import pallas as pl
from jax.experimental.pallas import tpu as pltpu
from jax.sharding import PartitionSpec as P

HEADS = 16
BLK = 256
PIECE = 64


epsilon = 1e-05
relax = 32.0


def layer_norm(value, gain, shift):
    mean = jnp.mean(value, axis=-1, keepdims=True)
    centered = value - mean
    spread = jnp.mean(centered * centered, axis=-1, keepdims=True)
    return centered * lax.rsqrt(spread + epsilon) * gain + shift


def gelu_tanh(value):
    return jax.nn.gelu(value, approximate=True)


def rows_dot(left, weight):
    return jnp.einsum("std,de->ste", left, weight, preferred_element_type=jnp.float32)


def weight_grad(left, right):
    return jnp.einsum("std,ste->de", left, right, preferred_element_type=jnp.float32)


def back_dot(grad, weight):
    return jnp.einsum("ste,de->std", grad, weight, preferred_element_type=jnp.float32)


def row_total(value):
    return jnp.sum(value.astype(jnp.float32), axis=(0, 1))


def general_device(
    layer_input,
    out_grad,
    deal,
    w_qkv,
    w_out,
    w_up,
    w_down,
    norm_gain,
    norm_shift,
    bias_width,
    up_bias,
):
    seqs, rows, width = layer_input.shape
    heads = HEADS
    head = width // heads
    prescale = 1.0 / (relax * math.sqrt(head))
    ranks = lax.axis_size("ctx")
    length = rows * ranks
    per_block = BLK // PIECE
    rank = lax.axis_index("ctx")
    chosen = jnp.arange(ranks, dtype=jnp.int32) == rank
    mine = jnp.sum(jnp.where(chosen[:, None], deal, 0), axis=0)
    query_blocks = jnp.repeat(mine, rows // 2) // per_block
    key_blocks = jnp.repeat(deal.reshape(-1), rows // 2) // per_block
    full_qkv, full_out, full_up, full_down, gains, shifts, biases, up_shift = (
        lax.all_gather(w_qkv, "wt", axis=0, tiled=True),
        lax.all_gather(w_out, "wt", axis=0, tiled=True),
        lax.all_gather(w_up, "wt", axis=0, tiled=True),
        lax.all_gather(w_down, "wt", axis=0, tiled=True),
        lax.all_gather(norm_gain, "wt", axis=1, tiled=True),
        lax.all_gather(norm_shift, "wt", axis=1, tiled=True),
        lax.all_gather(bias_width, "wt", axis=1, tiled=True),
        lax.all_gather(up_bias, "wt", axis=0, tiled=True),
    )
    gains = gains.astype(jnp.float32)
    shifts = shifts.astype(jnp.float32)
    biases = biases.astype(jnp.float32)
    up_shift = up_shift.astype(jnp.float32)
    input_float = layer_input.astype(jnp.float32)
    first = layer_norm(input_float, gains[0], shifts[0]).astype(jnp.bfloat16)
    mixed = rows_dot(first, full_qkv)
    query = (mixed[..., :width] + biases[0]).astype(jnp.bfloat16)
    kv_local = jnp.concatenate(
        [mixed[..., width : 2 * width], mixed[..., 2 * width :] + biases[1]], axis=-1
    ).astype(jnp.bfloat16)
    kv_all = lax.all_gather(kv_local, "ctx", axis=1, tiled=True)
    step = math.gcd(length, 1024)
    count = length // step
    query4 = query.reshape(seqs, rows, heads, head)

    def score_block(left, right):
        return (
            jnp.einsum("sqhd,skhd->shqk", left, right, preferred_element_type=jnp.float32)
            * prescale
        )

    def key_block(index):
        start = index * step
        piece = lax.dynamic_slice_in_dim(kv_all, start, step, 1)
        keys4 = piece[..., :width].reshape(seqs, step, heads, head)
        values4 = piece[..., width:].reshape(seqs, step, heads, head)
        visible = (
            query_blocks[:, None] >= lax.dynamic_slice_in_dim(key_blocks, start, step, 0)[None, :]
        )
        return (keys4, values4, visible)

    def probs(raw, visible, totals):
        return jnp.where(visible, jnp.exp(raw * relax - totals[..., None]), 0.0)

    def online(index, carry):
        top, total, acc = carry
        keys4, values4, visible = key_block(index)
        raw = jnp.where(visible, score_block(query4, keys4), -1e30)
        new_top = jnp.maximum(top, jnp.max(raw, axis=-1))
        terms = jnp.where(visible, jnp.exp((raw - new_top[..., None]) * relax), 0.0)
        factor = jnp.exp((top - new_top) * relax)
        total = total * factor + jnp.sum(terms, axis=-1)
        acc = acc * jnp.transpose(factor, (0, 2, 1))[..., None]
        acc = acc + jnp.einsum(
            "shqk,skhd->sqhd",
            terms.astype(jnp.bfloat16),
            values4,
            preferred_element_type=jnp.float32,
        )
        return (new_top, total, acc)

    start_top = jnp.full((seqs, heads, rows), -1e30, jnp.float32)
    start_total = jnp.zeros((seqs, heads, rows), jnp.float32)
    start_acc = jnp.zeros((seqs, rows, heads, head), jnp.float32)
    top, total, acc = lax.fori_loop(0, count, online, (start_top, start_total, start_acc))
    log_total = top * relax + jnp.log(total)
    attended_float = acc / jnp.transpose(total, (0, 2, 1))[..., None]
    attended = attended_float.reshape(seqs, rows, width).astype(jnp.bfloat16)
    branch = rows_dot(attended, full_out) + biases[2]
    resid = input_float + layer_norm(branch, gains[1], shifts[1])
    second = layer_norm(resid, gains[2], shifts[2]).astype(jnp.bfloat16)
    upper = rows_dot(second, full_up) + up_shift
    hidden = gelu_tanh(upper).astype(jnp.bfloat16)
    ffn = rows_dot(hidden, full_down) + biases[3]
    top_norm, pull_four = jax.vjp(layer_norm, ffn, gains[3], shifts[3])
    result = resid + top_norm
    d_out = out_grad.astype(jnp.float32)
    d_ffn, d_gain3, d_shift3 = pull_four(d_out)
    d_ffn = d_ffn.astype(jnp.bfloat16)
    d_bias3 = row_total(d_ffn)
    g_down = weight_grad(hidden, d_ffn)
    d_hidden = back_dot(d_ffn, full_down)
    _, pull_gelu = jax.vjp(gelu_tanh, upper)
    d_upper = pull_gelu(d_hidden)[0].astype(jnp.bfloat16)
    d_up_shift = row_total(d_upper)
    g_up = weight_grad(second, d_upper)
    d_second = back_dot(d_upper, full_up)
    _, pull_three = jax.vjp(layer_norm, resid, gains[2], shifts[2])
    d_resid_part, d_gain2, d_shift2 = pull_three(d_second)
    d_resid = d_out + d_resid_part
    _, pull_two = jax.vjp(layer_norm, branch, gains[1], shifts[1])
    d_branch, d_gain1, d_shift1 = pull_two(d_resid)
    d_branch = d_branch.astype(jnp.bfloat16)
    d_bias2 = row_total(d_branch)
    g_out = weight_grad(attended, d_branch)
    d_attended = back_dot(d_branch, full_out).astype(jnp.bfloat16)
    d_out4 = d_attended.reshape(seqs, rows, heads, head)
    delta = jnp.einsum("sqhd,sqhd->shq", d_out4.astype(jnp.float32), attended_float)

    def score_grads(q_rows, do_rows, k_rows, v_rows, visible, lse_rows, delta_rows):
        weights = probs(score_block(q_rows, k_rows), visible, lse_rows)
        d_probs = jnp.einsum("sqhd,skhd->shqk", do_rows, v_rows, preferred_element_type=jnp.float32)
        d_scores = (relax * weights * (d_probs - delta_rows[..., None])).astype(jnp.bfloat16)
        return (d_scores, weights.astype(jnp.bfloat16))

    zero_query = jnp.zeros((seqs, rows, heads, head), jnp.float32)

    def local_grads(d_query, index):
        keys4, values4, visible = key_block(index)
        d_scores, weights = score_grads(query4, d_out4, keys4, values4, visible, log_total, delta)
        d_query = (
            d_query
            + jnp.einsum("shqk,skhd->sqhd", d_scores, keys4, preferred_element_type=jnp.float32)
            * prescale
        )
        d_keys = (
            jnp.einsum("shqk,sqhd->kshd", d_scores, query4, preferred_element_type=jnp.float32)
            * prescale
        )
        d_values = jnp.einsum(
            "shqk,sqhd->kshd", weights, d_out4, preferred_element_type=jnp.float32
        )
        joined = jnp.concatenate(
            [d_keys.reshape(step, seqs, width), d_values.reshape(step, seqs, width)], axis=-1
        )
        return (d_query, joined)

    d_query, pieces = lax.scan(local_grads, zero_query, jnp.arange(count, dtype=jnp.int32))
    terms = pieces.reshape(length, seqs, 2 * width)
    d_kv = jnp.transpose(lax.psum_scatter(terms, "ctx", scatter_dimension=0, tiled=True), (1, 0, 2))
    d_query = d_query.reshape(seqs, rows, width).astype(jnp.bfloat16)
    d_kv = d_kv.astype(jnp.bfloat16)
    d_bias0 = row_total(d_query)
    d_bias1 = row_total(d_kv[..., width:])
    d_mixed = jnp.concatenate([d_query, d_kv], axis=-1)
    g_qkv = weight_grad(first, d_mixed)
    d_first = back_dot(d_mixed, full_qkv)
    _, pull_one = jax.vjp(layer_norm, input_float, gains[0], shifts[0])
    d_input_part, d_gain0, d_shift0 = pull_one(d_first)
    input_grad = d_resid + d_input_part
    grad_gain = jnp.stack([d_gain0, d_gain1, d_gain2, d_gain3])
    grad_shift = jnp.stack([d_shift0, d_shift1, d_shift2, d_shift3])
    grad_bias = jnp.stack([d_bias0, d_bias1, d_bias2, d_bias3])
    owned = (
        lax.psum_scatter(g_qkv.astype(jnp.bfloat16), "wt", scatter_dimension=0, tiled=True).astype(
            jnp.float32
        ),
        lax.psum_scatter(g_out.astype(jnp.bfloat16), "wt", scatter_dimension=0, tiled=True).astype(
            jnp.float32
        ),
        lax.psum_scatter(g_up.astype(jnp.bfloat16), "wt", scatter_dimension=0, tiled=True).astype(
            jnp.float32
        ),
        lax.psum_scatter(g_down.astype(jnp.bfloat16), "wt", scatter_dimension=0, tiled=True).astype(
            jnp.float32
        ),
        lax.psum_scatter(
            grad_gain.astype(jnp.bfloat16), "wt", scatter_dimension=1, tiled=True
        ).astype(jnp.float32),
        lax.psum_scatter(
            grad_shift.astype(jnp.bfloat16), "wt", scatter_dimension=1, tiled=True
        ).astype(jnp.float32),
        lax.psum_scatter(
            grad_bias.astype(jnp.bfloat16), "wt", scatter_dimension=1, tiled=True
        ).astype(jnp.float32),
        lax.psum_scatter(
            d_up_shift.astype(jnp.bfloat16), "wt", scatter_dimension=0, tiled=True
        ).astype(jnp.float32),
    )
    summed = lax.psum(
        (owned[0], owned[1], owned[2], owned[3], owned[4], owned[5], owned[6], owned[7]), "ctx"
    )
    return (
        result.astype(jnp.bfloat16),
        input_grad,
        summed[0],
        summed[1],
        summed[2],
        summed[3],
        summed[4],
        summed[5],
        summed[6],
        summed[7],
    )


F32 = jnp.float32
BF16 = jnp.bfloat16
WT = 4
CTX = 8
PART = 256
SMALL = 16
GELU_A = math.sqrt(2.0 / math.pi)
GELU_B = 0.044715


def swap(value, axis, bit):
    size = lax.axis_size(axis)
    return lax.ppermute(value, axis, [(i, i ^ bit) for i in range(size)])


def gather_wt(block):
    far = swap(block, "wt", 2)
    return block, swap(block, "wt", 1), far, swap(far, "wt", 1)


def gather_ctx(block):
    far, near, side = (swap(block, "ctx", bit) for bit in (4, 2, 1))
    near = after(near, side)
    near_side = swap(near, "ctx", 1)
    far = after(far, near_side)
    corner = swap(far, "ctx", 2)
    far_side = swap(far, "ctx", 1)
    return [block, side, near, near_side, far, far_side, corner, swap(after(corner, far_side), "ctx", 1)]


def gather_ctx_z(block):
    blocks = {0: block}
    for bit in (1, 4, 2):
        blocks.update({d ^ bit: swap(value, "ctx", bit) for d, value in blocks.items()})
    return [blocks[d] for d in range(CTX)]


def after(value, *others):
    return lax.optimization_barrier((value, *others))[0]


def floats(value):
    return value.astype(F32)


def dot(left, right):
    return jnp.dot(left, right, preferred_element_type=F32)


def dot_t(left, right):
    return lax.dot_general(left, right, (((1,), (1,)), ((), ())), preferred_element_type=F32)


def t_dot(left, right):
    return lax.dot_general(left, right, (((0,), (0,)), ((), ())), preferred_element_type=F32)


def at(start, size):
    return pl.ds(pl.multiple_of(start * size, size), size)


def shape(*dims, dtype=jnp.bfloat16):
    return jax.ShapeDtypeStruct(dims, dtype)


def call(body, name, ins, outs, smem=0, raw=(), hbm=(), views=None, hbm_out=(), scratch=(), parts=(), slack=10):
    views = views or {}
    ends = [i for i in hbm_out if i not in parts]
    vmem, dma = pltpu.VMEM, pltpu.SemaphoreType.DMA

    def kernel(*refs):
        sources, results = refs[: len(ins)], list(refs[len(ins) : len(ins) + len(outs)])
        rest = list(refs[len(ins) + len(outs) :])
        buffers = {i: rest.pop(0) for i in hbm}
        targets = {i: rest.pop(0) for i in hbm_out}
        in_sems, out_sems = rest.pop(0), rest.pop(0)
        loads, stores = {}, {}
        for i in hbm:
            source = views[i][1](sources[i]) if i in views else sources[i]
            loads[i] = pltpu.make_async_copy(source, buffers[i], in_sems.at[i])
            loads[i].start()

        def inn(i):
            if i not in buffers:
                return sources[i]
            if i in loads:
                loads.pop(i).wait()
            return buffers[i]

        def give(i):
            if i in targets:
                stores[i] = pltpu.make_async_copy(targets[i], results[i], out_sems.at[i])
                stores[i].start()

        body(inn, [targets.get(i, ref) for i, ref in enumerate(results)], give, *rest, *[results[i] for i in parts])
        for i in ends:
            if i not in stores:
                give(i)
        for store in stores.values():
            store.wait()

    buffers = [(views[i][0] if i in views else ins[i].shape, ins[i].dtype) for i in hbm]
    buffers += [(outs[i].shape, outs[i].dtype) for i in hbm_out]
    held = buffers + [(s.shape, s.dtype) for s in scratch if s.dtype in (BF16, F32)]
    limit = slack + -(-sum(math.prod(dims) * jnp.dtype(kind).itemsize for dims, kind in held) >> 20)
    spaces = [pltpu.SMEM if i < smem else pltpu.HBM if i in hbm or i in raw else vmem for i in range(len(ins))]
    out_spaces = [pltpu.HBM if i in hbm_out else vmem for i in range(len(outs))]
    results = [space(o.shape, o.dtype) for space, o in zip(out_spaces, outs)]
    out_specs = [pl.BlockSpec(memory_space=space) for space in out_spaces]
    single = len(outs) == 1
    return pl.pallas_call(
        kernel,
        name=name,
        out_shape=results[0] if single else tuple(results),
        in_specs=[pl.BlockSpec(memory_space=space) for space in spaces],
        out_specs=out_specs[0] if single else tuple(out_specs),
        scratch_shapes=[vmem(*b) for b in buffers] + [dma((len(ins),)), dma((len(outs),))] + list(scratch),
        compiler_params=pltpu.CompilerParams(vmem_limit_bytes=limit << 20),
        cost_estimate=pl.CostEstimate(flops=0, bytes_accessed=1024, transcendentals=0),
    )(*ins[:smem], *[pltpu.with_memory_space_constraint(a, s) for a, s in list(zip(ins, spaces))[smem:]])


def unit(value):
    centered = value - jnp.mean(value, axis=-1, keepdims=True)
    spread = jnp.mean(centered * centered, axis=-1, keepdims=True)
    scale = lax.rsqrt(spread + epsilon)
    return centered * scale, scale


def unit_back(grad, normal, scale):
    mean = jnp.mean(grad, axis=-1, keepdims=True)
    along = jnp.mean(grad * normal, axis=-1, keepdims=True)
    return scale * (grad - mean - normal * along)


def column_sum(value):
    return jnp.sum(value, axis=0, keepdims=True)


def prepare(inn, out, give, sems):
    c, w = lax.axis_index("ctx"), lax.axis_index("wt")
    qkv, up, pack = inn(0), inn(1), out[0]
    rows, width = qkv.shape[0], qkv.shape[1] // 3
    span, size = pack.shape[1] // 3, out[1].shape[1]
    copies = []
    for part in range(3):
        source = qkv.at[:, at(part * (width // span) + c, span)]
        copies.append((source, pack.at[pl.ds(0, rows), pl.ds(part * span, span)]))
    copies += [(up.at[:, at(w ^ d, size)], out[d]) for d in (2, 3, 1)]
    copies = [pltpu.make_async_copy(a, b, sems.at[i]) for i, (a, b) in enumerate(copies)]
    for copy in copies:
        copy.start()
    low = pl.ds(rows, SMALL)
    pack[low, :] = jnp.zeros((SMALL, pack.shape[1]), BF16)
    for i in range(3):
        ref = inn(2 + i)
        pack[pl.ds(rows + 4 * i, 4), pl.ds(0, ref.shape[1])] = ref[...]
    for copy in copies:
        copy.wait()


def attend(inn, out, give, xs, norm):
    first, mixed, sent, stats, small = out
    c, w = lax.axis_index("ctx"), lax.axis_index("wt")
    deal = inn(0)
    length, width = xs.shape
    span = sent.shape[2]
    heads = stats.shape[0] // 2
    head = span // heads
    packs = [inn(1 + d) for d in range(WT)]
    for d in range(WT):
        small[:, at(w ^ d, PART)] = floats(packs[d][pl.ds(PART, SMALL), pl.ds(0, PART)])
    for d in range(CTX):
        block = inn(1 + WT + d)
        for t in range(2):
            xs[at(deal[c ^ d, t], PIECE), :] = block[pl.ds(PIECE * t, PIECE), :]
    bias_q = small[pl.ds(8, 1), at(c, span)]
    bias_v = small[pl.ds(9, 1), at(c, span)]

    @pl.loop(0, length // BLK)
    def _(i):
        rows = at(i, BLK)
        normal, _scale = unit(floats(xs[rows, :]))
        first[rows, :] = (normal * small[pl.ds(0, 1), :] + small[pl.ds(4, 1), :]).astype(BF16)
        total = dot(first[rows, at(w, PART)], packs[0][pl.ds(0, PART), :])
        for d in range(1, WT):
            total += dot(first[rows, at(w ^ d, PART)], packs[d][pl.ds(0, PART), :])
        mixed[rows, pl.ds(0, span)] = (total[:, :span] + bias_q).astype(BF16)
        mixed[rows, pl.ds(span, span)] = total[:, span : 2 * span].astype(BF16)
        mixed[rows, pl.ds(2 * span, span)] = (total[:, 2 * span :] + bias_v).astype(BF16)

    give(0)
    give(1)
    give(4)
    lane = lax.broadcasted_iota(jnp.int32, (BLK, span), 1) // head
    factor = 1.0 / math.sqrt(head)
    for b in range(length // BLK):
        rows, seen = pl.ds(b * BLK, BLK), pl.ds(0, (b + 1) * BLK)
        query = mixed[rows, pl.ds(0, span)]
        parts = []
        for h in range(heads):
            masked = jnp.where(lane == h, query, jnp.zeros_like(query))
            raw = dot_t(mixed[seen, pl.ds(span, span)], masked)
            top = jnp.max(raw, axis=0, keepdims=True)
            terms = jnp.exp((raw - top) * factor)
            inverse = 1.0 / jnp.sum(terms, axis=0, keepdims=True)
            stats[pl.ds(2 * h, 1), rows] = top
            stats[pl.ds(2 * h + 1, 1), rows] = inverse
            weights = (terms * inverse).astype(BF16)
            values = mixed[seen, pl.ds(2 * span, span)]
            parts.append(t_dot(values, weights)[h * head : (h + 1) * head, :])
        norm[rows, :] = jnp.concatenate(parts, axis=0).T.astype(BF16)
    for j in range(CTX):
        for t in range(2):
            sent[j, pl.ds(PIECE * t, PIECE), :] = norm[at(deal[j, t], PIECE), :]


def project(inn, out, give):
    branch, resid, second = out
    w = lax.axis_index("wt")
    small, attended, own = inn(0), inn(1), inn(2)
    span = attended.shape[2]
    total = small[pl.ds(10, 1), :]
    for d in range(WT):
        ref = inn(3 + d)
        for j in range(PART // span):
            total = total + dot(attended[(w ^ d) * (PART // span) + j], ref[pl.ds(span * j, span), :])
    branch[...] = total
    give(0)
    normal, _ = unit(total)
    total = floats(own[...]) + (normal * small[pl.ds(1, 1), :] + small[pl.ds(5, 1), :])
    resid[...] = total
    give(1)
    normal, _ = unit(total)
    second[...] = (normal * small[pl.ds(2, 1), :] + small[pl.ds(6, 1), :]).astype(BF16)


def join_slots(inn, start, target):
    for i, d in enumerate((0, 2, 1, 3)):
        ref = inn(start + d)
        rows = ref.shape[0]
        target[pl.ds(rows * i, rows), :] = ref[...]


def feed(inn, out, give):
    all_rows, hidden, slope, near, far = out
    w = lax.axis_index("wt")
    join_slots(inn, 0, all_rows)
    give(0)
    ups, bias = [inn(4 + d) for d in range(WT)], inn(8)
    half_rows = near.shape[0]

    @pl.loop(0, hidden.shape[1] // PART)
    def _(n):
        cols = at(n, PART)
        upper = floats(bias[pl.ds(0, 1), cols])
        for d in range(WT):
            upper = upper + dot(all_rows[:, at(w ^ d, PART)], ups[d][:, cols])
        square = upper * upper
        curve = jnp.tanh(GELU_A * (upper + GELU_B * (square * upper)))
        half = 0.5 * (1.0 + curve)
        hidden[:, cols] = (upper * half).astype(BF16)
        slope[:, cols] = half + (0.5 * GELU_A) * upper * (1.0 - curve * curve) * (
            1.0 + (3.0 * GELU_B) * square
        )

    give(1)
    give(2)
    down = inn(9)

    @pl.loop(0, near.shape[1] // PART)
    def _(n):
        cols = at(n, PART)
        total = dot(hidden[...], down[:, cols])
        near[:, cols] = total[:half_rows]
        far[:, cols] = total[half_rows:].astype(BF16)


def returned(inn, rows):
    own = pl.ds(0, rows)
    return inn(0)[own, :] + floats(inn(1)[own, :]) + floats(inn(2)[...])


def top_norm(inn, out, give):
    result, d_ffn, sums = out
    small, resid, grad = inn(3), inn(4), inn(5)
    normal, scale = unit(returned(inn, resid.shape[0]) + small[pl.ds(11, 1), :])
    gain = small[pl.ds(3, 1), :]
    d_out = floats(grad[...])
    low = unit_back(d_out * gain, normal, scale).astype(BF16)
    d_ffn[...] = low
    give(1)
    result[...] = (resid[...] + (normal * gain + small[pl.ds(7, 1), :])).astype(BF16)
    sums[pl.ds(0, 1), :] = column_sum(d_out * normal)
    sums[pl.ds(1, 1), :] = column_sum(d_out)
    sums[pl.ds(2, 1), :] = column_sum(floats(low))


def feed_back(inn, out, give):
    all_rows, d_upper, near, far, sums = out
    w = lax.axis_index("wt")
    join_slots(inn, 0, all_rows)
    give(0)
    down, slope = inn(4), inn(5)
    half_rows = near.shape[0]

    @pl.loop(0, d_upper.shape[1] // PART)
    def _(n):
        cols = at(n, PART)
        low = (dot_t(all_rows[...], down[cols, :]) * slope[:, cols]).astype(BF16)
        d_upper[:, cols] = low
        sums[pl.ds(0, 1), cols] = column_sum(floats(low))

    give(1)
    for d in range(WT):
        cols = at(w ^ d, PART)
        total = dot_t(d_upper[...], inn(6 + d)[...])
        near[:, cols] = total[:half_rows]
        far[:, cols] = total[half_rows:].astype(BF16)


PLACES = ((0, 0, 0), (0, 1, 4), (1, 0, 2), (1, 1, 6), (2, 0, 1), (2, 1, 5), (3, 0, 3), (3, 1, 7))


def grad_down(inn, out, give):
    c = lax.axis_index("ctx")
    hidden, grads = inn(0), inn(1)
    size = out[0].shape[1]
    for target, i, d in ((2, 0, 3), (2, 1, 7), (2, 2, 1), (2, 3, 5), (1, 0, 2), (1, 1, 6), (0, 0, 0), (0, 1, 4)):
        out[target][i] = t_dot(hidden[:, at(c ^ d, size)], grads[...]).astype(BF16)
        if d == 5:
            give(2)


def grad_up(inn, out, give, part):
    c = lax.axis_index("ctx")
    cut = PART // CTX
    rows_in, grads = inn(0), inn(1)

    @pl.loop(0, WT)
    def _(k):
        part[...] = t_dot(rows_in[:, at(k, PART)], grads[...]).astype(BF16)
        for which, i, d in PLACES:
            out[which][i, at(k, cut), :] = part[at(c ^ d, cut), :]


def middle_norms(inn, out, give):
    sent, d_att, d_resid, sums = out
    w = lax.axis_index("wt")
    small, resid, branch, grad = inn(3), inn(4), inn(5), inn(6)
    rows, span = resid.shape[0], sent.shape[2]
    normal3, scale3 = unit(resid[...])
    normal2, scale2 = unit(branch[...])
    d_second = returned(inn, rows)
    total = floats(grad[...]) + unit_back(d_second * small[pl.ds(2, 1), :], normal3, scale3)
    low = unit_back(total * small[pl.ds(1, 1), :], normal2, scale2).astype(BF16)
    d_att[...] = low
    d_resid[...] = total
    give(2)
    for d in (1, 2, 3, 0):
        part = dot_t(low, inn(7 + d)[...]).astype(BF16)
        for j in range(PART // span):
            sent[(w ^ d) * (PART // span) + j] = part[:, span * j : span * (j + 1)]
    sums[pl.ds(0, 1), :] = column_sum(d_second * normal3)
    sums[pl.ds(1, 1), :] = column_sum(d_second)
    sums[pl.ds(2, 1), :] = column_sum(total * normal2)
    sums[pl.ds(3, 1), :] = column_sum(total)
    sums[pl.ds(4, 1), :] = column_sum(floats(low))


def grad_out(inn, out, give):
    w = lax.axis_index("wt")
    attended, grads = inn(0), inn(1)
    span = attended.shape[2]
    for d in (1, 3, 0, 2):
        for j in range(PART // span):
            part = t_dot(attended[(w ^ d) * (PART // span) + j], grads[...])
            out[d % 2][d // 2, pl.ds(span * j, span), :] = part.astype(BF16)
        if d == 3:
            give(1)


def attend_back(inn, out, give, d_out, d_keys, d_values):
    natural, dealt = out
    deal, mixed, stats, got = (inn(i) for i in range(4))
    length, span = d_out.shape
    heads = stats.shape[0] // 2
    head = span // heads
    factor = 1.0 / math.sqrt(head)
    prescale = factor / relax
    for j in range(CTX):
        for t in range(2):
            d_out[at(deal[j, t], PIECE), :] = got[j, pl.ds(PIECE * t, PIECE), :]
    lane = lax.broadcasted_iota(jnp.int32, (BLK, span), 1) // head
    d_keys[...] = jnp.zeros_like(d_keys)
    d_values[...] = jnp.zeros_like(d_values)
    for b in range(length // BLK):
        rows, seen = pl.ds(b * BLK, BLK), pl.ds(0, (b + 1) * BLK)
        query, grads = mixed[rows, pl.ds(0, span)], d_out[rows, :]
        parts = []
        for h in range(heads):
            query_h = jnp.where(lane == h, query, jnp.zeros_like(query))
            grads_h = jnp.where(lane == h, grads, jnp.zeros_like(grads))
            keys = mixed[seen, pl.ds(span, span)]
            raw = dot_t(keys, query_h)
            weights = jnp.exp((raw - stats[pl.ds(2 * h, 1), rows]) * factor) * stats[pl.ds(2 * h + 1, 1), rows]
            d_probs = dot_t(mixed[seen, pl.ds(2 * span, span)], grads_h)
            delta = jnp.sum(weights * d_probs, axis=0, keepdims=True)
            d_scores = (relax * weights * (d_probs - delta)).astype(BF16)
            d_values[seen, :] += dot(weights.astype(BF16), grads_h)
            d_keys[seen, :] += dot(d_scores, query_h)
            parts.append(t_dot(keys, d_scores)[h * head : (h + 1) * head, :])
        natural[rows, pl.ds(0, span)] = (jnp.concatenate(parts, axis=0).T * prescale).astype(BF16)
    natural[:, pl.ds(span, span)] = (d_keys[...] * prescale).astype(BF16)
    natural[:, pl.ds(2 * span, span)] = d_values[...].astype(BF16)
    for j in range(CTX):
        for t in range(2):
            dealt[j, pl.ds(PIECE * t, PIECE), :] = natural[at(deal[j, t], PIECE), :]


def grad_qkv(inn, out, give):
    w = lax.axis_index("wt")
    first, grads = inn(0), inn(1)
    for d in (1, 3, 0, 2):
        out[d % 2][d // 2] = t_dot(first[:, at(w ^ d, PART)], grads[...]).astype(BF16)
        if d == 3:
            give(1)


def bottom_norm(inn, out, give, joined, d_first):
    input_grad, keep, send = out
    w = lax.axis_index("wt")
    got, own, d_resid, small = (inn(i) for i in range(4))
    _, rows, triple = got.shape
    span, width = triple // 3, own.shape[1]
    for j in range(CTX):
        for part in range(3):
            joined[:, pl.ds(part * width + span * j, span)] = got[j, :, pl.ds(span * part, span)]
    half = PART // 2
    for d in range(WT):
        for h in range(2):
            block = inn(4 + 2 * d + h)
            d_first[:, at(2 * (w ^ d) + h, half)] = dot_t(joined[...], block[...])
    normal, scale = unit(floats(own[...]))
    grads = d_first[...]
    input_grad[...] = d_resid[...] + unit_back(grads * small[pl.ds(0, 1), :], normal, scale)
    give(0)
    middle, top, up = inn(12), inn(13), inn(14)
    lines = {
        0: column_sum(grads * normal),
        4: column_sum(grads),
        8: column_sum(floats(joined[:, pl.ds(0, width)])),
        9: column_sum(floats(joined[:, pl.ds(2 * width, width)])),
    }
    for i, line in enumerate((2, 6, 1, 5, 10)):
        lines[line] = middle[pl.ds(i, 1), :]
    for i, line in enumerate((3, 7, 11)):
        lines[line] = top[pl.ds(i, 1), :]
    for line, value in lines.items():
        d_first[pl.ds(line, 1), :] = value
    for d in range(WT):
        target = send if d % 2 else keep
        target[d // 2, pl.ds(0, 12), :] = d_first[pl.ds(0, 12), at(w ^ d, PART)]
        target[d // 2, pl.ds(12, 4), :] = jnp.zeros((4, PART), F32)
    for i in range(4):
        keep[0, pl.ds(12 + i, 1), :] = up[:, pl.ds(PART * i, PART)]


def add_second(inn, out, give):
    out[0][...] = (floats(inn(0)[1]) + floats(inn(1)[1])).astype(out[0].dtype)


def add_first(inn, out, give):
    out[0][...] = (floats(inn(0)[0]) + floats(inn(1)[0]) + floats(inn(2)[...])).astype(out[0].dtype)


def add_rest(inn, out, give):
    rows = out[0].shape[0]
    rest = pl.ds(rows, rows)
    out[0][...] = (inn(0)[rest, :] + floats(inn(1)[rest, :])).astype(BF16)


def add_high(inn, out, give):
    keep, got = inn(0), inn(1)
    for i in range(2):
        out[0][i] = (floats(keep[i]) + floats(got[i])).astype(BF16)


def add_high_last(inn, out, give):
    keep, got = inn(0), inn(1)
    for i in range(2):
        out[0][i] = (floats(keep[2 + i]) + floats(got[2 + i])).astype(BF16)


def add_low(first, inn, out, give):
    keep, got, after_z = inn(0), inn(1), inn(2)
    out[1][...] = (floats(keep[1]) + floats(got[first + 1]) + floats(after_z[1])).astype(BF16)
    out[0][...] = floats(keep[0]) + floats(got[first]) + floats(after_z[0])


def add_last(inn, out, give):
    out[0][...] = (inn(0)[...] + floats(inn(1)[...])).astype(BF16)


def add_out(inn, out, give, total):
    c = lax.axis_index("ctx")
    cut = out[0].shape[1]
    total[...] = (floats(inn(0)[0]) + floats(inn(1)[0]) + floats(inn(2)[...])).astype(BF16)
    for i, d in enumerate((0, 4, 2, 6)):
        out[0][i] = total[at(c ^ d, cut), :]
        out[1][i] = total[at(c ^ d ^ 1, cut), :]


def add_last_up(inn, out, give, total):
    w = lax.axis_index("wt")
    cut = out[0].shape[0]
    total[...] = (inn(0)[...] + floats(inn(1)[...])).astype(BF16)
    for d in range(WT):
        out[d][...] = total[at(w ^ d, cut), :]


def pack_rest(inn, out, give):
    block = out[0]
    cut = inn(0).shape[0]
    for i in range(WT + 1):
        block[pl.ds(cut * i, cut), :] = inn(i)[...]
    block[pl.ds(cut * (WT + 1), SMALL), :] = jnp.zeros((SMALL, block.shape[1]), BF16)
    sums = inn(WT + 1)[0] + inn(WT + 2)[0] + inn(WT + 3)[...]
    block[pl.ds(cut * (WT + 1), SMALL), pl.ds(0, PART)] = sums.astype(BF16)


def spread_qkv(inn, out, give):
    c = lax.axis_index("ctx")
    (full,) = out
    span = full.shape[1] // (3 * CTX)
    for d in range(CTX):
        block = inn(d)
        for part in range(3):
            full[:, at(part * CTX + (c ^ d), span)] = floats(block[:, pl.ds(span * part, span)])


def spread_down(inn, out, give, sems, result):
    c = lax.axis_index("ctx")
    stores = []
    for d in range(CTX):
        block = inn(d)
        rows = at(c ^ d, block.shape[0])
        out[0][rows, :] = floats(block[...])
        stores.append(pltpu.make_async_copy(out[0].at[rows, :], result.at[rows, :], sems.at[d]))
        stores[-1].start()
    for store in stores:
        store.wait()


def spread_rest(inn, out, give, total):
    up, proj, gain, shift, bias, up_bias = out
    c, w = lax.axis_index("ctx"), lax.axis_index("wt")
    cut = PART // CTX
    width = proj.shape[1]
    total[...] = jnp.zeros_like(total)
    for d in range(CTX):
        block = inn(d)
        for k in range(WT):
            up[at(c ^ d, cut), at(w ^ k, width)] = floats(block[pl.ds(cut * k, cut), :])
        proj[at(c ^ d, cut), :] = floats(block[pl.ds(cut * WT, cut), :])
        total[...] += floats(block[pl.ds(cut * (WT + 1), SMALL), pl.ds(0, PART)])
    for i, ref in enumerate((gain, shift, bias, up_bias)):
        ref[...] = total[pl.ds(4 * i, 4), :]


def split_device(
    layer_input,
    out_grad,
    deal,
    w_qkv,
    w_out,
    w_up,
    w_down,
    norm_gain,
    norm_shift,
    bias_width,
    up_bias,
):
    _, rows, width = layer_input.shape
    w = lax.axis_index("wt")
    per = HEADS // CTX
    span = per * (width // HEADS)
    length = rows * CTX
    hidden_width = w_down.shape[0]
    everyone = WT * rows
    own, grad = layer_input[0], out_grad[0]
    vmem, dma = pltpu.VMEM, pltpu.SemaphoreType.DMA

    sequence = gather_ctx(own)
    outs_x = swap(w_out, "wt", 2)
    begin = lax.optimization_barrier((w_qkv, w_up, norm_gain, norm_shift, bias_width, *sequence[1:3]))[:5]
    pack, *ups = call(
        prepare,
        "prepare",
        begin,
        [shape(PART + SMALL, 3 * span)] + [shape(PART, hidden_width)] * 3,
        raw=(0, 1),
        scratch=[dma((6,))],
    )
    packs = gather_wt(pack)
    up_core, up_x, up_both = ups
    up_x = swap(after(up_x, packs[2]), "wt", 2)
    up_both = swap(up_both, "wt", 3)
    outs_x, up_x, *packs = lax.optimization_barrier((outs_x, up_x, *packs))

    first, mixed, sent, stats, small = call(
        attend,
        "attend",
        (deal, *packs, *sequence),
        [
            shape(length, width),
            shape(length, 3 * span),
            shape(CTX, rows, span),
            shape(2 * per, length, dtype=F32),
            shape(SMALL, width, dtype=F32),
        ],
        smem=1,
        hbm=range(1, 1 + WT + CTX),
        hbm_out=(0, 1),
        scratch=[vmem((length, width), BF16), vmem((length, span), BF16)],
    )
    attended = lax.all_to_all(after(sent, up_both), "ctx", 0, 0, tiled=True)
    outs_own, outs_x, up_core = lax.optimization_barrier((w_out, outs_x, up_core, sent))[:3]
    outs = w_out, swap(outs_own, "wt", 1), outs_x, swap(outs_x, "wt", 1)
    ups = w_up, swap(up_core, "wt", 1), up_x, up_both
    half = PART // 2
    qkv_x0 = swap(after(w_qkv[:half], up_both), "wt", 2)
    attended = after(attended, *outs, *ups[1:], qkv_x0)

    branch, resid, second = call(
        project,
        "project",
        (small, attended, own, *outs),
        [shape(rows, width, dtype=F32), shape(rows, width, dtype=F32), shape(rows, width)],
        hbm=(2, 3),
    )

    own_columns = ((PART, hidden_width), lambda ref: ref.at[:, at(lax.axis_index("wt"), hidden_width)])
    halves = [shape(2 * rows, width, dtype=F32), shape(2 * rows, width)]
    seconds, hidden, slope, near, far = call(
        feed,
        "feed",
        (*gather_wt(second), *ups, up_bias.reshape(1, hidden_width), w_down),
        [shape(everyone, width), shape(everyone, hidden_width), shape(everyone, hidden_width, dtype=F32)]
        + halves,
        hbm=(4, 8, 9),
        hbm_out=(0,),
        views={4: own_columns},
    )

    def return_rows(near, far):
        got = swap(far, "wt", 1)
        back = call(add_rest, "add_rest", (near, got), [shape(rows, width)])
        return near, got, swap(back, "wt", 2)

    result, d_ffn, sums3 = call(
        top_norm,
        "top_norm",
        (*return_rows(near, far), small, resid, grad),
        [shape(rows, width), shape(rows, width), shape(3, width, dtype=F32)],
        hbm=(5,),
    )
    d_ffns, d_upper, near, far, up_sum = call(
        feed_back,
        "feed_back",
        (*gather_wt(d_ffn), w_down, slope, *ups),
        [shape(everyone, width), shape(everyone, hidden_width)] + halves + [shape(1, hidden_width, dtype=F32)],
        hbm=(4, 6),
        views={6: own_columns},
    )
    got = swap(far, "wt", 1)
    eighth = hidden_width // CTX
    keep_low_a, keep_high_a, send_a = call(
        grad_down,
        "grad_down",
        (hidden, d_ffns),
        [shape(2, eighth, width)] * 2 + [shape(4, eighth, width)],
        hbm_out=range(3),
    )
    got_a = swap(send_a, "ctx", 1)
    back = call(add_rest, "add_rest", (after(near, send_a), got), [shape(rows, width)])
    far = swap(back, "wt", 2)
    keep_low_b, keep_high_b, send_low_b, send_high_b = call(
        grad_up,
        "grad_up",
        (after(seconds, back), d_upper),
        [shape(2, eighth, width)] * 4,
        hbm=(0,),
        hbm_out=range(4),
        scratch=[vmem((PART, hidden_width), BF16)],
    )
    got_high_b = swap(send_high_b, "ctx", 1)
    got_low_b = swap(send_low_b, "ctx", 1)
    sent, d_att, d_resid, sums21 = call(
        middle_norms,
        "middle_norms",
        (near, got, after(far, send_low_b), small, resid, branch, grad, *outs),
        [
            shape(CTX, rows, span),
            shape(rows, width),
            shape(rows, width, dtype=F32),
            shape(5, width, dtype=F32),
        ],
        hbm=(6, 7),
        hbm_out=(2,),
    )
    qkv_x1 = swap(after(w_qkv[half:], far), "wt", 2)
    high_a = call(add_high, "add_high_a", (keep_high_a, got_a), [shape(2, eighth, width)], hbm=(0,))
    next_a = swap(high_a, "ctx", 2)
    got = lax.all_to_all(after(sent, high_a), "ctx", 0, 0, tiled=True)
    pieces = [shape(2, PART, width)] * 2
    keep_out, send_out = call(grad_out, "grad_out", (attended, d_att), pieces, hbm_out=(0, 1))
    got_out = swap(send_out, "wt", 1)
    back_out = call(add_second, "add_second_out", (keep_out, got_out), [shape(PART, width)], hbm=(0,))
    out_x = swap(back_out, "wt", 2)
    low_pair = [shape(eighth, width, dtype=F32), shape(eighth, width)]
    first_a, second_a = call(
        functools.partial(add_low, 2), "add_low_a", (keep_low_a, got_a, next_a), low_pair, hbm=(0,)
    )
    last_a = swap(second_a, "ctx", 4)
    high_b = call(add_high, "add_high_b", (keep_high_b, after(got_high_b, got)), [shape(2, eighth, width)], hbm=(0,))
    next_b = swap(high_b, "ctx", 2)

    natural, dealt = call(
        attend_back,
        "attend_back",
        (deal, mixed, stats, after(got, back_out, second_a, high_b, qkv_x1)),
        [shape(length, 3 * span), shape(CTX, rows, 3 * span)],
        smem=1,
        hbm=(1,),
        scratch=[vmem((length, span), BF16), vmem((length, span), F32), vmem((length, span), F32)],
    )
    pieces = [shape(2, PART, 3 * span)] * 2
    keep_qkv, send_qkv = call(grad_qkv, "grad_qkv", (first, natural), pieces, hbm=(0,), hbm_out=(0, 1))
    cut = PART // CTX
    keep_c, send_c = call(
        add_out,
        "add_out",
        (keep_out, got_out, after(out_x, natural)),
        [shape(4, cut, width)] * 2,
        hbm=(0,),
        scratch=[vmem((PART, width), BF16)],
    )
    got_c = swap(send_c, "ctx", 1)
    part_a = call(add_last, "add_last_a", (first_a, last_a), [shape(eighth, width)])
    down_slots = gather_ctx(part_a)
    first_b, second_b = call(
        functools.partial(add_low, 0), "add_low_b", (keep_low_b, after(got_low_b, natural), next_b), low_pair, hbm=(0,)
    )
    last_b = swap(second_b, "ctx", 4)
    got_rows = lax.all_to_all(after(dealt, second_b, send_c, send_qkv), "ctx", 0, 0, tiled=True)
    got_qkv = swap(after(send_qkv, second_b), "wt", 1)
    back_qkv = call(add_second, "add_second_qkv", (keep_qkv, got_qkv), [shape(PART, 3 * span)], hbm=(0,))
    qkv_x = swap(back_qkv, "wt", 2)
    qkv_own, qkv_x0, qkv_x1 = lax.optimization_barrier((w_qkv, qkv_x0, qkv_x1, second_b))[:3]
    qkv_core = swap(qkv_own, "wt", 1)
    all_qkv = [w_qkv, w_qkv, qkv_core, qkv_core, qkv_x0, qkv_x1, swap(qkv_x0, "wt", 1), swap(qkv_x1, "wt", 1)]
    half_rows = [((half, 3 * width), lambda ref, h=h: ref.at[pl.ds(half * h, half), :]) for h in range(2)]
    input_grad, keep, send = call(
        bottom_norm,
        "bottom_norm",
        (after(got_rows, down_slots[1], back_qkv), own, d_resid, small, *all_qkv, sums21, sums3, up_sum),
        [shape(rows, width, dtype=F32)] + [shape(2, SMALL, PART, dtype=F32)] * 2,
        hbm=(1, 2, *range(4, 12)),
        views={4 + i: half_rows[i % 2] for i in range(4)},
        hbm_out=(0,),
        scratch=[vmem((rows, 3 * width), BF16), vmem((rows, width), F32)],
    )
    got_sums = swap(send, "wt", 1)
    back_sums = call(add_second, "add_second_sums", (keep, got_sums), [shape(SMALL, PART, dtype=F32)])
    sums_x = swap(back_sums, "wt", 2)

    high_c = call(add_high_last, "add_high_c", (keep_c, got_c), [shape(2, cut, width)])
    next_c = swap(high_c, "ctx", 2)
    low_pair = [shape(cut, width, dtype=F32), shape(cut, width)]
    first_c, second_c = call(functools.partial(add_low, 0), "add_low_c", (keep_c, got_c, next_c), low_pair)
    last_c = swap(second_c, "ctx", 4)
    own_up, *up_parts = call(
        add_last_up,
        "add_last_up",
        (first_b, last_b),
        [shape(cut, width)] * WT,
        scratch=[vmem((eighth, width), BF16)],
    )
    up_parts = [swap(part, "wt", d) for part, d in zip(up_parts, (1, 2, 3))]
    out_part = call(add_last, "add_last_c", (first_c, last_c), [shape(cut, width)])
    qkv_part = call(
        add_first, "add_first_qkv", (keep_qkv, got_qkv, qkv_x), [shape(PART, 3 * span)], hbm=(0,)
    )
    qkv_slots = gather_ctx_z(after(qkv_part, down_slots[6]))
    rest = call(
        pack_rest,
        "pack_rest",
        (after(own_up, down_slots[1], down_slots[2]), *up_parts, out_part, keep, got_sums, sums_x),
        [shape((WT + 1) * cut + SMALL, width)],
    )
    rest_slots = gather_ctx(rest)
    full_qkv = call(spread_qkv, "spread_qkv", qkv_slots, [shape(PART, 3 * width, dtype=F32)], hbm_out=(0,))
    full_down = call(
        spread_down,
        "spread_down",
        down_slots,
        [shape(hidden_width, width, dtype=F32)],
        hbm_out=(0,),
        scratch=[dma((CTX,))],
        parts=(0,),
    )
    four = [shape(4, PART, dtype=F32)] * 4
    full_up, full_out, gain, shift, bias, up_total = call(
        spread_rest,
        "spread_rest",
        rest_slots,
        [shape(PART, WT * hidden_width, dtype=F32), shape(PART, width, dtype=F32)] + four,
        hbm_out=range(6),
        scratch=[vmem((SMALL, PART), F32)],
    )
    return (
        result[None],
        input_grad[None],
        full_qkv,
        full_out,
        full_up,
        full_down,
        gain,
        shift,
        bias,
        up_total.reshape(hidden_width),
    )


def solution(mesh):
    small = mesh.shape["ctx"] == CTX and mesh.shape["wt"] == WT
    per_device = split_device if small else general_device
    in_specs = (
        P("wt", "ctx", None),
        P("wt", "ctx", None),
        P(),
        P("wt", None),
        P("wt", None),
        P("wt", None),
        P("wt", None),
        P(None, "wt"),
        P(None, "wt"),
        P(None, "wt"),
        P("wt"),
    )
    out_specs = (
        P("wt", "ctx", None),
        P("wt", "ctx", None),
        P("wt", None),
        P("wt", None),
        P("wt", None),
        P("wt", None),
        P(None, "wt"),
        P(None, "wt"),
        P(None, "wt"),
        P("wt"),
    )
    return jax.shard_map(
        per_device, mesh=mesh, in_specs=in_specs, out_specs=out_specs, check_vma=False
    )
```

```python
import functools
import math

import jax
import jax.numpy as jnp
from jax import lax
from jax.experimental import pallas as pl
from jax.experimental.pallas import tpu as pltpu
from jax.sharding import PartitionSpec as P

HEADS = 16
BLK = 256
PIECE = 64


epsilon = 1e-05
relax = 32.0


def layer_norm(value, gain, shift):
    mean = jnp.mean(value, axis=-1, keepdims=True)
    centered = value - mean
    spread = jnp.mean(centered * centered, axis=-1, keepdims=True)
    return centered * lax.rsqrt(spread + epsilon) * gain + shift


def gelu_tanh(value):
    return jax.nn.gelu(value, approximate=True)


def rows_dot(left, weight):
    return jnp.einsum("std,de->ste", left, weight, preferred_element_type=jnp.float32)


def weight_grad(left, right):
    return jnp.einsum("std,ste->de", left, right, preferred_element_type=jnp.float32)


def back_dot(grad, weight):
    return jnp.einsum("ste,de->std", grad, weight, preferred_element_type=jnp.float32)


def row_total(value):
    return jnp.sum(value.astype(jnp.float32), axis=(0, 1))


def general_device(
    layer_input,
    out_grad,
    deal,
    w_qkv,
    w_out,
    w_up,
    w_down,
    norm_gain,
    norm_shift,
    bias_width,
    up_bias,
):
    seqs, rows, width = layer_input.shape
    heads = HEADS
    head = width // heads
    prescale = 1.0 / (relax * math.sqrt(head))
    ranks = lax.axis_size("ctx")
    length = rows * ranks
    per_block = BLK // PIECE
    rank = lax.axis_index("ctx")
    chosen = jnp.arange(ranks, dtype=jnp.int32) == rank
    mine = jnp.sum(jnp.where(chosen[:, None], deal, 0), axis=0)
    query_blocks = jnp.repeat(mine, rows // 2) // per_block
    key_blocks = jnp.repeat(deal.reshape(-1), rows // 2) // per_block
    full_qkv, full_out, full_up, full_down, gains, shifts, biases, up_shift = (
        lax.all_gather(w_qkv, "wt", axis=0, tiled=True),
        lax.all_gather(w_out, "wt", axis=0, tiled=True),
        lax.all_gather(w_up, "wt", axis=0, tiled=True),
        lax.all_gather(w_down, "wt", axis=0, tiled=True),
        lax.all_gather(norm_gain, "wt", axis=1, tiled=True),
        lax.all_gather(norm_shift, "wt", axis=1, tiled=True),
        lax.all_gather(bias_width, "wt", axis=1, tiled=True),
        lax.all_gather(up_bias, "wt", axis=0, tiled=True),
    )
    gains = gains.astype(jnp.float32)
    shifts = shifts.astype(jnp.float32)
    biases = biases.astype(jnp.float32)
    up_shift = up_shift.astype(jnp.float32)
    input_float = layer_input.astype(jnp.float32)
    first = layer_norm(input_float, gains[0], shifts[0]).astype(jnp.bfloat16)
    mixed = rows_dot(first, full_qkv)
    query = (mixed[..., :width] + biases[0]).astype(jnp.bfloat16)
    kv_local = jnp.concatenate(
        [mixed[..., width : 2 * width], mixed[..., 2 * width :] + biases[1]], axis=-1
    ).astype(jnp.bfloat16)
    kv_all = lax.all_gather(kv_local, "ctx", axis=1, tiled=True)
    step = math.gcd(length, 1024)
    count = length // step
    query4 = query.reshape(seqs, rows, heads, head)

    def score_block(left, right):
        return (
            jnp.einsum("sqhd,skhd->shqk", left, right, preferred_element_type=jnp.float32)
            * prescale
        )

    def key_block(index):
        start = index * step
        piece = lax.dynamic_slice_in_dim(kv_all, start, step, 1)
        keys4 = piece[..., :width].reshape(seqs, step, heads, head)
        values4 = piece[..., width:].reshape(seqs, step, heads, head)
        visible = (
            query_blocks[:, None] >= lax.dynamic_slice_in_dim(key_blocks, start, step, 0)[None, :]
        )
        return (keys4, values4, visible)

    def probs(raw, visible, totals):
        return jnp.where(visible, jnp.exp(raw * relax - totals[..., None]), 0.0)

    def online(index, carry):
        top, total, acc = carry
        keys4, values4, visible = key_block(index)
        raw = jnp.where(visible, score_block(query4, keys4), -1e30)
        new_top = jnp.maximum(top, jnp.max(raw, axis=-1))
        terms = jnp.where(visible, jnp.exp((raw - new_top[..., None]) * relax), 0.0)
        factor = jnp.exp((top - new_top) * relax)
        total = total * factor + jnp.sum(terms, axis=-1)
        acc = acc * jnp.transpose(factor, (0, 2, 1))[..., None]
        acc = acc + jnp.einsum(
            "shqk,skhd->sqhd",
            terms.astype(jnp.bfloat16),
            values4,
            preferred_element_type=jnp.float32,
        )
        return (new_top, total, acc)

    start_top = jnp.full((seqs, heads, rows), -1e30, jnp.float32)
    start_total = jnp.zeros((seqs, heads, rows), jnp.float32)
    start_acc = jnp.zeros((seqs, rows, heads, head), jnp.float32)
    top, total, acc = lax.fori_loop(0, count, online, (start_top, start_total, start_acc))
    log_total = top * relax + jnp.log(total)
    attended_float = acc / jnp.transpose(total, (0, 2, 1))[..., None]
    attended = attended_float.reshape(seqs, rows, width).astype(jnp.bfloat16)
    branch = rows_dot(attended, full_out) + biases[2]
    resid = input_float + layer_norm(branch, gains[1], shifts[1])
    second = layer_norm(resid, gains[2], shifts[2]).astype(jnp.bfloat16)
    upper = rows_dot(second, full_up) + up_shift
    hidden = gelu_tanh(upper).astype(jnp.bfloat16)
    ffn = rows_dot(hidden, full_down) + biases[3]
    top_norm, pull_four = jax.vjp(layer_norm, ffn, gains[3], shifts[3])
    result = resid + top_norm
    d_out = out_grad.astype(jnp.float32)
    d_ffn, d_gain3, d_shift3 = pull_four(d_out)
    d_ffn = d_ffn.astype(jnp.bfloat16)
    d_bias3 = row_total(d_ffn)
    g_down = weight_grad(hidden, d_ffn)
    d_hidden = back_dot(d_ffn, full_down)
    _, pull_gelu = jax.vjp(gelu_tanh, upper)
    d_upper = pull_gelu(d_hidden)[0].astype(jnp.bfloat16)
    d_up_shift = row_total(d_upper)
    g_up = weight_grad(second, d_upper)
    d_second = back_dot(d_upper, full_up)
    _, pull_three = jax.vjp(layer_norm, resid, gains[2], shifts[2])
    d_resid_part, d_gain2, d_shift2 = pull_three(d_second)
    d_resid = d_out + d_resid_part
    _, pull_two = jax.vjp(layer_norm, branch, gains[1], shifts[1])
    d_branch, d_gain1, d_shift1 = pull_two(d_resid)
    d_branch = d_branch.astype(jnp.bfloat16)
    d_bias2 = row_total(d_branch)
    g_out = weight_grad(attended, d_branch)
    d_attended = back_dot(d_branch, full_out).astype(jnp.bfloat16)
    d_out4 = d_attended.reshape(seqs, rows, heads, head)
    delta = jnp.einsum("sqhd,sqhd->shq", d_out4.astype(jnp.float32), attended_float)

    def score_grads(q_rows, do_rows, k_rows, v_rows, visible, lse_rows, delta_rows):
        weights = probs(score_block(q_rows, k_rows), visible, lse_rows)
        d_probs = jnp.einsum("sqhd,skhd->shqk", do_rows, v_rows, preferred_element_type=jnp.float32)
        d_scores = (relax * weights * (d_probs - delta_rows[..., None])).astype(jnp.bfloat16)
        return (d_scores, weights.astype(jnp.bfloat16))

    zero_query = jnp.zeros((seqs, rows, heads, head), jnp.float32)

    def local_grads(d_query, index):
        keys4, values4, visible = key_block(index)
        d_scores, weights = score_grads(query4, d_out4, keys4, values4, visible, log_total, delta)
        d_query = (
            d_query
            + jnp.einsum("shqk,skhd->sqhd", d_scores, keys4, preferred_element_type=jnp.float32)
            * prescale
        )
        d_keys = (
            jnp.einsum("shqk,sqhd->kshd", d_scores, query4, preferred_element_type=jnp.float32)
            * prescale
        )
        d_values = jnp.einsum(
            "shqk,sqhd->kshd", weights, d_out4, preferred_element_type=jnp.float32
        )
        joined = jnp.concatenate(
            [d_keys.reshape(step, seqs, width), d_values.reshape(step, seqs, width)], axis=-1
        )
        return (d_query, joined)

    d_query, pieces = lax.scan(local_grads, zero_query, jnp.arange(count, dtype=jnp.int32))
    terms = pieces.reshape(length, seqs, 2 * width)
    d_kv = jnp.transpose(lax.psum_scatter(terms, "ctx", scatter_dimension=0, tiled=True), (1, 0, 2))
    d_query = d_query.reshape(seqs, rows, width).astype(jnp.bfloat16)
    d_kv = d_kv.astype(jnp.bfloat16)
    d_bias0 = row_total(d_query)
    d_bias1 = row_total(d_kv[..., width:])
    d_mixed = jnp.concatenate([d_query, d_kv], axis=-1)
    g_qkv = weight_grad(first, d_mixed)
    d_first = back_dot(d_mixed, full_qkv)
    _, pull_one = jax.vjp(layer_norm, input_float, gains[0], shifts[0])
    d_input_part, d_gain0, d_shift0 = pull_one(d_first)
    input_grad = d_resid + d_input_part
    grad_gain = jnp.stack([d_gain0, d_gain1, d_gain2, d_gain3])
    grad_shift = jnp.stack([d_shift0, d_shift1, d_shift2, d_shift3])
    grad_bias = jnp.stack([d_bias0, d_bias1, d_bias2, d_bias3])
    owned = (
        lax.psum_scatter(g_qkv.astype(jnp.bfloat16), "wt", scatter_dimension=0, tiled=True).astype(
            jnp.float32
        ),
        lax.psum_scatter(g_out.astype(jnp.bfloat16), "wt", scatter_dimension=0, tiled=True).astype(
            jnp.float32
        ),
        lax.psum_scatter(g_up.astype(jnp.bfloat16), "wt", scatter_dimension=0, tiled=True).astype(
            jnp.float32
        ),
        lax.psum_scatter(g_down.astype(jnp.bfloat16), "wt", scatter_dimension=0, tiled=True).astype(
            jnp.float32
        ),
        lax.psum_scatter(
            grad_gain.astype(jnp.bfloat16), "wt", scatter_dimension=1, tiled=True
        ).astype(jnp.float32),
        lax.psum_scatter(
            grad_shift.astype(jnp.bfloat16), "wt", scatter_dimension=1, tiled=True
        ).astype(jnp.float32),
        lax.psum_scatter(
            grad_bias.astype(jnp.bfloat16), "wt", scatter_dimension=1, tiled=True
        ).astype(jnp.float32),
        lax.psum_scatter(
            d_up_shift.astype(jnp.bfloat16), "wt", scatter_dimension=0, tiled=True
        ).astype(jnp.float32),
    )
    summed = lax.psum(
        (owned[0], owned[1], owned[2], owned[3], owned[4], owned[5], owned[6], owned[7]), "ctx"
    )
    return (
        result.astype(jnp.bfloat16),
        input_grad,
        summed[0],
        summed[1],
        summed[2],
        summed[3],
        summed[4],
        summed[5],
        summed[6],
        summed[7],
    )


F32 = jnp.float32
BF16 = jnp.bfloat16
WT = 4
CTX = 8
PART = 256
SMALL = 16
GELU_A = math.sqrt(2.0 / math.pi)
GELU_B = 0.044715


def swap(value, axis, bit):
    size = lax.axis_size(axis)
    return lax.ppermute(value, axis, [(i, i ^ bit) for i in range(size)])


def gather_wt(block):
    far = swap(block, "wt", 2)
    return block, swap(block, "wt", 1), far, swap(far, "wt", 1)


def gather_ctx(block):
    far, near, side = (swap(block, "ctx", bit) for bit in (4, 2, 1))
    near = after(near, side)
    near_side = swap(near, "ctx", 1)
    far = after(far, near_side)
    corner = swap(far, "ctx", 2)
    far_side = swap(far, "ctx", 1)
    return [block, side, near, near_side, far, far_side, corner, swap(after(corner, far_side), "ctx", 1)]


def gather_ctx_z(block):
    blocks = {0: block}
    for bit in (1, 4, 2):
        blocks.update({d ^ bit: swap(value, "ctx", bit) for d, value in blocks.items()})
    return [blocks[d] for d in range(CTX)]


def after(value, *others):
    return lax.optimization_barrier((value, *others))[0]


def floats(value):
    return value.astype(F32)


def dot(left, right):
    return jnp.dot(left, right, preferred_element_type=F32)


def dot_t(left, right):
    return lax.dot_general(left, right, (((1,), (1,)), ((), ())), preferred_element_type=F32)


def t_dot(left, right):
    return lax.dot_general(left, right, (((0,), (0,)), ((), ())), preferred_element_type=F32)


def at(start, size):
    return pl.ds(pl.multiple_of(start * size, size), size)


def shape(*dims, dtype=jnp.bfloat16):
    return jax.ShapeDtypeStruct(dims, dtype)


def call(body, name, ins, outs, smem=0, raw=(), hbm=(), views=None, hbm_out=(), scratch=(), parts=(), slack=10):
    views = views or {}
    ends = [i for i in hbm_out if i not in parts]
    vmem, dma = pltpu.VMEM, pltpu.SemaphoreType.DMA

    def kernel(*refs):
        sources, results = refs[: len(ins)], list(refs[len(ins) : len(ins) + len(outs)])
        rest = list(refs[len(ins) + len(outs) :])
        buffers = {i: rest.pop(0) for i in hbm}
        targets = {i: rest.pop(0) for i in hbm_out}
        in_sems, out_sems = rest.pop(0), rest.pop(0)
        loads, stores = {}, {}
        for i in hbm:
            source = views[i][1](sources[i]) if i in views else sources[i]
            loads[i] = pltpu.make_async_copy(source, buffers[i], in_sems.at[i])
            loads[i].start()

        def inn(i):
            if i not in buffers:
                return sources[i]
            if i in loads:
                loads.pop(i).wait()
            return buffers[i]

        def give(i):
            if i in targets:
                stores[i] = pltpu.make_async_copy(targets[i], results[i], out_sems.at[i])
                stores[i].start()

        body(inn, [targets.get(i, ref) for i, ref in enumerate(results)], give, *rest, *[results[i] for i in parts])
        for i in ends:
            if i not in stores:
                give(i)
        for store in stores.values():
            store.wait()

    buffers = [(views[i][0] if i in views else ins[i].shape, ins[i].dtype) for i in hbm]
    buffers += [(outs[i].shape, outs[i].dtype) for i in hbm_out]
    held = buffers + [(s.shape, s.dtype) for s in scratch if s.dtype in (BF16, F32)]
    limit = slack + -(-sum(math.prod(dims) * jnp.dtype(kind).itemsize for dims, kind in held) >> 20)
    spaces = [pltpu.SMEM if i < smem else pltpu.HBM if i in hbm or i in raw else vmem for i in range(len(ins))]
    out_spaces = [pltpu.HBM if i in hbm_out else vmem for i in range(len(outs))]
    results = [space(o.shape, o.dtype) for space, o in zip(out_spaces, outs)]
    out_specs = [pl.BlockSpec(memory_space=space) for space in out_spaces]
    single = len(outs) == 1
    return pl.pallas_call(
        kernel,
        name=name,
        out_shape=results[0] if single else tuple(results),
        in_specs=[pl.BlockSpec(memory_space=space) for space in spaces],
        out_specs=out_specs[0] if single else tuple(out_specs),
        scratch_shapes=[vmem(*b) for b in buffers] + [dma((len(ins),)), dma((len(outs),))] + list(scratch),
        compiler_params=pltpu.CompilerParams(vmem_limit_bytes=limit << 20),
        cost_estimate=pl.CostEstimate(flops=0, bytes_accessed=1024, transcendentals=0),
    )(*ins[:smem], *[pltpu.with_memory_space_constraint(a, s) for a, s in list(zip(ins, spaces))[smem:]])


def unit(value):
    centered = value - jnp.mean(value, axis=-1, keepdims=True)
    spread = jnp.mean(centered * centered, axis=-1, keepdims=True)
    scale = lax.rsqrt(spread + epsilon)
    return centered * scale, scale


def unit_back(grad, normal, scale):
    mean = jnp.mean(grad, axis=-1, keepdims=True)
    along = jnp.mean(grad * normal, axis=-1, keepdims=True)
    return scale * (grad - mean - normal * along)


def column_sum(value):
    return jnp.sum(value, axis=0, keepdims=True)


def prepare(inn, out, give, sems):
    c, w = lax.axis_index("ctx"), lax.axis_index("wt")
    qkv, up, pack = inn(0), inn(1), out[0]
    rows, width = qkv.shape[0], qkv.shape[1] // 3
    span, size = pack.shape[1] // 3, out[1].shape[1]
    copies = []
    for part in range(3):
        source = qkv.at[:, at(part * (width // span) + c, span)]
        copies.append((source, pack.at[pl.ds(0, rows), pl.ds(part * span, span)]))
    copies += [(up.at[:, at(w ^ d, size)], out[d]) for d in (2, 3, 1)]
    copies = [pltpu.make_async_copy(a, b, sems.at[i]) for i, (a, b) in enumerate(copies)]
    for copy in copies:
        copy.start()
    low = pl.ds(rows, SMALL)
    pack[low, :] = jnp.zeros((SMALL, pack.shape[1]), BF16)
    for i in range(3):
        ref = inn(2 + i)
        pack[pl.ds(rows + 4 * i, 4), pl.ds(0, ref.shape[1])] = ref[...]
    for copy in copies:
        copy.wait()


def attend(inn, out, give, xs, norm):
    first, mixed, sent, stats, small = out
    c, w = lax.axis_index("ctx"), lax.axis_index("wt")
    deal = inn(0)
    length, width = xs.shape
    span = sent.shape[2]
    heads = stats.shape[0] // 2
    head = span // heads
    packs = [inn(1 + d) for d in range(WT)]
    for d in range(WT):
        small[:, at(w ^ d, PART)] = floats(packs[d][pl.ds(PART, SMALL), pl.ds(0, PART)])
    for d in range(CTX):
        block = inn(1 + WT + d)
        for t in range(2):
            xs[at(deal[c ^ d, t], PIECE), :] = block[pl.ds(PIECE * t, PIECE), :]
    bias_q = small[pl.ds(8, 1), at(c, span)]
    bias_v = small[pl.ds(9, 1), at(c, span)]

    @pl.loop(0, length // BLK)
    def _(i):
        rows = at(i, BLK)
        normal, _scale = unit(floats(xs[rows, :]))
        first[rows, :] = (normal * small[pl.ds(0, 1), :] + small[pl.ds(4, 1), :]).astype(BF16)
        total = dot(first[rows, at(w, PART)], packs[0][pl.ds(0, PART), :])
        for d in range(1, WT):
            total += dot(first[rows, at(w ^ d, PART)], packs[d][pl.ds(0, PART), :])
        mixed[rows, pl.ds(0, span)] = (total[:, :span] + bias_q).astype(BF16)
        mixed[rows, pl.ds(span, span)] = total[:, span : 2 * span].astype(BF16)
        mixed[rows, pl.ds(2 * span, span)] = (total[:, 2 * span :] + bias_v).astype(BF16)

    give(0)
    give(1)
    give(4)
    lane = lax.broadcasted_iota(jnp.int32, (BLK, span), 1) // head
    factor = 1.0 / math.sqrt(head)
    for b in range(length // BLK):
        rows, seen = pl.ds(b * BLK, BLK), pl.ds(0, (b + 1) * BLK)
        query = mixed[rows, pl.ds(0, span)]
        parts = []
        for h in range(heads):
            masked = jnp.where(lane == h, query, jnp.zeros_like(query))
            raw = dot_t(mixed[seen, pl.ds(span, span)], masked)
            top = jnp.max(raw, axis=0, keepdims=True)
            terms = jnp.exp((raw - top) * factor)
            inverse = 1.0 / jnp.sum(terms, axis=0, keepdims=True)
            stats[pl.ds(2 * h, 1), rows] = top
            stats[pl.ds(2 * h + 1, 1), rows] = inverse
            weights = (terms * inverse).astype(BF16)
            values = mixed[seen, pl.ds(2 * span, span)]
            parts.append(t_dot(values, weights)[h * head : (h + 1) * head, :])
        norm[rows, :] = jnp.concatenate(parts, axis=0).T.astype(BF16)
    for j in range(CTX):
        for t in range(2):
            sent[j, pl.ds(PIECE * t, PIECE), :] = norm[at(deal[j, t], PIECE), :]


def project(inn, out, give):
    branch, resid, second = out
    w = lax.axis_index("wt")
    small, attended, own = inn(0), inn(1), inn(2)
    span = attended.shape[2]
    total = small[pl.ds(10, 1), :]
    for d in range(WT):
        ref = inn(3 + d)
        for j in range(PART // span):
            total = total + dot(attended[(w ^ d) * (PART // span) + j], ref[pl.ds(span * j, span), :])
    branch[...] = total
    give(0)
    normal, _ = unit(total)
    total = floats(own[...]) + (normal * small[pl.ds(1, 1), :] + small[pl.ds(5, 1), :])
    resid[...] = total
    give(1)
    normal, _ = unit(total)
    second[...] = (normal * small[pl.ds(2, 1), :] + small[pl.ds(6, 1), :]).astype(BF16)


def join_slots(inn, start, target):
    for i, d in enumerate((0, 2, 1, 3)):
        ref = inn(start + d)
        rows = ref.shape[0]
        target[pl.ds(rows * i, rows), :] = ref[...]


def feed(inn, out, give):
    all_rows, hidden, slope, near, far = out
    w = lax.axis_index("wt")
    join_slots(inn, 0, all_rows)
    give(0)
    ups, bias = [inn(4 + d) for d in range(WT)], inn(8)
    half_rows = near.shape[0]

    @pl.loop(0, hidden.shape[1] // PART)
    def _(n):
        cols = at(n, PART)
        upper = floats(bias[pl.ds(0, 1), cols])
        for d in range(WT):
            upper = upper + dot(all_rows[:, at(w ^ d, PART)], ups[d][:, cols])
        square = upper * upper
        curve = jnp.tanh(GELU_A * (upper + GELU_B * (square * upper)))
        half = 0.5 * (1.0 + curve)
        hidden[:, cols] = (upper * half).astype(BF16)
        slope[:, cols] = half + (0.5 * GELU_A) * upper * (1.0 - curve * curve) * (
            1.0 + (3.0 * GELU_B) * square
        )

    give(1)
    give(2)
    down = inn(9)

    @pl.loop(0, near.shape[1] // PART)
    def _(n):
        cols = at(n, PART)
        total = dot(hidden[...], down[:, cols])
        near[:, cols] = total[:half_rows]
        far[:, cols] = total[half_rows:].astype(BF16)


def returned(inn, rows):
    own = pl.ds(0, rows)
    return inn(0)[own, :] + floats(inn(1)[own, :]) + floats(inn(2)[...])


def top_norm(inn, out, give):
    result, d_ffn, sums = out
    small, resid, grad = inn(3), inn(4), inn(5)
    normal, scale = unit(returned(inn, resid.shape[0]) + small[pl.ds(11, 1), :])
    gain = small[pl.ds(3, 1), :]
    d_out = floats(grad[...])
    low = unit_back(d_out * gain, normal, scale).astype(BF16)
    d_ffn[...] = low
    give(1)
    result[...] = (resid[...] + (normal * gain + small[pl.ds(7, 1), :])).astype(BF16)
    sums[pl.ds(0, 1), :] = column_sum(d_out * normal)
    sums[pl.ds(1, 1), :] = column_sum(d_out)
    sums[pl.ds(2, 1), :] = column_sum(floats(low))


def feed_back(inn, out, give):
    all_rows, d_upper, near, far, sums = out
    w = lax.axis_index("wt")
    join_slots(inn, 0, all_rows)
    give(0)
    down, slope = inn(4), inn(5)
    half_rows = near.shape[0]

    @pl.loop(0, d_upper.shape[1] // PART)
    def _(n):
        cols = at(n, PART)
        low = (dot_t(all_rows[...], down[cols, :]) * slope[:, cols]).astype(BF16)
        d_upper[:, cols] = low
        sums[pl.ds(0, 1), cols] = column_sum(floats(low))

    give(1)
    for d in range(WT):
        cols = at(w ^ d, PART)
        total = dot_t(d_upper[...], inn(6 + d)[...])
        near[:, cols] = total[:half_rows]
        far[:, cols] = total[half_rows:].astype(BF16)


PLACES = ((0, 0, 0), (0, 1, 4), (1, 0, 2), (1, 1, 6), (2, 0, 1), (2, 1, 5), (3, 0, 3), (3, 1, 7))


def grad_down(inn, out, give):
    c = lax.axis_index("ctx")
    hidden, grads = inn(0), inn(1)
    size = out[0].shape[1]
    for target, i, d in ((2, 0, 3), (2, 1, 7), (2, 2, 1), (2, 3, 5), (1, 0, 2), (1, 1, 6), (0, 0, 0), (0, 1, 4)):
        out[target][i] = t_dot(hidden[:, at(c ^ d, size)], grads[...]).astype(BF16)
        if d == 5:
            give(2)


def grad_up(inn, out, give, part):
    c = lax.axis_index("ctx")
    cut = PART // CTX
    rows_in, grads = inn(0), inn(1)

    @pl.loop(0, WT)
    def _(k):
        part[...] = t_dot(rows_in[:, at(k, PART)], grads[...]).astype(BF16)
        for which, i, d in PLACES:
            out[which][i, at(k, cut), :] = part[at(c ^ d, cut), :]


def middle_norms(inn, out, give):
    sent, d_att, d_resid, sums = out
    w = lax.axis_index("wt")
    small, resid, branch, grad = inn(3), inn(4), inn(5), inn(6)
    rows, span = resid.shape[0], sent.shape[2]
    normal3, scale3 = unit(resid[...])
    normal2, scale2 = unit(branch[...])
    d_second = returned(inn, rows)
    total = floats(grad[...]) + unit_back(d_second * small[pl.ds(2, 1), :], normal3, scale3)
    low = unit_back(total * small[pl.ds(1, 1), :], normal2, scale2).astype(BF16)
    d_att[...] = low
    d_resid[...] = total
    give(2)
    for d in (1, 2, 3, 0):
        part = dot_t(low, inn(7 + d)[...]).astype(BF16)
        for j in range(PART // span):
            sent[(w ^ d) * (PART // span) + j] = part[:, span * j : span * (j + 1)]
    sums[pl.ds(0, 1), :] = column_sum(d_second * normal3)
    sums[pl.ds(1, 1), :] = column_sum(d_second)
    sums[pl.ds(2, 1), :] = column_sum(total * normal2)
    sums[pl.ds(3, 1), :] = column_sum(total)
    sums[pl.ds(4, 1), :] = column_sum(floats(low))


def grad_out(inn, out, give):
    w = lax.axis_index("wt")
    attended, grads = inn(0), inn(1)
    span = attended.shape[2]
    for d in (1, 3, 0, 2):
        for j in range(PART // span):
            part = t_dot(attended[(w ^ d) * (PART // span) + j], grads[...])
            out[d % 2][d // 2, pl.ds(span * j, span), :] = part.astype(BF16)
        if d == 3:
            give(1)


def attend_back(inn, out, give, d_out, d_keys, d_values):
    natural, dealt = out
    deal, mixed, stats, got = (inn(i) for i in range(4))
    length, span = d_out.shape
    heads = stats.shape[0] // 2
    head = span // heads
    factor = 1.0 / math.sqrt(head)
    prescale = factor / relax
    for j in range(CTX):
        for t in range(2):
            d_out[at(deal[j, t], PIECE), :] = got[j, pl.ds(PIECE * t, PIECE), :]
    lane = lax.broadcasted_iota(jnp.int32, (BLK, span), 1) // head
    d_keys[...] = jnp.zeros_like(d_keys)
    d_values[...] = jnp.zeros_like(d_values)
    for b in range(length // BLK):
        rows, seen = pl.ds(b * BLK, BLK), pl.ds(0, (b + 1) * BLK)
        query, grads = mixed[rows, pl.ds(0, span)], d_out[rows, :]
        parts = []
        for h in range(heads):
            query_h = jnp.where(lane == h, query, jnp.zeros_like(query))
            grads_h = jnp.where(lane == h, grads, jnp.zeros_like(grads))
            keys = mixed[seen, pl.ds(span, span)]
            raw = dot_t(keys, query_h)
            weights = jnp.exp((raw - stats[pl.ds(2 * h, 1), rows]) * factor) * stats[pl.ds(2 * h + 1, 1), rows]
            d_probs = dot_t(mixed[seen, pl.ds(2 * span, span)], grads_h)
            delta = jnp.sum(weights * d_probs, axis=0, keepdims=True)
            d_scores = (relax * weights * (d_probs - delta)).astype(BF16)
            d_values[seen, :] += dot(weights.astype(BF16), grads_h)
            d_keys[seen, :] += dot(d_scores, query_h)
            parts.append(t_dot(keys, d_scores)[h * head : (h + 1) * head, :])
        natural[rows, pl.ds(0, span)] = (jnp.concatenate(parts, axis=0).T * prescale).astype(BF16)
    natural[:, pl.ds(span, span)] = (d_keys[...] * prescale).astype(BF16)
    natural[:, pl.ds(2 * span, span)] = d_values[...].astype(BF16)
    for j in range(CTX):
        for t in range(2):
            dealt[j, pl.ds(PIECE * t, PIECE), :] = natural[at(deal[j, t], PIECE), :]


def grad_qkv(inn, out, give):
    w = lax.axis_index("wt")
    first, grads = inn(0), inn(1)
    for d in (1, 3, 0, 2):
        out[d % 2][d // 2] = t_dot(first[:, at(w ^ d, PART)], grads[...]).astype(BF16)
        if d == 3:
            give(1)


def bottom_norm(inn, out, give, joined, d_first):
    input_grad, keep, send = out
    w = lax.axis_index("wt")
    got, own, d_resid, small = (inn(i) for i in range(4))
    _, rows, triple = got.shape
    span, width = triple // 3, own.shape[1]
    for j in range(CTX):
        for part in range(3):
            joined[:, pl.ds(part * width + span * j, span)] = got[j, :, pl.ds(span * part, span)]
    for d in range(WT):
        d_first[:, at(w ^ d, PART)] = dot_t(joined[...], inn(4 + d)[...])
    normal, scale = unit(floats(own[...]))
    grads = d_first[...]
    input_grad[...] = d_resid[...] + unit_back(grads * small[pl.ds(0, 1), :], normal, scale)
    give(0)
    middle, top, up = inn(8), inn(9), inn(10)
    lines = {
        0: column_sum(grads * normal),
        4: column_sum(grads),
        8: column_sum(floats(joined[:, pl.ds(0, width)])),
        9: column_sum(floats(joined[:, pl.ds(2 * width, width)])),
    }
    for i, line in enumerate((2, 6, 1, 5, 10)):
        lines[line] = middle[pl.ds(i, 1), :]
    for i, line in enumerate((3, 7, 11)):
        lines[line] = top[pl.ds(i, 1), :]
    for line, value in lines.items():
        d_first[pl.ds(line, 1), :] = value
    for d in range(WT):
        target = send if d % 2 else keep
        target[d // 2, pl.ds(0, 12), :] = d_first[pl.ds(0, 12), at(w ^ d, PART)]
        target[d // 2, pl.ds(12, 4), :] = jnp.zeros((4, PART), F32)
    for i in range(4):
        keep[0, pl.ds(12 + i, 1), :] = up[:, pl.ds(PART * i, PART)]


def add_second(inn, out, give):
    out[0][...] = (floats(inn(0)[1]) + floats(inn(1)[1])).astype(out[0].dtype)


def add_first(inn, out, give):
    out[0][...] = (floats(inn(0)[0]) + floats(inn(1)[0]) + floats(inn(2)[...])).astype(out[0].dtype)


def add_rest(inn, out, give):
    rows = out[0].shape[0]
    rest = pl.ds(rows, rows)
    out[0][...] = (inn(0)[rest, :] + floats(inn(1)[rest, :])).astype(BF16)


def add_high(inn, out, give):
    keep, got = inn(0), inn(1)
    for i in range(2):
        out[0][i] = (floats(keep[i]) + floats(got[i])).astype(BF16)


def add_high_last(inn, out, give):
    keep, got = inn(0), inn(1)
    for i in range(2):
        out[0][i] = (floats(keep[2 + i]) + floats(got[2 + i])).astype(BF16)


def add_low(first, inn, out, give):
    keep, got, after_z = inn(0), inn(1), inn(2)
    out[1][...] = (floats(keep[1]) + floats(got[first + 1]) + floats(after_z[1])).astype(BF16)
    out[0][...] = floats(keep[0]) + floats(got[first]) + floats(after_z[0])


def add_last(inn, out, give):
    out[0][...] = (inn(0)[...] + floats(inn(1)[...])).astype(BF16)


def add_out(inn, out, give, total):
    c = lax.axis_index("ctx")
    cut = out[0].shape[1]
    total[...] = (floats(inn(0)[0]) + floats(inn(1)[0]) + floats(inn(2)[...])).astype(BF16)
    for i, d in enumerate((0, 4, 2, 6)):
        out[0][i] = total[at(c ^ d, cut), :]
        out[1][i] = total[at(c ^ d ^ 1, cut), :]


def add_last_up(inn, out, give, total):
    w = lax.axis_index("wt")
    cut = out[0].shape[0]
    total[...] = (inn(0)[...] + floats(inn(1)[...])).astype(BF16)
    for d in range(WT):
        out[d][...] = total[at(w ^ d, cut), :]


def pack_up(inn, out, give):
    rows = inn(0).shape[0]
    for i in range(WT):
        out[0][pl.ds(rows * i, rows), :] = inn(i)[...]


def pack_small(inn, out, give):
    block, rows = out[0], inn(0).shape[0]
    block[pl.ds(0, rows), :] = inn(0)[...]
    block[pl.ds(rows, SMALL), :] = jnp.zeros((SMALL, block.shape[1]), BF16)
    block[pl.ds(rows, SMALL), pl.ds(0, PART)] = (inn(1)[0] + inn(2)[0] + inn(3)[...]).astype(BF16)


def spread_qkv(inn, out, give):
    c = lax.axis_index("ctx")
    (full,) = out
    span = full.shape[1] // (3 * CTX)
    for d in range(CTX):
        block = inn(d)
        for part in range(3):
            full[:, at(part * CTX + (c ^ d), span)] = floats(block[:, pl.ds(span * part, span)])


def spread_down(inn, out, give, sems, result):
    c = lax.axis_index("ctx")
    stores = []
    for d in range(CTX):
        block = inn(d)
        rows = at(c ^ d, block.shape[0])
        out[0][rows, :] = floats(block[...])
        stores.append(pltpu.make_async_copy(out[0].at[rows, :], result.at[rows, :], sems.at[d]))
        stores[-1].start()
    for store in stores:
        store.wait()


def spread_up(inn, out, give, sems, result):
    c, w = lax.axis_index("ctx"), lax.axis_index("wt")
    cut = PART // CTX
    width = out[0].shape[1] // WT
    stores = []
    for d in range(CTX):
        block, rows = inn(d), at(c ^ d, cut)
        for k in range(WT):
            out[0][rows, at(w ^ k, width)] = floats(block[pl.ds(cut * k, cut), :])
        stores.append(pltpu.make_async_copy(out[0].at[rows, :], result.at[rows, :], sems.at[d]))
        stores[-1].start()
    for store in stores:
        store.wait()


def spread_small(inn, out, give, total):
    proj, gain, shift, bias, up_bias = out
    c = lax.axis_index("ctx")
    cut = PART // CTX
    total[...] = jnp.zeros_like(total)
    for d in range(CTX):
        block = inn(d)
        proj[at(c ^ d, cut), :] = floats(block[pl.ds(0, cut), :])
        total[...] += floats(block[pl.ds(cut, SMALL), pl.ds(0, PART)])
    for i, ref in enumerate((gain, shift, bias, up_bias)):
        ref[...] = total[pl.ds(4 * i, 4), :]


def split_device(
    layer_input,
    out_grad,
    deal,
    w_qkv,
    w_out,
    w_up,
    w_down,
    norm_gain,
    norm_shift,
    bias_width,
    up_bias,
):
    _, rows, width = layer_input.shape
    w = lax.axis_index("wt")
    per = HEADS // CTX
    span = per * (width // HEADS)
    length = rows * CTX
    hidden_width = w_down.shape[0]
    everyone = WT * rows
    own, grad = layer_input[0], out_grad[0]
    vmem, dma = pltpu.VMEM, pltpu.SemaphoreType.DMA

    sequence = gather_ctx(own)
    begin = lax.optimization_barrier((w_qkv, w_up, norm_gain, norm_shift, bias_width, sequence[1]))[:5]
    pack, *ups = call(
        prepare,
        "prepare",
        begin,
        [shape(PART + SMALL, 3 * span)] + [shape(PART, hidden_width)] * 3,
        raw=(0, 1),
        hbm=(2, 3, 4),
        scratch=[dma((6,))],
    )
    packs = gather_wt(pack)
    up_core, up_x, up_both = ups
    outs_x = swap(after(w_out, packs[2]), "wt", 2)
    up_x = swap(after(up_x, packs[2]), "wt", 2)

    first, mixed, sent, stats, small = call(
        attend,
        "attend",
        (deal, *packs, *sequence),
        [
            shape(length, width),
            shape(length, 3 * span),
            shape(CTX, rows, span),
            shape(2 * per, length, dtype=F32),
            shape(SMALL, width, dtype=F32),
        ],
        smem=1,
        hbm=range(1, 1 + WT + CTX),
        hbm_out=(0, 1),
        scratch=[vmem((length, width), BF16), vmem((length, span), BF16)],
    )
    attended = lax.all_to_all(after(sent, outs_x, up_x), "ctx", 0, 0, tiled=True)
    up_both = swap(up_both, "wt", 3)
    outs_own, outs_x, up_core = lax.optimization_barrier((w_out, outs_x, up_core, sent))[:3]
    outs = w_out, swap(outs_own, "wt", 1), outs_x, swap(outs_x, "wt", 1)
    ups = w_up, swap(up_core, "wt", 1), up_x, up_both
    attended = after(attended, *outs, *ups[1:])

    branch, resid, second = call(
        project,
        "project",
        (small, attended, own, *outs),
        [shape(rows, width, dtype=F32), shape(rows, width, dtype=F32), shape(rows, width)],
        hbm=(2, 3),
    )

    own_columns = ((PART, hidden_width), lambda ref: ref.at[:, at(lax.axis_index("wt"), hidden_width)])
    halves = [shape(2 * rows, width, dtype=F32), shape(2 * rows, width)]
    seconds, hidden, slope, near, far = call(
        feed,
        "feed",
        (*gather_wt(second), *ups, up_bias.reshape(1, hidden_width), w_down),
        [shape(everyone, width), shape(everyone, hidden_width), shape(everyone, hidden_width, dtype=F32)]
        + halves,
        hbm=(4, 8, 9),
        hbm_out=(0,),
        views={4: own_columns},
    )

    def return_rows(near, far):
        got = swap(far, "wt", 1)
        back = call(add_rest, "add_rest", (near, got), [shape(rows, width)])
        return near, got, swap(back, "wt", 2)

    result, d_ffn, sums3 = call(
        top_norm,
        "top_norm",
        (*return_rows(near, far), small, resid, grad),
        [shape(rows, width), shape(rows, width), shape(3, width, dtype=F32)],
        hbm=(5,),
    )
    d_ffns, d_upper, near, far, up_sum = call(
        feed_back,
        "feed_back",
        (*gather_wt(d_ffn), w_down, slope, *ups),
        [shape(everyone, width), shape(everyone, hidden_width)] + halves + [shape(1, hidden_width, dtype=F32)],
        hbm=(4, 6),
        views={6: own_columns},
    )
    got = swap(far, "wt", 1)
    eighth = hidden_width // CTX
    keep_low_a, keep_high_a, send_a = call(
        grad_down,
        "grad_down",
        (hidden, d_ffns),
        [shape(2, eighth, width)] * 2 + [shape(4, eighth, width)],
        hbm_out=range(3),
    )
    got_a = swap(send_a, "ctx", 1)
    back = call(add_rest, "add_rest", (after(near, send_a), got), [shape(rows, width)])
    far = swap(back, "wt", 2)
    keep_low_b, keep_high_b, send_low_b, send_high_b = call(
        grad_up,
        "grad_up",
        (after(seconds, back), d_upper),
        [shape(2, eighth, width)] * 4,
        hbm=(0,),
        hbm_out=range(4),
        scratch=[vmem((PART, hidden_width), BF16)],
    )
    got_high_b = swap(send_high_b, "ctx", 1)
    got_low_b = swap(send_low_b, "ctx", 1)
    far = after(far, send_low_b)
    sent, d_att, d_resid, sums21 = call(
        middle_norms,
        "middle_norms",
        (near, got, far, small, resid, branch, grad, *outs),
        [
            shape(CTX, rows, span),
            shape(rows, width),
            shape(rows, width, dtype=F32),
            shape(5, width, dtype=F32),
        ],
        hbm=(6, 7),
        hbm_out=(2,),
    )
    weights_x = swap(after(w_qkv, far), "wt", 2)
    high_a = call(add_high, "add_high_a", (keep_high_a, got_a), [shape(2, eighth, width)], hbm=(0,))
    next_a = swap(high_a, "ctx", 2)
    got = lax.all_to_all(after(sent, high_a), "ctx", 0, 0, tiled=True)
    pieces = [shape(2, PART, width)] * 2
    keep_out, send_out = call(grad_out, "grad_out", (attended, d_att), pieces, hbm_out=(0, 1))
    got_out = swap(send_out, "wt", 1)
    back_out = call(add_second, "add_second_out", (keep_out, got_out), [shape(PART, width)], hbm=(0,))
    out_x = swap(back_out, "wt", 2)
    low_pair = [shape(eighth, width, dtype=F32), shape(eighth, width)]
    first_a, second_a = call(
        functools.partial(add_low, 2), "add_low_a", (keep_low_a, got_a, next_a), low_pair, hbm=(0,)
    )
    last_a = swap(second_a, "ctx", 4)
    high_b = call(add_high, "add_high_b", (keep_high_b, after(got_high_b, got)), [shape(2, eighth, width)], hbm=(0,))
    next_b = swap(high_b, "ctx", 2)

    natural, dealt = call(
        attend_back,
        "attend_back",
        (deal, mixed, stats, after(got, back_out, second_a, high_b)),
        [shape(length, 3 * span), shape(CTX, rows, 3 * span)],
        smem=1,
        hbm=(1,),
        scratch=[vmem((length, span), BF16), vmem((length, span), F32), vmem((length, span), F32)],
    )
    first_b, second_b = call(
        functools.partial(add_low, 0), "add_low_b", (keep_low_b, after(got_low_b, natural), next_b), low_pair, hbm=(0,)
    )
    last_b = swap(second_b, "ctx", 4)
    part_a = call(add_last, "add_last_a", (first_a, last_a), [shape(eighth, width)])
    down_slots = gather_ctx(part_a)
    pieces = [shape(2, PART, 3 * span)] * 2
    keep_qkv, send_qkv = call(grad_qkv, "grad_qkv", (first, after(natural, last_a, second_b)), pieces, hbm=(0,), hbm_out=(0, 1))
    cut = PART // CTX
    keep_c, send_c = call(
        add_out,
        "add_out",
        (keep_out, got_out, after(out_x, natural)),
        [shape(4, cut, width)] * 2,
        hbm=(0,),
        scratch=[vmem((PART, width), BF16)],
    )
    got_c = swap(send_c, "ctx", 1)
    got_rows = lax.all_to_all(after(dealt, down_slots[1], send_c, send_qkv), "ctx", 0, 0, tiled=True)
    got_qkv = swap(after(send_qkv, second_b), "wt", 1)
    back_qkv = call(add_second, "add_second_qkv", (keep_qkv, got_qkv), [shape(PART, 3 * span)], hbm=(0,))
    qkv_x = swap(back_qkv, "wt", 2)
    qkv_own, weights_x = lax.optimization_barrier((w_qkv, weights_x, second_b))[:2]
    all_qkv = w_qkv, swap(qkv_own, "wt", 1), weights_x, swap(weights_x, "wt", 1)
    input_grad, keep, send = call(
        bottom_norm,
        "bottom_norm",
        (after(got_rows, back_qkv), own, d_resid, small, *all_qkv, sums21, sums3, up_sum),
        [shape(rows, width, dtype=F32)] + [shape(2, SMALL, PART, dtype=F32)] * 2,
        hbm=(1, 2, 4, 5, 6, 7),
        hbm_out=(0,),
        scratch=[vmem((rows, 3 * width), BF16), vmem((rows, width), F32)],
    )
    got_sums = swap(send, "wt", 1)
    back_sums = call(add_second, "add_second_sums", (keep, got_sums), [shape(SMALL, PART, dtype=F32)])
    sums_x = swap(back_sums, "wt", 2)

    high_c = call(add_high_last, "add_high_c", (keep_c, got_c), [shape(2, cut, width)])
    next_c = swap(high_c, "ctx", 2)
    low_pair = [shape(cut, width, dtype=F32), shape(cut, width)]
    first_c, second_c = call(functools.partial(add_low, 0), "add_low_c", (keep_c, got_c, next_c), low_pair)
    last_c = swap(second_c, "ctx", 4)
    own_up, *up_parts = call(
        add_last_up,
        "add_last_up",
        (first_b, last_b),
        [shape(cut, width)] * WT,
        scratch=[vmem((eighth, width), BF16)],
    )
    up_parts = [swap(part, "wt", d) for part, d in zip(up_parts, (1, 2, 3))]
    out_part = call(add_last, "add_last_c", (first_c, last_c), [shape(cut, width)])
    qkv_part = call(
        add_first, "add_first_qkv", (keep_qkv, got_qkv, qkv_x), [shape(PART, 3 * span)], hbm=(0,)
    )
    qkv_slots = gather_ctx_z(after(qkv_part, down_slots[6]))
    up_block = call(
        pack_up, "pack_up", (after(own_up, down_slots[1], down_slots[2]), *up_parts), [shape(eighth, width)]
    )
    up_slots = gather_ctx(up_block)
    small_block = call(
        pack_small, "pack_small", (out_part, keep, got_sums, sums_x), [shape(cut + SMALL, width)]
    )
    small_slots = gather_ctx(small_block)
    full_qkv = call(spread_qkv, "spread_qkv", qkv_slots, [shape(PART, 3 * width, dtype=F32)], hbm_out=(0,))
    full_down = call(
        spread_down,
        "spread_down",
        down_slots,
        [shape(hidden_width, width, dtype=F32)],
        hbm_out=(0,),
        scratch=[dma((CTX,))],
        parts=(0,),
    )
    full_up = call(
        spread_up,
        "spread_up",
        up_slots,
        [shape(PART, WT * hidden_width, dtype=F32)],
        hbm_out=(0,),
        scratch=[dma((CTX,))],
        parts=(0,),
    )
    full_out, gain, shift, bias, up_total = call(
        spread_small,
        "spread_small",
        small_slots,
        [shape(PART, width, dtype=F32)] + [shape(4, PART, dtype=F32)] * 4,
        hbm_out=range(5),
        scratch=[vmem((SMALL, PART), F32)],
    )
    return (
        result[None],
        input_grad[None],
        full_qkv,
        full_out,
        full_up,
        full_down,
        gain,
        shift,
        bias,
        up_total.reshape(hidden_width),
    )


def solution(mesh):
    small = mesh.shape["ctx"] == CTX and mesh.shape["wt"] == WT
    per_device = split_device if small else general_device
    in_specs = (
        P("wt", "ctx", None),
        P("wt", "ctx", None),
        P(),
        P("wt", None),
        P("wt", None),
        P("wt", None),
        P("wt", None),
        P(None, "wt"),
        P(None, "wt"),
        P(None, "wt"),
        P("wt"),
    )
    out_specs = (
        P("wt", "ctx", None),
        P("wt", "ctx", None),
        P("wt", None),
        P("wt", None),
        P("wt", None),
        P("wt", None),
        P(None, "wt"),
        P(None, "wt"),
        P(None, "wt"),
        P("wt"),
    )
    return jax.shard_map(
        per_device, mesh=mesh, in_specs=in_specs, out_specs=out_specs, check_vma=False
    )
```

```python
import functools
import math

import jax
import jax.numpy as jnp
from jax import lax
from jax.experimental import pallas as pl
from jax.experimental.pallas import tpu as pltpu
from jax.sharding import PartitionSpec as P

HEADS = 16
BLK = 256
PIECE = 64


epsilon = 1e-05
relax = 32.0


def layer_norm(value, gain, shift):
    mean = jnp.mean(value, axis=-1, keepdims=True)
    centered = value - mean
    spread = jnp.mean(centered * centered, axis=-1, keepdims=True)
    return centered * lax.rsqrt(spread + epsilon) * gain + shift


def gelu_tanh(value):
    return jax.nn.gelu(value, approximate=True)


def rows_dot(left, weight):
    return jnp.einsum("std,de->ste", left, weight, preferred_element_type=jnp.float32)


def weight_grad(left, right):
    return jnp.einsum("std,ste->de", left, right, preferred_element_type=jnp.float32)


def back_dot(grad, weight):
    return jnp.einsum("ste,de->std", grad, weight, preferred_element_type=jnp.float32)


def row_total(value):
    return jnp.sum(value.astype(jnp.float32), axis=(0, 1))


def general_device(
    layer_input,
    out_grad,
    deal,
    w_qkv,
    w_out,
    w_up,
    w_down,
    norm_gain,
    norm_shift,
    bias_width,
    up_bias,
):
    seqs, rows, width = layer_input.shape
    heads = HEADS
    head = width // heads
    prescale = 1.0 / (relax * math.sqrt(head))
    ranks = lax.axis_size("ctx")
    length = rows * ranks
    per_block = BLK // PIECE
    rank = lax.axis_index("ctx")
    chosen = jnp.arange(ranks, dtype=jnp.int32) == rank
    mine = jnp.sum(jnp.where(chosen[:, None], deal, 0), axis=0)
    query_blocks = jnp.repeat(mine, rows // 2) // per_block
    key_blocks = jnp.repeat(deal.reshape(-1), rows // 2) // per_block
    full_qkv, full_out, full_up, full_down, gains, shifts, biases, up_shift = (
        lax.all_gather(w_qkv, "wt", axis=0, tiled=True),
        lax.all_gather(w_out, "wt", axis=0, tiled=True),
        lax.all_gather(w_up, "wt", axis=0, tiled=True),
        lax.all_gather(w_down, "wt", axis=0, tiled=True),
        lax.all_gather(norm_gain, "wt", axis=1, tiled=True),
        lax.all_gather(norm_shift, "wt", axis=1, tiled=True),
        lax.all_gather(bias_width, "wt", axis=1, tiled=True),
        lax.all_gather(up_bias, "wt", axis=0, tiled=True),
    )
    gains = gains.astype(jnp.float32)
    shifts = shifts.astype(jnp.float32)
    biases = biases.astype(jnp.float32)
    up_shift = up_shift.astype(jnp.float32)
    input_float = layer_input.astype(jnp.float32)
    first = layer_norm(input_float, gains[0], shifts[0]).astype(jnp.bfloat16)
    mixed = rows_dot(first, full_qkv)
    query = (mixed[..., :width] + biases[0]).astype(jnp.bfloat16)
    kv_local = jnp.concatenate(
        [mixed[..., width : 2 * width], mixed[..., 2 * width :] + biases[1]], axis=-1
    ).astype(jnp.bfloat16)
    kv_all = lax.all_gather(kv_local, "ctx", axis=1, tiled=True)
    step = math.gcd(length, 1024)
    count = length // step
    query4 = query.reshape(seqs, rows, heads, head)

    def score_block(left, right):
        return (
            jnp.einsum("sqhd,skhd->shqk", left, right, preferred_element_type=jnp.float32)
            * prescale
        )

    def key_block(index):
        start = index * step
        piece = lax.dynamic_slice_in_dim(kv_all, start, step, 1)
        keys4 = piece[..., :width].reshape(seqs, step, heads, head)
        values4 = piece[..., width:].reshape(seqs, step, heads, head)
        visible = (
            query_blocks[:, None] >= lax.dynamic_slice_in_dim(key_blocks, start, step, 0)[None, :]
        )
        return (keys4, values4, visible)

    def probs(raw, visible, totals):
        return jnp.where(visible, jnp.exp(raw * relax - totals[..., None]), 0.0)

    def online(index, carry):
        top, total, acc = carry
        keys4, values4, visible = key_block(index)
        raw = jnp.where(visible, score_block(query4, keys4), -1e30)
        new_top = jnp.maximum(top, jnp.max(raw, axis=-1))
        terms = jnp.where(visible, jnp.exp((raw - new_top[..., None]) * relax), 0.0)
        factor = jnp.exp((top - new_top) * relax)
        total = total * factor + jnp.sum(terms, axis=-1)
        acc = acc * jnp.transpose(factor, (0, 2, 1))[..., None]
        acc = acc + jnp.einsum(
            "shqk,skhd->sqhd",
            terms.astype(jnp.bfloat16),
            values4,
            preferred_element_type=jnp.float32,
        )
        return (new_top, total, acc)

    start_top = jnp.full((seqs, heads, rows), -1e30, jnp.float32)
    start_total = jnp.zeros((seqs, heads, rows), jnp.float32)
    start_acc = jnp.zeros((seqs, rows, heads, head), jnp.float32)
    top, total, acc = lax.fori_loop(0, count, online, (start_top, start_total, start_acc))
    log_total = top * relax + jnp.log(total)
    attended_float = acc / jnp.transpose(total, (0, 2, 1))[..., None]
    attended = attended_float.reshape(seqs, rows, width).astype(jnp.bfloat16)
    branch = rows_dot(attended, full_out) + biases[2]
    resid = input_float + layer_norm(branch, gains[1], shifts[1])
    second = layer_norm(resid, gains[2], shifts[2]).astype(jnp.bfloat16)
    upper = rows_dot(second, full_up) + up_shift
    hidden = gelu_tanh(upper).astype(jnp.bfloat16)
    ffn = rows_dot(hidden, full_down) + biases[3]
    top_norm, pull_four = jax.vjp(layer_norm, ffn, gains[3], shifts[3])
    result = resid + top_norm
    d_out = out_grad.astype(jnp.float32)
    d_ffn, d_gain3, d_shift3 = pull_four(d_out)
    d_ffn = d_ffn.astype(jnp.bfloat16)
    d_bias3 = row_total(d_ffn)
    g_down = weight_grad(hidden, d_ffn)
    d_hidden = back_dot(d_ffn, full_down)
    _, pull_gelu = jax.vjp(gelu_tanh, upper)
    d_upper = pull_gelu(d_hidden)[0].astype(jnp.bfloat16)
    d_up_shift = row_total(d_upper)
    g_up = weight_grad(second, d_upper)
    d_second = back_dot(d_upper, full_up)
    _, pull_three = jax.vjp(layer_norm, resid, gains[2], shifts[2])
    d_resid_part, d_gain2, d_shift2 = pull_three(d_second)
    d_resid = d_out + d_resid_part
    _, pull_two = jax.vjp(layer_norm, branch, gains[1], shifts[1])
    d_branch, d_gain1, d_shift1 = pull_two(d_resid)
    d_branch = d_branch.astype(jnp.bfloat16)
    d_bias2 = row_total(d_branch)
    g_out = weight_grad(attended, d_branch)
    d_attended = back_dot(d_branch, full_out).astype(jnp.bfloat16)
    d_out4 = d_attended.reshape(seqs, rows, heads, head)
    delta = jnp.einsum("sqhd,sqhd->shq", d_out4.astype(jnp.float32), attended_float)

    def score_grads(q_rows, do_rows, k_rows, v_rows, visible, lse_rows, delta_rows):
        weights = probs(score_block(q_rows, k_rows), visible, lse_rows)
        d_probs = jnp.einsum("sqhd,skhd->shqk", do_rows, v_rows, preferred_element_type=jnp.float32)
        d_scores = (relax * weights * (d_probs - delta_rows[..., None])).astype(jnp.bfloat16)
        return (d_scores, weights.astype(jnp.bfloat16))

    zero_query = jnp.zeros((seqs, rows, heads, head), jnp.float32)

    def local_grads(d_query, index):
        keys4, values4, visible = key_block(index)
        d_scores, weights = score_grads(query4, d_out4, keys4, values4, visible, log_total, delta)
        d_query = (
            d_query
            + jnp.einsum("shqk,skhd->sqhd", d_scores, keys4, preferred_element_type=jnp.float32)
            * prescale
        )
        d_keys = (
            jnp.einsum("shqk,sqhd->kshd", d_scores, query4, preferred_element_type=jnp.float32)
            * prescale
        )
        d_values = jnp.einsum(
            "shqk,sqhd->kshd", weights, d_out4, preferred_element_type=jnp.float32
        )
        joined = jnp.concatenate(
            [d_keys.reshape(step, seqs, width), d_values.reshape(step, seqs, width)], axis=-1
        )
        return (d_query, joined)

    d_query, pieces = lax.scan(local_grads, zero_query, jnp.arange(count, dtype=jnp.int32))
    terms = pieces.reshape(length, seqs, 2 * width)
    d_kv = jnp.transpose(lax.psum_scatter(terms, "ctx", scatter_dimension=0, tiled=True), (1, 0, 2))
    d_query = d_query.reshape(seqs, rows, width).astype(jnp.bfloat16)
    d_kv = d_kv.astype(jnp.bfloat16)
    d_bias0 = row_total(d_query)
    d_bias1 = row_total(d_kv[..., width:])
    d_mixed = jnp.concatenate([d_query, d_kv], axis=-1)
    g_qkv = weight_grad(first, d_mixed)
    d_first = back_dot(d_mixed, full_qkv)
    _, pull_one = jax.vjp(layer_norm, input_float, gains[0], shifts[0])
    d_input_part, d_gain0, d_shift0 = pull_one(d_first)
    input_grad = d_resid + d_input_part
    grad_gain = jnp.stack([d_gain0, d_gain1, d_gain2, d_gain3])
    grad_shift = jnp.stack([d_shift0, d_shift1, d_shift2, d_shift3])
    grad_bias = jnp.stack([d_bias0, d_bias1, d_bias2, d_bias3])
    owned = (
        lax.psum_scatter(g_qkv.astype(jnp.bfloat16), "wt", scatter_dimension=0, tiled=True).astype(
            jnp.float32
        ),
        lax.psum_scatter(g_out.astype(jnp.bfloat16), "wt", scatter_dimension=0, tiled=True).astype(
            jnp.float32
        ),
        lax.psum_scatter(g_up.astype(jnp.bfloat16), "wt", scatter_dimension=0, tiled=True).astype(
            jnp.float32
        ),
        lax.psum_scatter(g_down.astype(jnp.bfloat16), "wt", scatter_dimension=0, tiled=True).astype(
            jnp.float32
        ),
        lax.psum_scatter(
            grad_gain.astype(jnp.bfloat16), "wt", scatter_dimension=1, tiled=True
        ).astype(jnp.float32),
        lax.psum_scatter(
            grad_shift.astype(jnp.bfloat16), "wt", scatter_dimension=1, tiled=True
        ).astype(jnp.float32),
        lax.psum_scatter(
            grad_bias.astype(jnp.bfloat16), "wt", scatter_dimension=1, tiled=True
        ).astype(jnp.float32),
        lax.psum_scatter(
            d_up_shift.astype(jnp.bfloat16), "wt", scatter_dimension=0, tiled=True
        ).astype(jnp.float32),
    )
    summed = lax.psum(
        (owned[0], owned[1], owned[2], owned[3], owned[4], owned[5], owned[6], owned[7]), "ctx"
    )
    return (
        result.astype(jnp.bfloat16),
        input_grad,
        summed[0],
        summed[1],
        summed[2],
        summed[3],
        summed[4],
        summed[5],
        summed[6],
        summed[7],
    )


F32 = jnp.float32
BF16 = jnp.bfloat16
WT = 4
CTX = 8
PART = 256
SMALL = 16
GELU_A = math.sqrt(2.0 / math.pi)
GELU_B = 0.044715


def swap(value, axis, bit):
    size = lax.axis_size(axis)
    return lax.ppermute(value, axis, [(i, i ^ bit) for i in range(size)])


def gather_wt(block):
    far = swap(block, "wt", 2)
    return block, swap(block, "wt", 1), far, swap(far, "wt", 1)


def gather_ctx(block):
    far, near, side = (swap(block, "ctx", bit) for bit in (4, 2, 1))
    near = after(near, side)
    near_side = swap(near, "ctx", 1)
    far = after(far, near_side)
    corner = swap(far, "ctx", 2)
    far_side = swap(far, "ctx", 1)
    return [block, side, near, near_side, far, far_side, corner, swap(after(corner, far_side), "ctx", 1)]


def gather_ctx_z(block):
    blocks = {0: block}
    for bit in (1, 4, 2):
        blocks.update({d ^ bit: swap(value, "ctx", bit) for d, value in blocks.items()})
    return [blocks[d] for d in range(CTX)]


def after(value, *others):
    return lax.optimization_barrier((value, *others))[0]


def floats(value):
    return value.astype(F32)


def dot(left, right):
    return jnp.dot(left, right, preferred_element_type=F32)


def dot_t(left, right):
    return lax.dot_general(left, right, (((1,), (1,)), ((), ())), preferred_element_type=F32)


def t_dot(left, right):
    return lax.dot_general(left, right, (((0,), (0,)), ((), ())), preferred_element_type=F32)


def at(start, size):
    return pl.ds(pl.multiple_of(start * size, size), size)


def shape(*dims, dtype=jnp.bfloat16):
    return jax.ShapeDtypeStruct(dims, dtype)


def call(body, name, ins, outs, smem=0, raw=(), hbm=(), views=None, hbm_out=(), scratch=(), parts=(), slack=10):
    views = views or {}
    ends = [i for i in hbm_out if i not in parts]
    vmem, dma = pltpu.VMEM, pltpu.SemaphoreType.DMA

    def kernel(*refs):
        sources, results = refs[: len(ins)], list(refs[len(ins) : len(ins) + len(outs)])
        rest = list(refs[len(ins) + len(outs) :])
        buffers = {i: rest.pop(0) for i in hbm}
        targets = {i: rest.pop(0) for i in hbm_out}
        in_sems, out_sems = rest.pop(0), rest.pop(0)
        loads, stores = {}, {}
        for i in hbm:
            source = views[i][1](sources[i]) if i in views else sources[i]
            loads[i] = pltpu.make_async_copy(source, buffers[i], in_sems.at[i])
            loads[i].start()

        def inn(i):
            if i not in buffers:
                return sources[i]
            if i in loads:
                loads.pop(i).wait()
            return buffers[i]

        def give(i):
            if i in targets:
                stores[i] = pltpu.make_async_copy(targets[i], results[i], out_sems.at[i])
                stores[i].start()

        body(inn, [targets.get(i, ref) for i, ref in enumerate(results)], give, *rest, *[results[i] for i in parts])
        for i in ends:
            if i not in stores:
                give(i)
        for store in stores.values():
            store.wait()

    buffers = [(views[i][0] if i in views else ins[i].shape, ins[i].dtype) for i in hbm]
    buffers += [(outs[i].shape, outs[i].dtype) for i in hbm_out]
    held = buffers + [(s.shape, s.dtype) for s in scratch if s.dtype in (BF16, F32)]
    limit = slack + -(-sum(math.prod(dims) * jnp.dtype(kind).itemsize for dims, kind in held) >> 20)
    spaces = [pltpu.SMEM if i < smem else pltpu.HBM if i in hbm or i in raw else vmem for i in range(len(ins))]
    out_spaces = [pltpu.HBM if i in hbm_out else vmem for i in range(len(outs))]
    results = [space(o.shape, o.dtype) for space, o in zip(out_spaces, outs)]
    out_specs = [pl.BlockSpec(memory_space=space) for space in out_spaces]
    single = len(outs) == 1
    return pl.pallas_call(
        kernel,
        name=name,
        out_shape=results[0] if single else tuple(results),
        in_specs=[pl.BlockSpec(memory_space=space) for space in spaces],
        out_specs=out_specs[0] if single else tuple(out_specs),
        scratch_shapes=[vmem(*b) for b in buffers] + [dma((len(ins),)), dma((len(outs),))] + list(scratch),
        compiler_params=pltpu.CompilerParams(vmem_limit_bytes=limit << 20),
        cost_estimate=pl.CostEstimate(flops=0, bytes_accessed=1024, transcendentals=0),
    )(*ins[:smem], *[pltpu.with_memory_space_constraint(a, s) for a, s in list(zip(ins, spaces))[smem:]])


def unit(value):
    centered = value - jnp.mean(value, axis=-1, keepdims=True)
    spread = jnp.mean(centered * centered, axis=-1, keepdims=True)
    scale = lax.rsqrt(spread + epsilon)
    return centered * scale, scale


def unit_back(grad, normal, scale):
    mean = jnp.mean(grad, axis=-1, keepdims=True)
    along = jnp.mean(grad * normal, axis=-1, keepdims=True)
    return scale * (grad - mean - normal * along)


def column_sum(value):
    return jnp.sum(value, axis=0, keepdims=True)


def prepare(inn, out, give, sems):
    c, w = lax.axis_index("ctx"), lax.axis_index("wt")
    qkv, up, pack = inn(0), inn(1), out[0]
    rows, width = qkv.shape[0], qkv.shape[1] // 3
    span, size = pack.shape[1] // 3, out[1].shape[1]
    copies = []
    for part in range(3):
        source = qkv.at[:, at(part * (width // span) + c, span)]
        copies.append((source, pack.at[pl.ds(0, rows), pl.ds(part * span, span)]))
    copies += [(up.at[:, at(w ^ d, size)], out[d]) for d in (2, 3, 1)]
    copies = [pltpu.make_async_copy(a, b, sems.at[i]) for i, (a, b) in enumerate(copies)]
    for copy in copies:
        copy.start()
    low = pl.ds(rows, SMALL)
    pack[low, :] = jnp.zeros((SMALL, pack.shape[1]), BF16)
    for i in range(3):
        ref = inn(2 + i)
        pack[pl.ds(rows + 4 * i, 4), pl.ds(0, ref.shape[1])] = ref[...]
    for copy in copies:
        copy.wait()


def attend(inn, out, give, xs, norm):
    first, mixed, sent, stats, small = out
    c, w = lax.axis_index("ctx"), lax.axis_index("wt")
    deal = inn(0)
    length, width = xs.shape
    span = sent.shape[2]
    heads = stats.shape[0] // 2
    head = span // heads
    packs = [inn(1 + d) for d in range(WT)]
    for d in range(WT):
        small[:, at(w ^ d, PART)] = floats(packs[d][pl.ds(PART, SMALL), pl.ds(0, PART)])
    for d in range(CTX):
        block = inn(1 + WT + d)
        for t in range(2):
            xs[at(deal[c ^ d, t], PIECE), :] = block[pl.ds(PIECE * t, PIECE), :]
    bias_q = small[pl.ds(8, 1), at(c, span)]
    bias_v = small[pl.ds(9, 1), at(c, span)]

    @pl.loop(0, length // BLK)
    def _(i):
        rows = at(i, BLK)
        normal, _scale = unit(floats(xs[rows, :]))
        first[rows, :] = (normal * small[pl.ds(0, 1), :] + small[pl.ds(4, 1), :]).astype(BF16)
        total = dot(first[rows, at(w, PART)], packs[0][pl.ds(0, PART), :])
        for d in range(1, WT):
            total += dot(first[rows, at(w ^ d, PART)], packs[d][pl.ds(0, PART), :])
        mixed[rows, pl.ds(0, span)] = (total[:, :span] + bias_q).astype(BF16)
        mixed[rows, pl.ds(span, span)] = total[:, span : 2 * span].astype(BF16)
        mixed[rows, pl.ds(2 * span, span)] = (total[:, 2 * span :] + bias_v).astype(BF16)

    give(0)
    give(1)
    give(4)
    lane = lax.broadcasted_iota(jnp.int32, (BLK, span), 1) // head
    factor = 1.0 / math.sqrt(head)
    for b in range(length // BLK):
        rows, seen = pl.ds(b * BLK, BLK), pl.ds(0, (b + 1) * BLK)
        query = mixed[rows, pl.ds(0, span)]
        parts = []
        for h in range(heads):
            masked = jnp.where(lane == h, query, jnp.zeros_like(query))
            raw = dot_t(mixed[seen, pl.ds(span, span)], masked)
            top = jnp.max(raw, axis=0, keepdims=True)
            terms = jnp.exp((raw - top) * factor)
            inverse = 1.0 / jnp.sum(terms, axis=0, keepdims=True)
            stats[pl.ds(2 * h, 1), rows] = top
            stats[pl.ds(2 * h + 1, 1), rows] = inverse
            weights = (terms * inverse).astype(BF16)
            values = mixed[seen, pl.ds(2 * span, span)]
            parts.append(t_dot(values, weights)[h * head : (h + 1) * head, :])
        norm[rows, :] = jnp.concatenate(parts, axis=0).T.astype(BF16)
    for j in range(CTX):
        for t in range(2):
            sent[j, pl.ds(PIECE * t, PIECE), :] = norm[at(deal[j, t], PIECE), :]


def project(inn, out, give):
    branch, resid, second = out
    w = lax.axis_index("wt")
    small, attended, own = inn(0), inn(1), inn(2)
    span = attended.shape[2]
    total = small[pl.ds(10, 1), :]
    for d in range(WT):
        ref = inn(3 + d)
        for j in range(PART // span):
            total = total + dot(attended[(w ^ d) * (PART // span) + j], ref[pl.ds(span * j, span), :])
    branch[...] = total
    give(0)
    normal, _ = unit(total)
    total = floats(own[...]) + (normal * small[pl.ds(1, 1), :] + small[pl.ds(5, 1), :])
    resid[...] = total
    give(1)
    normal, _ = unit(total)
    second[...] = (normal * small[pl.ds(2, 1), :] + small[pl.ds(6, 1), :]).astype(BF16)


def join_slots(inn, start, target):
    for i, d in enumerate((0, 2, 1, 3)):
        ref = inn(start + d)
        rows = ref.shape[0]
        target[pl.ds(rows * i, rows), :] = ref[...]


def feed(inn, out, give):
    all_rows, hidden, slope, near, far = out
    w = lax.axis_index("wt")
    join_slots(inn, 0, all_rows)
    give(0)
    ups, bias = [inn(4 + d) for d in range(WT)], inn(8)
    half_rows = near.shape[0]

    @pl.loop(0, hidden.shape[1] // PART)
    def _(n):
        cols = at(n, PART)
        upper = floats(bias[pl.ds(0, 1), cols])
        for d in range(WT):
            upper = upper + dot(all_rows[:, at(w ^ d, PART)], ups[d][:, cols])
        square = upper * upper
        curve = jnp.tanh(GELU_A * (upper + GELU_B * (square * upper)))
        half = 0.5 * (1.0 + curve)
        hidden[:, cols] = (upper * half).astype(BF16)
        slope[:, cols] = half + (0.5 * GELU_A) * upper * (1.0 - curve * curve) * (
            1.0 + (3.0 * GELU_B) * square
        )

    give(1)
    give(2)
    down = inn(9)

    @pl.loop(0, near.shape[1] // PART)
    def _(n):
        cols = at(n, PART)
        total = dot(hidden[...], down[:, cols])
        near[:, cols] = total[:half_rows]
        far[:, cols] = total[half_rows:].astype(BF16)


def returned(inn, rows):
    own = pl.ds(0, rows)
    return inn(0)[own, :] + floats(inn(1)[own, :]) + floats(inn(2)[...])


def top_norm(inn, out, give):
    result, d_ffn, sums = out
    small, resid, grad = inn(3), inn(4), inn(5)
    normal, scale = unit(returned(inn, resid.shape[0]) + small[pl.ds(11, 1), :])
    gain = small[pl.ds(3, 1), :]
    d_out = floats(grad[...])
    low = unit_back(d_out * gain, normal, scale).astype(BF16)
    d_ffn[...] = low
    give(1)
    result[...] = (resid[...] + (normal * gain + small[pl.ds(7, 1), :])).astype(BF16)
    sums[pl.ds(0, 1), :] = column_sum(d_out * normal)
    sums[pl.ds(1, 1), :] = column_sum(d_out)
    sums[pl.ds(2, 1), :] = column_sum(floats(low))


def feed_back(inn, out, give):
    all_rows, d_upper, near, far, sums = out
    w = lax.axis_index("wt")
    join_slots(inn, 0, all_rows)
    give(0)
    down, slope = inn(4), inn(5)
    half_rows = near.shape[0]

    @pl.loop(0, d_upper.shape[1] // PART)
    def _(n):
        cols = at(n, PART)
        low = (dot_t(all_rows[...], down[cols, :]) * slope[:, cols]).astype(BF16)
        d_upper[:, cols] = low
        sums[pl.ds(0, 1), cols] = column_sum(floats(low))

    give(1)
    for d in range(WT):
        cols = at(w ^ d, PART)
        total = dot_t(d_upper[...], inn(6 + d)[...])
        near[:, cols] = total[:half_rows]
        far[:, cols] = total[half_rows:].astype(BF16)


PLACES = ((2, 0, 3), (2, 1, 7), (2, 2, 1), (2, 3, 5), (1, 0, 2), (1, 1, 6), (0, 0, 0), (0, 1, 4))


def grad_down(inn, out, give):
    c = lax.axis_index("ctx")
    hidden, grads = inn(0), inn(1)
    size = out[0].shape[1]
    for which, i, d in PLACES:
        out[which][i] = t_dot(hidden[:, at(c ^ d, size)], grads[...]).astype(BF16)
        if d == 5:
            give(2)


def grad_up(inn, out, give, part):
    c = lax.axis_index("ctx")
    cut = PART // CTX
    rows_in, grads = inn(0), inn(1)

    @pl.loop(0, WT)
    def _(k):
        part[...] = t_dot(rows_in[:, at(k, PART)], grads[...]).astype(BF16)
        for which, i, d in PLACES:
            out[which][i, at(k, cut), :] = part[at(c ^ d, cut), :]


def middle_norms(inn, out, give):
    sent, d_att, d_resid, sums = out
    w = lax.axis_index("wt")
    small, resid, branch, grad = inn(3), inn(4), inn(5), inn(6)
    rows, span = resid.shape[0], sent.shape[2]
    normal3, scale3 = unit(resid[...])
    normal2, scale2 = unit(branch[...])
    d_second = returned(inn, rows)
    total = floats(grad[...]) + unit_back(d_second * small[pl.ds(2, 1), :], normal3, scale3)
    low = unit_back(total * small[pl.ds(1, 1), :], normal2, scale2).astype(BF16)
    d_att[...] = low
    d_resid[...] = total
    give(2)
    for d in (1, 2, 3, 0):
        part = dot_t(low, inn(7 + d)[...]).astype(BF16)
        for j in range(PART // span):
            sent[(w ^ d) * (PART // span) + j] = part[:, span * j : span * (j + 1)]
    sums[pl.ds(0, 1), :] = column_sum(d_second * normal3)
    sums[pl.ds(1, 1), :] = column_sum(d_second)
    sums[pl.ds(2, 1), :] = column_sum(total * normal2)
    sums[pl.ds(3, 1), :] = column_sum(total)
    sums[pl.ds(4, 1), :] = column_sum(floats(low))


def grad_out(inn, out, give):
    w = lax.axis_index("wt")
    attended, grads = inn(0), inn(1)
    span = attended.shape[2]
    for d in (1, 3, 0, 2):
        for j in range(PART // span):
            part = t_dot(attended[(w ^ d) * (PART // span) + j], grads[...])
            out[d % 2][d // 2, pl.ds(span * j, span), :] = part.astype(BF16)
        if d == 3:
            give(1)


def attend_back(inn, out, give, d_out, d_keys, d_values):
    natural, dealt = out
    deal, mixed, stats, got = (inn(i) for i in range(4))
    length, span = d_out.shape
    heads = stats.shape[0] // 2
    head = span // heads
    factor = 1.0 / math.sqrt(head)
    prescale = factor / relax
    for j in range(CTX):
        for t in range(2):
            d_out[at(deal[j, t], PIECE), :] = got[j, pl.ds(PIECE * t, PIECE), :]
    lane = lax.broadcasted_iota(jnp.int32, (BLK, span), 1) // head
    d_keys[...] = jnp.zeros_like(d_keys)
    d_values[...] = jnp.zeros_like(d_values)
    for b in range(length // BLK):
        rows, seen = pl.ds(b * BLK, BLK), pl.ds(0, (b + 1) * BLK)
        query, grads = mixed[rows, pl.ds(0, span)], d_out[rows, :]
        parts = []
        for h in range(heads):
            query_h = jnp.where(lane == h, query, jnp.zeros_like(query))
            grads_h = jnp.where(lane == h, grads, jnp.zeros_like(grads))
            keys = mixed[seen, pl.ds(span, span)]
            raw = dot_t(keys, query_h)
            weights = jnp.exp((raw - stats[pl.ds(2 * h, 1), rows]) * factor) * stats[pl.ds(2 * h + 1, 1), rows]
            d_probs = dot_t(mixed[seen, pl.ds(2 * span, span)], grads_h)
            delta = jnp.sum(weights * d_probs, axis=0, keepdims=True)
            d_scores = (relax * weights * (d_probs - delta)).astype(BF16)
            d_values[seen, :] += dot(weights.astype(BF16), grads_h)
            d_keys[seen, :] += dot(d_scores, query_h)
            parts.append(t_dot(keys, d_scores)[h * head : (h + 1) * head, :])
        natural[rows, pl.ds(0, span)] = (jnp.concatenate(parts, axis=0).T * prescale).astype(BF16)
    natural[:, pl.ds(span, span)] = (d_keys[...] * prescale).astype(BF16)
    natural[:, pl.ds(2 * span, span)] = d_values[...].astype(BF16)
    for j in range(CTX):
        for t in range(2):
            dealt[j, pl.ds(PIECE * t, PIECE), :] = natural[at(deal[j, t], PIECE), :]


def grad_qkv(inn, out, give):
    w = lax.axis_index("wt")
    first, grads = inn(0), inn(1)
    for d in (1, 3, 0, 2):
        out[d % 2][d // 2] = t_dot(first[:, at(w ^ d, PART)], grads[...]).astype(BF16)
        if d == 3:
            give(1)


def bottom_norm(inn, out, give, joined, d_first):
    input_grad, keep, send = out
    w = lax.axis_index("wt")
    got, own, d_resid, small = (inn(i) for i in range(4))
    _, rows, triple = got.shape
    span, width = triple // 3, own.shape[1]
    for j in range(CTX):
        for part in range(3):
            joined[:, pl.ds(part * width + span * j, span)] = got[j, :, pl.ds(span * part, span)]
    for d in range(WT):
        d_first[:, at(w ^ d, PART)] = dot_t(joined[...], inn(4 + d)[...])
    normal, scale = unit(floats(own[...]))
    grads = d_first[...]
    input_grad[...] = d_resid[...] + unit_back(grads * small[pl.ds(0, 1), :], normal, scale)
    give(0)
    middle, top, up = inn(8), inn(9), inn(10)
    lines = {
        0: column_sum(grads * normal),
        4: column_sum(grads),
        8: column_sum(floats(joined[:, pl.ds(0, width)])),
        9: column_sum(floats(joined[:, pl.ds(2 * width, width)])),
    }
    for i, line in enumerate((2, 6, 1, 5, 10)):
        lines[line] = middle[pl.ds(i, 1), :]
    for i, line in enumerate((3, 7, 11)):
        lines[line] = top[pl.ds(i, 1), :]
    for line, value in lines.items():
        d_first[pl.ds(line, 1), :] = value
    for d in range(WT):
        target = send if d % 2 else keep
        target[d // 2, pl.ds(0, 12), :] = d_first[pl.ds(0, 12), at(w ^ d, PART)]
        target[d // 2, pl.ds(12, 4), :] = jnp.zeros((4, PART), F32)
    for i in range(4):
        keep[0, pl.ds(12 + i, 1), :] = up[:, pl.ds(PART * i, PART)]


def add_second(inn, out, give):
    out[0][...] = (floats(inn(0)[1]) + floats(inn(1)[1])).astype(out[0].dtype)


def add_first(inn, out, give):
    out[0][...] = (floats(inn(0)[0]) + floats(inn(1)[0]) + floats(inn(2)[...])).astype(out[0].dtype)


def add_rest(inn, out, give):
    rows = out[0].shape[0]
    rest = pl.ds(rows, rows)
    out[0][...] = (inn(0)[rest, :] + floats(inn(1)[rest, :])).astype(BF16)


def add_high(inn, out, give):
    keep, got = inn(0), inn(1)
    for i in range(2):
        out[0][i] = (floats(keep[i]) + floats(got[i])).astype(BF16)


def add_high_last(inn, out, give):
    keep, got = inn(0), inn(1)
    for i in range(2):
        out[0][i] = (floats(keep[2 + i]) + floats(got[2 + i])).astype(BF16)


def add_low(first, inn, out, give):
    keep, got, after_z = inn(0), inn(1), inn(2)
    out[1][...] = (floats(keep[1]) + floats(got[first + 1]) + floats(after_z[1])).astype(BF16)
    out[0][...] = floats(keep[0]) + floats(got[first]) + floats(after_z[0])


def add_last(inn, out, give):
    out[0][...] = (inn(0)[...] + floats(inn(1)[...])).astype(BF16)


def add_out(inn, out, give, total):
    c = lax.axis_index("ctx")
    cut = out[0].shape[1]
    total[...] = (floats(inn(0)[0]) + floats(inn(1)[0]) + floats(inn(2)[...])).astype(BF16)
    for i, d in enumerate((0, 4, 2, 6)):
        out[0][i] = total[at(c ^ d, cut), :]
        out[1][i] = total[at(c ^ d ^ 1, cut), :]


def add_last_up(inn, out, give, total):
    w = lax.axis_index("wt")
    cut = out[0].shape[0]
    total[...] = (inn(0)[...] + floats(inn(1)[...])).astype(BF16)
    for d in range(WT):
        out[d][...] = total[at(w ^ d, cut), :]


def pack_up(inn, out, give):
    rows = inn(0).shape[0]
    for i in range(WT):
        out[0][pl.ds(rows * i, rows), :] = inn(i)[...]


def pack_small(inn, out, give):
    block, rows = out[0], inn(0).shape[0]
    block[pl.ds(0, rows), :] = inn(0)[...]
    block[pl.ds(rows, SMALL), :] = jnp.zeros((SMALL, block.shape[1]), BF16)
    block[pl.ds(rows, SMALL), pl.ds(0, PART)] = (inn(1)[0] + inn(2)[0] + inn(3)[...]).astype(BF16)


def spread_qkv(inn, out, give):
    c = lax.axis_index("ctx")
    (full,) = out
    span = full.shape[1] // (3 * CTX)
    for d in range(CTX):
        block = inn(d)
        for part in range(3):
            full[:, at(part * CTX + (c ^ d), span)] = floats(block[:, pl.ds(span * part, span)])


def spread_down(inn, out, give, sems, result):
    c = lax.axis_index("ctx")
    stores = []
    for d in range(CTX):
        block = inn(d)
        rows = at(c ^ d, block.shape[0])
        out[0][rows, :] = floats(block[...])
        stores.append(pltpu.make_async_copy(out[0].at[rows, :], result.at[rows, :], sems.at[d]))
        stores[-1].start()
    for store in stores:
        store.wait()


def spread_up(inn, out, give, sems, result):
    c, w = lax.axis_index("ctx"), lax.axis_index("wt")
    cut = PART // CTX
    width = out[0].shape[1] // WT
    stores = []
    for d in range(CTX):
        block, rows = inn(d), at(c ^ d, cut)
        for k in range(WT):
            out[0][rows, at(w ^ k, width)] = floats(block[pl.ds(cut * k, cut), :])
        stores.append(pltpu.make_async_copy(out[0].at[rows, :], result.at[rows, :], sems.at[d]))
        stores[-1].start()
    for store in stores:
        store.wait()


def spread_small(inn, out, give, total):
    proj, gain, shift, bias, up_bias = out
    c = lax.axis_index("ctx")
    cut = PART // CTX
    total[...] = jnp.zeros_like(total)
    for d in range(CTX):
        block = inn(d)
        proj[at(c ^ d, cut), :] = floats(block[pl.ds(0, cut), :])
        total[...] += floats(block[pl.ds(cut, SMALL), pl.ds(0, PART)])
    for i, ref in enumerate((gain, shift, bias, up_bias)):
        ref[...] = total[pl.ds(4 * i, 4), :]


def split_device(
    layer_input,
    out_grad,
    deal,
    w_qkv,
    w_out,
    w_up,
    w_down,
    norm_gain,
    norm_shift,
    bias_width,
    up_bias,
):
    _, rows, width = layer_input.shape
    w = lax.axis_index("wt")
    per = HEADS // CTX
    span = per * (width // HEADS)
    length = rows * CTX
    hidden_width = w_down.shape[0]
    everyone = WT * rows
    own, grad = layer_input[0], out_grad[0]
    vmem, dma = pltpu.VMEM, pltpu.SemaphoreType.DMA

    sequence = gather_ctx(own)
    begin = lax.optimization_barrier((w_qkv, w_up, norm_gain, norm_shift, bias_width, sequence[1]))[:5]
    pack, *ups = call(
        prepare,
        "prepare",
        begin,
        [shape(PART + SMALL, 3 * span)] + [shape(PART, hidden_width)] * 3,
        raw=(0, 1),
        hbm=(2, 3, 4),
        scratch=[dma((6,))],
    )
    packs = gather_wt(pack)
    up_core, up_x, up_both = ups
    outs_x = swap(after(w_out, packs[2]), "wt", 2)
    up_x = swap(after(up_x, packs[2]), "wt", 2)

    first, mixed, sent, stats, small = call(
        attend,
        "attend",
        (deal, *packs, *sequence),
        [
            shape(length, width),
            shape(length, 3 * span),
            shape(CTX, rows, span),
            shape(2 * per, length, dtype=F32),
            shape(SMALL, width, dtype=F32),
        ],
        smem=1,
        hbm=range(1, 1 + WT + CTX),
        hbm_out=(0, 1),
        scratch=[vmem((length, width), BF16), vmem((length, span), BF16)],
    )
    attended = lax.all_to_all(after(sent, outs_x, up_x), "ctx", 0, 0, tiled=True)
    up_both = swap(up_both, "wt", 3)
    outs_own, outs_x, up_core = lax.optimization_barrier((w_out, outs_x, up_core, sent))[:3]
    outs = w_out, swap(outs_own, "wt", 1), outs_x, swap(outs_x, "wt", 1)
    ups = w_up, swap(up_core, "wt", 1), up_x, up_both
    attended = after(attended, *outs, *ups[1:])

    branch, resid, second = call(
        project,
        "project",
        (small, attended, own, *outs),
        [shape(rows, width, dtype=F32), shape(rows, width, dtype=F32), shape(rows, width)],
        hbm=(2, 3),
    )

    own_columns = ((PART, hidden_width), lambda ref: ref.at[:, at(lax.axis_index("wt"), hidden_width)])
    halves = [shape(2 * rows, width, dtype=F32), shape(2 * rows, width)]
    seconds, hidden, slope, near, far = call(
        feed,
        "feed",
        (*gather_wt(second), *ups, up_bias.reshape(1, hidden_width), w_down),
        [shape(everyone, width), shape(everyone, hidden_width), shape(everyone, hidden_width, dtype=F32)]
        + halves,
        hbm=(4, 8, 9),
        hbm_out=(0,),
        views={4: own_columns},
    )

    def return_rows(near, far):
        got = swap(far, "wt", 1)
        back = call(add_rest, "add_rest", (near, got), [shape(rows, width)])
        return near, got, swap(back, "wt", 2)

    result, d_ffn, sums3 = call(
        top_norm,
        "top_norm",
        (*return_rows(near, far), small, resid, grad),
        [shape(rows, width), shape(rows, width), shape(3, width, dtype=F32)],
        hbm=(5,),
    )
    d_ffns, d_upper, near, far, up_sum = call(
        feed_back,
        "feed_back",
        (*gather_wt(d_ffn), w_down, slope, *ups),
        [shape(everyone, width), shape(everyone, hidden_width)] + halves + [shape(1, hidden_width, dtype=F32)],
        hbm=(4, 6),
        views={6: own_columns},
    )
    got = swap(far, "wt", 1)
    eighth = hidden_width // CTX
    chunks = [shape(2, eighth, width)] * 2 + [shape(4, eighth, width)]
    keep_low_a, keep_high_a, send_a = call(grad_down, "grad_down", (hidden, d_ffns), chunks, hbm_out=range(3))
    got_a = swap(send_a, "ctx", 1)
    back = call(add_rest, "add_rest", (after(near, send_a), got), [shape(rows, width)])
    far = swap(back, "wt", 2)
    keep_low_b, keep_high_b, send_b = call(
        grad_up,
        "grad_up",
        (after(seconds, back), d_upper),
        chunks,
        hbm=(0,),
        hbm_out=range(3),
        scratch=[vmem((PART, hidden_width), BF16)],
    )
    got_b = swap(send_b, "ctx", 1)
    sent, d_att, d_resid, sums21 = call(
        middle_norms,
        "middle_norms",
        (near, got, after(far, send_b), small, resid, branch, grad, *outs),
        [
            shape(CTX, rows, span),
            shape(rows, width),
            shape(rows, width, dtype=F32),
            shape(5, width, dtype=F32),
        ],
        hbm=(6, 7),
        hbm_out=(2,),
    )
    got = lax.all_to_all(sent, "ctx", 0, 0, tiled=True)
    pieces = [shape(2, PART, width)] * 2
    keep_out, send_out = call(grad_out, "grad_out", (attended, d_att), pieces, hbm_out=(0, 1))
    got_out = swap(send_out, "wt", 1)
    back_out = call(add_second, "add_second_out", (keep_out, got_out), [shape(PART, width)], hbm=(0,))
    out_x = swap(back_out, "wt", 2)
    two = [shape(2, eighth, width)]
    high_a = call(add_high, "add_high_a", (keep_high_a, got_a), two, hbm=(0,))
    next_a = swap(high_a, "ctx", 2)

    natural, dealt = call(
        attend_back,
        "attend_back",
        (deal, mixed, stats, after(got, back_out, high_a)),
        [shape(length, 3 * span), shape(CTX, rows, 3 * span)],
        smem=1,
        hbm=(1,),
        scratch=[vmem((length, span), BF16), vmem((length, span), F32), vmem((length, span), F32)],
    )
    low_pair = [shape(eighth, width, dtype=F32), shape(eighth, width)]
    low_half = functools.partial(add_low, 2)
    first_a, second_a = call(
        low_half, "add_low_a", (keep_low_a, got_a, after(next_a, natural)), low_pair, hbm=(0,)
    )
    last_a = swap(second_a, "ctx", 4)
    pieces = [shape(2, PART, 3 * span)] * 2
    keep_qkv, send_qkv = call(
        grad_qkv, "grad_qkv", (first, after(natural, second_a)), pieces, hbm=(0,), hbm_out=(0, 1)
    )
    high_b = call(add_high, "add_high_b", (keep_high_b, after(got_b, send_qkv)), two, hbm=(0,))
    next_b = swap(high_b, "ctx", 2)
    got_rows = lax.all_to_all(after(dealt, high_b), "ctx", 0, 0, tiled=True)
    part_a = call(add_last, "add_last_a", (first_a, after(last_a, high_b, dealt)), [shape(eighth, width)])
    down_slots = gather_ctx(part_a)
    first_b, second_b = call(
        low_half, "add_low_b", (keep_low_b, got_b, after(next_b, down_slots[1], down_slots[2])), low_pair, hbm=(0,)
    )
    last_b = swap(second_b, "ctx", 4)
    cut = PART // CTX
    keep_c, send_c = call(
        add_out,
        "add_out",
        (keep_out, got_out, after(out_x, part_a)),
        [shape(4, cut, width)] * 2,
        hbm=(0,),
        scratch=[vmem((PART, width), BF16)],
    )
    got_c = swap(send_c, "ctx", 1)
    got_qkv = swap(after(send_qkv, second_b), "wt", 1)
    back_qkv = call(add_second, "add_second_qkv", (keep_qkv, got_qkv), [shape(PART, 3 * span)], hbm=(0,))
    qkv_x = swap(back_qkv, "wt", 2)
    high_c = call(add_high_last, "add_high_c", (keep_c, got_c), [shape(2, cut, width)])
    next_c = swap(high_c, "ctx", 2)
    low_pair = [shape(cut, width, dtype=F32), shape(cut, width)]
    first_c, second_c = call(functools.partial(add_low, 0), "add_low_c", (keep_c, got_c, next_c), low_pair)
    last_c = swap(second_c, "ctx", 4)
    own_up, *up_parts = call(
        add_last_up,
        "add_last_up",
        (first_b, after(last_b, got_rows, down_slots[4])),
        [shape(cut, width)] * WT,
        scratch=[vmem((eighth, width), BF16)],
    )
    up_parts = [swap(part, "wt", d) for part, d in zip(up_parts, (1, 2, 3))]
    out_part = call(add_last, "add_last_c", (first_c, last_c), [shape(cut, width)])
    qkv_part = call(
        add_first, "add_first_qkv", (keep_qkv, got_qkv, qkv_x), [shape(PART, 3 * span)], hbm=(0,)
    )
    qkv_slots = gather_ctx_z(qkv_part)
    up_block = call(
        pack_up, "pack_up", (own_up, *up_parts), [shape(eighth, width)]
    )
    up_slots = gather_ctx(up_block)
    weights_x = swap(after(w_qkv, send_c), "wt", 2)
    qkv_own, weights_x = lax.optimization_barrier((w_qkv, weights_x, own_up))[:2]
    all_qkv = w_qkv, swap(qkv_own, "wt", 1), weights_x, swap(weights_x, "wt", 1)
    input_grad, keep, send = call(
        bottom_norm,
        "bottom_norm",
        (after(got_rows, back_qkv, own_up), own, d_resid, small, *all_qkv, sums21, sums3, up_sum),
        [shape(rows, width, dtype=F32)] + [shape(2, SMALL, PART, dtype=F32)] * 2,
        hbm=(1, 2, 4, 5, 6, 7),
        hbm_out=(0,),
        scratch=[vmem((rows, 3 * width), BF16), vmem((rows, width), F32)],
    )
    got_sums = swap(send, "wt", 1)
    back_sums = call(add_second, "add_second_sums", (keep, got_sums), [shape(SMALL, PART, dtype=F32)])
    sums_x = swap(back_sums, "wt", 2)

    small_block = call(
        pack_small, "pack_small", (out_part, keep, got_sums, sums_x), [shape(cut + SMALL, width)]
    )
    small_slots = gather_ctx(small_block)
    full_qkv = call(spread_qkv, "spread_qkv", qkv_slots, [shape(PART, 3 * width, dtype=F32)], hbm_out=(0,))
    full_down = call(
        spread_down,
        "spread_down",
        down_slots,
        [shape(hidden_width, width, dtype=F32)],
        hbm_out=(0,),
        scratch=[dma((CTX,))],
        parts=(0,),
    )
    full_up = call(
        spread_up,
        "spread_up",
        up_slots,
        [shape(PART, WT * hidden_width, dtype=F32)],
        hbm_out=(0,),
        scratch=[dma((CTX,))],
        parts=(0,),
    )
    full_out, gain, shift, bias, up_total = call(
        spread_small,
        "spread_small",
        small_slots,
        [shape(PART, width, dtype=F32)] + [shape(4, PART, dtype=F32)] * 4,
        hbm_out=range(5),
        scratch=[vmem((SMALL, PART), F32)],
    )
    up_total = up_total.reshape(hidden_width)
    return (
        result[None],
        input_grad[None],
        full_qkv,
        full_out,
        full_up,
        full_down,
        gain,
        shift,
        bias,
        up_total,
    )


def solution(mesh):
    small = mesh.shape["ctx"] == CTX and mesh.shape["wt"] == WT
    per_device = split_device if small else general_device
    in_specs = (
        P("wt", "ctx", None),
        P("wt", "ctx", None),
        P(),
        P("wt", None),
        P("wt", None),
        P("wt", None),
        P("wt", None),
        P(None, "wt"),
        P(None, "wt"),
        P(None, "wt"),
        P("wt"),
    )
    out_specs = (
        P("wt", "ctx", None),
        P("wt", "ctx", None),
        P("wt", None),
        P("wt", None),
        P("wt", None),
        P("wt", None),
        P(None, "wt"),
        P(None, "wt"),
        P(None, "wt"),
        P("wt"),
    )
    return jax.shard_map(
        per_device, mesh=mesh, in_specs=in_specs, out_specs=out_specs, check_vma=False
    )
```

```python
import functools
import math

import jax
import jax.numpy as jnp
from jax import lax
from jax.experimental import pallas as pl
from jax.experimental.pallas import tpu as pltpu
from jax.sharding import PartitionSpec as P

HEADS = 16
BLK = 256
PIECE = 64


epsilon = 1e-05
relax = 32.0


def layer_norm(value, gain, shift):
    mean = jnp.mean(value, axis=-1, keepdims=True)
    centered = value - mean
    spread = jnp.mean(centered * centered, axis=-1, keepdims=True)
    return centered * lax.rsqrt(spread + epsilon) * gain + shift


def gelu_tanh(value):
    return jax.nn.gelu(value, approximate=True)


def rows_dot(left, weight):
    return jnp.einsum("std,de->ste", left, weight, preferred_element_type=jnp.float32)


def weight_grad(left, right):
    return jnp.einsum("std,ste->de", left, right, preferred_element_type=jnp.float32)


def back_dot(grad, weight):
    return jnp.einsum("ste,de->std", grad, weight, preferred_element_type=jnp.float32)


def row_total(value):
    return jnp.sum(value.astype(jnp.float32), axis=(0, 1))


def general_device(
    layer_input,
    out_grad,
    deal,
    w_qkv,
    w_out,
    w_up,
    w_down,
    norm_gain,
    norm_shift,
    bias_width,
    up_bias,
):
    seqs, rows, width = layer_input.shape
    heads = HEADS
    head = width // heads
    prescale = 1.0 / (relax * math.sqrt(head))
    ranks = lax.axis_size("ctx")
    length = rows * ranks
    per_block = BLK // PIECE
    rank = lax.axis_index("ctx")
    chosen = jnp.arange(ranks, dtype=jnp.int32) == rank
    mine = jnp.sum(jnp.where(chosen[:, None], deal, 0), axis=0)
    query_blocks = jnp.repeat(mine, rows // 2) // per_block
    key_blocks = jnp.repeat(deal.reshape(-1), rows // 2) // per_block
    full_qkv, full_out, full_up, full_down, gains, shifts, biases, up_shift = (
        lax.all_gather(w_qkv, "wt", axis=0, tiled=True),
        lax.all_gather(w_out, "wt", axis=0, tiled=True),
        lax.all_gather(w_up, "wt", axis=0, tiled=True),
        lax.all_gather(w_down, "wt", axis=0, tiled=True),
        lax.all_gather(norm_gain, "wt", axis=1, tiled=True),
        lax.all_gather(norm_shift, "wt", axis=1, tiled=True),
        lax.all_gather(bias_width, "wt", axis=1, tiled=True),
        lax.all_gather(up_bias, "wt", axis=0, tiled=True),
    )
    gains = gains.astype(jnp.float32)
    shifts = shifts.astype(jnp.float32)
    biases = biases.astype(jnp.float32)
    up_shift = up_shift.astype(jnp.float32)
    input_float = layer_input.astype(jnp.float32)
    first = layer_norm(input_float, gains[0], shifts[0]).astype(jnp.bfloat16)
    mixed = rows_dot(first, full_qkv)
    query = (mixed[..., :width] + biases[0]).astype(jnp.bfloat16)
    kv_local = jnp.concatenate(
        [mixed[..., width : 2 * width], mixed[..., 2 * width :] + biases[1]], axis=-1
    ).astype(jnp.bfloat16)
    kv_all = lax.all_gather(kv_local, "ctx", axis=1, tiled=True)
    step = math.gcd(length, 1024)
    count = length // step
    query4 = query.reshape(seqs, rows, heads, head)

    def score_block(left, right):
        return (
            jnp.einsum("sqhd,skhd->shqk", left, right, preferred_element_type=jnp.float32)
            * prescale
        )

    def key_block(index):
        start = index * step
        piece = lax.dynamic_slice_in_dim(kv_all, start, step, 1)
        keys4 = piece[..., :width].reshape(seqs, step, heads, head)
        values4 = piece[..., width:].reshape(seqs, step, heads, head)
        visible = (
            query_blocks[:, None] >= lax.dynamic_slice_in_dim(key_blocks, start, step, 0)[None, :]
        )
        return (keys4, values4, visible)

    def probs(raw, visible, totals):
        return jnp.where(visible, jnp.exp(raw * relax - totals[..., None]), 0.0)

    def online(index, carry):
        top, total, acc = carry
        keys4, values4, visible = key_block(index)
        raw = jnp.where(visible, score_block(query4, keys4), -1e30)
        new_top = jnp.maximum(top, jnp.max(raw, axis=-1))
        terms = jnp.where(visible, jnp.exp((raw - new_top[..., None]) * relax), 0.0)
        factor = jnp.exp((top - new_top) * relax)
        total = total * factor + jnp.sum(terms, axis=-1)
        acc = acc * jnp.transpose(factor, (0, 2, 1))[..., None]
        acc = acc + jnp.einsum(
            "shqk,skhd->sqhd",
            terms.astype(jnp.bfloat16),
            values4,
            preferred_element_type=jnp.float32,
        )
        return (new_top, total, acc)

    start_top = jnp.full((seqs, heads, rows), -1e30, jnp.float32)
    start_total = jnp.zeros((seqs, heads, rows), jnp.float32)
    start_acc = jnp.zeros((seqs, rows, heads, head), jnp.float32)
    top, total, acc = lax.fori_loop(0, count, online, (start_top, start_total, start_acc))
    log_total = top * relax + jnp.log(total)
    attended_float = acc / jnp.transpose(total, (0, 2, 1))[..., None]
    attended = attended_float.reshape(seqs, rows, width).astype(jnp.bfloat16)
    branch = rows_dot(attended, full_out) + biases[2]
    resid = input_float + layer_norm(branch, gains[1], shifts[1])
    second = layer_norm(resid, gains[2], shifts[2]).astype(jnp.bfloat16)
    upper = rows_dot(second, full_up) + up_shift
    hidden = gelu_tanh(upper).astype(jnp.bfloat16)
    ffn = rows_dot(hidden, full_down) + biases[3]
    top_norm, pull_four = jax.vjp(layer_norm, ffn, gains[3], shifts[3])
    result = resid + top_norm
    d_out = out_grad.astype(jnp.float32)
    d_ffn, d_gain3, d_shift3 = pull_four(d_out)
    d_ffn = d_ffn.astype(jnp.bfloat16)
    d_bias3 = row_total(d_ffn)
    g_down = weight_grad(hidden, d_ffn)
    d_hidden = back_dot(d_ffn, full_down)
    _, pull_gelu = jax.vjp(gelu_tanh, upper)
    d_upper = pull_gelu(d_hidden)[0].astype(jnp.bfloat16)
    d_up_shift = row_total(d_upper)
    g_up = weight_grad(second, d_upper)
    d_second = back_dot(d_upper, full_up)
    _, pull_three = jax.vjp(layer_norm, resid, gains[2], shifts[2])
    d_resid_part, d_gain2, d_shift2 = pull_three(d_second)
    d_resid = d_out + d_resid_part
    _, pull_two = jax.vjp(layer_norm, branch, gains[1], shifts[1])
    d_branch, d_gain1, d_shift1 = pull_two(d_resid)
    d_branch = d_branch.astype(jnp.bfloat16)
    d_bias2 = row_total(d_branch)
    g_out = weight_grad(attended, d_branch)
    d_attended = back_dot(d_branch, full_out).astype(jnp.bfloat16)
    d_out4 = d_attended.reshape(seqs, rows, heads, head)
    delta = jnp.einsum("sqhd,sqhd->shq", d_out4.astype(jnp.float32), attended_float)

    def score_grads(q_rows, do_rows, k_rows, v_rows, visible, lse_rows, delta_rows):
        weights = probs(score_block(q_rows, k_rows), visible, lse_rows)
        d_probs = jnp.einsum("sqhd,skhd->shqk", do_rows, v_rows, preferred_element_type=jnp.float32)
        d_scores = (relax * weights * (d_probs - delta_rows[..., None])).astype(jnp.bfloat16)
        return (d_scores, weights.astype(jnp.bfloat16))

    zero_query = jnp.zeros((seqs, rows, heads, head), jnp.float32)

    def local_grads(d_query, index):
        keys4, values4, visible = key_block(index)
        d_scores, weights = score_grads(query4, d_out4, keys4, values4, visible, log_total, delta)
        d_query = (
            d_query
            + jnp.einsum("shqk,skhd->sqhd", d_scores, keys4, preferred_element_type=jnp.float32)
            * prescale
        )
        d_keys = (
            jnp.einsum("shqk,sqhd->kshd", d_scores, query4, preferred_element_type=jnp.float32)
            * prescale
        )
        d_values = jnp.einsum(
            "shqk,sqhd->kshd", weights, d_out4, preferred_element_type=jnp.float32
        )
        joined = jnp.concatenate(
            [d_keys.reshape(step, seqs, width), d_values.reshape(step, seqs, width)], axis=-1
        )
        return (d_query, joined)

    d_query, pieces = lax.scan(local_grads, zero_query, jnp.arange(count, dtype=jnp.int32))
    terms = pieces.reshape(length, seqs, 2 * width)
    d_kv = jnp.transpose(lax.psum_scatter(terms, "ctx", scatter_dimension=0, tiled=True), (1, 0, 2))
    d_query = d_query.reshape(seqs, rows, width).astype(jnp.bfloat16)
    d_kv = d_kv.astype(jnp.bfloat16)
    d_bias0 = row_total(d_query)
    d_bias1 = row_total(d_kv[..., width:])
    d_mixed = jnp.concatenate([d_query, d_kv], axis=-1)
    g_qkv = weight_grad(first, d_mixed)
    d_first = back_dot(d_mixed, full_qkv)
    _, pull_one = jax.vjp(layer_norm, input_float, gains[0], shifts[0])
    d_input_part, d_gain0, d_shift0 = pull_one(d_first)
    input_grad = d_resid + d_input_part
    grad_gain = jnp.stack([d_gain0, d_gain1, d_gain2, d_gain3])
    grad_shift = jnp.stack([d_shift0, d_shift1, d_shift2, d_shift3])
    grad_bias = jnp.stack([d_bias0, d_bias1, d_bias2, d_bias3])
    owned = (
        lax.psum_scatter(g_qkv.astype(jnp.bfloat16), "wt", scatter_dimension=0, tiled=True).astype(
            jnp.float32
        ),
        lax.psum_scatter(g_out.astype(jnp.bfloat16), "wt", scatter_dimension=0, tiled=True).astype(
            jnp.float32
        ),
        lax.psum_scatter(g_up.astype(jnp.bfloat16), "wt", scatter_dimension=0, tiled=True).astype(
            jnp.float32
        ),
        lax.psum_scatter(g_down.astype(jnp.bfloat16), "wt", scatter_dimension=0, tiled=True).astype(
            jnp.float32
        ),
        lax.psum_scatter(
            grad_gain.astype(jnp.bfloat16), "wt", scatter_dimension=1, tiled=True
        ).astype(jnp.float32),
        lax.psum_scatter(
            grad_shift.astype(jnp.bfloat16), "wt", scatter_dimension=1, tiled=True
        ).astype(jnp.float32),
        lax.psum_scatter(
            grad_bias.astype(jnp.bfloat16), "wt", scatter_dimension=1, tiled=True
        ).astype(jnp.float32),
        lax.psum_scatter(
            d_up_shift.astype(jnp.bfloat16), "wt", scatter_dimension=0, tiled=True
        ).astype(jnp.float32),
    )
    summed = lax.psum(
        (owned[0], owned[1], owned[2], owned[3], owned[4], owned[5], owned[6], owned[7]), "ctx"
    )
    return (
        result.astype(jnp.bfloat16),
        input_grad,
        summed[0],
        summed[1],
        summed[2],
        summed[3],
        summed[4],
        summed[5],
        summed[6],
        summed[7],
    )


F32 = jnp.float32
BF16 = jnp.bfloat16
WT = 4
CTX = 8
PART = 256
SMALL = 16
GELU_A = math.sqrt(2.0 / math.pi)
GELU_B = 0.044715
SPLIT = (0, 1)


def swap(value, axis, bit):
    size = lax.axis_size(axis)
    return lax.ppermute(value, axis, [(i, i ^ bit) for i in range(size)])


def gather_wt(block):
    far = swap(block, "wt", 2)
    return block, swap(block, "wt", 1), far, swap(far, "wt", 1)


def gather_ctx(block):
    far, near, side = (swap(block, "ctx", bit) for bit in (4, 2, 1))
    near = after(near, side)
    near_side = swap(near, "ctx", 1)
    far = after(far, near_side)
    corner = swap(far, "ctx", 2)
    far_side = swap(far, "ctx", 1)
    return [block, side, near, near_side, far, far_side, corner, swap(after(corner, far_side), "ctx", 1)]


def gather_free(block, others=()):
    far, side = swap(block, "ctx", 4), swap(block, "ctx", 1)
    near = swap(after(block, *others) if others else block, "ctx", 2)
    near_side, corner, far_side = swap(near, "ctx", 1), swap(far, "ctx", 2), swap(far, "ctx", 1)
    return [block, side, near, near_side, far, far_side, corner, swap(corner, "ctx", 1)]


def gather_ctx_z(block):
    blocks = {0: block}
    for bit in (1, 4, 2):
        blocks.update({d ^ bit: swap(value, "ctx", bit) for d, value in blocks.items()})
    return [blocks[d] for d in range(CTX)]


def after(value, *others):
    return lax.optimization_barrier((value, *others))[0]


def floats(value):
    return value.astype(F32)


def dot(left, right):
    return jnp.dot(left, right, preferred_element_type=F32)


def dot_t(left, right):
    return lax.dot_general(left, right, (((1,), (1,)), ((), ())), preferred_element_type=F32)


def t_dot(left, right):
    return lax.dot_general(left, right, (((0,), (0,)), ((), ())), preferred_element_type=F32)


def at(start, size):
    return pl.ds(pl.multiple_of(start * size, size), size)


def shape(*dims, dtype=jnp.bfloat16):
    return jax.ShapeDtypeStruct(dims, dtype)


def call(body, name, ins, outs, smem=0, raw=(), hbm=(), views=None, hbm_out=(), scratch=(), parts=(), slack=10):
    views = views or {}
    ends = [i for i in hbm_out if i not in parts]
    vmem, dma = pltpu.VMEM, pltpu.SemaphoreType.DMA

    def kernel(*refs):
        sources, results = refs[: len(ins)], list(refs[len(ins) : len(ins) + len(outs)])
        rest = list(refs[len(ins) + len(outs) :])
        buffers = {i: rest.pop(0) for i in hbm}
        targets = {i: rest.pop(0) for i in hbm_out}
        in_sems, out_sems = rest.pop(0), rest.pop(0)
        loads, stores = {}, {}
        for i in hbm:
            source = views[i][1](sources[i]) if i in views else sources[i]
            loads[i] = pltpu.make_async_copy(source, buffers[i], in_sems.at[i])
            loads[i].start()

        def inn(i):
            if i not in buffers:
                return sources[i]
            if i in loads:
                loads.pop(i).wait()
            return buffers[i]

        def give(i):
            if i in targets:
                stores[i] = pltpu.make_async_copy(targets[i], results[i], out_sems.at[i])
                stores[i].start()

        body(inn, [targets.get(i, ref) for i, ref in enumerate(results)], give, *rest, *[results[i] for i in parts])
        for i in ends:
            if i not in stores:
                give(i)
        for store in stores.values():
            store.wait()

    buffers = [(views[i][0] if i in views else ins[i].shape, ins[i].dtype) for i in hbm]
    buffers += [(outs[i].shape, outs[i].dtype) for i in hbm_out]
    held = buffers + [(s.shape, s.dtype) for s in scratch if s.dtype in (BF16, F32)]
    limit = slack + -(-sum(math.prod(dims) * jnp.dtype(kind).itemsize for dims, kind in held) >> 20)
    spaces = [pltpu.SMEM if i < smem else pltpu.HBM if i in hbm or i in raw else vmem for i in range(len(ins))]
    out_spaces = [pltpu.HBM if i in hbm_out else vmem for i in range(len(outs))]
    results = [space(o.shape, o.dtype) for space, o in zip(out_spaces, outs)]
    out_specs = [pl.BlockSpec(memory_space=space) for space in out_spaces]
    single = len(outs) == 1
    return pl.pallas_call(
        kernel,
        name=name,
        out_shape=results[0] if single else tuple(results),
        in_specs=[pl.BlockSpec(memory_space=space) for space in spaces],
        out_specs=out_specs[0] if single else tuple(out_specs),
        scratch_shapes=[vmem(*b) for b in buffers] + [dma((len(ins),)), dma((len(outs),))] + list(scratch),
        compiler_params=pltpu.CompilerParams(vmem_limit_bytes=limit << 20),
        cost_estimate=pl.CostEstimate(flops=0, bytes_accessed=1024, transcendentals=0),
    )(*ins[:smem], *[pltpu.with_memory_space_constraint(a, s) for a, s in list(zip(ins, spaces))[smem:]])


def unit(value):
    centered = value - jnp.mean(value, axis=-1, keepdims=True)
    spread = jnp.mean(centered * centered, axis=-1, keepdims=True)
    scale = lax.rsqrt(spread + epsilon)
    return centered * scale, scale


def unit_back(grad, normal, scale):
    mean = jnp.mean(grad, axis=-1, keepdims=True)
    along = jnp.mean(grad * normal, axis=-1, keepdims=True)
    return scale * (grad - mean - normal * along)


def column_sum(value):
    return jnp.sum(value, axis=0, keepdims=True)


def prepare(inn, out, give, sems):
    c, w = lax.axis_index("ctx"), lax.axis_index("wt")
    qkv, up, pack = inn(0), inn(1), out[0]
    rows, width = qkv.shape[0], qkv.shape[1] // 3
    span, size = pack.shape[1] // 3, out[1].shape[1]
    copies = []
    for part in range(3):
        source = qkv.at[:, at(part * (width // span) + c, span)]
        copies.append((source, pack.at[pl.ds(0, rows), pl.ds(part * span, span)]))
    copies += [(up.at[:, at(w ^ d, size)], out[d]) for d in (2, 3, 1)]
    copies = [pltpu.make_async_copy(a, b, sems.at[i]) for i, (a, b) in enumerate(copies)]
    for copy in copies:
        copy.start()
    low = pl.ds(rows, SMALL)
    pack[low, :] = jnp.zeros((SMALL, pack.shape[1]), BF16)
    for i in range(3):
        ref = inn(2 + i)
        pack[pl.ds(rows + 4 * i, 4), pl.ds(0, ref.shape[1])] = ref[...]
    for copy in copies:
        copy.wait()


def attend(inn, out, give, xs, norm, sems):
    first, mixed, sent, stats, small = out
    c, w = lax.axis_index("ctx"), lax.axis_index("wt")
    deal = inn(0)
    length, width = xs.shape
    span = sent.shape[2]
    heads = stats.shape[0] // 2
    head = span // heads
    loads = []
    for d in range(CTX):
        for t in range(2):
            piece = inn(1 + WT + d).at[pl.ds(PIECE * t, PIECE), :]
            target = xs.at[at(deal[c ^ d, t], PIECE), :]
            loads.append(pltpu.make_async_copy(piece, target, sems.at[2 * d + t]))
            loads[-1].start()
    packs = [inn(1 + d) for d in range(WT)]
    for d in range(WT):
        small[:, at(w ^ d, PART)] = floats(packs[d][pl.ds(PART, SMALL), pl.ds(0, PART)])
    for load in loads:
        load.wait()
    bias_q = small[pl.ds(8, 1), at(c, span)]
    bias_v = small[pl.ds(9, 1), at(c, span)]

    @pl.loop(0, length // BLK)
    def _(i):
        rows = at(i, BLK)
        normal, _scale = unit(floats(xs[rows, :]))
        first[rows, :] = (normal * small[pl.ds(0, 1), :] + small[pl.ds(4, 1), :]).astype(BF16)
        total = dot(first[rows, at(w, PART)], packs[0][pl.ds(0, PART), :])
        for d in range(1, WT):
            total += dot(first[rows, at(w ^ d, PART)], packs[d][pl.ds(0, PART), :])
        mixed[rows, pl.ds(0, span)] = (total[:, :span] + bias_q).astype(BF16)
        mixed[rows, pl.ds(span, span)] = total[:, span : 2 * span].astype(BF16)
        mixed[rows, pl.ds(2 * span, span)] = (total[:, 2 * span :] + bias_v).astype(BF16)

    give(0)
    give(1)
    give(4)
    lane = lax.broadcasted_iota(jnp.int32, (BLK, span), 1) // head
    factor = 1.0 / math.sqrt(head)
    for b in range(length // BLK):
        rows, seen = pl.ds(b * BLK, BLK), pl.ds(0, (b + 1) * BLK)
        query = mixed[rows, pl.ds(0, span)]
        parts = []
        for h in range(heads):
            masked = jnp.where(lane == h, query, jnp.zeros_like(query))
            raw = dot_t(mixed[seen, pl.ds(span, span)], masked)
            top = jnp.max(raw, axis=0, keepdims=True)
            terms = jnp.exp((raw - top) * factor)
            inverse = 1.0 / jnp.sum(terms, axis=0, keepdims=True)
            stats[pl.ds(2 * h, 1), rows] = top
            stats[pl.ds(2 * h + 1, 1), rows] = inverse
            weights = (terms * inverse).astype(BF16)
            values = mixed[seen, pl.ds(2 * span, span)]
            parts.append(t_dot(values, weights)[h * head : (h + 1) * head, :])
        norm[rows, :] = jnp.concatenate(parts, axis=0).T.astype(BF16)
    for j in range(CTX):
        for t in range(2):
            sent[j, pl.ds(PIECE * t, PIECE), :] = norm[at(deal[j, t], PIECE), :]


def project(inn, out, give):
    branch, resid, second = out
    w = lax.axis_index("wt")
    small, attended, own = inn(0), inn(1), inn(2)
    span = attended.shape[2]
    total = small[pl.ds(10, 1), :]
    for d in range(WT):
        ref = inn(3 + d)
        for j in range(PART // span):
            total = total + dot(attended[(w ^ d) * (PART // span) + j], ref[pl.ds(span * j, span), :])
    branch[...] = total
    give(0)
    normal, _ = unit(total)
    total = floats(own[...]) + (normal * small[pl.ds(1, 1), :] + small[pl.ds(5, 1), :])
    resid[...] = total
    give(1)
    normal, _ = unit(total)
    second[...] = (normal * small[pl.ds(2, 1), :] + small[pl.ds(6, 1), :]).astype(BF16)


def join_slots(inn, start, target):
    for i, d in enumerate((0, 2, 1, 3)):
        ref = inn(start + d)
        rows = ref.shape[0]
        target[pl.ds(rows * i, rows), :] = ref[...]


def feed(inn, out, give):
    all_rows, hidden, slope, near, far = out
    w = lax.axis_index("wt")
    join_slots(inn, 0, all_rows)
    give(0)
    ups, bias = [inn(4 + d) for d in range(WT)], inn(8)
    half_rows = near.shape[0]

    @pl.loop(0, hidden.shape[1] // PART)
    def _(n):
        cols = at(n, PART)
        upper = floats(bias[pl.ds(0, 1), cols])
        for d in range(WT):
            upper = upper + dot(all_rows[:, at(w ^ d, PART)], ups[d][:, cols])
        square = upper * upper
        curve = jnp.tanh(GELU_A * (upper + GELU_B * (square * upper)))
        half = 0.5 * (1.0 + curve)
        hidden[:, cols] = (upper * half).astype(BF16)
        slope[:, cols] = half + (0.5 * GELU_A) * upper * (1.0 - curve * curve) * (
            1.0 + (3.0 * GELU_B) * square
        )

    give(1)
    give(2)
    down = inn(9)

    @pl.loop(0, near.shape[1] // PART)
    def _(n):
        cols = at(n, PART)
        total = dot(hidden[...], down[:, cols])
        near[:, cols] = total[:half_rows]
        far[:, cols] = total[half_rows:].astype(BF16)


def returned(inn, rows):
    own = pl.ds(0, rows)
    return inn(0)[own, :] + floats(inn(1)[own, :]) + floats(inn(2)[...])


def top_norm(inn, out, give):
    result, d_ffn, sums = out
    small, resid, grad = inn(3), inn(4), inn(5)
    normal, scale = unit(returned(inn, resid.shape[0]) + small[pl.ds(11, 1), :])
    gain = small[pl.ds(3, 1), :]
    d_out = floats(grad[...])
    low = unit_back(d_out * gain, normal, scale).astype(BF16)
    d_ffn[...] = low
    give(1)
    result[...] = (resid[...] + (normal * gain + small[pl.ds(7, 1), :])).astype(BF16)
    sums[pl.ds(0, 1), :] = column_sum(d_out * normal)
    sums[pl.ds(1, 1), :] = column_sum(d_out)
    sums[pl.ds(2, 1), :] = column_sum(floats(low))


def feed_back(inn, out, give):
    all_rows, d_upper, near, far, sums = out
    w = lax.axis_index("wt")
    join_slots(inn, 0, all_rows)
    give(0)
    down, slope = inn(4), inn(5)
    half_rows = near.shape[0]

    @pl.loop(0, d_upper.shape[1] // PART)
    def _(n):
        cols = at(n, PART)
        low = (dot_t(all_rows[...], down[cols, :]) * slope[:, cols]).astype(BF16)
        d_upper[:, cols] = low
        sums[pl.ds(0, 1), cols] = column_sum(floats(low))

    give(1)
    for d in range(WT):
        cols = at(w ^ d, PART)
        total = dot_t(d_upper[...], inn(6 + d)[...])
        near[:, cols] = total[:half_rows]
        far[:, cols] = total[half_rows:].astype(BF16)


KEPT = ((0, 0, 0), (0, 1, 4), (1, 0, 2), (1, 1, 6))
SENT = ((0, 3), (1, 7), (2, 1), (3, 5))


def places(out):
    sent = [(out[2 + i * (len(out) - 3) // 2], i if len(out) == 3 else i % 2, d) for i, d in SENT]
    return sent + [(out[which], i, d) for which, i, d in KEPT]


def grad_down(inn, out, give):
    c = lax.axis_index("ctx")
    hidden, grads = inn(0), inn(1)
    size = out[0].shape[1]
    for n, (target, i, d) in enumerate(places(out)):
        target[i] = t_dot(hidden[:, at(c ^ d, size)], grads[...]).astype(BF16)
        if n in (1, 3) and len(out) == 4:
            give(2 + n // 2)
        elif n == 3:
            give(2)


def grad_up(inn, out, give, part):
    c = lax.axis_index("ctx")
    cut = PART // CTX
    rows_in, grads = inn(0), inn(1)

    @pl.loop(0, WT)
    def _(k):
        part[...] = t_dot(rows_in[:, at(k, PART)], grads[...]).astype(BF16)
        for target, i, d in places(out):
            target[i, at(k, cut), :] = part[at(c ^ d, cut), :]


def middle_norms(inn, out, give):
    sent, d_att, d_resid, sums = out
    w = lax.axis_index("wt")
    small, resid, branch, grad = inn(3), inn(4), inn(5), inn(6)
    rows, span = resid.shape[0], sent.shape[2]
    normal3, scale3 = unit(resid[...])
    normal2, scale2 = unit(branch[...])
    d_second = returned(inn, rows)
    total = floats(grad[...]) + unit_back(d_second * small[pl.ds(2, 1), :], normal3, scale3)
    low = unit_back(total * small[pl.ds(1, 1), :], normal2, scale2).astype(BF16)
    d_att[...] = low
    d_resid[...] = total
    give(2)
    for d in (1, 2, 3, 0):
        part = dot_t(low, inn(7 + d)[...]).astype(BF16)
        for j in range(PART // span):
            sent[(w ^ d) * (PART // span) + j] = part[:, span * j : span * (j + 1)]
    sums[pl.ds(0, 1), :] = column_sum(d_second * normal3)
    sums[pl.ds(1, 1), :] = column_sum(d_second)
    sums[pl.ds(2, 1), :] = column_sum(total * normal2)
    sums[pl.ds(3, 1), :] = column_sum(total)
    sums[pl.ds(4, 1), :] = column_sum(floats(low))


def grad_out(inn, out, give):
    w = lax.axis_index("wt")
    attended, grads = inn(0), inn(1)
    span = attended.shape[2]
    for d in (1, 3, 0, 2):
        for j in range(PART // span):
            part = t_dot(attended[(w ^ d) * (PART // span) + j], grads[...])
            out[d % 2][d // 2, pl.ds(span * j, span), :] = part.astype(BF16)
        if d == 3:
            give(1)


def attend_back(inn, out, give, d_out, d_keys, d_values):
    natural, dealt = out
    deal, mixed, stats, got = (inn(i) for i in range(4))
    length, span = d_out.shape
    heads = stats.shape[0] // 2
    head = span // heads
    factor = 1.0 / math.sqrt(head)
    prescale = factor / relax
    for j in range(CTX):
        for t in range(2):
            d_out[at(deal[j, t], PIECE), :] = got[j, pl.ds(PIECE * t, PIECE), :]
    lane = lax.broadcasted_iota(jnp.int32, (BLK, span), 1) // head
    d_keys[...] = jnp.zeros_like(d_keys)
    d_values[...] = jnp.zeros_like(d_values)
    for b in range(length // BLK):
        rows, seen = pl.ds(b * BLK, BLK), pl.ds(0, (b + 1) * BLK)
        query, grads = mixed[rows, pl.ds(0, span)], d_out[rows, :]
        parts = []
        for h in range(heads):
            query_h = jnp.where(lane == h, query, jnp.zeros_like(query))
            grads_h = jnp.where(lane == h, grads, jnp.zeros_like(grads))
            keys = mixed[seen, pl.ds(span, span)]
            raw = dot_t(keys, query_h)
            weights = jnp.exp((raw - stats[pl.ds(2 * h, 1), rows]) * factor) * stats[pl.ds(2 * h + 1, 1), rows]
            d_probs = dot_t(mixed[seen, pl.ds(2 * span, span)], grads_h)
            delta = jnp.sum(weights * d_probs, axis=0, keepdims=True)
            d_scores = (relax * weights * (d_probs - delta)).astype(BF16)
            d_values[seen, :] += dot(weights.astype(BF16), grads_h)
            d_keys[seen, :] += dot(d_scores, query_h)
            parts.append(t_dot(keys, d_scores)[h * head : (h + 1) * head, :])
        natural[rows, pl.ds(0, span)] = (jnp.concatenate(parts, axis=0).T * prescale).astype(BF16)
    natural[:, pl.ds(span, span)] = (d_keys[...] * prescale).astype(BF16)
    natural[:, pl.ds(2 * span, span)] = d_values[...].astype(BF16)
    for j in range(CTX):
        for t in range(2):
            dealt[j, pl.ds(PIECE * t, PIECE), :] = natural[at(deal[j, t], PIECE), :]


def grad_qkv(inn, out, give):
    w = lax.axis_index("wt")
    first, grads = inn(0), inn(1)
    for d in (1, 3, 0, 2):
        out[d % 2][d // 2] = t_dot(first[:, at(w ^ d, PART)], grads[...]).astype(BF16)
        if d == 3:
            give(1)


def bottom_norm(inn, out, give, joined, d_first):
    input_grad, keep, send = out
    w = lax.axis_index("wt")
    got, own, d_resid, small = (inn(i) for i in range(4))
    _, rows, triple = got.shape
    span, width = triple // 3, own.shape[1]
    for j in range(CTX):
        for part in range(3):
            joined[:, pl.ds(part * width + span * j, span)] = got[j, :, pl.ds(span * part, span)]
    for d in range(WT):
        d_first[:, at(w ^ d, PART)] = dot_t(joined[...], inn(4 + d)[...])
    normal, scale = unit(floats(own[...]))
    grads = d_first[...]
    input_grad[...] = d_resid[...] + unit_back(grads * small[pl.ds(0, 1), :], normal, scale)
    give(0)
    middle, top, up = inn(8), inn(9), inn(10)
    lines = {
        0: column_sum(grads * normal),
        4: column_sum(grads),
        8: column_sum(floats(joined[:, pl.ds(0, width)])),
        9: column_sum(floats(joined[:, pl.ds(2 * width, width)])),
    }
    for i, line in enumerate((2, 6, 1, 5, 10)):
        lines[line] = middle[pl.ds(i, 1), :]
    for i, line in enumerate((3, 7, 11)):
        lines[line] = top[pl.ds(i, 1), :]
    for line, value in lines.items():
        d_first[pl.ds(line, 1), :] = value
    for d in range(WT):
        target = send if d % 2 else keep
        target[d // 2, pl.ds(0, 12), :] = d_first[pl.ds(0, 12), at(w ^ d, PART)]
        target[d // 2, pl.ds(12, 4), :] = jnp.zeros((4, PART), F32)
    for i in range(4):
        keep[0, pl.ds(12 + i, 1), :] = up[:, pl.ds(PART * i, PART)]


def add_second(inn, out, give):
    out[0][...] = (floats(inn(0)[1]) + floats(inn(1)[1])).astype(out[0].dtype)


def add_rest(inn, out, give):
    rows = out[0].shape[0]
    rest = pl.ds(rows, rows)
    out[0][...] = (inn(0)[rest, :] + floats(inn(1)[rest, :])).astype(BF16)


def add_high(inn, out, give):
    keep, got = inn(0), inn(1)
    for i in range(2):
        out[0][i] = (floats(keep[i]) + floats(got[i])).astype(BF16)


def add_high_last(inn, out, give):
    keep, got = inn(0), inn(1)
    for i in range(2):
        out[0][i] = (floats(keep[2 + i]) + floats(got[2 + i])).astype(BF16)


def add_low(first, inn, out, give):
    keep, got, after_z = inn(0), inn(1), inn(2)
    out[1][...] = (floats(keep[1]) + floats(got[first + 1]) + floats(after_z[1])).astype(BF16)
    out[0][...] = floats(keep[0]) + floats(got[first]) + floats(after_z[0])


def add_last(inn, out, give):
    out[0][...] = (inn(0)[...] + floats(inn(1)[...])).astype(BF16)


def add_out(inn, out, give, total):
    c = lax.axis_index("ctx")
    cut = out[0].shape[1]
    total[...] = (floats(inn(0)[0]) + floats(inn(1)[0]) + floats(inn(2)[...])).astype(BF16)
    for i, d in enumerate((0, 4, 2, 6)):
        out[0][i] = total[at(c ^ d, cut), :]
        out[1][i] = total[at(c ^ d ^ 1, cut), :]


def add_last_up(inn, out, give, total):
    w = lax.axis_index("wt")
    cut = out[0].shape[0]
    total[...] = (inn(0)[...] + floats(inn(1)[...])).astype(BF16)
    for d in range(WT):
        out[d][...] = total[at(w ^ d, cut), :]


def pack_up(inn, out, give):
    rows = inn(0).shape[0]
    for i in range(WT):
        out[0][pl.ds(rows * i, rows), :] = inn(i)[...]


def pack_mixed(inn, out, give, small):
    block = out[0]
    rows = inn(0).shape[1]
    block[pl.ds(0, rows), :] = (floats(inn(0)[0]) + floats(inn(1)[0]) + floats(inn(2)[...])).astype(BF16)
    cut, lanes = inn(3).shape[0], 128
    small[...] = jnp.zeros_like(small)
    small[pl.ds(0, cut), :] = (inn(3)[...] + floats(inn(4)[...])).astype(BF16)
    small[pl.ds(cut, SMALL), pl.ds(0, PART)] = (inn(5)[0] + inn(6)[0] + inn(7)[...]).astype(BF16)
    height, across = small.shape[0], block.shape[1] // lanes
    tiles = small.shape[1] // lanes
    for k in range(-(-tiles // across) * across):
        part = small[:, pl.ds(lanes * k, lanes)] if k < tiles else jnp.zeros((height, lanes), BF16)
        block[pl.ds(rows + height * (k // across), height), pl.ds(lanes * (k % across), lanes)] = part


def spread_mixed(inn, out, give, total):
    full, proj, gain, shift, bias, up_bias = out
    c = lax.axis_index("ctx")
    span = full.shape[1] // (3 * CTX)
    cut, lanes, rows = PART // CTX, 128, full.shape[0]
    height, across = cut + SMALL, inn(0).shape[1] // lanes
    total[...] = jnp.zeros_like(total)
    for d in range(CTX):
        block = inn(d)
        for part in range(3):
            full[:, at(part * CTX + (c ^ d), span)] = floats(block[pl.ds(0, rows), pl.ds(span * part, span)])
        for k in range(proj.shape[1] // lanes):
            top, left = rows + height * (k // across), pl.ds(lanes * (k % across), lanes)
            proj[at(c ^ d, cut), pl.ds(lanes * k, lanes)] = floats(block[pl.ds(top, cut), left])
            if lanes * k < PART:
                total[:, pl.ds(lanes * k, lanes)] += floats(block[pl.ds(top + cut, SMALL), left])
    for i, ref in enumerate((gain, shift, bias, up_bias)):
        ref[...] = total[pl.ds(4 * i, 4), :]


def spread_down(inn, out, give, sems, result):
    c = lax.axis_index("ctx")
    stores = []
    for d in range(CTX):
        block = inn(d)
        rows = at(c ^ d, block.shape[0])
        out[0][rows, :] = floats(block[...])
        stores.append(pltpu.make_async_copy(out[0].at[rows, :], result.at[rows, :], sems.at[d]))
        stores[-1].start()
    for store in stores:
        store.wait()


def spread_up(inn, out, give, sems, result):
    c, w = lax.axis_index("ctx"), lax.axis_index("wt")
    cut = PART // CTX
    width = out[0].shape[1] // WT
    stores = []
    for d in range(CTX):
        block, rows = inn(d), at(c ^ d, cut)
        for k in range(WT):
            out[0][rows, at(w ^ k, width)] = floats(block[pl.ds(cut * k, cut), :])
        stores.append(pltpu.make_async_copy(out[0].at[rows, :], result.at[rows, :], sems.at[d]))
        stores[-1].start()
    for store in stores:
        store.wait()


def split_device(
    layer_input,
    out_grad,
    deal,
    w_qkv,
    w_out,
    w_up,
    w_down,
    norm_gain,
    norm_shift,
    bias_width,
    up_bias,
):
    _, rows, width = layer_input.shape
    w = lax.axis_index("wt")
    per = HEADS // CTX
    span = per * (width // HEADS)
    length = rows * CTX
    hidden_width = w_down.shape[0]
    everyone = WT * rows
    own, grad = layer_input[0], out_grad[0]
    vmem, dma = pltpu.VMEM, pltpu.SemaphoreType.DMA

    sequence = gather_ctx(own)
    begin = lax.optimization_barrier((w_qkv, w_up, norm_gain, norm_shift, bias_width, sequence[1]))[:5]
    pack, *ups = call(
        prepare,
        "prepare",
        begin,
        [shape(PART + SMALL, 3 * span)] + [shape(PART, hidden_width)] * 3,
        raw=(0, 1),
        hbm=(2, 3, 4),
        scratch=[dma((6,))],
    )
    packs = gather_wt(pack)
    up_core, up_x, up_both = ups
    outs_x = swap(after(w_out, packs[2]), "wt", 2)
    up_x = swap(after(up_x, packs[2]), "wt", 2)

    first, mixed, sent, stats, small = call(
        attend,
        "attend",
        (deal, *packs, *sequence),
        [
            shape(length, width),
            shape(length, 3 * span),
            shape(CTX, rows, span),
            shape(2 * per, length, dtype=F32),
            shape(SMALL, width, dtype=F32),
        ],
        smem=1,
        hbm=range(1, 1 + WT),
        raw=range(1 + WT, 1 + WT + CTX),
        hbm_out=(0, 1),
        scratch=[vmem((length, width), BF16), vmem((length, span), BF16), dma((2 * CTX,))],
    )
    attended = lax.all_to_all(after(sent, outs_x, up_x), "ctx", 0, 0, tiled=True)
    up_both = swap(up_both, "wt", 3)
    outs_own, outs_x, up_core = lax.optimization_barrier((w_out, outs_x, up_core, sent))[:3]
    outs = w_out, swap(outs_own, "wt", 1), outs_x, swap(outs_x, "wt", 1)
    ups = w_up, swap(up_core, "wt", 1), up_x, up_both
    attended = after(attended, *outs, *ups[1:])

    branch, resid, second = call(
        project,
        "project",
        (small, attended, own, *outs),
        [shape(rows, width, dtype=F32), shape(rows, width, dtype=F32), shape(rows, width)],
    )

    own_columns = ((PART, hidden_width), lambda ref: ref.at[:, at(lax.axis_index("wt"), hidden_width)])
    halves = [shape(2 * rows, width, dtype=F32), shape(2 * rows, width)]
    seconds, hidden, slope, near, far = call(
        feed,
        "feed",
        (*gather_wt(second), *ups, up_bias.reshape(1, hidden_width), w_down),
        [shape(everyone, width), shape(everyone, hidden_width), shape(everyone, hidden_width, dtype=F32)]
        + halves,
        hbm=(4, 8, 9),
        hbm_out=(0,),
        views={4: own_columns},
    )

    def return_rows(near, far):
        got = swap(far, "wt", 1)
        back = call(add_rest, "add_rest", (near, got), [shape(rows, width)])
        return near, got, swap(back, "wt", 2)

    result, d_ffn, sums3 = call(
        top_norm,
        "top_norm",
        (*return_rows(near, far), small, resid, grad),
        [shape(rows, width), shape(rows, width), shape(3, width, dtype=F32)],
    )
    d_ffns, d_upper, near, far, up_sum = call(
        feed_back,
        "feed_back",
        (*gather_wt(d_ffn), w_down, slope, *ups),
        [shape(everyone, width), shape(everyone, hidden_width)] + halves + [shape(1, hidden_width, dtype=F32)],
        hbm=(4, 6),
        views={6: own_columns},
    )
    got = swap(far, "wt", 1)
    def sends(terms):
        if len(terms) == 3:
            whole = swap(terms[2], "ctx", 1)
            return (whole, 0), (whole, 2)
        return (swap(terms[2], "ctx", 1), 0), (swap(terms[3], "ctx", 1), 0)

    def chunks(split):
        sent = [shape(2, eighth, width)] * 2 if split else [shape(4, eighth, width)]
        return [shape(2, eighth, width)] * 2 + sent

    def added_high(name, terms, got):
        return call(
            add_high,
            "add_high_" + name,
            (terms[1], got),
            [shape(2, eighth, width)],
            hbm=(0,),
        )

    def added_low(name, terms, got, along):
        return call(
            functools.partial(add_low, got[1]),
            "add_low_" + name,
            (terms[0], got[0], along),
            [shape(eighth, width, dtype=F32), shape(eighth, width)],
            hbm=(0,),
        )

    eighth = hidden_width // CTX
    cut = PART // CTX
    terms_a = call(
        grad_down, "grad_down", (hidden, d_ffns), chunks(SPLIT[0]), hbm_out=range(3 + SPLIT[0])
    )
    high_got_a, low_got_a = sends(terms_a)
    back = call(add_rest, "add_rest", (after(near, terms_a[2]), got), [shape(rows, width)])
    far = swap(back, "wt", 2)
    terms_b = call(
        grad_up,
        "grad_up",
        (after(seconds, back), d_upper),
        chunks(SPLIT[1]),
        hbm=(0,),
        hbm_out=range(3 + SPLIT[1]),
        scratch=[vmem((PART, hidden_width), BF16)],
    )
    high_got_b, low_got_b = sends(terms_b)
    high_a = added_high("a", terms_a, high_got_a[0])
    next_a = swap(high_a, "ctx", 2)
    sent, d_att, d_resid, sums21 = call(
        middle_norms,
        "middle_norms",
        (near, got, far, small, resid, branch, grad, *outs),
        [
            shape(CTX, rows, span),
            shape(rows, width),
            shape(rows, width, dtype=F32),
            shape(5, width, dtype=F32),
        ],
    )
    got = lax.all_to_all(sent, "ctx", 0, 0, tiled=True)
    pieces = [shape(2, PART, width)] * 2
    keep_out, send_out = call(
        grad_out, "grad_out", (attended, d_att), pieces, hbm_out=(0, 1)
    )
    got_out = swap(send_out, "wt", 1)
    back_out = call(
        add_second,
        "add_second_out",
        (keep_out, got_out),
        [shape(PART, width)],
        hbm=(0,),
    )
    out_x = swap(back_out, "wt", 2)
    high_b = added_high("b", terms_b, after(high_got_b[0], got))
    next_b = swap(high_b, "ctx", 2)
    first_a, second_a = added_low("a", terms_a, low_got_a, next_a)
    last_a = swap(second_a, "ctx", 4)

    natural, dealt = call(
        attend_back,
        "attend_back",
        (deal, mixed, stats, after(got, back_out)),
        [shape(length, 3 * span), shape(CTX, rows, 3 * span)],
        smem=1,
        hbm=(1,),
        scratch=[vmem((length, span), BF16), vmem((length, span), F32), vmem((length, span), F32)],
    )
    first_b, second_b = added_low("b", terms_b, low_got_b, next_b)
    last_b = swap(second_b, "ctx", 4)
    part_a = call(add_last, "add_last_a", (first_a, last_a), [shape(eighth, width)])
    down_slots = gather_free(after(part_a, back), (high_b, back,))
    pieces = [shape(2, PART, 3 * span)] * 2
    keep_qkv, send_qkv = call(
        grad_qkv, "grad_qkv", (first, after(natural, last_a, second_b)), pieces, hbm=(0,), hbm_out=(0, 1)
    )
    keep_c, send_c = call(
        add_out,
        "add_out",
        (keep_out, got_out, after(out_x, natural, last_b)),
        [shape(4, cut, width)] * 2,
        hbm=(0,),
        scratch=[vmem((PART, width), BF16)],
    )
    got_c = swap(send_c, "ctx", 1)
    got_rows = lax.all_to_all(after(dealt, down_slots[1], send_c), "ctx", 0, 0, tiled=True)
    got_qkv = swap(send_qkv, "wt", 1)
    back_qkv = call(
        add_second,
        "add_second_qkv",
        (keep_qkv, got_qkv),
        [shape(PART, 3 * span)],
        hbm=(0,),
    )
    qkv_x = swap(back_qkv, "wt", 2)
    own_up, *up_parts = call(
        add_last_up,
        "add_last_up",
        (first_b, last_b),
        [shape(cut, width)] * WT,
        scratch=[vmem((eighth, width), BF16)],
    )
    up_parts = [swap(part, "wt", d) for part, d in zip(up_parts, (1, 2, 3))]
    up_block = call(
        pack_up, "pack_up", (after(own_up, down_slots[1], send_c), *up_parts), [shape(eighth, width)]
    )
    up_slots = gather_free(up_block)
    weights_x = swap(after(w_qkv, far), "wt", 2)
    qkv_own, weights_x = after(w_qkv, second_b), weights_x
    all_qkv = w_qkv, swap(qkv_own, "wt", 1), weights_x, swap(weights_x, "wt", 1)
    high_c = call(
        add_high_last, "add_high_c", (keep_c, got_c), [shape(2, cut, width)]
    )
    next_c = swap(high_c, "ctx", 2)
    first_c, second_c = call(
        functools.partial(add_low, 0),
        "add_low_c",
        (keep_c, got_c, next_c),
        [shape(cut, width, dtype=F32), shape(cut, width)],
    )
    last_c = swap(second_c, "ctx", 4)
    input_grad, keep, send = call(
        bottom_norm,
        "bottom_norm",
        (after(got_rows, back_qkv), own, d_resid, small, *all_qkv, sums21, sums3, up_sum),
        [shape(rows, width, dtype=F32)] + [shape(2, SMALL, PART, dtype=F32)] * 2,
        hbm=(1, 2, 4, 5, 6, 7),
        hbm_out=(0,),
        scratch=[vmem((rows, 3 * width), BF16), vmem((rows, width), F32)],
    )
    got_sums = swap(send, "wt", 1)
    back_sums = call(add_second, "add_second_sums", (keep, got_sums), [shape(SMALL, PART, dtype=F32)])
    sums_x = swap(back_sums, "wt", 2)
    mixed_block = call(
        pack_mixed,
        "pack_mixed",
        (keep_qkv, got_qkv, after(qkv_x, up_slots[3], sums_x), first_c, last_c, keep, got_sums, sums_x),
        [shape(PART + 3 * (cut + SMALL), 3 * span)],
        hbm=(0,),
        scratch=[vmem((cut + SMALL, width), BF16)],
    )
    mixed_slots = gather_ctx_z(mixed_block)
    full_qkv, full_out, gain, shift, bias, up_total = call(
        spread_mixed,
        "spread_mixed",
        mixed_slots,
        [shape(PART, 3 * width, dtype=F32), shape(PART, width, dtype=F32)] + [shape(4, PART, dtype=F32)] * 4,
        hbm_out=range(6),
        scratch=[vmem((SMALL, PART), F32)],
    )
    up_total = up_total.reshape(hidden_width)
    full_down = call(
        spread_down,
        "spread_down",
        down_slots,
        [shape(hidden_width, width, dtype=F32)],
        hbm_out=(0,),
        scratch=[dma((CTX,))],
        parts=(0,),
    )
    full_up = call(
        spread_up,
        "spread_up",
        up_slots,
        [shape(PART, WT * hidden_width, dtype=F32)],
        hbm_out=(0,),
        scratch=[dma((CTX,))],
        parts=(0,),
    )
    return (
        result[None],
        input_grad[None],
        full_qkv,
        full_out,
        full_up,
        full_down,
        gain,
        shift,
        bias,
        up_total,
    )


def solution(mesh):
    small = mesh.shape["ctx"] == CTX and mesh.shape["wt"] == WT
    per_device = split_device if small else general_device
    in_specs = (
        P("wt", "ctx", None),
        P("wt", "ctx", None),
        P(),
        P("wt", None),
        P("wt", None),
        P("wt", None),
        P("wt", None),
        P(None, "wt"),
        P(None, "wt"),
        P(None, "wt"),
        P("wt"),
    )
    out_specs = (
        P("wt", "ctx", None),
        P("wt", "ctx", None),
        P("wt", None),
        P("wt", None),
        P("wt", None),
        P("wt", None),
        P(None, "wt"),
        P(None, "wt"),
        P(None, "wt"),
        P("wt"),
    )
    return jax.shard_map(
        per_device, mesh=mesh, in_specs=in_specs, out_specs=out_specs, check_vma=False
    )
```

```python
import functools
import math

import jax
import jax.numpy as jnp
from jax import lax
from jax.experimental import pallas as pl
from jax.experimental.pallas import tpu as pltpu
from jax.sharding import PartitionSpec as P

HEADS = 16
BLK = 256
PIECE = 64


epsilon = 1e-05
relax = 32.0


def layer_norm(value, gain, shift):
    mean = jnp.mean(value, axis=-1, keepdims=True)
    centered = value - mean
    spread = jnp.mean(centered * centered, axis=-1, keepdims=True)
    return centered * lax.rsqrt(spread + epsilon) * gain + shift


def gelu_tanh(value):
    return jax.nn.gelu(value, approximate=True)


def rows_dot(left, weight):
    return jnp.einsum("std,de->ste", left, weight, preferred_element_type=jnp.float32)


def weight_grad(left, right):
    return jnp.einsum("std,ste->de", left, right, preferred_element_type=jnp.float32)


def back_dot(grad, weight):
    return jnp.einsum("ste,de->std", grad, weight, preferred_element_type=jnp.float32)


def row_total(value):
    return jnp.sum(value.astype(jnp.float32), axis=(0, 1))


def general_device(
    layer_input,
    out_grad,
    deal,
    w_qkv,
    w_out,
    w_up,
    w_down,
    norm_gain,
    norm_shift,
    bias_width,
    up_bias,
):
    seqs, rows, width = layer_input.shape
    heads = HEADS
    head = width // heads
    prescale = 1.0 / (relax * math.sqrt(head))
    ranks = lax.axis_size("ctx")
    length = rows * ranks
    per_block = BLK // PIECE
    rank = lax.axis_index("ctx")
    chosen = jnp.arange(ranks, dtype=jnp.int32) == rank
    mine = jnp.sum(jnp.where(chosen[:, None], deal, 0), axis=0)
    query_blocks = jnp.repeat(mine, rows // 2) // per_block
    key_blocks = jnp.repeat(deal.reshape(-1), rows // 2) // per_block
    full_qkv, full_out, full_up, full_down, gains, shifts, biases, up_shift = (
        lax.all_gather(w_qkv, "wt", axis=0, tiled=True),
        lax.all_gather(w_out, "wt", axis=0, tiled=True),
        lax.all_gather(w_up, "wt", axis=0, tiled=True),
        lax.all_gather(w_down, "wt", axis=0, tiled=True),
        lax.all_gather(norm_gain, "wt", axis=1, tiled=True),
        lax.all_gather(norm_shift, "wt", axis=1, tiled=True),
        lax.all_gather(bias_width, "wt", axis=1, tiled=True),
        lax.all_gather(up_bias, "wt", axis=0, tiled=True),
    )
    gains = gains.astype(jnp.float32)
    shifts = shifts.astype(jnp.float32)
    biases = biases.astype(jnp.float32)
    up_shift = up_shift.astype(jnp.float32)
    input_float = layer_input.astype(jnp.float32)
    first = layer_norm(input_float, gains[0], shifts[0]).astype(jnp.bfloat16)
    mixed = rows_dot(first, full_qkv)
    query = (mixed[..., :width] + biases[0]).astype(jnp.bfloat16)
    kv_local = jnp.concatenate(
        [mixed[..., width : 2 * width], mixed[..., 2 * width :] + biases[1]], axis=-1
    ).astype(jnp.bfloat16)
    kv_all = lax.all_gather(kv_local, "ctx", axis=1, tiled=True)
    step = math.gcd(length, 1024)
    count = length // step
    query4 = query.reshape(seqs, rows, heads, head)

    def score_block(left, right):
        return (
            jnp.einsum("sqhd,skhd->shqk", left, right, preferred_element_type=jnp.float32)
            * prescale
        )

    def key_block(index):
        start = index * step
        piece = lax.dynamic_slice_in_dim(kv_all, start, step, 1)
        keys4 = piece[..., :width].reshape(seqs, step, heads, head)
        values4 = piece[..., width:].reshape(seqs, step, heads, head)
        visible = (
            query_blocks[:, None] >= lax.dynamic_slice_in_dim(key_blocks, start, step, 0)[None, :]
        )
        return (keys4, values4, visible)

    def probs(raw, visible, totals):
        return jnp.where(visible, jnp.exp(raw * relax - totals[..., None]), 0.0)

    def online(index, carry):
        top, total, acc = carry
        keys4, values4, visible = key_block(index)
        raw = jnp.where(visible, score_block(query4, keys4), -1e30)
        new_top = jnp.maximum(top, jnp.max(raw, axis=-1))
        terms = jnp.where(visible, jnp.exp((raw - new_top[..., None]) * relax), 0.0)
        factor = jnp.exp((top - new_top) * relax)
        total = total * factor + jnp.sum(terms, axis=-1)
        acc = acc * jnp.transpose(factor, (0, 2, 1))[..., None]
        acc = acc + jnp.einsum(
            "shqk,skhd->sqhd",
            terms.astype(jnp.bfloat16),
            values4,
            preferred_element_type=jnp.float32,
        )
        return (new_top, total, acc)

    start_top = jnp.full((seqs, heads, rows), -1e30, jnp.float32)
    start_total = jnp.zeros((seqs, heads, rows), jnp.float32)
    start_acc = jnp.zeros((seqs, rows, heads, head), jnp.float32)
    top, total, acc = lax.fori_loop(0, count, online, (start_top, start_total, start_acc))
    log_total = top * relax + jnp.log(total)
    attended_float = acc / jnp.transpose(total, (0, 2, 1))[..., None]
    attended = attended_float.reshape(seqs, rows, width).astype(jnp.bfloat16)
    branch = rows_dot(attended, full_out) + biases[2]
    resid = input_float + layer_norm(branch, gains[1], shifts[1])
    second = layer_norm(resid, gains[2], shifts[2]).astype(jnp.bfloat16)
    upper = rows_dot(second, full_up) + up_shift
    hidden = gelu_tanh(upper).astype(jnp.bfloat16)
    ffn = rows_dot(hidden, full_down) + biases[3]
    top_norm, pull_four = jax.vjp(layer_norm, ffn, gains[3], shifts[3])
    result = resid + top_norm
    d_out = out_grad.astype(jnp.float32)
    d_ffn, d_gain3, d_shift3 = pull_four(d_out)
    d_ffn = d_ffn.astype(jnp.bfloat16)
    d_bias3 = row_total(d_ffn)
    g_down = weight_grad(hidden, d_ffn)
    d_hidden = back_dot(d_ffn, full_down)
    _, pull_gelu = jax.vjp(gelu_tanh, upper)
    d_upper = pull_gelu(d_hidden)[0].astype(jnp.bfloat16)
    d_up_shift = row_total(d_upper)
    g_up = weight_grad(second, d_upper)
    d_second = back_dot(d_upper, full_up)
    _, pull_three = jax.vjp(layer_norm, resid, gains[2], shifts[2])
    d_resid_part, d_gain2, d_shift2 = pull_three(d_second)
    d_resid = d_out + d_resid_part
    _, pull_two = jax.vjp(layer_norm, branch, gains[1], shifts[1])
    d_branch, d_gain1, d_shift1 = pull_two(d_resid)
    d_branch = d_branch.astype(jnp.bfloat16)
    d_bias2 = row_total(d_branch)
    g_out = weight_grad(attended, d_branch)
    d_attended = back_dot(d_branch, full_out).astype(jnp.bfloat16)
    d_out4 = d_attended.reshape(seqs, rows, heads, head)
    delta = jnp.einsum("sqhd,sqhd->shq", d_out4.astype(jnp.float32), attended_float)

    def score_grads(q_rows, do_rows, k_rows, v_rows, visible, lse_rows, delta_rows):
        weights = probs(score_block(q_rows, k_rows), visible, lse_rows)
        d_probs = jnp.einsum("sqhd,skhd->shqk", do_rows, v_rows, preferred_element_type=jnp.float32)
        d_scores = (relax * weights * (d_probs - delta_rows[..., None])).astype(jnp.bfloat16)
        return (d_scores, weights.astype(jnp.bfloat16))

    zero_query = jnp.zeros((seqs, rows, heads, head), jnp.float32)

    def local_grads(d_query, index):
        keys4, values4, visible = key_block(index)
        d_scores, weights = score_grads(query4, d_out4, keys4, values4, visible, log_total, delta)
        d_query = (
            d_query
            + jnp.einsum("shqk,skhd->sqhd", d_scores, keys4, preferred_element_type=jnp.float32)
            * prescale
        )
        d_keys = (
            jnp.einsum("shqk,sqhd->kshd", d_scores, query4, preferred_element_type=jnp.float32)
            * prescale
        )
        d_values = jnp.einsum(
            "shqk,sqhd->kshd", weights, d_out4, preferred_element_type=jnp.float32
        )
        joined = jnp.concatenate(
            [d_keys.reshape(step, seqs, width), d_values.reshape(step, seqs, width)], axis=-1
        )
        return (d_query, joined)

    d_query, pieces = lax.scan(local_grads, zero_query, jnp.arange(count, dtype=jnp.int32))
    terms = pieces.reshape(length, seqs, 2 * width)
    d_kv = jnp.transpose(lax.psum_scatter(terms, "ctx", scatter_dimension=0, tiled=True), (1, 0, 2))
    d_query = d_query.reshape(seqs, rows, width).astype(jnp.bfloat16)
    d_kv = d_kv.astype(jnp.bfloat16)
    d_bias0 = row_total(d_query)
    d_bias1 = row_total(d_kv[..., width:])
    d_mixed = jnp.concatenate([d_query, d_kv], axis=-1)
    g_qkv = weight_grad(first, d_mixed)
    d_first = back_dot(d_mixed, full_qkv)
    _, pull_one = jax.vjp(layer_norm, input_float, gains[0], shifts[0])
    d_input_part, d_gain0, d_shift0 = pull_one(d_first)
    input_grad = d_resid + d_input_part
    grad_gain = jnp.stack([d_gain0, d_gain1, d_gain2, d_gain3])
    grad_shift = jnp.stack([d_shift0, d_shift1, d_shift2, d_shift3])
    grad_bias = jnp.stack([d_bias0, d_bias1, d_bias2, d_bias3])
    owned = (
        lax.psum_scatter(g_qkv.astype(jnp.bfloat16), "wt", scatter_dimension=0, tiled=True).astype(
            jnp.float32
        ),
        lax.psum_scatter(g_out.astype(jnp.bfloat16), "wt", scatter_dimension=0, tiled=True).astype(
            jnp.float32
        ),
        lax.psum_scatter(g_up.astype(jnp.bfloat16), "wt", scatter_dimension=0, tiled=True).astype(
            jnp.float32
        ),
        lax.psum_scatter(g_down.astype(jnp.bfloat16), "wt", scatter_dimension=0, tiled=True).astype(
            jnp.float32
        ),
        lax.psum_scatter(
            grad_gain.astype(jnp.bfloat16), "wt", scatter_dimension=1, tiled=True
        ).astype(jnp.float32),
        lax.psum_scatter(
            grad_shift.astype(jnp.bfloat16), "wt", scatter_dimension=1, tiled=True
        ).astype(jnp.float32),
        lax.psum_scatter(
            grad_bias.astype(jnp.bfloat16), "wt", scatter_dimension=1, tiled=True
        ).astype(jnp.float32),
        lax.psum_scatter(
            d_up_shift.astype(jnp.bfloat16), "wt", scatter_dimension=0, tiled=True
        ).astype(jnp.float32),
    )
    summed = lax.psum(
        (owned[0], owned[1], owned[2], owned[3], owned[4], owned[5], owned[6], owned[7]), "ctx"
    )
    return (
        result.astype(jnp.bfloat16),
        input_grad,
        summed[0],
        summed[1],
        summed[2],
        summed[3],
        summed[4],
        summed[5],
        summed[6],
        summed[7],
    )


F32 = jnp.float32
BF16 = jnp.bfloat16
WT = 4
CTX = 8
PART = 256
SMALL = 16
GELU_A = math.sqrt(2.0 / math.pi)
GELU_B = 0.044715
SPLIT = (0, 1)


def swap(value, axis, bit):
    size = lax.axis_size(axis)
    return lax.ppermute(value, axis, [(i, i ^ bit) for i in range(size)])


def gather_wt(block):
    far = swap(block, "wt", 2)
    return block, swap(block, "wt", 1), far, swap(far, "wt", 1)


def gather_ctx(block):
    far, near, side = (swap(block, "ctx", bit) for bit in (4, 2, 1))
    near = after(near, side)
    near_side = swap(near, "ctx", 1)
    far = after(far, near_side)
    corner = swap(far, "ctx", 2)
    far_side = swap(far, "ctx", 1)
    return [block, side, near, near_side, far, far_side, corner, swap(after(corner, far_side), "ctx", 1)]


def held(value, others):
    return after(value, *others) if others else value


def gather_free(block, go4=(), go2=(), go1=(), near=(), far=(), corner=()):
    far_z = held(swap(held(block, go4), "ctx", 4), far)
    near_z = held(swap(held(block, go2), "ctx", 2), near)
    side = swap(held(block, go1), "ctx", 1)
    near_side, corner_z, far_side = swap(near_z, "ctx", 1), swap(far_z, "ctx", 2), swap(far_z, "ctx", 1)
    corner_z = held(corner_z, corner)
    return [block, side, near_z, near_side, far_z, far_side, corner_z, swap(corner_z, "ctx", 1)]


def gather_ctx_z(block):
    blocks = {0: block}
    for bit in (1, 4, 2):
        blocks.update({d ^ bit: swap(value, "ctx", bit) for d, value in blocks.items()})
    return [blocks[d] for d in range(CTX)]


def after(value, *others):
    return lax.optimization_barrier((value, *others))[0]


def floats(value):
    return value.astype(F32)


def dot(left, right):
    return jnp.dot(left, right, preferred_element_type=F32)


def dot_t(left, right):
    return lax.dot_general(left, right, (((1,), (1,)), ((), ())), preferred_element_type=F32)


def t_dot(left, right):
    return lax.dot_general(left, right, (((0,), (0,)), ((), ())), preferred_element_type=F32)


def at(start, size):
    return pl.ds(pl.multiple_of(start * size, size), size)


def shape(*dims, dtype=jnp.bfloat16):
    return jax.ShapeDtypeStruct(dims, dtype)


def call(body, name, ins, outs, smem=0, raw=(), hbm=(), views=None, hbm_out=(), scratch=(), parts=(), slack=10):
    views = views or {}
    ends = [i for i in hbm_out if i not in parts]
    vmem, dma = pltpu.VMEM, pltpu.SemaphoreType.DMA

    def kernel(*refs):
        sources, results = refs[: len(ins)], list(refs[len(ins) : len(ins) + len(outs)])
        rest = list(refs[len(ins) + len(outs) :])
        buffers = {i: rest.pop(0) for i in hbm}
        targets = {i: rest.pop(0) for i in hbm_out}
        in_sems, out_sems = rest.pop(0), rest.pop(0)
        loads, stores = {}, {}
        for i in hbm:
            source = views[i][1](sources[i]) if i in views else sources[i]
            loads[i] = pltpu.make_async_copy(source, buffers[i], in_sems.at[i])
            loads[i].start()

        def inn(i):
            if i not in buffers:
                return sources[i]
            if i in loads:
                loads.pop(i).wait()
            return buffers[i]

        def give(i):
            if i in targets:
                stores[i] = pltpu.make_async_copy(targets[i], results[i], out_sems.at[i])
                stores[i].start()

        body(inn, [targets.get(i, ref) for i, ref in enumerate(results)], give, *rest, *[results[i] for i in parts])
        for i in ends:
            if i not in stores:
                give(i)
        for store in stores.values():
            store.wait()

    buffers = [(views[i][0] if i in views else ins[i].shape, ins[i].dtype) for i in hbm]
    buffers += [(outs[i].shape, outs[i].dtype) for i in hbm_out]
    held = buffers + [(s.shape, s.dtype) for s in scratch if s.dtype in (BF16, F32)]
    limit = slack + -(-sum(math.prod(dims) * jnp.dtype(kind).itemsize for dims, kind in held) >> 20)
    spaces = [pltpu.SMEM if i < smem else pltpu.HBM if i in hbm or i in raw else vmem for i in range(len(ins))]
    out_spaces = [pltpu.HBM if i in hbm_out else vmem for i in range(len(outs))]
    results = [space(o.shape, o.dtype) for space, o in zip(out_spaces, outs)]
    out_specs = [pl.BlockSpec(memory_space=space) for space in out_spaces]
    single = len(outs) == 1
    return pl.pallas_call(
        kernel,
        name=name,
        out_shape=results[0] if single else tuple(results),
        in_specs=[pl.BlockSpec(memory_space=space) for space in spaces],
        out_specs=out_specs[0] if single else tuple(out_specs),
        scratch_shapes=[vmem(*b) for b in buffers] + [dma((len(ins),)), dma((len(outs),))] + list(scratch),
        compiler_params=pltpu.CompilerParams(vmem_limit_bytes=limit << 20),
        cost_estimate=pl.CostEstimate(flops=0, bytes_accessed=1024, transcendentals=0),
    )(*ins[:smem], *[pltpu.with_memory_space_constraint(a, s) for a, s in list(zip(ins, spaces))[smem:]])


def unit(value):
    centered = value - jnp.mean(value, axis=-1, keepdims=True)
    spread = jnp.mean(centered * centered, axis=-1, keepdims=True)
    scale = lax.rsqrt(spread + epsilon)
    return centered * scale, scale


def unit_back(grad, normal, scale):
    mean = jnp.mean(grad, axis=-1, keepdims=True)
    along = jnp.mean(grad * normal, axis=-1, keepdims=True)
    return scale * (grad - mean - normal * along)


def column_sum(value):
    return jnp.sum(value, axis=0, keepdims=True)


def prepare(inn, out, give, sems):
    c, w = lax.axis_index("ctx"), lax.axis_index("wt")
    qkv, up, pack = inn(0), inn(1), out[0]
    rows, width = qkv.shape[0], qkv.shape[1] // 3
    span, size = pack.shape[1] // 3, out[1].shape[1]
    copies = []
    for part in range(3):
        source = qkv.at[:, at(part * (width // span) + c, span)]
        copies.append((source, pack.at[pl.ds(0, rows), pl.ds(part * span, span)]))
    copies += [(up.at[:, at(w ^ d, size)], out[d]) for d in (2, 3, 1)]
    copies = [pltpu.make_async_copy(a, b, sems.at[i]) for i, (a, b) in enumerate(copies)]
    for copy in copies:
        copy.start()
    low = pl.ds(rows, SMALL)
    pack[low, :] = jnp.zeros((SMALL, pack.shape[1]), BF16)
    for i in range(3):
        ref = inn(2 + i)
        pack[pl.ds(rows + 4 * i, 4), pl.ds(0, ref.shape[1])] = ref[...]
    for copy in copies:
        copy.wait()


def attend(inn, out, give, xs, norm, sems):
    first, mixed, sent, stats, small = out
    c, w = lax.axis_index("ctx"), lax.axis_index("wt")
    deal = inn(0)
    length, width = xs.shape
    span = sent.shape[2]
    heads = stats.shape[0] // 2
    head = span // heads
    loads = []
    for d in range(CTX):
        for t in range(2):
            piece = inn(1 + WT + d).at[pl.ds(PIECE * t, PIECE), :]
            target = xs.at[at(deal[c ^ d, t], PIECE), :]
            loads.append(pltpu.make_async_copy(piece, target, sems.at[2 * d + t]))
            loads[-1].start()
    packs = [inn(1 + d) for d in range(WT)]
    for d in range(WT):
        small[:, at(w ^ d, PART)] = floats(packs[d][pl.ds(PART, SMALL), pl.ds(0, PART)])
    for load in loads:
        load.wait()
    bias_q = small[pl.ds(8, 1), at(c, span)]
    bias_v = small[pl.ds(9, 1), at(c, span)]

    @pl.loop(0, length // BLK)
    def _(i):
        rows = at(i, BLK)
        normal, _scale = unit(floats(xs[rows, :]))
        first[rows, :] = (normal * small[pl.ds(0, 1), :] + small[pl.ds(4, 1), :]).astype(BF16)
        total = dot(first[rows, at(w, PART)], packs[0][pl.ds(0, PART), :])
        for d in range(1, WT):
            total += dot(first[rows, at(w ^ d, PART)], packs[d][pl.ds(0, PART), :])
        mixed[rows, pl.ds(0, span)] = (total[:, :span] + bias_q).astype(BF16)
        mixed[rows, pl.ds(span, span)] = total[:, span : 2 * span].astype(BF16)
        mixed[rows, pl.ds(2 * span, span)] = (total[:, 2 * span :] + bias_v).astype(BF16)

    give(0)
    give(1)
    give(4)
    lane = lax.broadcasted_iota(jnp.int32, (BLK, span), 1) // head
    factor = 1.0 / math.sqrt(head)
    for b in range(length // BLK):
        rows, seen = pl.ds(b * BLK, BLK), pl.ds(0, (b + 1) * BLK)
        query = mixed[rows, pl.ds(0, span)]
        parts = []
        for h in range(heads):
            masked = jnp.where(lane == h, query, jnp.zeros_like(query))
            raw = dot_t(mixed[seen, pl.ds(span, span)], masked)
            top = jnp.max(raw, axis=0, keepdims=True)
            terms = jnp.exp((raw - top) * factor)
            inverse = 1.0 / jnp.sum(terms, axis=0, keepdims=True)
            stats[pl.ds(2 * h, 1), rows] = top
            stats[pl.ds(2 * h + 1, 1), rows] = inverse
            weights = (terms * inverse).astype(BF16)
            values = mixed[seen, pl.ds(2 * span, span)]
            parts.append(t_dot(values, weights)[h * head : (h + 1) * head, :])
        norm[rows, :] = jnp.concatenate(parts, axis=0).T.astype(BF16)
    for j in range(CTX):
        for t in range(2):
            sent[j, pl.ds(PIECE * t, PIECE), :] = norm[at(deal[j, t], PIECE), :]


def project(inn, out, give):
    branch, resid, second = out
    w = lax.axis_index("wt")
    small, attended, own = inn(0), inn(1), inn(2)
    span = attended.shape[2]
    total = small[pl.ds(10, 1), :]
    for d in range(WT):
        ref = inn(3 + d)
        for j in range(PART // span):
            total = total + dot(attended[(w ^ d) * (PART // span) + j], ref[pl.ds(span * j, span), :])
    branch[...] = total
    give(0)
    normal, _ = unit(total)
    total = floats(own[...]) + (normal * small[pl.ds(1, 1), :] + small[pl.ds(5, 1), :])
    resid[...] = total
    give(1)
    normal, _ = unit(total)
    second[...] = (normal * small[pl.ds(2, 1), :] + small[pl.ds(6, 1), :]).astype(BF16)


def join_slots(inn, start, target):
    for i, d in enumerate((0, 2, 1, 3)):
        ref = inn(start + d)
        rows = ref.shape[0]
        target[pl.ds(rows * i, rows), :] = ref[...]


def feed(inn, out, give):
    all_rows, hidden, slope, near, far = out
    w = lax.axis_index("wt")
    join_slots(inn, 0, all_rows)
    give(0)
    ups, bias = [inn(4 + d) for d in range(WT)], inn(8)
    half_rows = near.shape[0]

    @pl.loop(0, hidden.shape[1] // PART)
    def _(n):
        cols = at(n, PART)
        upper = floats(bias[pl.ds(0, 1), cols])
        for d in range(WT):
            upper = upper + dot(all_rows[:, at(w ^ d, PART)], ups[d][:, cols])
        square = upper * upper
        curve = jnp.tanh(GELU_A * (upper + GELU_B * (square * upper)))
        half = 0.5 * (1.0 + curve)
        hidden[:, cols] = (upper * half).astype(BF16)
        slope[:, cols] = half + (0.5 * GELU_A) * upper * (1.0 - curve * curve) * (
            1.0 + (3.0 * GELU_B) * square
        )

    give(1)
    give(2)
    down = inn(9)

    @pl.loop(0, near.shape[1] // PART)
    def _(n):
        cols = at(n, PART)
        total = dot(hidden[...], down[:, cols])
        near[:, cols] = total[:half_rows]
        far[:, cols] = total[half_rows:].astype(BF16)


def returned(inn, rows):
    own = pl.ds(0, rows)
    return inn(0)[own, :] + floats(inn(1)[own, :]) + floats(inn(2)[...])


def top_norm(inn, out, give):
    result, d_ffn, sums = out
    small, resid, grad = inn(3), inn(4), inn(5)
    normal, scale = unit(returned(inn, resid.shape[0]) + small[pl.ds(11, 1), :])
    gain = small[pl.ds(3, 1), :]
    d_out = floats(grad[...])
    low = unit_back(d_out * gain, normal, scale).astype(BF16)
    d_ffn[...] = low
    give(1)
    result[...] = (resid[...] + (normal * gain + small[pl.ds(7, 1), :])).astype(BF16)
    sums[pl.ds(0, 1), :] = column_sum(d_out * normal)
    sums[pl.ds(1, 1), :] = column_sum(d_out)
    sums[pl.ds(2, 1), :] = column_sum(floats(low))


def feed_back(inn, out, give):
    all_rows, d_upper, near, far, sums = out
    w = lax.axis_index("wt")
    join_slots(inn, 0, all_rows)
    give(0)
    down, slope = inn(4), inn(5)
    half_rows = near.shape[0]

    @pl.loop(0, d_upper.shape[1] // PART)
    def _(n):
        cols = at(n, PART)
        low = (dot_t(all_rows[...], down[cols, :]) * slope[:, cols]).astype(BF16)
        d_upper[:, cols] = low
        sums[pl.ds(0, 1), cols] = column_sum(floats(low))

    give(1)
    for d in range(WT):
        cols = at(w ^ d, PART)
        total = dot_t(d_upper[...], inn(6 + d)[...])
        near[:, cols] = total[:half_rows]
        far[:, cols] = total[half_rows:].astype(BF16)


KEPT = ((0, 0, 0), (0, 1, 4), (1, 0, 2), (1, 1, 6))
SENT = ((0, 3), (1, 7), (2, 1), (3, 5))


def places(out):
    sent = [(out[2 + i * (len(out) - 3) // 2], i if len(out) == 3 else i % 2, d) for i, d in SENT]
    return sent + [(out[which], i, d) for which, i, d in KEPT]


def grad_down(inn, out, give):
    c = lax.axis_index("ctx")
    hidden, grads = inn(0), inn(1)
    size = out[0].shape[1]
    for n, (target, i, d) in enumerate(places(out)):
        target[i] = t_dot(hidden[:, at(c ^ d, size)], grads[...]).astype(BF16)
        if n in (1, 3) and len(out) == 4:
            give(2 + n // 2)
        elif n == 3:
            give(2)


def grad_up(inn, out, give, part):
    c = lax.axis_index("ctx")
    cut = PART // CTX
    rows_in, grads = inn(0), inn(1)

    @pl.loop(0, WT)
    def _(k):
        part[...] = t_dot(rows_in[:, at(k, PART)], grads[...]).astype(BF16)
        for target, i, d in places(out):
            target[i, at(k, cut), :] = part[at(c ^ d, cut), :]


def middle_norms(inn, out, give):
    sent, d_att, d_resid, sums = out
    w = lax.axis_index("wt")
    small, resid, branch, grad = inn(3), inn(4), inn(5), inn(6)
    rows, span = resid.shape[0], sent.shape[2]
    normal3, scale3 = unit(resid[...])
    normal2, scale2 = unit(branch[...])
    d_second = returned(inn, rows)
    total = floats(grad[...]) + unit_back(d_second * small[pl.ds(2, 1), :], normal3, scale3)
    low = unit_back(total * small[pl.ds(1, 1), :], normal2, scale2).astype(BF16)
    d_att[...] = low
    d_resid[...] = total
    give(2)
    for d in (1, 2, 3, 0):
        part = dot_t(low, inn(7 + d)[...]).astype(BF16)
        for j in range(PART // span):
            sent[(w ^ d) * (PART // span) + j] = part[:, span * j : span * (j + 1)]
    sums[pl.ds(0, 1), :] = column_sum(d_second * normal3)
    sums[pl.ds(1, 1), :] = column_sum(d_second)
    sums[pl.ds(2, 1), :] = column_sum(total * normal2)
    sums[pl.ds(3, 1), :] = column_sum(total)
    sums[pl.ds(4, 1), :] = column_sum(floats(low))


def grad_out(inn, out, give):
    w = lax.axis_index("wt")
    attended, grads = inn(0), inn(1)
    span = attended.shape[2]
    for d in (1, 3, 0, 2):
        for j in range(PART // span):
            part = t_dot(attended[(w ^ d) * (PART // span) + j], grads[...])
            out[d % 2][d // 2, pl.ds(span * j, span), :] = part.astype(BF16)
        if d == 3:
            give(1)


def attend_back(inn, out, give, d_out, d_keys, d_values):
    natural, dealt = out
    deal, mixed, stats, got = (inn(i) for i in range(4))
    length, span = d_out.shape
    heads = stats.shape[0] // 2
    head = span // heads
    factor = 1.0 / math.sqrt(head)
    prescale = factor / relax
    for j in range(CTX):
        for t in range(2):
            d_out[at(deal[j, t], PIECE), :] = got[j, pl.ds(PIECE * t, PIECE), :]
    lane = lax.broadcasted_iota(jnp.int32, (BLK, span), 1) // head
    d_keys[...] = jnp.zeros_like(d_keys)
    d_values[...] = jnp.zeros_like(d_values)
    for b in range(length // BLK):
        rows, seen = pl.ds(b * BLK, BLK), pl.ds(0, (b + 1) * BLK)
        query, grads = mixed[rows, pl.ds(0, span)], d_out[rows, :]
        parts = []
        for h in range(heads):
            query_h = jnp.where(lane == h, query, jnp.zeros_like(query))
            grads_h = jnp.where(lane == h, grads, jnp.zeros_like(grads))
            keys = mixed[seen, pl.ds(span, span)]
            raw = dot_t(keys, query_h)
            weights = jnp.exp((raw - stats[pl.ds(2 * h, 1), rows]) * factor) * stats[pl.ds(2 * h + 1, 1), rows]
            d_probs = dot_t(mixed[seen, pl.ds(2 * span, span)], grads_h)
            delta = jnp.sum(weights * d_probs, axis=0, keepdims=True)
            d_scores = (relax * weights * (d_probs - delta)).astype(BF16)
            d_values[seen, :] += dot(weights.astype(BF16), grads_h)
            d_keys[seen, :] += dot(d_scores, query_h)
            parts.append(t_dot(keys, d_scores)[h * head : (h + 1) * head, :])
        natural[rows, pl.ds(0, span)] = (jnp.concatenate(parts, axis=0).T * prescale).astype(BF16)
    natural[:, pl.ds(span, span)] = (d_keys[...] * prescale).astype(BF16)
    natural[:, pl.ds(2 * span, span)] = d_values[...].astype(BF16)
    for j in range(CTX):
        for t in range(2):
            dealt[j, pl.ds(PIECE * t, PIECE), :] = natural[at(deal[j, t], PIECE), :]


def grad_qkv(inn, out, give):
    w = lax.axis_index("wt")
    first, grads = inn(0), inn(1)
    for d in (1, 3, 0, 2):
        out[d % 2][d // 2] = t_dot(first[:, at(w ^ d, PART)], grads[...]).astype(BF16)
        if d == 3:
            give(1)


def bottom_norm(inn, out, give, joined, d_first):
    input_grad, keep, send = out
    w = lax.axis_index("wt")
    got, own, d_resid, small = (inn(i) for i in range(4))
    _, rows, triple = got.shape
    span, width = triple // 3, own.shape[1]
    for j in range(CTX):
        for part in range(3):
            joined[:, pl.ds(part * width + span * j, span)] = got[j, :, pl.ds(span * part, span)]
    for d in range(WT):
        d_first[:, at(w ^ d, PART)] = dot_t(joined[...], inn(4 + d)[...])
    normal, scale = unit(floats(own[...]))
    grads = d_first[...]
    input_grad[...] = d_resid[...] + unit_back(grads * small[pl.ds(0, 1), :], normal, scale)
    give(0)
    middle, top, up = inn(8), inn(9), inn(10)
    lines = {
        0: column_sum(grads * normal),
        4: column_sum(grads),
        8: column_sum(floats(joined[:, pl.ds(0, width)])),
        9: column_sum(floats(joined[:, pl.ds(2 * width, width)])),
    }
    for i, line in enumerate((2, 6, 1, 5, 10)):
        lines[line] = middle[pl.ds(i, 1), :]
    for i, line in enumerate((3, 7, 11)):
        lines[line] = top[pl.ds(i, 1), :]
    for line, value in lines.items():
        d_first[pl.ds(line, 1), :] = value
    for d in range(WT):
        target = send if d % 2 else keep
        target[d // 2, pl.ds(0, 12), :] = d_first[pl.ds(0, 12), at(w ^ d, PART)]
        target[d // 2, pl.ds(12, 4), :] = jnp.zeros((4, PART), F32)
    for i in range(4):
        keep[0, pl.ds(12 + i, 1), :] = up[:, pl.ds(PART * i, PART)]


def add_second(inn, out, give):
    out[0][...] = (floats(inn(0)[1]) + floats(inn(1)[1])).astype(out[0].dtype)


def add_rest(inn, out, give):
    rows = out[0].shape[0]
    rest = pl.ds(rows, rows)
    out[0][...] = (inn(0)[rest, :] + floats(inn(1)[rest, :])).astype(BF16)


def add_high(inn, out, give):
    keep, got = inn(0), inn(1)
    for i in range(2):
        out[0][i] = (floats(keep[i]) + floats(got[i])).astype(BF16)


def add_high_last(inn, out, give):
    keep, got = inn(0), inn(1)
    for i in range(2):
        out[0][i] = (floats(keep[2 + i]) + floats(got[2 + i])).astype(BF16)


def add_low(first, inn, out, give):
    keep, got, after_z = inn(0), inn(1), inn(2)
    out[1][...] = (floats(keep[1]) + floats(got[first + 1]) + floats(after_z[1])).astype(BF16)
    out[0][...] = floats(keep[0]) + floats(got[first]) + floats(after_z[0])


def add_last(inn, out, give):
    out[0][...] = (inn(0)[...] + floats(inn(1)[...])).astype(BF16)


def add_out(inn, out, give, total):
    c = lax.axis_index("ctx")
    cut = out[0].shape[1]
    total[...] = (floats(inn(0)[0]) + floats(inn(1)[0]) + floats(inn(2)[...])).astype(BF16)
    for i, d in enumerate((0, 4, 2, 6)):
        out[0][i] = total[at(c ^ d, cut), :]
        out[1][i] = total[at(c ^ d ^ 1, cut), :]


def add_last_up(inn, out, give, total):
    w = lax.axis_index("wt")
    cut = out[0].shape[0]
    total[...] = (inn(0)[...] + floats(inn(1)[...])).astype(BF16)
    for d in range(WT):
        out[d][...] = total[at(w ^ d, cut), :]


def pack_up(inn, out, give):
    rows = inn(0).shape[0]
    for i in range(WT):
        out[0][pl.ds(rows * i, rows), :] = inn(i)[...]


def pack_mixed(inn, out, give, small):
    block = out[0]
    rows = inn(0).shape[1]
    block[pl.ds(0, rows), :] = (floats(inn(0)[0]) + floats(inn(1)[0]) + floats(inn(2)[...])).astype(BF16)
    cut, lanes = inn(3).shape[0], 128
    small[...] = jnp.zeros_like(small)
    small[pl.ds(0, cut), :] = (inn(3)[...] + floats(inn(4)[...])).astype(BF16)
    small[pl.ds(cut, SMALL), pl.ds(0, PART)] = (inn(5)[0] + inn(6)[0] + inn(7)[...]).astype(BF16)
    height, across = small.shape[0], block.shape[1] // lanes
    tiles = small.shape[1] // lanes
    for k in range(-(-tiles // across) * across):
        part = small[:, pl.ds(lanes * k, lanes)] if k < tiles else jnp.zeros((height, lanes), BF16)
        block[pl.ds(rows + height * (k // across), height), pl.ds(lanes * (k % across), lanes)] = part


def spread_mixed(inn, out, give, total):
    full, proj, gain, shift, bias, up_bias = out
    c = lax.axis_index("ctx")
    span = full.shape[1] // (3 * CTX)
    cut, lanes, rows = PART // CTX, 128, full.shape[0]
    height, across = cut + SMALL, inn(0).shape[1] // lanes
    total[...] = jnp.zeros_like(total)
    for d in range(CTX):
        block = inn(d)
        for part in range(3):
            full[:, at(part * CTX + (c ^ d), span)] = floats(block[pl.ds(0, rows), pl.ds(span * part, span)])
        for k in range(proj.shape[1] // lanes):
            top, left = rows + height * (k // across), pl.ds(lanes * (k % across), lanes)
            proj[at(c ^ d, cut), pl.ds(lanes * k, lanes)] = floats(block[pl.ds(top, cut), left])
            if lanes * k < PART:
                total[:, pl.ds(lanes * k, lanes)] += floats(block[pl.ds(top + cut, SMALL), left])
    for i, ref in enumerate((gain, shift, bias)):
        ref[...] = total[pl.ds(4 * i, 4), :]
    for i in range(4):
        up_bias[pl.ds(PART * i, PART)] = total[12 + i, :]


def spread_down(inn, out, give, sems, result):
    c = lax.axis_index("ctx")
    stores = []
    for d in range(CTX):
        block = inn(d)
        rows = at(c ^ d, block.shape[0])
        out[0][rows, :] = floats(block[...])
        stores.append(pltpu.make_async_copy(out[0].at[rows, :], result.at[rows, :], sems.at[d]))
        stores[-1].start()
    for store in stores:
        store.wait()


def spread_up(inn, out, give, sems, result):
    c, w = lax.axis_index("ctx"), lax.axis_index("wt")
    cut = PART // CTX
    width = out[0].shape[1] // WT
    stores = []
    for d in range(CTX):
        block, rows = inn(d), at(c ^ d, cut)
        for k in range(WT):
            out[0][rows, at(w ^ k, width)] = floats(block[pl.ds(cut * k, cut), :])
        stores.append(pltpu.make_async_copy(out[0].at[rows, :], result.at[rows, :], sems.at[d]))
        stores[-1].start()
    for store in stores:
        store.wait()


def split_device(
    layer_input,
    out_grad,
    deal,
    w_qkv,
    w_out,
    w_up,
    w_down,
    norm_gain,
    norm_shift,
    bias_width,
    up_bias,
):
    _, rows, width = layer_input.shape
    w = lax.axis_index("wt")
    per = HEADS // CTX
    span = per * (width // HEADS)
    length = rows * CTX
    hidden_width = w_down.shape[0]
    everyone = WT * rows
    own, grad = layer_input[0], out_grad[0]
    vmem, dma = pltpu.VMEM, pltpu.SemaphoreType.DMA

    sequence = gather_ctx(own)
    begin = lax.optimization_barrier((w_qkv, w_up, norm_gain, norm_shift, bias_width, sequence[1]))[:5]
    pack, *ups = call(
        prepare,
        "prepare",
        begin,
        [shape(PART + SMALL, 3 * span)] + [shape(PART, hidden_width)] * 3,
        raw=(0, 1),
        hbm=(2, 3, 4),
        scratch=[dma((6,))],
    )
    packs = gather_wt(pack)
    up_core, up_x, up_both = ups
    outs_x = swap(after(w_out, packs[2]), "wt", 2)
    up_x = swap(after(up_x, packs[2]), "wt", 2)

    first, mixed, sent, stats, small = call(
        attend,
        "attend",
        (deal, *packs, *sequence),
        [
            shape(length, width),
            shape(length, 3 * span),
            shape(CTX, rows, span),
            shape(2 * per, length, dtype=F32),
            shape(SMALL, width, dtype=F32),
        ],
        smem=1,
        hbm=range(1, 1 + WT),
        raw=range(1 + WT, 1 + WT + CTX),
        hbm_out=(0, 1),
        scratch=[vmem((length, width), BF16), vmem((length, span), BF16), dma((2 * CTX,))],
    )
    attended = lax.all_to_all(after(sent, outs_x, up_x), "ctx", 0, 0, tiled=True)
    up_both = swap(up_both, "wt", 3)
    outs_own, outs_x, up_core = lax.optimization_barrier((w_out, outs_x, up_core, sent))[:3]
    outs = w_out, swap(outs_own, "wt", 1), outs_x, swap(outs_x, "wt", 1)
    ups = w_up, swap(up_core, "wt", 1), up_x, up_both
    attended = after(attended, *outs, *ups[1:])

    branch, resid, second = call(
        project,
        "project",
        (small, attended, own, *outs),
        [shape(rows, width, dtype=F32), shape(rows, width, dtype=F32), shape(rows, width)],
    )

    own_columns = ((PART, hidden_width), lambda ref: ref.at[:, at(lax.axis_index("wt"), hidden_width)])
    halves = [shape(2 * rows, width, dtype=F32), shape(2 * rows, width)]
    seconds, hidden, slope, near, far = call(
        feed,
        "feed",
        (*gather_wt(second), *ups, up_bias.reshape(1, hidden_width), w_down),
        [shape(everyone, width), shape(everyone, hidden_width), shape(everyone, hidden_width, dtype=F32)]
        + halves,
        hbm=(4, 8, 9),
        hbm_out=(0,),
        views={4: own_columns},
    )

    def return_rows(near, far):
        got = swap(far, "wt", 1)
        back = call(add_rest, "add_rest", (near, got), [shape(rows, width)])
        return near, got, swap(back, "wt", 2)

    result, d_ffn, sums3 = call(
        top_norm,
        "top_norm",
        (*return_rows(near, far), small, resid, grad),
        [shape(rows, width), shape(rows, width), shape(3, width, dtype=F32)],
    )
    d_ffns, d_upper, near, far, up_sum = call(
        feed_back,
        "feed_back",
        (*gather_wt(d_ffn), w_down, slope, *ups),
        [shape(everyone, width), shape(everyone, hidden_width)] + halves + [shape(1, hidden_width, dtype=F32)],
        hbm=(4, 6),
        views={6: own_columns},
    )
    got = swap(far, "wt", 1)
    def sends(terms):
        if len(terms) == 3:
            whole = swap(terms[2], "ctx", 1)
            return (whole, 0), (whole, 2)
        return (swap(terms[2], "ctx", 1), 0), (swap(terms[3], "ctx", 1), 0)

    def chunks(split):
        sent = [shape(2, eighth, width)] * 2 if split else [shape(4, eighth, width)]
        return [shape(2, eighth, width)] * 2 + sent

    def added_high(name, terms, got):
        return call(
            add_high,
            "add_high_" + name,
            (terms[1], got),
            [shape(2, eighth, width)],
            hbm=(0,),
        )

    def added_low(name, terms, got, along):
        return call(
            functools.partial(add_low, got[1]),
            "add_low_" + name,
            (terms[0], got[0], along),
            [shape(eighth, width, dtype=F32), shape(eighth, width)],
            hbm=(0,),
        )

    eighth = hidden_width // CTX
    cut = PART // CTX
    terms_a = call(
        grad_down, "grad_down", (hidden, d_ffns), chunks(SPLIT[0]), hbm_out=range(3 + SPLIT[0])
    )
    high_got_a, low_got_a = sends(terms_a)
    back = call(add_rest, "add_rest", (after(near, terms_a[2]), got), [shape(rows, width)])
    far = swap(back, "wt", 2)
    terms_b = call(
        grad_up,
        "grad_up",
        (seconds, d_upper),
        chunks(SPLIT[1]),
        hbm=(0,),
        hbm_out=range(3 + SPLIT[1]),
        scratch=[vmem((PART, hidden_width), BF16)],
    )
    high_got_b, low_got_b = sends(terms_b)
    high_a = added_high("a", terms_a, high_got_a[0])
    next_a = swap(high_a, "ctx", 2)
    sent, d_att, d_resid, sums21 = call(
        middle_norms,
        "middle_norms",
        (near, got, far, small, resid, branch, grad, *outs),
        [
            shape(CTX, rows, span),
            shape(rows, width),
            shape(rows, width, dtype=F32),
            shape(5, width, dtype=F32),
        ],
    )
    got = lax.all_to_all(sent, "ctx", 0, 0, tiled=True)
    pieces = [shape(2, PART, width)] * 2
    keep_out, send_out = call(
        grad_out, "grad_out", (attended, d_att), pieces, hbm_out=(0, 1)
    )
    got_out = swap(send_out, "wt", 1)
    back_out = call(
        add_second,
        "add_second_out",
        (keep_out, got_out),
        [shape(PART, width)],
        hbm=(0,),
    )
    out_x = swap(back_out, "wt", 2)
    high_b = added_high("b", terms_b, after(high_got_b[0], got))
    next_b = swap(high_b, "ctx", 2)
    first_a, second_a = added_low("a", terms_a, low_got_a, next_a)
    last_a = swap(second_a, "ctx", 4)

    natural, dealt = call(
        attend_back,
        "attend_back",
        (deal, mixed, stats, got),
        [shape(length, 3 * span), shape(CTX, rows, 3 * span)],
        smem=1,
        hbm=(1,),
        scratch=[vmem((length, span), BF16), vmem((length, span), F32), vmem((length, span), F32)],
    )
    first_b, second_b = added_low("b", terms_b, low_got_b, after(next_b, low_got_a[0]))
    last_b = swap(second_b, "ctx", 4)
    part_a = call(add_last, "add_last_a", (first_a, last_a), [shape(eighth, width)])
    down_slots = gather_free(after(part_a, back), go2=(high_b, back,), go1=(terms_b[2],))
    pieces = [shape(2, PART, 3 * span)] * 2
    keep_qkv, send_qkv = call(
        grad_qkv, "grad_qkv", (first, after(natural, last_a, second_b)), pieces, hbm=(0,), hbm_out=(0, 1)
    )
    keep_c, send_c = call(
        add_out,
        "add_out",
        (keep_out, got_out, after(out_x, natural, last_b)),
        [shape(4, cut, width)] * 2,
        hbm=(0,),
        scratch=[vmem((PART, width), BF16)],
    )
    got_c = swap(send_c, "ctx", 1)
    got_rows = lax.all_to_all(after(dealt, down_slots[1], send_c), "ctx", 0, 0, tiled=True)
    got_qkv = swap(send_qkv, "wt", 1)
    back_qkv = call(
        add_second,
        "add_second_qkv",
        (keep_qkv, got_qkv),
        [shape(PART, 3 * span)],
        hbm=(0,),
    )
    qkv_x = swap(back_qkv, "wt", 2)
    own_up, *up_parts = call(
        add_last_up,
        "add_last_up",
        (first_b, after(last_b, part_a, terms_b[2])),
        [shape(cut, width)] * WT,
        scratch=[vmem((eighth, width), BF16)],
    )
    up_parts = [swap(part, "wt", d) for part, d in zip(up_parts, (1, 2, 3))]
    up_block = call(
        pack_up, "pack_up", (after(own_up, down_slots[1], send_c), *up_parts), [shape(eighth, width)]
    )
    up_slots = gather_free(up_block, far=(next_a,))
    weights_x = swap(after(w_qkv, far), "wt", 2)
    qkv_own, weights_x = after(w_qkv, second_b), weights_x
    all_qkv = w_qkv, swap(qkv_own, "wt", 1), weights_x, swap(weights_x, "wt", 1)
    high_c = call(
        add_high_last, "add_high_c", (keep_c, got_c), [shape(2, cut, width)]
    )
    next_c = swap(high_c, "ctx", 2)
    first_c, second_c = call(
        functools.partial(add_low, 0),
        "add_low_c",
        (keep_c, got_c, after(next_c, low_got_a[0])),
        [shape(cut, width, dtype=F32), shape(cut, width)],
    )
    last_c = swap(second_c, "ctx", 4)
    input_grad, keep, send = call(
        bottom_norm,
        "bottom_norm",
        (after(got_rows, back_qkv), own, d_resid, small, *all_qkv, sums21, sums3, up_sum),
        [shape(rows, width, dtype=F32)] + [shape(2, SMALL, PART, dtype=F32)] * 2,
        hbm=(1, 2, 4, 5, 6, 7),
        hbm_out=(0,),
        scratch=[vmem((rows, 3 * width), BF16), vmem((rows, width), F32)],
    )
    got_sums = swap(send, "wt", 1)
    back_sums = call(add_second, "add_second_sums", (keep, got_sums), [shape(SMALL, PART, dtype=F32)])
    sums_x = swap(back_sums, "wt", 2)
    mixed_block = call(
        pack_mixed,
        "pack_mixed",
        (keep_qkv, got_qkv, after(qkv_x, up_slots[3], sums_x), first_c, last_c, keep, got_sums, sums_x),
        [shape(PART + 3 * (cut + SMALL), 3 * span)],
        hbm=(0,),
        scratch=[vmem((cut + SMALL, width), BF16)],
    )
    mixed_slots = gather_ctx_z(mixed_block)
    full_qkv, full_out, gain, shift, bias, up_total = call(
        spread_mixed,
        "spread_mixed",
        mixed_slots,
        [shape(PART, 3 * width, dtype=F32), shape(PART, width, dtype=F32)]
        + [shape(4, PART, dtype=F32)] * 3
        + [shape(hidden_width, dtype=F32)],
        hbm_out=range(6),
        scratch=[vmem((SMALL, PART), F32)],
    )
    full_down = call(
        spread_down,
        "spread_down",
        down_slots,
        [shape(hidden_width, width, dtype=F32)],
        hbm_out=(0,),
        scratch=[dma((CTX,))],
        parts=(0,),
    )
    full_up = call(
        spread_up,
        "spread_up",
        up_slots,
        [shape(PART, WT * hidden_width, dtype=F32)],
        hbm_out=(0,),
        scratch=[dma((CTX,))],
        parts=(0,),
    )
    return (
        result[None],
        input_grad[None],
        full_qkv,
        full_out,
        full_up,
        full_down,
        gain,
        shift,
        bias,
        up_total,
    )


def solution(mesh):
    small = mesh.shape["ctx"] == CTX and mesh.shape["wt"] == WT
    per_device = split_device if small else general_device
    in_specs = (
        P("wt", "ctx", None),
        P("wt", "ctx", None),
        P(),
        P("wt", None),
        P("wt", None),
        P("wt", None),
        P("wt", None),
        P(None, "wt"),
        P(None, "wt"),
        P(None, "wt"),
        P("wt"),
    )
    out_specs = (
        P("wt", "ctx", None),
        P("wt", "ctx", None),
        P("wt", None),
        P("wt", None),
        P("wt", None),
        P("wt", None),
        P(None, "wt"),
        P(None, "wt"),
        P(None, "wt"),
        P("wt"),
    )
    return jax.shard_map(
        per_device, mesh=mesh, in_specs=in_specs, out_specs=out_specs, check_vma=False
    )
```

```python
import functools
import math

import jax
import jax.numpy as jnp
from jax import lax
from jax.experimental import pallas as pl
from jax.experimental.pallas import tpu as pltpu
from jax.sharding import PartitionSpec as P

HEADS = 16
BLK = 256
PIECE = 64


epsilon = 1e-05
relax = 32.0


def layer_norm(value, gain, shift):
    mean = jnp.mean(value, axis=-1, keepdims=True)
    centered = value - mean
    spread = jnp.mean(centered * centered, axis=-1, keepdims=True)
    return centered * lax.rsqrt(spread + epsilon) * gain + shift


def gelu_tanh(value):
    return jax.nn.gelu(value, approximate=True)


def rows_dot(left, weight):
    return jnp.einsum("std,de->ste", left, weight, preferred_element_type=jnp.float32)


def weight_grad(left, right):
    return jnp.einsum("std,ste->de", left, right, preferred_element_type=jnp.float32)


def back_dot(grad, weight):
    return jnp.einsum("ste,de->std", grad, weight, preferred_element_type=jnp.float32)


def row_total(value):
    return jnp.sum(value.astype(jnp.float32), axis=(0, 1))


def general_device(
    layer_input,
    out_grad,
    deal,
    w_qkv,
    w_out,
    w_up,
    w_down,
    norm_gain,
    norm_shift,
    bias_width,
    up_bias,
):
    seqs, rows, width = layer_input.shape
    heads = HEADS
    head = width // heads
    prescale = 1.0 / (relax * math.sqrt(head))
    ranks = lax.axis_size("ctx")
    length = rows * ranks
    per_block = BLK // PIECE
    rank = lax.axis_index("ctx")
    chosen = jnp.arange(ranks, dtype=jnp.int32) == rank
    mine = jnp.sum(jnp.where(chosen[:, None], deal, 0), axis=0)
    query_blocks = jnp.repeat(mine, rows // 2) // per_block
    key_blocks = jnp.repeat(deal.reshape(-1), rows // 2) // per_block
    full_qkv, full_out, full_up, full_down, gains, shifts, biases, up_shift = (
        lax.all_gather(w_qkv, "wt", axis=0, tiled=True),
        lax.all_gather(w_out, "wt", axis=0, tiled=True),
        lax.all_gather(w_up, "wt", axis=0, tiled=True),
        lax.all_gather(w_down, "wt", axis=0, tiled=True),
        lax.all_gather(norm_gain, "wt", axis=1, tiled=True),
        lax.all_gather(norm_shift, "wt", axis=1, tiled=True),
        lax.all_gather(bias_width, "wt", axis=1, tiled=True),
        lax.all_gather(up_bias, "wt", axis=0, tiled=True),
    )
    gains = gains.astype(jnp.float32)
    shifts = shifts.astype(jnp.float32)
    biases = biases.astype(jnp.float32)
    up_shift = up_shift.astype(jnp.float32)
    input_float = layer_input.astype(jnp.float32)
    first = layer_norm(input_float, gains[0], shifts[0]).astype(jnp.bfloat16)
    mixed = rows_dot(first, full_qkv)
    query = (mixed[..., :width] + biases[0]).astype(jnp.bfloat16)
    kv_local = jnp.concatenate(
        [mixed[..., width : 2 * width], mixed[..., 2 * width :] + biases[1]], axis=-1
    ).astype(jnp.bfloat16)
    kv_all = lax.all_gather(kv_local, "ctx", axis=1, tiled=True)
    step = math.gcd(length, 1024)
    count = length // step
    query4 = query.reshape(seqs, rows, heads, head)

    def score_block(left, right):
        return (
            jnp.einsum("sqhd,skhd->shqk", left, right, preferred_element_type=jnp.float32)
            * prescale
        )

    def key_block(index):
        start = index * step
        piece = lax.dynamic_slice_in_dim(kv_all, start, step, 1)
        keys4 = piece[..., :width].reshape(seqs, step, heads, head)
        values4 = piece[..., width:].reshape(seqs, step, heads, head)
        visible = (
            query_blocks[:, None] >= lax.dynamic_slice_in_dim(key_blocks, start, step, 0)[None, :]
        )
        return (keys4, values4, visible)

    def probs(raw, visible, totals):
        return jnp.where(visible, jnp.exp(raw * relax - totals[..., None]), 0.0)

    def online(index, carry):
        top, total, acc = carry
        keys4, values4, visible = key_block(index)
        raw = jnp.where(visible, score_block(query4, keys4), -1e30)
        new_top = jnp.maximum(top, jnp.max(raw, axis=-1))
        terms = jnp.where(visible, jnp.exp((raw - new_top[..., None]) * relax), 0.0)
        factor = jnp.exp((top - new_top) * relax)
        total = total * factor + jnp.sum(terms, axis=-1)
        acc = acc * jnp.transpose(factor, (0, 2, 1))[..., None]
        acc = acc + jnp.einsum(
            "shqk,skhd->sqhd",
            terms.astype(jnp.bfloat16),
            values4,
            preferred_element_type=jnp.float32,
        )
        return (new_top, total, acc)

    start_top = jnp.full((seqs, heads, rows), -1e30, jnp.float32)
    start_total = jnp.zeros((seqs, heads, rows), jnp.float32)
    start_acc = jnp.zeros((seqs, rows, heads, head), jnp.float32)
    top, total, acc = lax.fori_loop(0, count, online, (start_top, start_total, start_acc))
    log_total = top * relax + jnp.log(total)
    attended_float = acc / jnp.transpose(total, (0, 2, 1))[..., None]
    attended = attended_float.reshape(seqs, rows, width).astype(jnp.bfloat16)
    branch = rows_dot(attended, full_out) + biases[2]
    resid = input_float + layer_norm(branch, gains[1], shifts[1])
    second = layer_norm(resid, gains[2], shifts[2]).astype(jnp.bfloat16)
    upper = rows_dot(second, full_up) + up_shift
    hidden = gelu_tanh(upper).astype(jnp.bfloat16)
    ffn = rows_dot(hidden, full_down) + biases[3]
    top_norm, pull_four = jax.vjp(layer_norm, ffn, gains[3], shifts[3])
    result = resid + top_norm
    d_out = out_grad.astype(jnp.float32)
    d_ffn, d_gain3, d_shift3 = pull_four(d_out)
    d_ffn = d_ffn.astype(jnp.bfloat16)
    d_bias3 = row_total(d_ffn)
    g_down = weight_grad(hidden, d_ffn)
    d_hidden = back_dot(d_ffn, full_down)
    _, pull_gelu = jax.vjp(gelu_tanh, upper)
    d_upper = pull_gelu(d_hidden)[0].astype(jnp.bfloat16)
    d_up_shift = row_total(d_upper)
    g_up = weight_grad(second, d_upper)
    d_second = back_dot(d_upper, full_up)
    _, pull_three = jax.vjp(layer_norm, resid, gains[2], shifts[2])
    d_resid_part, d_gain2, d_shift2 = pull_three(d_second)
    d_resid = d_out + d_resid_part
    _, pull_two = jax.vjp(layer_norm, branch, gains[1], shifts[1])
    d_branch, d_gain1, d_shift1 = pull_two(d_resid)
    d_branch = d_branch.astype(jnp.bfloat16)
    d_bias2 = row_total(d_branch)
    g_out = weight_grad(attended, d_branch)
    d_attended = back_dot(d_branch, full_out).astype(jnp.bfloat16)
    d_out4 = d_attended.reshape(seqs, rows, heads, head)
    delta = jnp.einsum("sqhd,sqhd->shq", d_out4.astype(jnp.float32), attended_float)

    def score_grads(q_rows, do_rows, k_rows, v_rows, visible, lse_rows, delta_rows):
        weights = probs(score_block(q_rows, k_rows), visible, lse_rows)
        d_probs = jnp.einsum("sqhd,skhd->shqk", do_rows, v_rows, preferred_element_type=jnp.float32)
        d_scores = (relax * weights * (d_probs - delta_rows[..., None])).astype(jnp.bfloat16)
        return (d_scores, weights.astype(jnp.bfloat16))

    zero_query = jnp.zeros((seqs, rows, heads, head), jnp.float32)

    def local_grads(d_query, index):
        keys4, values4, visible = key_block(index)
        d_scores, weights = score_grads(query4, d_out4, keys4, values4, visible, log_total, delta)
        d_query = (
            d_query
            + jnp.einsum("shqk,skhd->sqhd", d_scores, keys4, preferred_element_type=jnp.float32)
            * prescale
        )
        d_keys = (
            jnp.einsum("shqk,sqhd->kshd", d_scores, query4, preferred_element_type=jnp.float32)
            * prescale
        )
        d_values = jnp.einsum(
            "shqk,sqhd->kshd", weights, d_out4, preferred_element_type=jnp.float32
        )
        joined = jnp.concatenate(
            [d_keys.reshape(step, seqs, width), d_values.reshape(step, seqs, width)], axis=-1
        )
        return (d_query, joined)

    d_query, pieces = lax.scan(local_grads, zero_query, jnp.arange(count, dtype=jnp.int32))
    terms = pieces.reshape(length, seqs, 2 * width)
    d_kv = jnp.transpose(lax.psum_scatter(terms, "ctx", scatter_dimension=0, tiled=True), (1, 0, 2))
    d_query = d_query.reshape(seqs, rows, width).astype(jnp.bfloat16)
    d_kv = d_kv.astype(jnp.bfloat16)
    d_bias0 = row_total(d_query)
    d_bias1 = row_total(d_kv[..., width:])
    d_mixed = jnp.concatenate([d_query, d_kv], axis=-1)
    g_qkv = weight_grad(first, d_mixed)
    d_first = back_dot(d_mixed, full_qkv)
    _, pull_one = jax.vjp(layer_norm, input_float, gains[0], shifts[0])
    d_input_part, d_gain0, d_shift0 = pull_one(d_first)
    input_grad = d_resid + d_input_part
    grad_gain = jnp.stack([d_gain0, d_gain1, d_gain2, d_gain3])
    grad_shift = jnp.stack([d_shift0, d_shift1, d_shift2, d_shift3])
    grad_bias = jnp.stack([d_bias0, d_bias1, d_bias2, d_bias3])
    owned = (
        lax.psum_scatter(g_qkv.astype(jnp.bfloat16), "wt", scatter_dimension=0, tiled=True).astype(
            jnp.float32
        ),
        lax.psum_scatter(g_out.astype(jnp.bfloat16), "wt", scatter_dimension=0, tiled=True).astype(
            jnp.float32
        ),
        lax.psum_scatter(g_up.astype(jnp.bfloat16), "wt", scatter_dimension=0, tiled=True).astype(
            jnp.float32
        ),
        lax.psum_scatter(g_down.astype(jnp.bfloat16), "wt", scatter_dimension=0, tiled=True).astype(
            jnp.float32
        ),
        lax.psum_scatter(
            grad_gain.astype(jnp.bfloat16), "wt", scatter_dimension=1, tiled=True
        ).astype(jnp.float32),
        lax.psum_scatter(
            grad_shift.astype(jnp.bfloat16), "wt", scatter_dimension=1, tiled=True
        ).astype(jnp.float32),
        lax.psum_scatter(
            grad_bias.astype(jnp.bfloat16), "wt", scatter_dimension=1, tiled=True
        ).astype(jnp.float32),
        lax.psum_scatter(
            d_up_shift.astype(jnp.bfloat16), "wt", scatter_dimension=0, tiled=True
        ).astype(jnp.float32),
    )
    summed = lax.psum(
        (owned[0], owned[1], owned[2], owned[3], owned[4], owned[5], owned[6], owned[7]), "ctx"
    )
    return (
        result.astype(jnp.bfloat16),
        input_grad,
        summed[0],
        summed[1],
        summed[2],
        summed[3],
        summed[4],
        summed[5],
        summed[6],
        summed[7],
    )


F32 = jnp.float32
BF16 = jnp.bfloat16
WT = 4
CTX = 8
PART = 256
SMALL = 16
GELU_A = math.sqrt(2.0 / math.pi)
GELU_B = 0.044715
SPLIT = (0, 1)


def swap(value, axis, bit):
    size = lax.axis_size(axis)
    return lax.ppermute(value, axis, [(i, i ^ bit) for i in range(size)])


def gather_wt(block):
    far = swap(block, "wt", 2)
    return block, swap(block, "wt", 1), far, swap(far, "wt", 1)


def gather_ctx(block):
    far, near, side = (swap(block, "ctx", bit) for bit in (4, 2, 1))
    near = after(near, side)
    near_side = swap(near, "ctx", 1)
    far = after(far, near_side)
    corner = swap(far, "ctx", 2)
    far_side = swap(far, "ctx", 1)
    return [block, side, near, near_side, far, far_side, corner, swap(after(corner, far_side), "ctx", 1)]


def held(value, others):
    return after(value, *others) if others else value


def gather_free(block, go4=(), go2=(), go1=(), near=(), far=(), corner=()):
    far_z = held(swap(held(block, go4), "ctx", 4), far)
    near_z = held(swap(held(block, go2), "ctx", 2), near)
    side = swap(held(block, go1), "ctx", 1)
    near_side, corner_z, far_side = swap(near_z, "ctx", 1), swap(far_z, "ctx", 2), swap(far_z, "ctx", 1)
    corner_z = held(corner_z, corner)
    return [block, side, near_z, near_side, far_z, far_side, corner_z, swap(corner_z, "ctx", 1)]


def gather_ctx_z(block):
    blocks = {0: block}
    for bit in (1, 4, 2):
        blocks.update({d ^ bit: swap(value, "ctx", bit) for d, value in blocks.items()})
    return [blocks[d] for d in range(CTX)]


def after(value, *others):
    return lax.optimization_barrier((value, *others))[0]


def floats(value):
    return value.astype(F32)


def dot(left, right):
    return jnp.dot(left, right, preferred_element_type=F32)


def dot_t(left, right):
    return lax.dot_general(left, right, (((1,), (1,)), ((), ())), preferred_element_type=F32)


def t_dot(left, right):
    return lax.dot_general(left, right, (((0,), (0,)), ((), ())), preferred_element_type=F32)


def at(start, size):
    return pl.ds(pl.multiple_of(start * size, size), size)


def shape(*dims, dtype=jnp.bfloat16):
    return jax.ShapeDtypeStruct(dims, dtype)


def call(body, name, ins, outs, smem=0, raw=(), hbm=(), views=None, hbm_out=(), scratch=(), parts=(), slack=10):
    views = views or {}
    ends = [i for i in hbm_out if i not in parts]
    vmem, dma = pltpu.VMEM, pltpu.SemaphoreType.DMA

    def kernel(*refs):
        sources, results = refs[: len(ins)], list(refs[len(ins) : len(ins) + len(outs)])
        rest = list(refs[len(ins) + len(outs) :])
        buffers = {i: rest.pop(0) for i in hbm}
        targets = {i: rest.pop(0) for i in hbm_out}
        in_sems, out_sems = rest.pop(0), rest.pop(0)
        loads, stores = {}, {}
        for i in hbm:
            source = views[i][1](sources[i]) if i in views else sources[i]
            loads[i] = pltpu.make_async_copy(source, buffers[i], in_sems.at[i])
            loads[i].start()

        def inn(i):
            if i not in buffers:
                return sources[i]
            if i in loads:
                loads.pop(i).wait()
            return buffers[i]

        def give(i):
            if i in targets:
                stores[i] = pltpu.make_async_copy(targets[i], results[i], out_sems.at[i])
                stores[i].start()

        body(inn, [targets.get(i, ref) for i, ref in enumerate(results)], give, *rest, *[results[i] for i in parts])
        for i in ends:
            if i not in stores:
                give(i)
        for store in stores.values():
            store.wait()

    buffers = [(views[i][0] if i in views else ins[i].shape, ins[i].dtype) for i in hbm]
    buffers += [(outs[i].shape, outs[i].dtype) for i in hbm_out]
    held = buffers + [(s.shape, s.dtype) for s in scratch if s.dtype in (BF16, F32)]
    limit = slack + -(-sum(math.prod(dims) * jnp.dtype(kind).itemsize for dims, kind in held) >> 20)
    spaces = [pltpu.SMEM if i < smem else pltpu.HBM if i in hbm or i in raw else vmem for i in range(len(ins))]
    out_spaces = [pltpu.HBM if i in hbm_out else vmem for i in range(len(outs))]
    results = [space(o.shape, o.dtype) for space, o in zip(out_spaces, outs)]
    out_specs = [pl.BlockSpec(memory_space=space) for space in out_spaces]
    single = len(outs) == 1
    return pl.pallas_call(
        kernel,
        name=name,
        out_shape=results[0] if single else tuple(results),
        in_specs=[pl.BlockSpec(memory_space=space) for space in spaces],
        out_specs=out_specs[0] if single else tuple(out_specs),
        scratch_shapes=[vmem(*b) for b in buffers] + [dma((len(ins),)), dma((len(outs),))] + list(scratch),
        compiler_params=pltpu.CompilerParams(vmem_limit_bytes=limit << 20),
        cost_estimate=pl.CostEstimate(flops=0, bytes_accessed=1024, transcendentals=0),
    )(*ins[:smem], *[pltpu.with_memory_space_constraint(a, s) for a, s in list(zip(ins, spaces))[smem:]])


def unit(value):
    centered = value - jnp.mean(value, axis=-1, keepdims=True)
    spread = jnp.mean(centered * centered, axis=-1, keepdims=True)
    scale = lax.rsqrt(spread + epsilon)
    return centered * scale, scale


def unit_back(grad, normal, scale):
    mean = jnp.mean(grad, axis=-1, keepdims=True)
    along = jnp.mean(grad * normal, axis=-1, keepdims=True)
    return scale * (grad - mean - normal * along)


def column_sum(value):
    return jnp.sum(value, axis=0, keepdims=True)


def prepare(inn, out, give, sems):
    c, w = lax.axis_index("ctx"), lax.axis_index("wt")
    qkv, up, pack = inn(0), inn(1), out[0]
    rows, width = qkv.shape[0], qkv.shape[1] // 3
    span, size = pack.shape[1] // 3, out[1].shape[1]
    copies = []
    for part in range(3):
        source = qkv.at[:, at(part * (width // span) + c, span)]
        copies.append((source, pack.at[pl.ds(0, rows), pl.ds(part * span, span)]))
    copies += [(up.at[:, at(w ^ d, size)], out[d]) for d in (2, 3, 1)]
    copies = [pltpu.make_async_copy(a, b, sems.at[i]) for i, (a, b) in enumerate(copies)]
    for copy in copies:
        copy.start()
    low = pl.ds(rows, SMALL)
    pack[low, :] = jnp.zeros((SMALL, pack.shape[1]), BF16)
    for i in range(3):
        ref = inn(2 + i)
        pack[pl.ds(rows + 4 * i, 4), pl.ds(0, ref.shape[1])] = ref[...]
    for copy in copies:
        copy.wait()


def attend(inn, out, give, xs, norm, sems):
    first, mixed, sent, stats, small = out
    c, w = lax.axis_index("ctx"), lax.axis_index("wt")
    deal = inn(0)
    length, width = xs.shape
    span = sent.shape[2]
    heads = stats.shape[0] // 2
    head = span // heads
    loads = []
    for d in range(CTX):
        for t in range(2):
            piece = inn(1 + WT + d).at[pl.ds(PIECE * t, PIECE), :]
            target = xs.at[at(deal[c ^ d, t], PIECE), :]
            loads.append(pltpu.make_async_copy(piece, target, sems.at[2 * d + t]))
            loads[-1].start()
    packs = [inn(1 + d) for d in range(WT)]
    for d in range(WT):
        small[:, at(w ^ d, PART)] = floats(packs[d][pl.ds(PART, SMALL), pl.ds(0, PART)])
    for load in loads:
        load.wait()
    bias_q = small[pl.ds(8, 1), at(c, span)]
    bias_v = small[pl.ds(9, 1), at(c, span)]

    @pl.loop(0, length // BLK)
    def _(i):
        rows = at(i, BLK)
        normal, _scale = unit(floats(xs[rows, :]))
        first[rows, :] = (normal * small[pl.ds(0, 1), :] + small[pl.ds(4, 1), :]).astype(BF16)
        total = dot(first[rows, at(w, PART)], packs[0][pl.ds(0, PART), :])
        for d in range(1, WT):
            total += dot(first[rows, at(w ^ d, PART)], packs[d][pl.ds(0, PART), :])
        mixed[rows, pl.ds(0, span)] = (total[:, :span] + bias_q).astype(BF16)
        mixed[rows, pl.ds(span, span)] = total[:, span : 2 * span].astype(BF16)
        mixed[rows, pl.ds(2 * span, span)] = (total[:, 2 * span :] + bias_v).astype(BF16)

    give(0)
    give(1)
    give(4)
    lane = lax.broadcasted_iota(jnp.int32, (BLK, span), 1) // head
    factor = 1.0 / math.sqrt(head)
    for b in range(length // BLK):
        rows, seen = pl.ds(b * BLK, BLK), pl.ds(0, (b + 1) * BLK)
        query = mixed[rows, pl.ds(0, span)]
        parts = []
        for h in range(heads):
            masked = jnp.where(lane == h, query, jnp.zeros_like(query))
            raw = dot_t(mixed[seen, pl.ds(span, span)], masked)
            top = jnp.max(raw, axis=0, keepdims=True)
            terms = jnp.exp((raw - top) * factor)
            inverse = 1.0 / jnp.sum(terms, axis=0, keepdims=True)
            stats[pl.ds(2 * h, 1), rows] = top
            stats[pl.ds(2 * h + 1, 1), rows] = inverse
            weights = (terms * inverse).astype(BF16)
            values = mixed[seen, pl.ds(2 * span, span)]
            parts.append(t_dot(values, weights)[h * head : (h + 1) * head, :])
        norm[rows, :] = jnp.concatenate(parts, axis=0).T.astype(BF16)
    for j in range(CTX):
        for t in range(2):
            sent[j, pl.ds(PIECE * t, PIECE), :] = norm[at(deal[j, t], PIECE), :]


def project(inn, out, give):
    branch, resid, second = out
    w = lax.axis_index("wt")
    small, attended, own = inn(0), inn(1), inn(2)
    span = attended.shape[2]
    total = small[pl.ds(10, 1), :]
    for d in range(WT):
        ref = inn(3 + d)
        for j in range(PART // span):
            total = total + dot(attended[(w ^ d) * (PART // span) + j], ref[pl.ds(span * j, span), :])
    branch[...] = total
    give(0)
    normal, _ = unit(total)
    total = floats(own[...]) + (normal * small[pl.ds(1, 1), :] + small[pl.ds(5, 1), :])
    resid[...] = total
    give(1)
    normal, _ = unit(total)
    second[...] = (normal * small[pl.ds(2, 1), :] + small[pl.ds(6, 1), :]).astype(BF16)


def join_slots(inn, start, target):
    for i, d in enumerate((0, 2, 1, 3)):
        ref = inn(start + d)
        rows = ref.shape[0]
        target[pl.ds(rows * i, rows), :] = ref[...]


def feed(inn, out, give):
    all_rows, hidden, slope, near, far = out
    w = lax.axis_index("wt")
    join_slots(inn, 0, all_rows)
    give(0)
    ups, bias = [inn(4 + d) for d in range(WT)], inn(8)
    half_rows = near.shape[0]

    @pl.loop(0, hidden.shape[1] // PART)
    def _(n):
        cols = at(n, PART)
        upper = floats(bias[pl.ds(0, 1), cols])
        for d in range(WT):
            upper = upper + dot(all_rows[:, at(w ^ d, PART)], ups[d][:, cols])
        square = upper * upper
        curve = jnp.tanh(GELU_A * (upper + GELU_B * (square * upper)))
        half = 0.5 * (1.0 + curve)
        hidden[:, cols] = (upper * half).astype(BF16)
        slope[:, cols] = half + (0.5 * GELU_A) * upper * (1.0 - curve * curve) * (
            1.0 + (3.0 * GELU_B) * square
        )

    give(1)
    give(2)
    down = inn(9)

    @pl.loop(0, near.shape[1] // PART)
    def _(n):
        cols = at(n, PART)
        total = dot(hidden[...], down[:, cols])
        near[:, cols] = total[:half_rows]
        far[:, cols] = total[half_rows:].astype(BF16)


def returned(inn, rows):
    own = pl.ds(0, rows)
    return inn(0)[own, :] + floats(inn(1)[own, :]) + floats(inn(2)[...])


def top_norm(inn, out, give):
    result, d_ffn, sums = out
    small, resid, grad = inn(3), inn(4), inn(5)
    normal, scale = unit(returned(inn, resid.shape[0]) + small[pl.ds(11, 1), :])
    gain = small[pl.ds(3, 1), :]
    d_out = floats(grad[...])
    low = unit_back(d_out * gain, normal, scale).astype(BF16)
    d_ffn[...] = low
    give(1)
    result[...] = (resid[...] + (normal * gain + small[pl.ds(7, 1), :])).astype(BF16)
    sums[pl.ds(0, 1), :] = column_sum(d_out * normal)
    sums[pl.ds(1, 1), :] = column_sum(d_out)
    sums[pl.ds(2, 1), :] = column_sum(floats(low))


def feed_back(inn, out, give):
    all_rows, d_upper, near, far, sums = out
    w = lax.axis_index("wt")
    join_slots(inn, 0, all_rows)
    give(0)
    down, slope = inn(4), inn(5)
    half_rows = near.shape[0]

    @pl.loop(0, d_upper.shape[1] // PART)
    def _(n):
        cols = at(n, PART)
        low = (dot_t(all_rows[...], down[cols, :]) * slope[:, cols]).astype(BF16)
        d_upper[:, cols] = low
        sums[pl.ds(0, 1), cols] = column_sum(floats(low))

    give(1)
    for d in range(WT):
        cols = at(w ^ d, PART)
        total = dot_t(d_upper[...], inn(6 + d)[...])
        near[:, cols] = total[:half_rows]
        far[:, cols] = total[half_rows:].astype(BF16)


KEPT = ((0, 0, 0), (0, 1, 4), (1, 0, 2), (1, 1, 6))
SENT = ((0, 3), (1, 7), (2, 1), (3, 5))


def places(out):
    sent = [(out[2 + i * (len(out) - 3) // 2], i if len(out) == 3 else i % 2, d) for i, d in SENT]
    return sent + [(out[which], i, d) for which, i, d in KEPT]


def grad_down(inn, out, give):
    c = lax.axis_index("ctx")
    hidden, grads = inn(0), inn(1)
    size = out[0].shape[1]
    for n, (target, i, d) in enumerate(places(out)):
        target[i] = t_dot(hidden[:, at(c ^ d, size)], grads[...]).astype(BF16)
        if n in (1, 3) and len(out) == 4:
            give(2 + n // 2)
        elif n == 3:
            give(2)


def grad_up(inn, out, give, part):
    c = lax.axis_index("ctx")
    cut = PART // CTX
    rows_in, grads = inn(0), inn(1)

    @pl.loop(0, WT)
    def _(k):
        part[...] = t_dot(rows_in[:, at(k, PART)], grads[...]).astype(BF16)
        for target, i, d in places(out):
            target[i, at(k, cut), :] = part[at(c ^ d, cut), :]


def middle_norms(inn, out, give):
    sent, d_att, d_resid, sums = out
    w = lax.axis_index("wt")
    small, resid, branch, grad = inn(3), inn(4), inn(5), inn(6)
    rows, span = resid.shape[0], sent.shape[2]
    normal3, scale3 = unit(resid[...])
    normal2, scale2 = unit(branch[...])
    d_second = returned(inn, rows)
    total = floats(grad[...]) + unit_back(d_second * small[pl.ds(2, 1), :], normal3, scale3)
    low = unit_back(total * small[pl.ds(1, 1), :], normal2, scale2).astype(BF16)
    d_att[...] = low
    d_resid[...] = total
    give(2)
    for d in (1, 2, 3, 0):
        part = dot_t(low, inn(7 + d)[...]).astype(BF16)
        for j in range(PART // span):
            sent[(w ^ d) * (PART // span) + j] = part[:, span * j : span * (j + 1)]
    sums[pl.ds(0, 1), :] = column_sum(d_second * normal3)
    sums[pl.ds(1, 1), :] = column_sum(d_second)
    sums[pl.ds(2, 1), :] = column_sum(total * normal2)
    sums[pl.ds(3, 1), :] = column_sum(total)
    sums[pl.ds(4, 1), :] = column_sum(floats(low))


def grad_out(inn, out, give):
    w = lax.axis_index("wt")
    attended, grads = inn(0), inn(1)
    span = attended.shape[2]
    for d in (1, 3, 0, 2):
        for j in range(PART // span):
            part = t_dot(attended[(w ^ d) * (PART // span) + j], grads[...])
            out[d % 2][d // 2, pl.ds(span * j, span), :] = part.astype(BF16)
        if d == 3:
            give(1)


def attend_back(inn, out, give, d_out, d_keys, d_values):
    natural, dealt = out
    deal, mixed, stats, got = (inn(i) for i in range(4))
    length, span = d_out.shape
    heads = stats.shape[0] // 2
    head = span // heads
    factor = 1.0 / math.sqrt(head)
    prescale = factor / relax
    for j in range(CTX):
        for t in range(2):
            d_out[at(deal[j, t], PIECE), :] = got[j, pl.ds(PIECE * t, PIECE), :]
    lane = lax.broadcasted_iota(jnp.int32, (BLK, span), 1) // head
    d_keys[...] = jnp.zeros_like(d_keys)
    d_values[...] = jnp.zeros_like(d_values)
    for b in range(length // BLK):
        rows, seen = pl.ds(b * BLK, BLK), pl.ds(0, (b + 1) * BLK)
        query, grads = mixed[rows, pl.ds(0, span)], d_out[rows, :]
        parts = []
        for h in range(heads):
            query_h = jnp.where(lane == h, query, jnp.zeros_like(query))
            grads_h = jnp.where(lane == h, grads, jnp.zeros_like(grads))
            keys = mixed[seen, pl.ds(span, span)]
            raw = dot_t(keys, query_h)
            weights = jnp.exp((raw - stats[pl.ds(2 * h, 1), rows]) * factor) * stats[pl.ds(2 * h + 1, 1), rows]
            d_probs = dot_t(mixed[seen, pl.ds(2 * span, span)], grads_h)
            delta = jnp.sum(weights * d_probs, axis=0, keepdims=True)
            d_scores = (relax * weights * (d_probs - delta)).astype(BF16)
            d_values[seen, :] += dot(weights.astype(BF16), grads_h)
            d_keys[seen, :] += dot(d_scores, query_h)
            parts.append(t_dot(keys, d_scores)[h * head : (h + 1) * head, :])
        natural[rows, pl.ds(0, span)] = (jnp.concatenate(parts, axis=0).T * prescale).astype(BF16)
    natural[:, pl.ds(span, span)] = (d_keys[...] * prescale).astype(BF16)
    natural[:, pl.ds(2 * span, span)] = d_values[...].astype(BF16)
    for j in range(CTX):
        for t in range(2):
            dealt[j, pl.ds(PIECE * t, PIECE), :] = natural[at(deal[j, t], PIECE), :]


def grad_qkv(inn, out, give):
    w = lax.axis_index("wt")
    first, grads = inn(0), inn(1)
    for d in (1, 3, 0, 2):
        out[d % 2][d // 2] = t_dot(first[:, at(w ^ d, PART)], grads[...]).astype(BF16)
        if d == 3:
            give(1)


def bottom_norm(inn, out, give, joined, d_first):
    input_grad, keep, send = out
    w = lax.axis_index("wt")
    got, own, d_resid, small = (inn(i) for i in range(4))
    _, rows, triple = got.shape
    span, width = triple // 3, own.shape[1]
    for j in range(CTX):
        for part in range(3):
            joined[:, pl.ds(part * width + span * j, span)] = got[j, :, pl.ds(span * part, span)]
    for d in range(WT):
        d_first[:, at(w ^ d, PART)] = dot_t(joined[...], inn(4 + d)[...])
    normal, scale = unit(floats(own[...]))
    grads = d_first[...]
    input_grad[...] = d_resid[...] + unit_back(grads * small[pl.ds(0, 1), :], normal, scale)
    give(0)
    middle, top, up = inn(8), inn(9), inn(10)
    lines = {
        0: column_sum(grads * normal),
        4: column_sum(grads),
        8: column_sum(floats(joined[:, pl.ds(0, width)])),
        9: column_sum(floats(joined[:, pl.ds(2 * width, width)])),
    }
    for i, line in enumerate((2, 6, 1, 5, 10)):
        lines[line] = middle[pl.ds(i, 1), :]
    for i, line in enumerate((3, 7, 11)):
        lines[line] = top[pl.ds(i, 1), :]
    for line, value in lines.items():
        d_first[pl.ds(line, 1), :] = value
    for d in range(WT):
        target = send if d % 2 else keep
        target[d // 2, pl.ds(0, 12), :] = d_first[pl.ds(0, 12), at(w ^ d, PART)]
        target[d // 2, pl.ds(12, 4), :] = jnp.zeros((4, PART), F32)
    for i in range(4):
        keep[0, pl.ds(12 + i, 1), :] = up[:, pl.ds(PART * i, PART)]


def add_second(inn, out, give):
    out[0][...] = (floats(inn(0)[1]) + floats(inn(1)[1])).astype(out[0].dtype)


def add_rest(inn, out, give):
    rows = out[0].shape[0]
    rest = pl.ds(rows, rows)
    out[0][...] = (inn(0)[rest, :] + floats(inn(1)[rest, :])).astype(BF16)


def add_high(inn, out, give):
    keep, got = inn(0), inn(1)
    for i in range(2):
        out[0][i] = (floats(keep[i]) + floats(got[i])).astype(BF16)


def add_high_last(inn, out, give):
    keep, got = inn(0), inn(1)
    for i in range(2):
        out[0][i] = (floats(keep[2 + i]) + floats(got[2 + i])).astype(BF16)


def add_low(first, inn, out, give):
    keep, got, after_z = inn(0), inn(1), inn(2)
    out[1][...] = (floats(keep[1]) + floats(got[first + 1]) + floats(after_z[1])).astype(BF16)
    out[0][...] = floats(keep[0]) + floats(got[first]) + floats(after_z[0])


def add_last(inn, out, give):
    out[0][...] = (inn(0)[...] + floats(inn(1)[...])).astype(BF16)


def add_out(inn, out, give, total):
    c = lax.axis_index("ctx")
    cut = out[0].shape[1]
    total[...] = (floats(inn(0)[0]) + floats(inn(1)[0]) + floats(inn(2)[...])).astype(BF16)
    for i, d in enumerate((0, 4, 2, 6)):
        out[0][i] = total[at(c ^ d, cut), :]
        out[1][i] = total[at(c ^ d ^ 1, cut), :]


def add_last_up(inn, out, give, total):
    w = lax.axis_index("wt")
    cut = out[0].shape[0]
    total[...] = (inn(0)[...] + floats(inn(1)[...])).astype(BF16)
    for d in range(WT):
        out[d][...] = total[at(w ^ d, cut), :]


def pack_up(inn, out, give):
    rows = inn(0).shape[0]
    for i in range(WT):
        out[0][pl.ds(rows * i, rows), :] = inn(i)[...]


def pack_mixed(inn, out, give, small):
    block = out[0]
    rows = inn(0).shape[1]
    block[pl.ds(0, rows), :] = (floats(inn(0)[0]) + floats(inn(1)[0]) + floats(inn(2)[...])).astype(BF16)
    cut, lanes = inn(3).shape[0], 128
    small[...] = jnp.zeros_like(small)
    small[pl.ds(0, cut), :] = (inn(3)[...] + floats(inn(4)[...])).astype(BF16)
    small[pl.ds(cut, SMALL), pl.ds(0, PART)] = (inn(5)[0] + inn(6)[0] + inn(7)[...]).astype(BF16)
    height, across = small.shape[0], block.shape[1] // lanes
    tiles = small.shape[1] // lanes
    for k in range(-(-tiles // across) * across):
        part = small[:, pl.ds(lanes * k, lanes)] if k < tiles else jnp.zeros((height, lanes), BF16)
        block[pl.ds(rows + height * (k // across), height), pl.ds(lanes * (k % across), lanes)] = part


def spread_mixed(inn, out, give, total):
    full, proj, gain, shift, bias, up_bias = out
    c = lax.axis_index("ctx")
    span = full.shape[1] // (3 * CTX)
    cut, lanes, rows = PART // CTX, 128, full.shape[0]
    height, across = cut + SMALL, inn(0).shape[1] // lanes
    total[...] = jnp.zeros_like(total)
    for d in range(CTX):
        block = inn(d)
        for part in range(3):
            full[:, at(part * CTX + (c ^ d), span)] = floats(block[pl.ds(0, rows), pl.ds(span * part, span)])
        for k in range(proj.shape[1] // lanes):
            top, left = rows + height * (k // across), pl.ds(lanes * (k % across), lanes)
            proj[at(c ^ d, cut), pl.ds(lanes * k, lanes)] = floats(block[pl.ds(top, cut), left])
            if lanes * k < PART:
                total[:, pl.ds(lanes * k, lanes)] += floats(block[pl.ds(top + cut, SMALL), left])
    for i, ref in enumerate((gain, shift, bias)):
        ref[...] = total[pl.ds(4 * i, 4), :]
    for i in range(4):
        up_bias[pl.ds(PART * i, PART)] = total[12 + i, :]


def spread_down(inn, out, give, sems, result):
    c = lax.axis_index("ctx")
    stores = []
    for d in range(CTX):
        block = inn(d)
        rows = at(c ^ d, block.shape[0])
        out[0][rows, :] = floats(block[...])
        stores.append(pltpu.make_async_copy(out[0].at[rows, :], result.at[rows, :], sems.at[d]))
        stores[-1].start()
    for store in stores:
        store.wait()


def spread_up(inn, out, give, sems, result):
    c, w = lax.axis_index("ctx"), lax.axis_index("wt")
    cut = PART // CTX
    width = out[0].shape[1] // WT
    stores = []
    for d in range(CTX):
        block, rows = inn(d), at(c ^ d, cut)
        for k in range(WT):
            out[0][rows, at(w ^ k, width)] = floats(block[pl.ds(cut * k, cut), :])
        stores.append(pltpu.make_async_copy(out[0].at[rows, :], result.at[rows, :], sems.at[d]))
        stores[-1].start()
    for store in stores:
        store.wait()


def split_device(
    layer_input,
    out_grad,
    deal,
    w_qkv,
    w_out,
    w_up,
    w_down,
    norm_gain,
    norm_shift,
    bias_width,
    up_bias,
):
    _, rows, width = layer_input.shape
    w = lax.axis_index("wt")
    per = HEADS // CTX
    span = per * (width // HEADS)
    length = rows * CTX
    hidden_width = w_down.shape[0]
    everyone = WT * rows
    own, grad = layer_input[0], out_grad[0]
    vmem, dma = pltpu.VMEM, pltpu.SemaphoreType.DMA

    sequence = gather_ctx(own)
    begin = lax.optimization_barrier((w_qkv, w_up, norm_gain, norm_shift, bias_width, sequence[1]))[:5]
    pack, *ups = call(
        prepare,
        "prepare",
        begin,
        [shape(PART + SMALL, 3 * span)] + [shape(PART, hidden_width)] * 3,
        raw=(0, 1),
        hbm=(2, 3, 4),
        scratch=[dma((6,))],
    )
    packs = gather_wt(pack)
    up_core, up_x, up_both = ups
    outs_x = swap(after(w_out, packs[2]), "wt", 2)
    up_x = swap(after(up_x, packs[2]), "wt", 2)

    first, mixed, sent, stats, small = call(
        attend,
        "attend",
        (deal, *packs, *sequence),
        [
            shape(length, width),
            shape(length, 3 * span),
            shape(CTX, rows, span),
            shape(2 * per, length, dtype=F32),
            shape(SMALL, width, dtype=F32),
        ],
        smem=1,
        hbm=range(1, 1 + WT),
        raw=range(1 + WT, 1 + WT + CTX),
        hbm_out=(0, 1),
        scratch=[vmem((length, width), BF16), vmem((length, span), BF16), dma((2 * CTX,))],
    )
    attended = lax.all_to_all(after(sent, outs_x, up_x), "ctx", 0, 0, tiled=True)
    up_both = swap(up_both, "wt", 3)
    outs_own, outs_x, up_core = lax.optimization_barrier((w_out, outs_x, up_core, sent))[:3]
    outs = w_out, swap(outs_own, "wt", 1), outs_x, swap(outs_x, "wt", 1)
    ups = w_up, swap(up_core, "wt", 1), up_x, up_both
    attended = after(attended, *outs, *ups[1:])

    branch, resid, second = call(
        project,
        "project",
        (small, attended, own, *outs),
        [shape(rows, width, dtype=F32), shape(rows, width, dtype=F32), shape(rows, width)],
    )

    own_columns = ((PART, hidden_width), lambda ref: ref.at[:, at(lax.axis_index("wt"), hidden_width)])
    halves = [shape(2 * rows, width, dtype=F32), shape(2 * rows, width)]
    seconds, hidden, slope, near, far = call(
        feed,
        "feed",
        (*gather_wt(second), *ups, up_bias.reshape(1, hidden_width), w_down),
        [shape(everyone, width), shape(everyone, hidden_width), shape(everyone, hidden_width, dtype=F32)]
        + halves,
        hbm=(4, 8, 9),
        hbm_out=(0,),
        views={4: own_columns},
    )

    def return_rows(near, far):
        got = swap(far, "wt", 1)
        back = call(add_rest, "add_rest", (near, got), [shape(rows, width)])
        return near, got, swap(back, "wt", 2)

    result, d_ffn, sums3 = call(
        top_norm,
        "top_norm",
        (*return_rows(near, far), small, resid, grad),
        [shape(rows, width), shape(rows, width), shape(3, width, dtype=F32)],
    )
    d_ffns, d_upper, near, far, up_sum = call(
        feed_back,
        "feed_back",
        (*gather_wt(d_ffn), w_down, slope, *ups),
        [shape(everyone, width), shape(everyone, hidden_width)] + halves + [shape(1, hidden_width, dtype=F32)],
        hbm=(4, 6),
        views={6: own_columns},
    )
    got = swap(far, "wt", 1)
    def sends(terms):
        if len(terms) == 3:
            whole = swap(terms[2], "ctx", 1)
            return (whole, 0), (whole, 2)
        return (swap(terms[2], "ctx", 1), 0), (swap(terms[3], "ctx", 1), 0)

    def chunks(split):
        sent = [shape(2, eighth, width)] * 2 if split else [shape(4, eighth, width)]
        return [shape(2, eighth, width)] * 2 + sent

    def added_high(name, terms, got):
        return call(
            add_high,
            "add_high_" + name,
            (terms[1], got),
            [shape(2, eighth, width)],
            hbm=(0,),
        )

    def added_low(name, terms, got, along):
        return call(
            functools.partial(add_low, got[1]),
            "add_low_" + name,
            (terms[0], got[0], along),
            [shape(eighth, width, dtype=F32), shape(eighth, width)],
            hbm=(0,),
        )

    eighth = hidden_width // CTX
    cut = PART // CTX
    terms_a = call(
        grad_down, "grad_down", (hidden, d_ffns), chunks(SPLIT[0]), hbm_out=range(3 + SPLIT[0])
    )
    high_got_a, low_got_a = sends(terms_a)
    back = call(add_rest, "add_rest", (after(near, terms_a[2]), got), [shape(rows, width)])
    far = swap(back, "wt", 2)
    terms_b = call(
        grad_up,
        "grad_up",
        (seconds, d_upper),
        chunks(SPLIT[1]),
        hbm=(0,),
        hbm_out=range(3 + SPLIT[1]),
        scratch=[vmem((PART, hidden_width), BF16)],
    )
    high_got_b, low_got_b = sends(terms_b)
    high_a = added_high("a", terms_a, high_got_a[0])
    next_a = swap(high_a, "ctx", 2)
    far = after(far, terms_b[2])
    sent, d_att, d_resid, sums21 = call(
        middle_norms,
        "middle_norms",
        (near, got, far, small, resid, branch, grad, *outs),
        [
            shape(CTX, rows, span),
            shape(rows, width),
            shape(rows, width, dtype=F32),
            shape(5, width, dtype=F32),
        ],
    )
    got = lax.all_to_all(sent, "ctx", 0, 0, tiled=True)
    pieces = [shape(2, PART, width)] * 2
    keep_out, send_out = call(
        grad_out, "grad_out", (attended, d_att), pieces, hbm_out=(0, 1)
    )
    got_out = swap(send_out, "wt", 1)
    back_out = call(
        add_second,
        "add_second_out",
        (keep_out, got_out),
        [shape(PART, width)],
        hbm=(0,),
    )
    out_x = swap(back_out, "wt", 2)
    high_b = added_high("b", terms_b, after(high_got_b[0], got))
    next_b = swap(high_b, "ctx", 2)
    first_a, second_a = added_low("a", terms_a, low_got_a, next_a)
    last_a = swap(second_a, "ctx", 4)

    natural, dealt = call(
        attend_back,
        "attend_back",
        (deal, mixed, stats, got),
        [shape(length, 3 * span), shape(CTX, rows, 3 * span)],
        smem=1,
        hbm=(1,),
        scratch=[vmem((length, span), BF16), vmem((length, span), F32), vmem((length, span), F32)],
    )
    first_b, second_b = added_low("b", terms_b, low_got_b, after(next_b, low_got_a[0]))
    last_b = swap(second_b, "ctx", 4)
    part_a = call(add_last, "add_last_a", (first_a, last_a), [shape(eighth, width)])
    down_slots = gather_free(after(part_a, back), go2=(high_b, back,), go1=(terms_b[2],))
    pieces = [shape(2, PART, 3 * span)] * 2
    keep_qkv, send_qkv = call(
        grad_qkv, "grad_qkv", (first, after(natural, last_a, second_b)), pieces, hbm=(0,), hbm_out=(0, 1)
    )
    keep_c, send_c = call(
        add_out,
        "add_out",
        (keep_out, got_out, after(out_x, natural, last_b)),
        [shape(4, cut, width)] * 2,
        hbm=(0,),
        scratch=[vmem((PART, width), BF16)],
    )
    got_c = swap(send_c, "ctx", 1)
    got_rows = lax.all_to_all(after(dealt, down_slots[1], send_c), "ctx", 0, 0, tiled=True)
    got_qkv = swap(send_qkv, "wt", 1)
    back_qkv = call(
        add_second,
        "add_second_qkv",
        (keep_qkv, got_qkv),
        [shape(PART, 3 * span)],
        hbm=(0,),
    )
    qkv_x = swap(back_qkv, "wt", 2)
    own_up, *up_parts = call(
        add_last_up,
        "add_last_up",
        (first_b, after(last_b, part_a, terms_b[2])),
        [shape(cut, width)] * WT,
        scratch=[vmem((eighth, width), BF16)],
    )
    up_parts = [swap(part, "wt", d) for part, d in zip(up_parts, (1, 2, 3))]
    up_block = call(
        pack_up, "pack_up", (after(own_up, down_slots[1], send_c), *up_parts), [shape(eighth, width)]
    )
    up_slots = gather_free(up_block, far=(next_a,))
    weights_x = swap(after(w_qkv, far), "wt", 2)
    qkv_own, weights_x = after(w_qkv, second_b), weights_x
    all_qkv = w_qkv, swap(qkv_own, "wt", 1), weights_x, swap(weights_x, "wt", 1)
    high_c = call(
        add_high_last, "add_high_c", (keep_c, got_c), [shape(2, cut, width)]
    )
    next_c = swap(high_c, "ctx", 2)
    first_c, second_c = call(
        functools.partial(add_low, 0),
        "add_low_c",
        (keep_c, got_c, after(next_c, low_got_a[0])),
        [shape(cut, width, dtype=F32), shape(cut, width)],
    )
    last_c = swap(second_c, "ctx", 4)
    input_grad, keep, send = call(
        bottom_norm,
        "bottom_norm",
        (after(got_rows, back_qkv), own, d_resid, small, *all_qkv, sums21, sums3, up_sum),
        [shape(rows, width, dtype=F32)] + [shape(2, SMALL, PART, dtype=F32)] * 2,
        hbm=(1, 2, 4, 5, 6, 7),
        hbm_out=(0,),
        scratch=[vmem((rows, 3 * width), BF16), vmem((rows, width), F32)],
    )
    got_sums = swap(send, "wt", 1)
    back_sums = call(add_second, "add_second_sums", (keep, got_sums), [shape(SMALL, PART, dtype=F32)])
    sums_x = swap(back_sums, "wt", 2)
    mixed_block = call(
        pack_mixed,
        "pack_mixed",
        (keep_qkv, got_qkv, after(qkv_x, up_slots[3], sums_x), first_c, last_c, keep, got_sums, sums_x),
        [shape(PART + 3 * (cut + SMALL), 3 * span)],
        hbm=(0,),
        scratch=[vmem((cut + SMALL, width), BF16)],
    )
    mixed_slots = gather_ctx_z(mixed_block)
    full_qkv, full_out, gain, shift, bias, up_total = call(
        spread_mixed,
        "spread_mixed",
        mixed_slots,
        [shape(PART, 3 * width, dtype=F32), shape(PART, width, dtype=F32)]
        + [shape(4, PART, dtype=F32)] * 3
        + [shape(hidden_width, dtype=F32)],
        hbm_out=range(6),
        scratch=[vmem((SMALL, PART), F32)],
    )
    full_down = call(
        spread_down,
        "spread_down",
        down_slots,
        [shape(hidden_width, width, dtype=F32)],
        hbm_out=(0,),
        scratch=[dma((CTX,))],
        parts=(0,),
    )
    full_up = call(
        spread_up,
        "spread_up",
        up_slots,
        [shape(PART, WT * hidden_width, dtype=F32)],
        hbm_out=(0,),
        scratch=[dma((CTX,))],
        parts=(0,),
    )
    return (
        result[None],
        input_grad[None],
        full_qkv,
        full_out,
        full_up,
        full_down,
        gain,
        shift,
        bias,
        up_total,
    )


def solution(mesh):
    small = mesh.shape["ctx"] == CTX and mesh.shape["wt"] == WT
    per_device = split_device if small else general_device
    in_specs = (
        P("wt", "ctx", None),
        P("wt", "ctx", None),
        P(),
        P("wt", None),
        P("wt", None),
        P("wt", None),
        P("wt", None),
        P(None, "wt"),
        P(None, "wt"),
        P(None, "wt"),
        P("wt"),
    )
    out_specs = (
        P("wt", "ctx", None),
        P("wt", "ctx", None),
        P("wt", None),
        P("wt", None),
        P("wt", None),
        P("wt", None),
        P(None, "wt"),
        P(None, "wt"),
        P(None, "wt"),
        P("wt"),
    )
    return jax.shard_map(
        per_device, mesh=mesh, in_specs=in_specs, out_specs=out_specs, check_vma=False
    )
```

```python
import functools
import math

import jax
import jax.numpy as jnp
from jax import lax
from jax.experimental import pallas as pl
from jax.experimental.pallas import tpu as pltpu
from jax.sharding import PartitionSpec as P

HEADS = 16
BLK = 256
PIECE = 64


epsilon = 1e-05
relax = 32.0


def layer_norm(value, gain, shift):
    mean = jnp.mean(value, axis=-1, keepdims=True)
    centered = value - mean
    spread = jnp.mean(centered * centered, axis=-1, keepdims=True)
    return centered * lax.rsqrt(spread + epsilon) * gain + shift


def gelu_tanh(value):
    return jax.nn.gelu(value, approximate=True)


def rows_dot(left, weight):
    return jnp.einsum("std,de->ste", left, weight, preferred_element_type=jnp.float32)


def weight_grad(left, right):
    return jnp.einsum("std,ste->de", left, right, preferred_element_type=jnp.float32)


def back_dot(grad, weight):
    return jnp.einsum("ste,de->std", grad, weight, preferred_element_type=jnp.float32)


def row_total(value):
    return jnp.sum(value.astype(jnp.float32), axis=(0, 1))


def general_device(
    layer_input,
    out_grad,
    deal,
    w_qkv,
    w_out,
    w_up,
    w_down,
    norm_gain,
    norm_shift,
    bias_width,
    up_bias,
):
    seqs, rows, width = layer_input.shape
    heads = HEADS
    head = width // heads
    prescale = 1.0 / (relax * math.sqrt(head))
    ranks = lax.axis_size("ctx")
    length = rows * ranks
    per_block = BLK // PIECE
    rank = lax.axis_index("ctx")
    chosen = jnp.arange(ranks, dtype=jnp.int32) == rank
    mine = jnp.sum(jnp.where(chosen[:, None], deal, 0), axis=0)
    query_blocks = jnp.repeat(mine, rows // 2) // per_block
    key_blocks = jnp.repeat(deal.reshape(-1), rows // 2) // per_block
    full_qkv, full_out, full_up, full_down, gains, shifts, biases, up_shift = (
        lax.all_gather(w_qkv, "wt", axis=0, tiled=True),
        lax.all_gather(w_out, "wt", axis=0, tiled=True),
        lax.all_gather(w_up, "wt", axis=0, tiled=True),
        lax.all_gather(w_down, "wt", axis=0, tiled=True),
        lax.all_gather(norm_gain, "wt", axis=1, tiled=True),
        lax.all_gather(norm_shift, "wt", axis=1, tiled=True),
        lax.all_gather(bias_width, "wt", axis=1, tiled=True),
        lax.all_gather(up_bias, "wt", axis=0, tiled=True),
    )
    gains = gains.astype(jnp.float32)
    shifts = shifts.astype(jnp.float32)
    biases = biases.astype(jnp.float32)
    up_shift = up_shift.astype(jnp.float32)
    input_float = layer_input.astype(jnp.float32)
    first = layer_norm(input_float, gains[0], shifts[0]).astype(jnp.bfloat16)
    mixed = rows_dot(first, full_qkv)
    query = (mixed[..., :width] + biases[0]).astype(jnp.bfloat16)
    kv_local = jnp.concatenate(
        [mixed[..., width : 2 * width], mixed[..., 2 * width :] + biases[1]], axis=-1
    ).astype(jnp.bfloat16)
    kv_all = lax.all_gather(kv_local, "ctx", axis=1, tiled=True)
    step = math.gcd(length, 1024)
    count = length // step
    query4 = query.reshape(seqs, rows, heads, head)

    def score_block(left, right):
        return (
            jnp.einsum("sqhd,skhd->shqk", left, right, preferred_element_type=jnp.float32)
            * prescale
        )

    def key_block(index):
        start = index * step
        piece = lax.dynamic_slice_in_dim(kv_all, start, step, 1)
        keys4 = piece[..., :width].reshape(seqs, step, heads, head)
        values4 = piece[..., width:].reshape(seqs, step, heads, head)
        visible = (
            query_blocks[:, None] >= lax.dynamic_slice_in_dim(key_blocks, start, step, 0)[None, :]
        )
        return (keys4, values4, visible)

    def probs(raw, visible, totals):
        return jnp.where(visible, jnp.exp(raw * relax - totals[..., None]), 0.0)

    def online(index, carry):
        top, total, acc = carry
        keys4, values4, visible = key_block(index)
        raw = jnp.where(visible, score_block(query4, keys4), -1e30)
        new_top = jnp.maximum(top, jnp.max(raw, axis=-1))
        terms = jnp.where(visible, jnp.exp((raw - new_top[..., None]) * relax), 0.0)
        factor = jnp.exp((top - new_top) * relax)
        total = total * factor + jnp.sum(terms, axis=-1)
        acc = acc * jnp.transpose(factor, (0, 2, 1))[..., None]
        acc = acc + jnp.einsum(
            "shqk,skhd->sqhd",
            terms.astype(jnp.bfloat16),
            values4,
            preferred_element_type=jnp.float32,
        )
        return (new_top, total, acc)

    start_top = jnp.full((seqs, heads, rows), -1e30, jnp.float32)
    start_total = jnp.zeros((seqs, heads, rows), jnp.float32)
    start_acc = jnp.zeros((seqs, rows, heads, head), jnp.float32)
    top, total, acc = lax.fori_loop(0, count, online, (start_top, start_total, start_acc))
    log_total = top * relax + jnp.log(total)
    attended_float = acc / jnp.transpose(total, (0, 2, 1))[..., None]
    attended = attended_float.reshape(seqs, rows, width).astype(jnp.bfloat16)
    branch = rows_dot(attended, full_out) + biases[2]
    resid = input_float + layer_norm(branch, gains[1], shifts[1])
    second = layer_norm(resid, gains[2], shifts[2]).astype(jnp.bfloat16)
    upper = rows_dot(second, full_up) + up_shift
    hidden = gelu_tanh(upper).astype(jnp.bfloat16)
    ffn = rows_dot(hidden, full_down) + biases[3]
    top_norm, pull_four = jax.vjp(layer_norm, ffn, gains[3], shifts[3])
    result = resid + top_norm
    d_out = out_grad.astype(jnp.float32)
    d_ffn, d_gain3, d_shift3 = pull_four(d_out)
    d_ffn = d_ffn.astype(jnp.bfloat16)
    d_bias3 = row_total(d_ffn)
    g_down = weight_grad(hidden, d_ffn)
    d_hidden = back_dot(d_ffn, full_down)
    _, pull_gelu = jax.vjp(gelu_tanh, upper)
    d_upper = pull_gelu(d_hidden)[0].astype(jnp.bfloat16)
    d_up_shift = row_total(d_upper)
    g_up = weight_grad(second, d_upper)
    d_second = back_dot(d_upper, full_up)
    _, pull_three = jax.vjp(layer_norm, resid, gains[2], shifts[2])
    d_resid_part, d_gain2, d_shift2 = pull_three(d_second)
    d_resid = d_out + d_resid_part
    _, pull_two = jax.vjp(layer_norm, branch, gains[1], shifts[1])
    d_branch, d_gain1, d_shift1 = pull_two(d_resid)
    d_branch = d_branch.astype(jnp.bfloat16)
    d_bias2 = row_total(d_branch)
    g_out = weight_grad(attended, d_branch)
    d_attended = back_dot(d_branch, full_out).astype(jnp.bfloat16)
    d_out4 = d_attended.reshape(seqs, rows, heads, head)
    delta = jnp.einsum("sqhd,sqhd->shq", d_out4.astype(jnp.float32), attended_float)

    def score_grads(q_rows, do_rows, k_rows, v_rows, visible, lse_rows, delta_rows):
        weights = probs(score_block(q_rows, k_rows), visible, lse_rows)
        d_probs = jnp.einsum("sqhd,skhd->shqk", do_rows, v_rows, preferred_element_type=jnp.float32)
        d_scores = (relax * weights * (d_probs - delta_rows[..., None])).astype(jnp.bfloat16)
        return (d_scores, weights.astype(jnp.bfloat16))

    zero_query = jnp.zeros((seqs, rows, heads, head), jnp.float32)

    def local_grads(d_query, index):
        keys4, values4, visible = key_block(index)
        d_scores, weights = score_grads(query4, d_out4, keys4, values4, visible, log_total, delta)
        d_query = (
            d_query
            + jnp.einsum("shqk,skhd->sqhd", d_scores, keys4, preferred_element_type=jnp.float32)
            * prescale
        )
        d_keys = (
            jnp.einsum("shqk,sqhd->kshd", d_scores, query4, preferred_element_type=jnp.float32)
            * prescale
        )
        d_values = jnp.einsum(
            "shqk,sqhd->kshd", weights, d_out4, preferred_element_type=jnp.float32
        )
        joined = jnp.concatenate(
            [d_keys.reshape(step, seqs, width), d_values.reshape(step, seqs, width)], axis=-1
        )
        return (d_query, joined)

    d_query, pieces = lax.scan(local_grads, zero_query, jnp.arange(count, dtype=jnp.int32))
    terms = pieces.reshape(length, seqs, 2 * width)
    d_kv = jnp.transpose(lax.psum_scatter(terms, "ctx", scatter_dimension=0, tiled=True), (1, 0, 2))
    d_query = d_query.reshape(seqs, rows, width).astype(jnp.bfloat16)
    d_kv = d_kv.astype(jnp.bfloat16)
    d_bias0 = row_total(d_query)
    d_bias1 = row_total(d_kv[..., width:])
    d_mixed = jnp.concatenate([d_query, d_kv], axis=-1)
    g_qkv = weight_grad(first, d_mixed)
    d_first = back_dot(d_mixed, full_qkv)
    _, pull_one = jax.vjp(layer_norm, input_float, gains[0], shifts[0])
    d_input_part, d_gain0, d_shift0 = pull_one(d_first)
    input_grad = d_resid + d_input_part
    grad_gain = jnp.stack([d_gain0, d_gain1, d_gain2, d_gain3])
    grad_shift = jnp.stack([d_shift0, d_shift1, d_shift2, d_shift3])
    grad_bias = jnp.stack([d_bias0, d_bias1, d_bias2, d_bias3])
    owned = (
        lax.psum_scatter(g_qkv.astype(jnp.bfloat16), "wt", scatter_dimension=0, tiled=True).astype(
            jnp.float32
        ),
        lax.psum_scatter(g_out.astype(jnp.bfloat16), "wt", scatter_dimension=0, tiled=True).astype(
            jnp.float32
        ),
        lax.psum_scatter(g_up.astype(jnp.bfloat16), "wt", scatter_dimension=0, tiled=True).astype(
            jnp.float32
        ),
        lax.psum_scatter(g_down.astype(jnp.bfloat16), "wt", scatter_dimension=0, tiled=True).astype(
            jnp.float32
        ),
        lax.psum_scatter(
            grad_gain.astype(jnp.bfloat16), "wt", scatter_dimension=1, tiled=True
        ).astype(jnp.float32),
        lax.psum_scatter(
            grad_shift.astype(jnp.bfloat16), "wt", scatter_dimension=1, tiled=True
        ).astype(jnp.float32),
        lax.psum_scatter(
            grad_bias.astype(jnp.bfloat16), "wt", scatter_dimension=1, tiled=True
        ).astype(jnp.float32),
        lax.psum_scatter(
            d_up_shift.astype(jnp.bfloat16), "wt", scatter_dimension=0, tiled=True
        ).astype(jnp.float32),
    )
    summed = lax.psum(
        (owned[0], owned[1], owned[2], owned[3], owned[4], owned[5], owned[6], owned[7]), "ctx"
    )
    return (
        result.astype(jnp.bfloat16),
        input_grad,
        summed[0],
        summed[1],
        summed[2],
        summed[3],
        summed[4],
        summed[5],
        summed[6],
        summed[7],
    )


F32 = jnp.float32
BF16 = jnp.bfloat16
WT = 4
CTX = 8
PART = 256
SMALL = 16
GELU_A = math.sqrt(2.0 / math.pi)
GELU_B = 0.044715
SPLIT = (0, 1)


def swap(value, axis, bit):
    size = lax.axis_size(axis)
    return lax.ppermute(value, axis, [(i, i ^ bit) for i in range(size)])


def gather_wt(block):
    far = swap(block, "wt", 2)
    return block, swap(block, "wt", 1), far, swap(far, "wt", 1)


def gather_ctx(block):
    far, near, side = (swap(block, "ctx", bit) for bit in (4, 2, 1))
    near = after(near, side)
    near_side = swap(near, "ctx", 1)
    far = after(far, near_side)
    corner = swap(far, "ctx", 2)
    far_side = swap(far, "ctx", 1)
    return [block, side, near, near_side, far, far_side, corner, swap(after(corner, far_side), "ctx", 1)]


def held(value, others):
    return after(value, *others) if others else value


def gather_free(block, go4=(), go2=(), go1=(), near=(), far=(), corner=()):
    far_z = held(swap(held(block, go4), "ctx", 4), far)
    near_z = held(swap(held(block, go2), "ctx", 2), near)
    side = swap(held(block, go1), "ctx", 1)
    near_side, corner_z, far_side = swap(near_z, "ctx", 1), swap(far_z, "ctx", 2), swap(far_z, "ctx", 1)
    corner_z = held(corner_z, corner)
    return [block, side, near_z, near_side, far_z, far_side, corner_z, swap(corner_z, "ctx", 1)]


def gather_ctx_z(block):
    blocks = {0: block}
    for bit in (1, 4, 2):
        blocks.update({d ^ bit: swap(value, "ctx", bit) for d, value in blocks.items()})
    return [blocks[d] for d in range(CTX)]


def after(value, *others):
    return lax.optimization_barrier((value, *others))[0]


def floats(value):
    return value.astype(F32)


def dot(left, right):
    return jnp.dot(left, right, preferred_element_type=F32)


def dot_t(left, right):
    return lax.dot_general(left, right, (((1,), (1,)), ((), ())), preferred_element_type=F32)


def t_dot(left, right):
    return lax.dot_general(left, right, (((0,), (0,)), ((), ())), preferred_element_type=F32)


def at(start, size):
    return pl.ds(pl.multiple_of(start * size, size), size)


def shape(*dims, dtype=jnp.bfloat16):
    return jax.ShapeDtypeStruct(dims, dtype)


def call(body, name, ins, outs, smem=0, raw=(), hbm=(), views=None, hbm_out=(), scratch=(), parts=(), slack=10):
    views = views or {}
    ends = [i for i in hbm_out if i not in parts]
    vmem, dma = pltpu.VMEM, pltpu.SemaphoreType.DMA

    def kernel(*refs):
        sources, results = refs[: len(ins)], list(refs[len(ins) : len(ins) + len(outs)])
        rest = list(refs[len(ins) + len(outs) :])
        buffers = {i: rest.pop(0) for i in hbm}
        targets = {i: rest.pop(0) for i in hbm_out}
        in_sems, out_sems = rest.pop(0), rest.pop(0)
        loads, stores = {}, {}
        for i in hbm:
            source = views[i][1](sources[i]) if i in views else sources[i]
            loads[i] = pltpu.make_async_copy(source, buffers[i], in_sems.at[i])
            loads[i].start()

        def inn(i):
            if i not in buffers:
                return sources[i]
            if i in loads:
                loads.pop(i).wait()
            return buffers[i]

        def give(i):
            if i in targets:
                stores[i] = pltpu.make_async_copy(targets[i], results[i], out_sems.at[i])
                stores[i].start()

        body(inn, [targets.get(i, ref) for i, ref in enumerate(results)], give, *rest, *[results[i] for i in parts])
        for i in ends:
            if i not in stores:
                give(i)
        for store in stores.values():
            store.wait()

    buffers = [(views[i][0] if i in views else ins[i].shape, ins[i].dtype) for i in hbm]
    buffers += [(outs[i].shape, outs[i].dtype) for i in hbm_out]
    held = buffers + [(s.shape, s.dtype) for s in scratch if s.dtype in (BF16, F32)]
    limit = slack + -(-sum(math.prod(dims) * jnp.dtype(kind).itemsize for dims, kind in held) >> 20)
    spaces = [pltpu.SMEM if i < smem else pltpu.HBM if i in hbm or i in raw else vmem for i in range(len(ins))]
    out_spaces = [pltpu.HBM if i in hbm_out else vmem for i in range(len(outs))]
    results = [space(o.shape, o.dtype) for space, o in zip(out_spaces, outs)]
    out_specs = [pl.BlockSpec(memory_space=space) for space in out_spaces]
    single = len(outs) == 1
    return pl.pallas_call(
        kernel,
        name=name,
        out_shape=results[0] if single else tuple(results),
        in_specs=[pl.BlockSpec(memory_space=space) for space in spaces],
        out_specs=out_specs[0] if single else tuple(out_specs),
        scratch_shapes=[vmem(*b) for b in buffers] + [dma((len(ins),)), dma((len(outs),))] + list(scratch),
        compiler_params=pltpu.CompilerParams(vmem_limit_bytes=limit << 20),
        cost_estimate=pl.CostEstimate(flops=0, bytes_accessed=1024, transcendentals=0),
    )(*ins[:smem], *[pltpu.with_memory_space_constraint(a, s) for a, s in list(zip(ins, spaces))[smem:]])


def unit(value):
    centered = value - jnp.mean(value, axis=-1, keepdims=True)
    spread = jnp.mean(centered * centered, axis=-1, keepdims=True)
    scale = lax.rsqrt(spread + epsilon)
    return centered * scale, scale


def unit_back(grad, normal, scale):
    mean = jnp.mean(grad, axis=-1, keepdims=True)
    along = jnp.mean(grad * normal, axis=-1, keepdims=True)
    return scale * (grad - mean - normal * along)


def column_sum(value):
    return jnp.sum(value, axis=0, keepdims=True)


def prepare(inn, out, give, sems):
    c, w = lax.axis_index("ctx"), lax.axis_index("wt")
    qkv, up, pack = inn(0), inn(1), out[0]
    rows, width = qkv.shape[0], qkv.shape[1] // 3
    span, size = pack.shape[1] // 3, out[1].shape[1]
    copies = []
    for part in range(3):
        source = qkv.at[:, at(part * (width // span) + c, span)]
        copies.append((source, pack.at[pl.ds(0, rows), pl.ds(part * span, span)]))
    copies += [(up.at[:, at(w ^ d, size)], out[d]) for d in (2, 3, 1)]
    copies = [pltpu.make_async_copy(a, b, sems.at[i]) for i, (a, b) in enumerate(copies)]
    for copy in copies:
        copy.start()
    low = pl.ds(rows, SMALL)
    pack[low, :] = jnp.zeros((SMALL, pack.shape[1]), BF16)
    for i in range(3):
        ref = inn(2 + i)
        pack[pl.ds(rows + 4 * i, 4), pl.ds(0, ref.shape[1])] = ref[...]
    for copy in copies:
        copy.wait()


def attend(inn, out, give, xs, norm, sems):
    first, mixed, sent, stats, small = out
    c, w = lax.axis_index("ctx"), lax.axis_index("wt")
    deal = inn(0)
    length, width = xs.shape
    span = sent.shape[2]
    heads = stats.shape[0] // 2
    head = span // heads
    loads = []
    for d in range(CTX):
        for t in range(2):
            piece = inn(1 + WT + d).at[pl.ds(PIECE * t, PIECE), :]
            target = xs.at[at(deal[c ^ d, t], PIECE), :]
            loads.append(pltpu.make_async_copy(piece, target, sems.at[2 * d + t]))
            loads[-1].start()
    packs = [inn(1 + d) for d in range(WT)]
    for d in range(WT):
        small[:, at(w ^ d, PART)] = floats(packs[d][pl.ds(PART, SMALL), pl.ds(0, PART)])
    for load in loads:
        load.wait()
    bias_q = small[pl.ds(8, 1), at(c, span)]
    bias_v = small[pl.ds(9, 1), at(c, span)]

    @pl.loop(0, length // BLK)
    def _(i):
        rows = at(i, BLK)
        normal, _scale = unit(floats(xs[rows, :]))
        first[rows, :] = (normal * small[pl.ds(0, 1), :] + small[pl.ds(4, 1), :]).astype(BF16)
        total = dot(first[rows, at(w, PART)], packs[0][pl.ds(0, PART), :])
        for d in range(1, WT):
            total += dot(first[rows, at(w ^ d, PART)], packs[d][pl.ds(0, PART), :])
        mixed[rows, pl.ds(0, span)] = (total[:, :span] + bias_q).astype(BF16)
        mixed[rows, pl.ds(span, span)] = total[:, span : 2 * span].astype(BF16)
        mixed[rows, pl.ds(2 * span, span)] = (total[:, 2 * span :] + bias_v).astype(BF16)

    give(0)
    give(1)
    give(4)
    lane = lax.broadcasted_iota(jnp.int32, (BLK, span), 1) // head
    factor = 1.0 / math.sqrt(head)
    for b in range(length // BLK):
        rows, seen = pl.ds(b * BLK, BLK), pl.ds(0, (b + 1) * BLK)
        query = mixed[rows, pl.ds(0, span)]
        parts = []
        for h in range(heads):
            masked = jnp.where(lane == h, query, jnp.zeros_like(query))
            raw = dot_t(mixed[seen, pl.ds(span, span)], masked)
            top = jnp.max(raw, axis=0, keepdims=True)
            terms = jnp.exp((raw - top) * factor)
            inverse = 1.0 / jnp.sum(terms, axis=0, keepdims=True)
            stats[pl.ds(2 * h, 1), rows] = top
            stats[pl.ds(2 * h + 1, 1), rows] = inverse
            weights = (terms * inverse).astype(BF16)
            values = mixed[seen, pl.ds(2 * span, span)]
            parts.append(t_dot(values, weights)[h * head : (h + 1) * head, :])
        norm[rows, :] = jnp.concatenate(parts, axis=0).T.astype(BF16)
    for j in range(CTX):
        for t in range(2):
            sent[j, pl.ds(PIECE * t, PIECE), :] = norm[at(deal[j, t], PIECE), :]


def project(inn, out, give):
    branch, resid, second = out
    w = lax.axis_index("wt")
    small, attended, own = inn(0), inn(1), inn(2)
    span = attended.shape[2]
    total = small[pl.ds(10, 1), :]
    for d in range(WT):
        ref = inn(3 + d)
        for j in range(PART // span):
            total = total + dot(attended[(w ^ d) * (PART // span) + j], ref[pl.ds(span * j, span), :])
    branch[...] = total
    give(0)
    normal, _ = unit(total)
    total = floats(own[...]) + (normal * small[pl.ds(1, 1), :] + small[pl.ds(5, 1), :])
    resid[...] = total
    give(1)
    normal, _ = unit(total)
    second[...] = (normal * small[pl.ds(2, 1), :] + small[pl.ds(6, 1), :]).astype(BF16)


def join_slots(inn, start, target):
    for i, d in enumerate((0, 2, 1, 3)):
        ref = inn(start + d)
        rows = ref.shape[0]
        target[pl.ds(rows * i, rows), :] = ref[...]


def feed(inn, out, give):
    all_rows, hidden, slope, near, far = out
    w = lax.axis_index("wt")
    join_slots(inn, 0, all_rows)
    give(0)
    ups, bias = [inn(4 + d) for d in range(WT)], inn(8)
    half_rows = near.shape[0]

    @pl.loop(0, hidden.shape[1] // PART)
    def _(n):
        cols = at(n, PART)
        upper = floats(bias[pl.ds(0, 1), cols])
        for d in range(WT):
            upper = upper + dot(all_rows[:, at(w ^ d, PART)], ups[d][:, cols])
        square = upper * upper
        curve = jnp.tanh(GELU_A * (upper + GELU_B * (square * upper)))
        half = 0.5 * (1.0 + curve)
        hidden[:, cols] = (upper * half).astype(BF16)
        slope[:, cols] = half + (0.5 * GELU_A) * upper * (1.0 - curve * curve) * (
            1.0 + (3.0 * GELU_B) * square
        )

    give(1)
    give(2)
    down = inn(9)

    @pl.loop(0, near.shape[1] // PART)
    def _(n):
        cols = at(n, PART)
        total = dot(hidden[...], down[:, cols])
        near[:, cols] = total[:half_rows]
        far[:, cols] = total[half_rows:].astype(BF16)


def returned(inn, rows):
    own = pl.ds(0, rows)
    return inn(0)[own, :] + floats(inn(1)[own, :]) + floats(inn(2)[...])


def top_norm(inn, out, give):
    result, d_ffn, sums = out
    small, resid, grad = inn(3), inn(4), inn(5)
    normal, scale = unit(returned(inn, resid.shape[0]) + small[pl.ds(11, 1), :])
    gain = small[pl.ds(3, 1), :]
    d_out = floats(grad[...])
    low = unit_back(d_out * gain, normal, scale).astype(BF16)
    d_ffn[...] = low
    give(1)
    result[...] = (resid[...] + (normal * gain + small[pl.ds(7, 1), :])).astype(BF16)
    sums[pl.ds(0, 1), :] = column_sum(d_out * normal)
    sums[pl.ds(1, 1), :] = column_sum(d_out)
    sums[pl.ds(2, 1), :] = column_sum(floats(low))


def feed_back(inn, out, give):
    all_rows, d_upper, near, far, sums = out
    w = lax.axis_index("wt")
    join_slots(inn, 0, all_rows)
    give(0)
    down, slope = inn(4), inn(5)
    half_rows = near.shape[0]

    @pl.loop(0, d_upper.shape[1] // PART)
    def _(n):
        cols = at(n, PART)
        low = (dot_t(all_rows[...], down[cols, :]) * slope[:, cols]).astype(BF16)
        d_upper[:, cols] = low
        sums[pl.ds(0, 1), cols] = column_sum(floats(low))

    give(1)
    for d in range(WT):
        cols = at(w ^ d, PART)
        total = dot_t(d_upper[...], inn(6 + d)[...])
        near[:, cols] = total[:half_rows]
        far[:, cols] = total[half_rows:].astype(BF16)


KEPT = ((0, 0, 0), (0, 1, 4), (1, 0, 2), (1, 1, 6))
SENT = ((0, 3), (1, 7), (2, 1), (3, 5))


def places(out):
    sent = [(out[2 + i * (len(out) - 3) // 2], i if len(out) == 3 else i % 2, d) for i, d in SENT]
    return sent + [(out[which], i, d) for which, i, d in KEPT]


def grad_down(inn, out, give):
    c = lax.axis_index("ctx")
    hidden, grads = inn(0), inn(1)
    size = out[0].shape[1]
    for n, (target, i, d) in enumerate(places(out)):
        target[i] = t_dot(hidden[:, at(c ^ d, size)], grads[...]).astype(BF16)
        if n in (1, 3) and len(out) == 4:
            give(2 + n // 2)
        elif n == 3:
            give(2)


def grad_up(inn, out, give, part):
    c = lax.axis_index("ctx")
    cut = PART // CTX
    rows_in, grads = inn(0), inn(1)

    @pl.loop(0, WT)
    def _(k):
        part[...] = t_dot(rows_in[:, at(k, PART)], grads[...]).astype(BF16)
        for target, i, d in places(out):
            target[i, at(k, cut), :] = part[at(c ^ d, cut), :]


def middle_norms(inn, out, give):
    sent, d_att, d_resid, sums = out
    w = lax.axis_index("wt")
    small, resid, branch, grad = inn(3), inn(4), inn(5), inn(6)
    rows, span = resid.shape[0], sent.shape[2]
    normal3, scale3 = unit(resid[...])
    normal2, scale2 = unit(branch[...])
    d_second = returned(inn, rows)
    total = floats(grad[...]) + unit_back(d_second * small[pl.ds(2, 1), :], normal3, scale3)
    low = unit_back(total * small[pl.ds(1, 1), :], normal2, scale2).astype(BF16)
    d_att[...] = low
    d_resid[...] = total
    give(2)
    for d in (1, 2, 3, 0):
        part = dot_t(low, inn(7 + d)[...]).astype(BF16)
        for j in range(PART // span):
            sent[(w ^ d) * (PART // span) + j] = part[:, span * j : span * (j + 1)]
    sums[pl.ds(0, 1), :] = column_sum(d_second * normal3)
    sums[pl.ds(1, 1), :] = column_sum(d_second)
    sums[pl.ds(2, 1), :] = column_sum(total * normal2)
    sums[pl.ds(3, 1), :] = column_sum(total)
    sums[pl.ds(4, 1), :] = column_sum(floats(low))


def grad_out(inn, out, give):
    w = lax.axis_index("wt")
    attended, grads = inn(0), inn(1)
    span = attended.shape[2]
    for d in (1, 3, 0, 2):
        for j in range(PART // span):
            part = t_dot(attended[(w ^ d) * (PART // span) + j], grads[...])
            out[d % 2][d // 2, pl.ds(span * j, span), :] = part.astype(BF16)
        if d == 3:
            give(1)


def attend_back(inn, out, give, d_out, d_keys, d_values):
    natural, dealt = out
    deal, mixed, stats, got = (inn(i) for i in range(4))
    length, span = d_out.shape
    heads = stats.shape[0] // 2
    head = span // heads
    factor = 1.0 / math.sqrt(head)
    prescale = factor / relax
    for j in range(CTX):
        for t in range(2):
            d_out[at(deal[j, t], PIECE), :] = got[j, pl.ds(PIECE * t, PIECE), :]
    lane = lax.broadcasted_iota(jnp.int32, (BLK, span), 1) // head
    d_keys[...] = jnp.zeros_like(d_keys)
    d_values[...] = jnp.zeros_like(d_values)
    for b in range(length // BLK):
        rows, seen = pl.ds(b * BLK, BLK), pl.ds(0, (b + 1) * BLK)
        query, grads = mixed[rows, pl.ds(0, span)], d_out[rows, :]
        parts = []
        for h in range(heads):
            query_h = jnp.where(lane == h, query, jnp.zeros_like(query))
            grads_h = jnp.where(lane == h, grads, jnp.zeros_like(grads))
            keys = mixed[seen, pl.ds(span, span)]
            raw = dot_t(keys, query_h)
            weights = jnp.exp((raw - stats[pl.ds(2 * h, 1), rows]) * factor) * stats[pl.ds(2 * h + 1, 1), rows]
            d_probs = dot_t(mixed[seen, pl.ds(2 * span, span)], grads_h)
            delta = jnp.sum(weights * d_probs, axis=0, keepdims=True)
            d_scores = (relax * weights * (d_probs - delta)).astype(BF16)
            d_values[seen, :] += dot(weights.astype(BF16), grads_h)
            d_keys[seen, :] += dot(d_scores, query_h)
            parts.append(t_dot(keys, d_scores)[h * head : (h + 1) * head, :])
        natural[rows, pl.ds(0, span)] = (jnp.concatenate(parts, axis=0).T * prescale).astype(BF16)
    natural[:, pl.ds(span, span)] = (d_keys[...] * prescale).astype(BF16)
    natural[:, pl.ds(2 * span, span)] = d_values[...].astype(BF16)
    for j in range(CTX):
        for t in range(2):
            dealt[j, pl.ds(PIECE * t, PIECE), :] = natural[at(deal[j, t], PIECE), :]


def grad_qkv(inn, out, give):
    w = lax.axis_index("wt")
    first, grads = inn(0), inn(1)
    for d in (1, 3, 0, 2):
        out[d % 2][d // 2] = t_dot(first[:, at(w ^ d, PART)], grads[...]).astype(BF16)
        if d == 3:
            give(1)


def bottom_norm(inn, out, give, joined, d_first):
    input_grad, keep, send = out
    w = lax.axis_index("wt")
    got, own, d_resid, small = (inn(i) for i in range(4))
    _, rows, triple = got.shape
    span, width = triple // 3, own.shape[1]
    for j in range(CTX):
        for part in range(3):
            joined[:, pl.ds(part * width + span * j, span)] = got[j, :, pl.ds(span * part, span)]
    for d in range(WT):
        d_first[:, at(w ^ d, PART)] = dot_t(joined[...], inn(4 + d)[...])
    normal, scale = unit(floats(own[...]))
    grads = d_first[...]
    input_grad[...] = d_resid[...] + unit_back(grads * small[pl.ds(0, 1), :], normal, scale)
    give(0)
    middle, top, up = inn(8), inn(9), inn(10)
    lines = {
        0: column_sum(grads * normal),
        4: column_sum(grads),
        8: column_sum(floats(joined[:, pl.ds(0, width)])),
        9: column_sum(floats(joined[:, pl.ds(2 * width, width)])),
    }
    for i, line in enumerate((2, 6, 1, 5, 10)):
        lines[line] = middle[pl.ds(i, 1), :]
    for i, line in enumerate((3, 7, 11)):
        lines[line] = top[pl.ds(i, 1), :]
    for line, value in lines.items():
        d_first[pl.ds(line, 1), :] = value
    for d in range(WT):
        target = send if d % 2 else keep
        target[d // 2, pl.ds(0, 12), :] = d_first[pl.ds(0, 12), at(w ^ d, PART)]
        target[d // 2, pl.ds(12, 4), :] = jnp.zeros((4, PART), F32)
    for i in range(4):
        keep[0, pl.ds(12 + i, 1), :] = up[:, pl.ds(PART * i, PART)]


def add_second(inn, out, give):
    out[0][...] = (floats(inn(0)[1]) + floats(inn(1)[1])).astype(out[0].dtype)


def add_rest(inn, out, give):
    rows = out[0].shape[0]
    rest = pl.ds(rows, rows)
    out[0][...] = (inn(0)[rest, :] + floats(inn(1)[rest, :])).astype(BF16)


def add_high(inn, out, give):
    keep, got = inn(0), inn(1)
    for i in range(2):
        out[0][i] = (floats(keep[i]) + floats(got[i])).astype(BF16)


def add_high_last(inn, out, give):
    keep, got = inn(0), inn(1)
    for i in range(2):
        out[0][i] = (floats(keep[2 + i]) + floats(got[2 + i])).astype(BF16)


def add_low(first, inn, out, give):
    keep, got, after_z = inn(0), inn(1), inn(2)
    out[1][...] = (floats(keep[1]) + floats(got[first + 1]) + floats(after_z[1])).astype(BF16)
    out[0][...] = floats(keep[0]) + floats(got[first]) + floats(after_z[0])


def add_last(inn, out, give):
    out[0][...] = (inn(0)[...] + floats(inn(1)[...])).astype(BF16)


def add_out(inn, out, give, total):
    c = lax.axis_index("ctx")
    cut = out[0].shape[1]
    total[...] = (floats(inn(0)[0]) + floats(inn(1)[0]) + floats(inn(2)[...])).astype(BF16)
    for i, d in enumerate((0, 4, 2, 6)):
        out[0][i] = total[at(c ^ d, cut), :]
        out[1][i] = total[at(c ^ d ^ 1, cut), :]


def add_last_up(inn, out, give, total):
    w = lax.axis_index("wt")
    cut = out[0].shape[0]
    total[...] = (inn(0)[...] + floats(inn(1)[...])).astype(BF16)
    for d in range(WT):
        out[d][...] = total[at(w ^ d, cut), :]


def pack_up(inn, out, give):
    rows = inn(0).shape[0]
    for i in range(WT):
        out[0][pl.ds(rows * i, rows), :] = inn(i)[...]


def pack_mixed(inn, out, give, small):
    block = out[0]
    rows = inn(0).shape[1]
    block[pl.ds(0, rows), :] = (floats(inn(0)[0]) + floats(inn(1)[0]) + floats(inn(2)[...])).astype(BF16)
    cut, lanes = inn(3).shape[0], 128
    small[...] = jnp.zeros_like(small)
    small[pl.ds(0, cut), :] = (inn(3)[...] + floats(inn(4)[...])).astype(BF16)
    small[pl.ds(cut, SMALL), pl.ds(0, PART)] = (inn(5)[0] + inn(6)[0] + inn(7)[...]).astype(BF16)
    height, across = small.shape[0], block.shape[1] // lanes
    tiles = small.shape[1] // lanes
    for k in range(-(-tiles // across) * across):
        part = small[:, pl.ds(lanes * k, lanes)] if k < tiles else jnp.zeros((height, lanes), BF16)
        block[pl.ds(rows + height * (k // across), height), pl.ds(lanes * (k % across), lanes)] = part


def spread_mixed(inn, out, give, total):
    full, proj, gain, shift, bias, up_bias = out
    c = lax.axis_index("ctx")
    span = full.shape[1] // (3 * CTX)
    cut, lanes, rows = PART // CTX, 128, full.shape[0]
    height, across = cut + SMALL, inn(0).shape[1] // lanes
    total[...] = jnp.zeros_like(total)
    for d in range(CTX):
        block = inn(d)
        for part in range(3):
            full[:, at(part * CTX + (c ^ d), span)] = floats(block[pl.ds(0, rows), pl.ds(span * part, span)])
        for k in range(proj.shape[1] // lanes):
            top, left = rows + height * (k // across), pl.ds(lanes * (k % across), lanes)
            proj[at(c ^ d, cut), pl.ds(lanes * k, lanes)] = floats(block[pl.ds(top, cut), left])
            if lanes * k < PART:
                total[:, pl.ds(lanes * k, lanes)] += floats(block[pl.ds(top + cut, SMALL), left])
    for i, ref in enumerate((gain, shift, bias)):
        ref[...] = total[pl.ds(4 * i, 4), :]
    for i in range(4):
        up_bias[pl.ds(PART * i, PART)] = total[12 + i, :]


def spread_down(inn, out, give, sems, result):
    c = lax.axis_index("ctx")
    stores = []
    for d in range(CTX):
        block = inn(d)
        rows = at(c ^ d, block.shape[0])
        out[0][rows, :] = floats(block[...])
        stores.append(pltpu.make_async_copy(out[0].at[rows, :], result.at[rows, :], sems.at[d]))
        stores[-1].start()
    for store in stores:
        store.wait()


def spread_up(inn, out, give, sems, result):
    c, w = lax.axis_index("ctx"), lax.axis_index("wt")
    cut = PART // CTX
    width = out[0].shape[1] // WT
    stores = []
    for d in range(CTX):
        block, rows = inn(d), at(c ^ d, cut)
        for k in range(WT):
            out[0][rows, at(w ^ k, width)] = floats(block[pl.ds(cut * k, cut), :])
        stores.append(pltpu.make_async_copy(out[0].at[rows, :], result.at[rows, :], sems.at[d]))
        stores[-1].start()
    for store in stores:
        store.wait()


def split_device(
    layer_input,
    out_grad,
    deal,
    w_qkv,
    w_out,
    w_up,
    w_down,
    norm_gain,
    norm_shift,
    bias_width,
    up_bias,
):
    _, rows, width = layer_input.shape
    w = lax.axis_index("wt")
    per = HEADS // CTX
    span = per * (width // HEADS)
    length = rows * CTX
    hidden_width = w_down.shape[0]
    everyone = WT * rows
    own, grad = layer_input[0], out_grad[0]
    vmem, dma = pltpu.VMEM, pltpu.SemaphoreType.DMA

    sequence = gather_ctx(own)
    begin = lax.optimization_barrier((w_qkv, w_up, norm_gain, norm_shift, bias_width, sequence[1]))[:5]
    pack, *ups = call(
        prepare,
        "prepare",
        begin,
        [shape(PART + SMALL, 3 * span)] + [shape(PART, hidden_width)] * 3,
        raw=(0, 1),
        hbm=(2, 3, 4),
        scratch=[dma((6,))],
    )
    packs = gather_wt(pack)
    up_core, up_x, up_both = ups
    outs_x = swap(after(w_out, packs[2]), "wt", 2)
    up_x = swap(after(up_x, packs[2]), "wt", 2)

    first, mixed, sent, stats, small = call(
        attend,
        "attend",
        (deal, *packs, *sequence),
        [
            shape(length, width),
            shape(length, 3 * span),
            shape(CTX, rows, span),
            shape(2 * per, length, dtype=F32),
            shape(SMALL, width, dtype=F32),
        ],
        smem=1,
        hbm=range(1, 1 + WT),
        raw=range(1 + WT, 1 + WT + CTX),
        hbm_out=(0, 1),
        scratch=[vmem((length, width), BF16), vmem((length, span), BF16), dma((2 * CTX,))],
    )
    attended = lax.all_to_all(after(sent, outs_x, up_x), "ctx", 0, 0, tiled=True)
    up_both = swap(up_both, "wt", 3)
    outs_own, outs_x, up_core = lax.optimization_barrier((w_out, outs_x, up_core, sent))[:3]
    outs = w_out, swap(outs_own, "wt", 1), outs_x, swap(outs_x, "wt", 1)
    ups = w_up, swap(up_core, "wt", 1), up_x, up_both
    attended = after(attended, *outs, *ups[1:])

    branch, resid, second = call(
        project,
        "project",
        (small, attended, own, *outs),
        [shape(rows, width, dtype=F32), shape(rows, width, dtype=F32), shape(rows, width)],
    )

    own_columns = ((PART, hidden_width), lambda ref: ref.at[:, at(lax.axis_index("wt"), hidden_width)])
    halves = [shape(2 * rows, width, dtype=F32), shape(2 * rows, width)]
    seconds, hidden, slope, near, far = call(
        feed,
        "feed",
        (*gather_wt(second), *ups, up_bias.reshape(1, hidden_width), w_down),
        [shape(everyone, width), shape(everyone, hidden_width), shape(everyone, hidden_width, dtype=F32)]
        + halves,
        hbm=(4, 8, 9),
        hbm_out=(0,),
        views={4: own_columns},
    )

    def return_rows(near, far):
        got = swap(far, "wt", 1)
        back = call(add_rest, "add_rest", (near, got), [shape(rows, width)])
        return near, got, swap(back, "wt", 2)

    result, d_ffn, sums3 = call(
        top_norm,
        "top_norm",
        (*return_rows(near, far), small, resid, grad),
        [shape(rows, width), shape(rows, width), shape(3, width, dtype=F32)],
    )
    d_ffns, d_upper, near, far, up_sum = call(
        feed_back,
        "feed_back",
        (*gather_wt(d_ffn), w_down, slope, *ups),
        [shape(everyone, width), shape(everyone, hidden_width)] + halves + [shape(1, hidden_width, dtype=F32)],
        hbm=(4, 6),
        views={6: own_columns},
    )
    got = swap(far, "wt", 1)
    def sends(terms):
        if len(terms) == 3:
            whole = swap(terms[2], "ctx", 1)
            return (whole, 0), (whole, 2)
        return (swap(terms[2], "ctx", 1), 0), (swap(terms[3], "ctx", 1), 0)

    def chunks(split):
        sent = [shape(2, eighth, width)] * 2 if split else [shape(4, eighth, width)]
        return [shape(2, eighth, width)] * 2 + sent

    def added_high(name, terms, got):
        return call(
            add_high,
            "add_high_" + name,
            (terms[1], got),
            [shape(2, eighth, width)],
            hbm=(0,),
        )

    def added_low(name, terms, got, along):
        return call(
            functools.partial(add_low, got[1]),
            "add_low_" + name,
            (terms[0], got[0], along),
            [shape(eighth, width, dtype=F32), shape(eighth, width)],
            hbm=(0,),
        )

    eighth = hidden_width // CTX
    cut = PART // CTX
    terms_a = call(
        grad_down, "grad_down", (hidden, d_ffns), chunks(SPLIT[0]), hbm_out=range(3 + SPLIT[0])
    )
    high_got_a, low_got_a = sends(terms_a)
    back = call(add_rest, "add_rest", (after(near, terms_a[2]), got), [shape(rows, width)])
    far = swap(back, "wt", 2)
    terms_b = call(
        grad_up,
        "grad_up",
        (seconds, d_upper),
        chunks(SPLIT[1]),
        hbm=(0,),
        hbm_out=range(3 + SPLIT[1]),
        scratch=[vmem((PART, hidden_width), BF16)],
    )
    high_got_b, low_got_b = sends(terms_b)
    high_a = added_high("a", terms_a, high_got_a[0])
    next_a = swap(high_a, "ctx", 2)
    far = after(far, terms_b[2])
    sent, d_att, d_resid, sums21 = call(
        middle_norms,
        "middle_norms",
        (near, got, far, small, resid, branch, grad, *outs),
        [
            shape(CTX, rows, span),
            shape(rows, width),
            shape(rows, width, dtype=F32),
            shape(5, width, dtype=F32),
        ],
    )
    got = lax.all_to_all(sent, "ctx", 0, 0, tiled=True)
    pieces = [shape(2, PART, width)] * 2
    keep_out, send_out = call(
        grad_out, "grad_out", (attended, d_att), pieces, hbm_out=(0, 1)
    )
    got_out = swap(send_out, "wt", 1)
    back_out = call(
        add_second,
        "add_second_out",
        (keep_out, got_out),
        [shape(PART, width)],
        hbm=(0,),
    )
    out_x = swap(back_out, "wt", 2)
    high_b = added_high("b", terms_b, after(high_got_b[0], got))
    next_b = swap(high_b, "ctx", 2)
    first_a, second_a = added_low("a", terms_a, low_got_a, next_a)
    last_a = swap(second_a, "ctx", 4)

    natural, dealt = call(
        attend_back,
        "attend_back",
        (deal, mixed, stats, got),
        [shape(length, 3 * span), shape(CTX, rows, 3 * span)],
        smem=1,
        hbm=(1,),
        scratch=[vmem((length, span), BF16), vmem((length, span), F32), vmem((length, span), F32)],
    )
    first_b, second_b = added_low("b", terms_b, low_got_b, after(next_b, low_got_a[0]))
    last_b = swap(second_b, "ctx", 4)
    part_a = call(add_last, "add_last_a", (first_a, last_a), [shape(eighth, width)])
    down_slots = gather_free(after(part_a, back), go2=(high_b, back,), go1=(terms_b[2],))
    pieces = [shape(2, PART, 3 * span)] * 2
    keep_qkv, send_qkv = call(
        grad_qkv, "grad_qkv", (first, after(natural, last_a, second_b)), pieces, hbm=(0,), hbm_out=(0, 1)
    )
    keep_c, send_c = call(
        add_out,
        "add_out",
        (keep_out, got_out, after(out_x, natural)),
        [shape(4, cut, width)] * 2,
        hbm=(0,),
        scratch=[vmem((PART, width), BF16)],
    )
    got_c = swap(send_c, "ctx", 1)
    got_rows = lax.all_to_all(after(dealt, down_slots[1], send_c), "ctx", 0, 0, tiled=True)
    got_qkv = swap(send_qkv, "wt", 1)
    back_qkv = call(
        add_second,
        "add_second_qkv",
        (keep_qkv, got_qkv),
        [shape(PART, 3 * span)],
        hbm=(0,),
    )
    qkv_x = swap(back_qkv, "wt", 2)
    own_up, *up_parts = call(
        add_last_up,
        "add_last_up",
        (first_b, after(last_b, part_a, terms_b[2])),
        [shape(cut, width)] * WT,
        scratch=[vmem((eighth, width), BF16)],
    )
    up_parts = [swap(part, "wt", d) for part, d in zip(up_parts, (1, 2, 3))]
    up_block = call(
        pack_up, "pack_up", (after(own_up, down_slots[1], send_c), *up_parts), [shape(eighth, width)]
    )
    up_slots = gather_free(up_block, far=(next_a,))
    weights_x = swap(after(w_qkv, far), "wt", 2)
    qkv_own, weights_x = after(w_qkv, second_b), weights_x
    all_qkv = w_qkv, swap(qkv_own, "wt", 1), weights_x, swap(weights_x, "wt", 1)
    high_c = call(
        add_high_last, "add_high_c", (keep_c, got_c), [shape(2, cut, width)]
    )
    next_c = swap(high_c, "ctx", 2)
    first_c, second_c = call(
        functools.partial(add_low, 0),
        "add_low_c",
        (keep_c, got_c, after(next_c, low_got_a[0])),
        [shape(cut, width, dtype=F32), shape(cut, width)],
    )
    last_c = swap(second_c, "ctx", 4)
    input_grad, keep, send = call(
        bottom_norm,
        "bottom_norm",
        (after(got_rows, back_qkv), own, d_resid, small, *all_qkv, sums21, sums3, up_sum),
        [shape(rows, width, dtype=F32)] + [shape(2, SMALL, PART, dtype=F32)] * 2,
        hbm=(1, 2, 4, 5, 6, 7),
        hbm_out=(0,),
        scratch=[vmem((rows, 3 * width), BF16), vmem((rows, width), F32)],
    )
    got_sums = swap(send, "wt", 1)
    back_sums = call(add_second, "add_second_sums", (keep, got_sums), [shape(SMALL, PART, dtype=F32)])
    sums_x = swap(back_sums, "wt", 2)
    mixed_block = call(
        pack_mixed,
        "pack_mixed",
        (keep_qkv, got_qkv, after(qkv_x, up_slots[3], sums_x), first_c, last_c, keep, got_sums, sums_x),
        [shape(PART + 3 * (cut + SMALL), 3 * span)],
        hbm=(0,),
        scratch=[vmem((cut + SMALL, width), BF16)],
    )
    mixed_slots = gather_ctx_z(mixed_block)
    full_qkv, full_out, gain, shift, bias, up_total = call(
        spread_mixed,
        "spread_mixed",
        mixed_slots,
        [shape(PART, 3 * width, dtype=F32), shape(PART, width, dtype=F32)]
        + [shape(4, PART, dtype=F32)] * 3
        + [shape(hidden_width, dtype=F32)],
        hbm_out=range(6),
        scratch=[vmem((SMALL, PART), F32)],
    )
    full_down = call(
        spread_down,
        "spread_down",
        down_slots,
        [shape(hidden_width, width, dtype=F32)],
        hbm_out=(0,),
        scratch=[dma((CTX,))],
        parts=(0,),
    )
    full_up = call(
        spread_up,
        "spread_up",
        up_slots,
        [shape(PART, WT * hidden_width, dtype=F32)],
        hbm_out=(0,),
        scratch=[dma((CTX,))],
        parts=(0,),
    )
    return (
        result[None],
        input_grad[None],
        full_qkv,
        full_out,
        full_up,
        full_down,
        gain,
        shift,
        bias,
        up_total,
    )


def solution(mesh):
    small = mesh.shape["ctx"] == CTX and mesh.shape["wt"] == WT
    per_device = split_device if small else general_device
    in_specs = (
        P("wt", "ctx", None),
        P("wt", "ctx", None),
        P(),
        P("wt", None),
        P("wt", None),
        P("wt", None),
        P("wt", None),
        P(None, "wt"),
        P(None, "wt"),
        P(None, "wt"),
        P("wt"),
    )
    out_specs = (
        P("wt", "ctx", None),
        P("wt", "ctx", None),
        P("wt", None),
        P("wt", None),
        P("wt", None),
        P("wt", None),
        P(None, "wt"),
        P(None, "wt"),
        P(None, "wt"),
        P("wt"),
    )
    return jax.shard_map(
        per_device, mesh=mesh, in_specs=in_specs, out_specs=out_specs, check_vma=False
    )
```
